32 devices in a mesh: batch: 4 (over z), expert: 8 (over y, x, core).
Axes of the slice: x: 2, y: 2, z: 4, core: 2. Of those that a mesh axis runs over, the one named last changes fastest.
Arguments:
- tokens: bfloat16 [8192, 1024], P(('batch', 'expert')), may hold values from -6 to 6
- doc_ends: int32 [32, 4], P(('batch', 'expert')), may hold values from 8 to 256, as said below
- routes: int32 [8192, 1], P(('batch', 'expert')), may hold values from 0 to 7, as said below
- w_query: bfloat16 [1024, 1024], replicated, may hold values from -0.1875 to 0.1875
- w_key: bfloat16 [1024, 1024], replicated, may hold values from -0.1875 to 0.1875
- w_value: bfloat16 [1024, 1024], replicated, may hold values from -0.1875 to 0.1875
- w_output: bfloat16 [1024, 1024], replicated, may hold values from -0.5 to 0.5
- attn_gain: float32 [1024], replicated, may hold values from 0.1 to 1.9
- centroids: float32 [8, 1024], replicated, may hold values from -0.15 to 0.15
- up_first: bfloat16 [8, 1024, 4096], P('expert'), may hold values from -0.1875 to 0.1875
- down_first: bfloat16 [8, 4096, 1024], P('expert'), may hold values from -0.09375 to 0.09375
- gain_first: float32 [8, 1024], P('expert'), may hold values from 0.1 to 1.9
- up_second: bfloat16 [8, 1024, 4096], P('expert'), may hold values from -0.1875 to 0.1875
- down_second: bfloat16 [8, 4096, 1024], P('expert'), may hold values from -0.09375 to 0.09375
- gain_second: float32 [8, 1024], P('expert'), may hold values from 0.1 to 1.9
- cotangent: bfloat16 [8192, 1024], P(('batch', 'expert')), may hold values from -6 to 6
Outputs:
- block_out: bfloat16 [8192, 1024], P(('batch', 'expert'))
- grad_tokens: float32 [8192, 1024], P(('batch', 'expert'))
- grad_query: float32 [1024, 1024], P(('batch', 'expert'))
- grad_key: float32 [1024, 1024], P(('batch', 'expert'))
- grad_value: float32 [1024, 1024], P(('batch', 'expert'))
- grad_output: float32 [1024, 1024], P(('batch', 'expert'))
- grad_attn_gain: float32 [1024], replicated
- grad_centroids: float32 [8, 1024], replicated
- grad_up_first: float32 [8, 1024, 4096], P('expert', None, 'batch')
- grad_down_first: float32 [8, 4096, 1024], P('expert', 'batch')
- grad_gain_first: float32 [8, 1024], P('expert', 'batch')
- grad_up_second: float32 [8, 1024, 4096], P('expert', None, 'batch')
- grad_down_second: float32 [8, 4096, 1024], P('expert', 'batch')
- grad_gain_second: float32 [8, 1024], P('expert', 'batch')
The draws below stay inside these ranges and needn't reach their ends.
Inputs may be any that keep to these rules, and one draw needn't show every extreme that they name: `routes`: each device's 256 slots send at most 44 to any one expert; one expert, chosen by the draw, receives exactly 44 slots from every device. `doc_ends`: each row holds 4 nondecreasing document ends of one device's slots; slots at or past the last end are padding; a document may be empty; on some device the last end is 256, and on some device the first end is 8.
All inputs are finite; a program needn't handle non-finite values.
Results may differ from the reference program's by a relative error of at most 0.014.
Values may be sent and summed in bfloat16 or wider, within the bound.
A program may use at most 256 MiB of HBM per device.

```python
import jax
import jax.numpy as jnp
from jax import lax

D = 1024
HEADS = 16
HEAD_DIM = 64
FF = 4096
TOK_DEV = 256
DOCS = 4
EXPERTS = 8
CAP = 44
TOKENS = 8192


def draw_routes(key, part):
    devices_all = TOKENS // TOK_DEV
    crowded = jax.random.randint(jax.random.fold_in(key, 11), (), 0, EXPERTS)
    device_keys = jax.random.split(jax.random.fold_in(key, 12), devices_all)

    def one_device(dev_key):
        first_key, second_key = jax.random.split(dev_key)
        others = jax.random.permutation(first_key, (EXPERTS - 1) * CAP)[:TOK_DEV - CAP] // CAP
        labels = jnp.concatenate([jnp.zeros((CAP,), jnp.int32) + crowded, ((crowded + 1 + others) % EXPERTS).astype(jnp.int32)])
        return jax.random.permutation(second_key, labels)
    return jax.vmap(one_device)(device_keys).reshape(TOKENS, 1).astype(jnp.int32)


def draw_doc_ends(key, part):
    devices_all = TOKENS // TOK_DEV
    stride = TOK_DEV // 32
    octave = jax.random.randint(jax.random.fold_in(key, 21), (devices_all, DOCS), 0, 4)
    spread = stride * jnp.left_shift(jnp.ones_like(octave), octave)
    jitter = jax.random.randint(jax.random.fold_in(key, 22), (devices_all, DOCS), 0, 1 << 20) % spread
    lengths = spread + jitter
    shortest = jax.random.randint(jax.random.fold_in(key, 24), (), 0, devices_all)
    lengths = lengths.at[shortest, 0].set(stride)
    ends_all = jnp.minimum(jnp.cumsum(lengths, axis=1), TOK_DEV)
    filled = jax.random.randint(jax.random.fold_in(key, 23), (), 0, devices_all)
    return ends_all.at[filled, DOCS - 1].set(TOK_DEV).astype(jnp.int32)


def level_of(rng, dims, pieces, low, top_value):
    def one(axis_at, parts):
        heights = jax.random.uniform(jax.random.fold_in(jax.random.fold_in(rng, 6), axis_at), (parts,), jnp.float32, low / len(pieces), top_value / len(pieces))
        return jnp.repeat(jnp.exp(heights), dims[axis_at] // parts).reshape((-1,) + (1,) * (len(dims) - axis_at - 1))

    loudness = one(*pieces[0])
    for cut in pieces[1:]:
        loudness = loudness * one(*cut)
    return loudness


def bell_draw(key, extent, deviation, most, cuts=(), held_as=jnp.bfloat16):
    gain = level_of(key, extent, cuts, -0.22, 0.18) if cuts else 1.0
    entries = jax.random.normal(key, extent, jnp.float32) * deviation * gain
    return jnp.minimum(jnp.maximum(entries, -most), most).astype(held_as)


def setup_inputs(seed: int = 0) -> dict:
    streams_of = jax.random.split(jax.random.key(seed), 17)
    tokens = bell_draw(streams_of[0], (TOKENS, D), 1.0, 6.0, ((0, 32),))
    doc_ends = draw_doc_ends(jax.random.fold_in(streams_of[16], 71), 0)
    routes = draw_routes(jax.random.fold_in(streams_of[16], 71), 0)
    w_query = bell_draw(streams_of[3], (D, D), D ** -0.5, 0.1875)
    w_key = bell_draw(streams_of[4], (D, D), D ** -0.5, 0.1875)
    w_value = bell_draw(streams_of[5], (D, D), D ** -0.5, 0.1875)
    w_output = bell_draw(streams_of[6], (D, D), (D // 8) ** -0.5, 0.5)
    attn_gain = jnp.clip(1.0 + 0.18 * jax.random.normal(streams_of[7], (D,), jnp.float32), 0.1, 1.9)
    centroids = bell_draw(streams_of[8], (EXPERTS, D), 0.025, 0.15, (), jnp.float32)
    up_first = bell_draw(streams_of[9], (EXPERTS, D, FF), D ** -0.5, 0.1875, ((0, 8),))
    down_first = bell_draw(streams_of[10], (EXPERTS, FF, D), FF ** -0.5, 0.09375, ((0, 8),))
    gain_first = jnp.clip(1.0 + 0.18 * jax.random.normal(streams_of[11], (EXPERTS, D), jnp.float32), 0.1, 1.9)
    up_second = bell_draw(streams_of[12], (EXPERTS, D, FF), D ** -0.5, 0.1875, ((0, 8),))
    down_second = bell_draw(streams_of[13], (EXPERTS, FF, D), FF ** -0.5, 0.09375, ((0, 8),))
    gain_second = jnp.clip(1.0 + 0.18 * jax.random.normal(streams_of[14], (EXPERTS, D), jnp.float32), 0.1, 1.9)
    cotangent = bell_draw(streams_of[15], (TOKENS, D), 1.0, 6.0, ((0, 32),))
    return {"tokens": tokens, "doc_ends": doc_ends, "routes": routes, "w_query": w_query, "w_key": w_key, "w_value": w_value, "w_output": w_output, "attn_gain": attn_gain, "centroids": centroids, "up_first": up_first, "down_first": down_first, "gain_first": gain_first, "up_second": up_second, "down_second": down_second, "gain_second": gain_second, "cotangent": cotangent}


@jax.custom_vjp
def low(v):
    return lax.optimization_barrier(v.astype(jnp.bfloat16)).astype(jnp.float32)

@jax.custom_vjp
def low_back(v):
    return v

def low_keep(v):
    return (low(v), None)

def low_pass(kept, grad):
    return (grad,)

def back_keep(v):
    return (v, None)

def back_low(kept, grad):
    return (low(grad),)
low.defvjp(low_keep, low_pass)
low_back.defvjp(back_keep, back_low)
EPSILON = 1e-05
MASKED = -1e+30
HIGHEST = lax.Precision.HIGHEST

def rounded_both(value):
    return low(low_back(value))

def layer_norm(stream, gain_vec):
    average = lax.optimization_barrier(jnp.mean(stream, axis=-1, keepdims=True))
    centred = stream - average
    variance = lax.optimization_barrier(jnp.mean(centred * centred, axis=-1, keepdims=True))
    return centred * lax.rsqrt(variance + EPSILON) * gain_vec

def sublayer(stream, up_proj, down_proj, gain_vec):
    normed = low(layer_norm(stream, gain_vec))
    pre_act = low_back(jnp.dot(normed, up_proj, precision=HIGHEST))
    middle = low(jax.nn.gelu(pre_act))
    return stream + low_back(jnp.dot(middle, down_proj, precision=HIGHEST))

def reference(tokens, doc_ends, routes, w_query, w_key, w_value, w_output, attn_gain, centroids, up_first, down_first, gain_first, up_second, down_second, gain_second, cotangent):
    groups = TOKENS // TOK_DEV
    route_flat = routes[:, 0]
    route_grid = route_flat.reshape(groups, TOK_DEV)
    expert_ids = jnp.arange(EXPERTS, dtype=jnp.int32)
    ones_grid = (route_grid[:, :, None] == expert_ids[None, None, :]).astype(jnp.int32)
    ranking = lax.optimization_barrier(jnp.sum(jnp.cumsum(ones_grid, axis=1) * ones_grid, axis=2)) - 1
    owners = jnp.arange(groups, dtype=jnp.int32)[:, None]
    slot_index = (route_grid * (groups * CAP) + owners * CAP + ranking).reshape(TOKENS).astype(jnp.int32)
    chosen = (route_flat[:, None] == expert_ids[None, :]).astype(jnp.float32)
    position = jnp.arange(TOK_DEV, dtype=jnp.int32)
    live_mask = (position[None, :] < doc_ends[:, -1:]).astype(jnp.float32).reshape(TOKENS, 1)
    factor = HEAD_DIM ** (-0.5)

    def forward(stream, wq, wk, wv, wo, gain_att, cents, up_one, down_one, gain_one, up_two, down_two, gain_two):
        normed = low(layer_norm(stream, gain_att))

        def attend(packed):
            rows, ends_row = packed
            segment = lax.optimization_barrier(jnp.sum((position[:, None] >= ends_row[None, :]).astype(jnp.int32), axis=1))
            allowed = (segment[:, None] == segment[None, :]) & (position[None, :] <= position[:, None])
            queries = rounded_both(jnp.dot(rows, wq, precision=HIGHEST)).reshape(TOK_DEV, HEADS, HEAD_DIM)
            key_rows = rounded_both(jnp.dot(rows, wk, precision=HIGHEST)).reshape(TOK_DEV, HEADS, HEAD_DIM)
            value_rows = rounded_both(jnp.dot(rows, wv, precision=HIGHEST)).reshape(TOK_DEV, HEADS, HEAD_DIM)
            raw = low_back(jnp.einsum('qhd,khd->hqk', queries, key_rows, precision=HIGHEST))
            scores = jnp.where(allowed[None], raw * factor, MASKED)
            shares = low(jax.nn.softmax(scores, axis=-1))
            mixed = jnp.einsum('hqk,khd->qhd', shares, value_rows, precision=HIGHEST)
            return rounded_both(mixed.reshape(TOK_DEV, D))
        attended = lax.map(jax.checkpoint(attend), (normed.reshape(groups, TOK_DEV, D), doc_ends))
        hidden = stream + low_back(jnp.dot(attended.reshape(TOKENS, D), wo, precision=HIGHEST))
        score = lax.optimization_barrier(jnp.sum(jnp.dot(hidden, cents.T, precision=HIGHEST) * chosen, axis=1, keepdims=True))
        gating = jax.nn.sigmoid(score)
        routed = rounded_both(hidden)
        buffer = jnp.zeros((EXPERTS * groups * CAP, D), jnp.float32).at[slot_index].set(routed)
        buffer = buffer.reshape(EXPERTS, groups * CAP, D)

        def run_expert(packed):
            rows, up_a, down_a, gain_a, up_b, down_b, gain_b = packed
            middle = sublayer(rows, up_a, down_a, gain_a)
            return sublayer(middle, up_b, down_b, gain_b)
        outputs = rounded_both(lax.map(jax.checkpoint(run_expert), (buffer, up_one, down_one, gain_one, up_two, down_two, gain_two)))
        returned = outputs.reshape(EXPERTS * groups * CAP, D)[slot_index]
        return live_mask * (gating * returned + (1.0 - gating) * hidden)
    primals = (tokens.astype(jnp.float32), w_query.astype(jnp.float32), w_key.astype(jnp.float32), w_value.astype(jnp.float32), w_output.astype(jnp.float32), attn_gain, centroids, up_first.astype(jnp.float32), down_first.astype(jnp.float32), gain_first, up_second.astype(jnp.float32), down_second.astype(jnp.float32), gain_second)
    result, pullback = jax.vjp(forward, *primals)
    grads = pullback(cotangent.astype(jnp.float32))
    return (result.astype(jnp.bfloat16), grads[0], grads[1], grads[2], grads[3], grads[4], grads[5], grads[6], grads[7], grads[8], grads[9], grads[10], grads[11], grads[12])
```

```python
import jax
import jax.numpy as jnp
from jax import lax
from jax.sharding import PartitionSpec as P

HEADS = 16


EPSILON = 1e-05
MASKED = -1e30
HIGHEST = lax.Precision.HIGHEST


def layer_norm(stream, gain_vec):
    average = jnp.mean(stream, axis=-1, keepdims=True)
    centred = stream - average
    variance = jnp.mean(centred * centred, axis=-1, keepdims=True)
    return centred * lax.rsqrt(variance + EPSILON) * gain_vec


def block_scores(query_blk, key_rows, segment_blk, place_blk, segment, place, factor):
    raw = jnp.einsum("qhd,khd->hqk", query_blk, key_rows, preferred_element_type=jnp.float32)
    allowed = (segment_blk[:, None] == segment[None, :]) & (place[None, :] <= place_blk[:, None])
    return jnp.where(allowed[None], raw * factor, MASKED)


def attend_forward(queries, key_rows, value_rows, segment, place):
    tok_rows, head_count, head_width = queries.shape
    block_rows = min(512, tok_rows)
    factor = head_width ** (-0.5)

    def one_block(block_index):
        scores = block_scores(queries, key_rows, segment, place, segment, place, factor)
        row_peak = jnp.max(scores, axis=-1, keepdims=True)
        raised = jnp.exp(scores - row_peak)
        summed = jnp.sum(raised, axis=-1, keepdims=True)
        shares = (raised / summed).astype(jnp.bfloat16)
        mixed = jnp.einsum("hqk,khd->qhd", shares, value_rows, preferred_element_type=jnp.float32)
        return (mixed.astype(jnp.bfloat16), (row_peak + jnp.log(summed))[..., 0])

    mixed, log_total = lax.map(one_block, jnp.arange(tok_rows // block_rows))
    return (mixed.reshape(tok_rows, head_count * head_width), log_total)


def attend_backward(grad_mixed, queries, key_rows, value_rows, log_total, segment, place):
    tok_rows, head_count, head_width = queries.shape
    block_rows = min(512, tok_rows)
    factor = head_width ** (-0.5)

    def one_block(running, block_index):
        grad_keys, grad_values = running
        scores = block_scores(queries, key_rows, segment, place, segment, place, factor)
        row_total = lax.dynamic_index_in_dim(log_total, block_index, 0, keepdims=False)
        shares = jnp.exp(scores - row_total[..., None])
        shares_low = shares.astype(jnp.bfloat16)
        grad_shares = jnp.einsum(
            "qhd,khd->hqk", grad_mixed, value_rows, preferred_element_type=jnp.float32
        )
        grad_values = grad_values + jnp.einsum(
            "hqk,qhd->khd", shares_low, grad_mixed, preferred_element_type=jnp.float32
        )
        grad_scores = shares * (grad_shares - jnp.sum(shares * grad_shares, axis=-1, keepdims=True))
        grad_raw = (grad_scores * factor).astype(jnp.bfloat16)
        grad_query_blk = jnp.einsum(
            "hqk,khd->qhd", grad_raw, key_rows, preferred_element_type=jnp.float32
        )
        grad_keys = grad_keys + jnp.einsum(
            "hqk,qhd->khd", grad_raw, queries, preferred_element_type=jnp.float32
        )
        return ((grad_keys, grad_values), grad_query_blk)

    empty = jnp.zeros(queries.shape, jnp.float32)
    (grad_keys, grad_values), grad_queries = lax.scan(
        one_block, (empty, empty), jnp.arange(tok_rows // block_rows)
    )
    width_all = head_count * head_width
    return tuple(
        (
            member.reshape(tok_rows, width_all).astype(jnp.bfloat16)
            for member in (grad_queries, grad_keys, grad_values)
        )
    )


def sublayer_forward(stream, up_proj, down_proj, gain_vec):
    normed = layer_norm(stream, gain_vec).astype(jnp.bfloat16)
    pre_act = jnp.dot(normed, up_proj, preferred_element_type=jnp.float32)
    middle = jax.nn.gelu(pre_act).astype(jnp.bfloat16)
    result = stream + jnp.dot(middle, down_proj, preferred_element_type=jnp.float32)
    return (result, (stream, normed, pre_act, middle))


def sublayer_backward(grad_result, kept, up_proj, down_proj, gain_vec):
    stream, normed, pre_act, middle = kept
    grad_low = grad_result.astype(jnp.bfloat16)
    grad_middle = jnp.einsum("rd,fd->rf", grad_low, down_proj, preferred_element_type=jnp.float32)
    gelu_pull = jax.vjp(jax.nn.gelu, pre_act)[1]
    grad_pre = gelu_pull(grad_middle)[0].astype(jnp.bfloat16)
    grad_normed = jnp.einsum("rf,df->rd", grad_pre, up_proj, preferred_element_type=jnp.float32)
    norm_pull = jax.vjp(layer_norm, stream, gain_vec)[1]
    grad_stream, grad_gain = norm_pull(grad_normed)
    return (grad_result + grad_stream, grad_low, grad_gain)


def ring_rows(rows, axis):
    count = lax.axis_size(axis)
    back = [(i, (i - 1) % count) for i in range(count)]
    held = [rows]
    for _ in range(count - 1):
        held.append(lax.ppermute(held[-1], axis, back))
    return jnp.concatenate(held, axis=0)


def weight_grads(normed_rows, grad_rows, up_proj, down_proj):
    count = lax.axis_size("batch")
    width = up_proj.shape[1] // count
    first = lax.axis_index("batch") * width
    up_part = lax.dynamic_slice_in_dim(up_proj, first, width, 1)
    down_part = lax.dynamic_slice_in_dim(down_proj, first, width, 0)
    pre_act = jnp.dot(normed_rows, up_part, preferred_element_type=jnp.float32)
    middle, gelu_pull = jax.vjp(jax.nn.gelu, pre_act)
    grad_middle = jnp.einsum("rd,fd->rf", grad_rows, down_part, preferred_element_type=jnp.float32)
    grad_pre = gelu_pull(grad_middle)[0].astype(jnp.bfloat16)
    grad_down = jnp.einsum(
        "rf,rd->fd", middle.astype(jnp.bfloat16), grad_rows, preferred_element_type=jnp.float32
    )
    grad_up = jnp.einsum("rd,rf->df", normed_rows, grad_pre, preferred_element_type=jnp.float32)
    return grad_up, grad_down


def halve(blocks, axis, bit, dim):
    count = lax.axis_size(axis)
    mine = (lax.axis_index(axis) // bit) % 2
    kept = lax.dynamic_index_in_dim(blocks, mine, dim, keepdims=False)
    sent = lax.dynamic_index_in_dim(blocks, 1 - mine, dim, keepdims=False)
    got = lax.ppermute(sent, axis, [(i, i ^ bit) for i in range(count)])
    return (kept.astype(jnp.float32) + got.astype(jnp.float32)).astype(blocks.dtype)


def scatter_sum(parts):
    experts, groups = lax.axis_size("expert"), lax.axis_size("batch")
    kinds, rows, width = parts.shape
    bits_e = experts.bit_length() - 1
    bits_b = groups.bit_length() - 1
    shape = (kinds,) + (2,) * (bits_b + bits_e) + (rows // (experts * groups), width)
    blocks = parts.reshape(shape)
    for k in range(bits_e):
        blocks = halve(blocks, "expert", 1 << k, bits_b + bits_e - k)
    for k in range(bits_b):
        blocks = halve(blocks, "batch", 1 << k, bits_b - k)
    return blocks


def all_sum(value):
    for axis in ("expert", "batch"):
        count = lax.axis_size(axis)
        bit = 1
        while bit < count:
            value = value + lax.ppermute(value, axis, [(i, i ^ bit) for i in range(count)])
            bit *= 2
    return value


def slot_layout(tokens, routes):
    tok_rows = tokens.shape[0]
    expert_count = lax.axis_size("expert")
    capacity = 11 * tok_rows // (8 * expert_count)
    ones_int = (routes == jnp.arange(expert_count, dtype=jnp.int32)[None, :]).astype(jnp.int32)
    ranking = jnp.sum(jnp.cumsum(ones_int, axis=0) * ones_int, axis=1) - 1
    slot_index = routes[:, 0] * capacity + ranking
    return (expert_count, capacity, ones_int.astype(jnp.float32), slot_index)


def forward_pass(params):
    (
        tokens,
        doc_ends,
        routes,
        w_query,
        w_key,
        w_value,
        w_output,
        attn_gain,
        centroids,
        up_first,
        down_first,
        gain_first,
        up_second,
        down_second,
        gain_second,
    ) = params
    tok_rows, width_all = tokens.shape
    expert_count, capacity, chosen, slot_index = slot_layout(tokens, routes)
    place = jnp.arange(tok_rows, dtype=jnp.int32)
    segment = jnp.sum((place[:, None] >= doc_ends[0][None, :]).astype(jnp.int32), axis=1)
    live_mask = (place < doc_ends[0, -1]).astype(jnp.float32)[:, None]
    stream = tokens.astype(jnp.float32)
    normed = layer_norm(stream, attn_gain).astype(jnp.bfloat16)
    heads_shape = (tok_rows, HEADS, width_all // HEADS)
    queries = (
        jnp.dot(normed, w_query, preferred_element_type=jnp.float32)
        .astype(jnp.bfloat16)
        .reshape(heads_shape)
    )
    key_rows = (
        jnp.dot(normed, w_key, preferred_element_type=jnp.float32)
        .astype(jnp.bfloat16)
        .reshape(heads_shape)
    )
    value_rows = (
        jnp.dot(normed, w_value, preferred_element_type=jnp.float32)
        .astype(jnp.bfloat16)
        .reshape(heads_shape)
    )
    mixed, log_total = attend_forward(queries, key_rows, value_rows, segment, place)
    hidden = stream + jnp.dot(mixed, w_output, preferred_element_type=jnp.float32)
    score = jnp.sum(jnp.dot(hidden, centroids.T, precision=HIGHEST) * chosen, axis=1, keepdims=True)
    gating = jax.nn.sigmoid(score)
    routed = hidden.astype(jnp.bfloat16)
    outgoing = (
        jnp.zeros((expert_count * capacity, width_all), jnp.bfloat16).at[slot_index].set(routed)
    )
    arrived = lax.all_to_all(
        outgoing.reshape(expert_count, capacity, width_all),
        "expert",
        split_axis=0,
        concat_axis=0,
        tiled=True,
    )
    arrived = arrived.reshape(expert_count * capacity, width_all).astype(jnp.float32)
    stream_one, kept_one = sublayer_forward(arrived, up_first[0], down_first[0], gain_first[0])
    stream_two, kept_two = sublayer_forward(
        stream_one, up_second[0], down_second[0], gain_second[0]
    )
    expert_low = stream_two.astype(jnp.bfloat16).reshape(expert_count, capacity, width_all)
    came_back = lax.all_to_all(expert_low, "expert", split_axis=0, concat_axis=0, tiled=True)
    returned = came_back.reshape(expert_count * capacity, width_all)[slot_index].astype(jnp.float32)
    block_out = (live_mask * (gating * returned + (1.0 - gating) * hidden)).astype(jnp.bfloat16)
    kept = (
        stream,
        normed,
        queries,
        key_rows,
        value_rows,
        log_total,
        mixed,
        hidden,
        gating,
        returned,
        kept_one,
        kept_two,
        segment,
        place,
        live_mask,
    )
    return (block_out, kept)


def per_device(
    tokens,
    doc_ends,
    routes,
    w_query,
    w_key,
    w_value,
    w_output,
    attn_gain,
    centroids,
    up_first,
    down_first,
    gain_first,
    up_second,
    down_second,
    gain_second,
    cotangent,
):
    params = (
        tokens,
        doc_ends,
        routes,
        w_query,
        w_key,
        w_value,
        w_output,
        attn_gain,
        centroids,
        up_first,
        down_first,
        gain_first,
        up_second,
        down_second,
        gain_second,
    )
    block_out, kept = forward_pass(params)
    (
        stream,
        normed,
        queries,
        key_rows,
        value_rows,
        log_total,
        mixed,
        hidden,
        gating,
        returned,
        kept_one,
        kept_two,
        segment,
        place,
        live_mask,
    ) = kept
    tok_rows, width_all = tokens.shape
    expert_count, capacity, chosen, slot_index = slot_layout(tokens, routes)
    grad_block = cotangent.astype(jnp.float32) * live_mask
    grad_sent = (gating * grad_block).astype(jnp.bfloat16)
    grad_gating = jnp.sum(grad_block * (returned - hidden), axis=1, keepdims=True)
    grad_score = grad_gating * gating * (1.0 - gating)
    grad_buffer = (
        jnp.zeros((expert_count * capacity, width_all), jnp.bfloat16).at[slot_index].set(grad_sent)
    )
    grad_rows = lax.all_to_all(
        grad_buffer.reshape(expert_count, capacity, width_all),
        "expert",
        split_axis=0,
        concat_axis=0,
        tiled=True,
    )
    grad_rows = grad_rows.reshape(expert_count * capacity, width_all).astype(jnp.float32)
    grad_stream_one, low_two, gain_two_grad = sublayer_backward(
        grad_rows, kept_two, up_second[0], down_second[0], gain_second[0]
    )
    grad_arrived, low_one, gain_one_grad = sublayer_backward(
        grad_stream_one, kept_one, up_first[0], down_first[0], gain_first[0]
    )
    grad_home = lax.all_to_all(
        grad_arrived.astype(jnp.bfloat16).reshape(expert_count, capacity, width_all),
        "expert",
        split_axis=0,
        concat_axis=0,
        tiled=True,
    )
    grad_routed = grad_home.reshape(expert_count * capacity, width_all)[slot_index].astype(
        jnp.float32
    )
    own_centroid = jnp.dot(chosen, centroids, precision=HIGHEST)
    grad_hidden = (1.0 - gating) * grad_block + grad_routed + grad_score * own_centroid
    grad_centroids = jnp.dot(chosen.T, grad_score * hidden, precision=HIGHEST)
    grad_attn_out = grad_hidden.astype(jnp.bfloat16)
    grad_output_w = jnp.einsum(
        "td,te->de", mixed, grad_attn_out, preferred_element_type=jnp.float32
    )
    grad_mixed = jnp.einsum(
        "te,de->td", grad_attn_out, w_output, preferred_element_type=jnp.float32
    ).astype(jnp.bfloat16)
    grad_q, grad_k, grad_v = attend_backward(
        grad_mixed.reshape(queries.shape), queries, key_rows, value_rows, log_total, segment, place
    )
    grad_query_w = jnp.einsum("td,te->de", normed, grad_q, preferred_element_type=jnp.float32)
    grad_key_w = jnp.einsum("td,te->de", normed, grad_k, preferred_element_type=jnp.float32)
    grad_value_w = jnp.einsum("td,te->de", normed, grad_v, preferred_element_type=jnp.float32)
    grad_normed = jnp.einsum("te,de->td", grad_q, w_query, preferred_element_type=jnp.float32)
    grad_normed = grad_normed + jnp.einsum(
        "te,de->td", grad_k, w_key, preferred_element_type=jnp.float32
    )
    grad_normed = grad_normed + jnp.einsum(
        "te,de->td", grad_v, w_value, preferred_element_type=jnp.float32
    )
    norm_pull = jax.vjp(layer_norm, stream, attn_gain)[1]
    grad_input_norm, grad_gain_att = norm_pull(grad_normed)
    grad_tokens = grad_hidden + grad_input_norm
    dense = scatter_sum(
        jnp.stack((grad_query_w, grad_key_w, grad_value_w, grad_output_w)).astype(jnp.bfloat16)
    ).astype(jnp.float32)
    small = all_sum(jnp.concatenate((grad_gain_att[None], grad_centroids), axis=0))
    up_two_grad, down_two_grad = weight_grads(
        ring_rows(kept_two[1], "batch"), ring_rows(low_two, "batch"), up_second[0], down_second[0]
    )
    up_one_grad, down_one_grad = weight_grads(
        ring_rows(kept_one[1], "batch"), ring_rows(low_one, "batch"), up_first[0], down_first[0]
    )
    gains = lax.all_gather(jnp.stack((gain_one_grad, gain_two_grad)), "batch")
    gain_part = gain_one_grad.shape[0] // lax.axis_size("batch")
    gains = lax.dynamic_slice_in_dim(
        jnp.sum(gains, axis=0), lax.axis_index("batch") * gain_part, gain_part, 1
    )
    expert_parts = (
        up_one_grad[None],
        down_one_grad[None],
        gains[0:1],
        up_two_grad[None],
        down_two_grad[None],
        gains[1:2],
    )
    return (
        block_out,
        grad_tokens,
        dense[0],
        dense[1],
        dense[2],
        dense[3],
        small[0],
        small[1:],
        expert_parts[0],
        expert_parts[1],
        expert_parts[2],
        expert_parts[3],
        expert_parts[4],
        expert_parts[5],
    )


def solution(mesh):
    return jax.shard_map(
        per_device,
        mesh=mesh,
        in_specs=(
            P(("batch", "expert"), None),
            P(("batch", "expert"), None),
            P(("batch", "expert"), None),
            P(),
            P(),
            P(),
            P(),
            P(),
            P(),
            P("expert", None, None),
            P("expert", None, None),
            P("expert", None),
            P("expert", None, None),
            P("expert", None, None),
            P("expert", None),
            P(("batch", "expert"), None),
        ),
        out_specs=(
            P(("batch", "expert"), None),
            P(("batch", "expert"), None),
            P(("batch", "expert"), None),
            P(("batch", "expert"), None),
            P(("batch", "expert"), None),
            P(("batch", "expert"), None),
            P(),
            P(),
            P("expert", None, "batch"),
            P("expert", "batch", None),
            P("expert", "batch"),
            P("expert", None, "batch"),
            P("expert", "batch", None),
            P("expert", "batch"),
        ),
        check_vma=False,
    )
```

```python
import functools
import jax, jax.numpy as jnp
from jax import lax
from jax.experimental import pallas as pl
from jax.experimental.pallas import tpu as pltpu

from jax.sharding import PartitionSpec as P

HEADS = 16


EPSILON = 1e-05
MASKED = -1e30
HIGHEST = lax.Precision.HIGHEST


def layer_norm(stream, gain_vec):
    average = jnp.mean(stream, axis=-1, keepdims=True)
    centred = stream - average
    variance = jnp.mean(centred * centred, axis=-1, keepdims=True)
    return centred * lax.rsqrt(variance + EPSILON) * gain_vec


def block_scores(query_blk, key_rows, segment_blk, place_blk, segment, place, factor):
    raw = jnp.einsum("qhd,khd->hqk", query_blk, key_rows, preferred_element_type=jnp.float32)
    allowed = (segment_blk[:, None] == segment[None, :]) & (place[None, :] <= place_blk[:, None])
    return jnp.where(allowed[None], raw * factor, MASKED)


def attend_forward(queries, key_rows, value_rows, segment, place):
    tok_rows, head_count, head_width = queries.shape
    block_rows = min(512, tok_rows)
    factor = head_width ** (-0.5)

    def one_block(block_index):
        scores = block_scores(queries, key_rows, segment, place, segment, place, factor)
        row_peak = jnp.max(scores, axis=-1, keepdims=True)
        raised = jnp.exp(scores - row_peak)
        summed = jnp.sum(raised, axis=-1, keepdims=True)
        shares = (raised / summed).astype(jnp.bfloat16)
        mixed = jnp.einsum("hqk,khd->qhd", shares, value_rows, preferred_element_type=jnp.float32)
        return (mixed.astype(jnp.bfloat16), (row_peak + jnp.log(summed))[..., 0])

    mixed, log_total = lax.map(one_block, jnp.arange(tok_rows // block_rows))
    return (mixed.reshape(tok_rows, head_count * head_width), log_total)


def attend_backward(grad_mixed, queries, key_rows, value_rows, log_total, segment, place):
    tok_rows, head_count, head_width = queries.shape
    block_rows = min(512, tok_rows)
    factor = head_width ** (-0.5)

    def one_block(running, block_index):
        grad_keys, grad_values = running
        scores = block_scores(queries, key_rows, segment, place, segment, place, factor)
        row_total = lax.dynamic_index_in_dim(log_total, block_index, 0, keepdims=False)
        shares = jnp.exp(scores - row_total[..., None])
        shares_low = shares.astype(jnp.bfloat16)
        grad_shares = jnp.einsum(
            "qhd,khd->hqk", grad_mixed, value_rows, preferred_element_type=jnp.float32
        )
        grad_values = grad_values + jnp.einsum(
            "hqk,qhd->khd", shares_low, grad_mixed, preferred_element_type=jnp.float32
        )
        grad_scores = shares * (grad_shares - jnp.sum(shares * grad_shares, axis=-1, keepdims=True))
        grad_raw = (grad_scores * factor).astype(jnp.bfloat16)
        grad_query_blk = jnp.einsum(
            "hqk,khd->qhd", grad_raw, key_rows, preferred_element_type=jnp.float32
        )
        grad_keys = grad_keys + jnp.einsum(
            "hqk,qhd->khd", grad_raw, queries, preferred_element_type=jnp.float32
        )
        return ((grad_keys, grad_values), grad_query_blk)

    empty = jnp.zeros(queries.shape, jnp.float32)
    (grad_keys, grad_values), grad_queries = lax.scan(
        one_block, (empty, empty), jnp.arange(tok_rows // block_rows)
    )
    width_all = head_count * head_width
    return tuple(
        (
            member.reshape(tok_rows, width_all).astype(jnp.bfloat16)
            for member in (grad_queries, grad_keys, grad_values)
        )
    )


def sublayer_forward(stream, up_proj, down_proj, gain_vec):
    normed = layer_norm(stream, gain_vec).astype(jnp.bfloat16)
    pre_act = jnp.dot(normed, up_proj, preferred_element_type=jnp.float32)
    middle = jax.nn.gelu(pre_act).astype(jnp.bfloat16)
    result = stream + jnp.dot(middle, down_proj, preferred_element_type=jnp.float32)
    return (result, (stream, normed, pre_act, middle))


def sublayer_backward(grad_result, kept, up_proj, down_proj, gain_vec):
    stream, normed, pre_act, middle = kept
    grad_low = grad_result.astype(jnp.bfloat16)
    grad_middle = jnp.einsum("rd,fd->rf", grad_low, down_proj, preferred_element_type=jnp.float32)
    gelu_pull = jax.vjp(jax.nn.gelu, pre_act)[1]
    grad_pre = gelu_pull(grad_middle)[0].astype(jnp.bfloat16)
    grad_normed = jnp.einsum("rf,df->rd", grad_pre, up_proj, preferred_element_type=jnp.float32)
    norm_pull = jax.vjp(layer_norm, stream, gain_vec)[1]
    grad_stream, grad_gain = norm_pull(grad_normed)
    return (grad_result + grad_stream, grad_low, grad_gain)


def ring_rows(rows, axis):
    count = lax.axis_size(axis)
    back = [(i, (i - 1) % count) for i in range(count)]
    held = [rows]
    for _ in range(count - 1):
        held.append(lax.ppermute(held[-1], axis, back))
    return jnp.concatenate(held, axis=0)


def weight_grads(normed_rows, grad_rows, up_proj, down_proj):
    count = lax.axis_size("batch")
    width = up_proj.shape[1] // count
    first = lax.axis_index("batch") * width
    up_part = lax.dynamic_slice_in_dim(up_proj, first, width, 1)
    down_part = lax.dynamic_slice_in_dim(down_proj, first, width, 0)
    pre_act = jnp.dot(normed_rows, up_part, preferred_element_type=jnp.float32)
    middle, gelu_pull = jax.vjp(jax.nn.gelu, pre_act)
    grad_middle = jnp.einsum("rd,fd->rf", grad_rows, down_part, preferred_element_type=jnp.float32)
    grad_pre = gelu_pull(grad_middle)[0].astype(jnp.bfloat16)
    grad_down = jnp.einsum(
        "rf,rd->fd", middle.astype(jnp.bfloat16), grad_rows, preferred_element_type=jnp.float32
    )
    grad_up = jnp.einsum("rd,rf->df", normed_rows, grad_pre, preferred_element_type=jnp.float32)
    return grad_up, grad_down


def halve(blocks, axis, bit, dim):
    count = lax.axis_size(axis)
    mine = (lax.axis_index(axis) // bit) % 2
    kept = lax.dynamic_index_in_dim(blocks, mine, dim, keepdims=False)
    sent = lax.dynamic_index_in_dim(blocks, 1 - mine, dim, keepdims=False)
    got = lax.ppermute(sent, axis, [(i, i ^ bit) for i in range(count)])
    return (kept.astype(jnp.float32) + got.astype(jnp.float32)).astype(blocks.dtype)


def scatter_sum(parts):
    experts, groups = lax.axis_size("expert"), lax.axis_size("batch")
    kinds, rows, width = parts.shape
    bits_e = experts.bit_length() - 1
    bits_b = groups.bit_length() - 1
    shape = (kinds,) + (2,) * (bits_b + bits_e) + (rows // (experts * groups), width)
    blocks = parts.reshape(shape)
    for k in range(bits_e):
        blocks = halve(blocks, "expert", 1 << k, bits_b + bits_e - k)
    for k in range(bits_b):
        blocks = halve(blocks, "batch", 1 << k, bits_b - k)
    return blocks


def all_sum(value):
    for axis in ("expert", "batch"):
        count = lax.axis_size(axis)
        bit = 1
        while bit < count:
            value = value + lax.ppermute(value, axis, [(i, i ^ bit) for i in range(count)])
            bit *= 2
    return value


MESH = pl.DeviceIdType.MESH
BF = jnp.bfloat16
F32 = jnp.float32
GELU_A = 0.7978845608028654
GELU_B = 0.044715


def gelu_pair(v):
    square = v * v
    bent = jnp.tanh(GELU_A * v * (1.0 + GELU_B * square))
    half = 0.5 * (1.0 + bent)
    slope = half + 0.5 * v * (1.0 - bent * bent) * (GELU_A * (1.0 + 3.0 * GELU_B * square))
    return v * half, slope


def dot(a, b, dims=((1,), (0,))):
    return lax.dot_general(a, b, (dims, ((), ())), preferred_element_type=F32)


def finish_kernel(
    groups, width,
    rows_in, up_first, down_first, up_second, down_second, dense_in, small_in, gains_in,
    up_out, down_out, dense_out, small_out, gains_out,
    rows, ups, downs, up_acc, down_acc, turned, part, d_one, d_two, d_three, d_four, d_five, keep, s_got, g_got,
    ring_send, ring_recv, dense_send, dense_recv, small_send, small_recv, gain_send, gain_recv, local_sem, out_sem,
):
    b, e = lax.axis_index("batch"), lax.axis_index("expert")
    steps = 2 * groups
    before = lax.rem(b + groups - 1, groups)
    after = lax.rem(b + 1, groups)
    core, x, y = lax.rem(e, 2), lax.rem(e // 2, 2), lax.rem(e // 4, 2)
    b0, b1 = lax.rem(b, 2), lax.rem(b // 2, 2)
    e_core = e + 1 - 2 * core
    e_x = e + 2 - 4 * x
    e_y = e + 4 - 8 * y
    b_lo = b + 1 - 2 * b0
    b_hi = b + 2 - 4 * b1
    peers = [(b, e_core), (b, e_x), (b, e_y), (before, e), (after, e), (b_hi, e)]
    barrier = pltpu.get_barrier_semaphore()
    for peer in peers:
        pl.semaphore_signal(barrier, inc=1, device_id=peer, device_id_type=MESH)

    loads = []
    col = pl.multiple_of(b * width, width)
    for s, (up, down) in enumerate(((up_first, down_first), (up_second, down_second))):
        loads.append(pltpu.make_async_copy(up.at[0, :, pl.ds(col, width)], ups.at[s], local_sem.at[0, s]))
        loads.append(pltpu.make_async_copy(down.at[0, pl.ds(col, width), :], downs.at[s], local_sem.at[1, s]))
    for s in range(2):
        for kind in range(2):
            loads.append(pltpu.make_async_copy(rows_in.at[kind, s], rows.at[kind, s, 0], local_sem.at[2 + kind, s]))
    mine = pltpu.make_async_copy(dense_in.at[core], part, local_sem.at[4, 0])
    for load in loads:
        load.start()
    mine.start()
    pl.semaphore_wait(barrier, len(peers))

    def remote(src, dst, send, recv, peer):
        return pltpu.make_async_remote_copy(
            src_ref=src, dst_ref=dst, send_sem=send, recv_sem=recv, device_id=peer, device_id_type=MESH
        )

    first_dense = remote(dense_in.at[1 - core], d_one, dense_send.at[0], dense_recv.at[0], (b, e_core))
    first_dense.start()

    def ring(kind, s, k):
        return remote(
            rows.at[kind, s, k - 1], rows.at[kind, s, k], ring_send.at[kind, s, k], ring_recv.at[kind, s, k], (before, e)
        )

    for s in (1, 0):
        for kind in range(2):
            pltpu.make_async_copy(rows_in.at[kind, s], rows.at[kind, s, 0], local_sem.at[2 + kind, s]).wait()
            ring(kind, s, 1).start()
    for s in range(2):
        loads[2 * s].wait()
        loads[2 * s + 1].wait()
    up_acc[...] = jnp.zeros_like(up_acc)
    down_acc[...] = jnp.zeros_like(down_acc)

    def small_step(level, peer):
        return remote(keep.at[level], s_got.at[level], small_send.at[level], small_recv.at[level], peer)

    def gain_step(level, peer):
        return remote(
            keep.at[5 + level, pl.ds(0, 8)], g_got.at[level], gain_send.at[level], gain_recv.at[level], peer
        )

    def second(m):
        if m < 2:
            return remote(part.at[m, 1 - x], d_two.at[m], dense_send.at[1 + m], dense_recv.at[1 + m], (b, e_x))
        return remote(part.at[m, :, 1 - y], d_two.at[m], dense_send.at[1 + m], dense_recv.at[1 + m], (b, e_y))

    def third(m):
        if m < 2:
            return remote(part.at[m, x, 1 - y], d_three.at[m], dense_send.at[5 + m], dense_recv.at[5 + m], (b, e_y))
        return remote(part.at[m, 1 - x, y], d_three.at[m], dense_send.at[5 + m], dense_recv.at[5 + m], (b, e_x))

    fourth = remote(d_four.at[:, 1 - b0], d_four.at[:, 2], dense_send.at[9], dense_recv.at[9], (b_lo, e))
    fifth = remote(d_five.at[:, 1 - b1], d_five.at[:, 2], dense_send.at[10], dense_recv.at[10], (b_hi, e))

    keep[0] = small_in[...]
    keep[5, pl.ds(0, 8)] = gains_in[...]
    small_step(0, (b, e_core)).start()
    gain_step(0, (b_lo, e)).start()

    def weight_step(i, carry):
        k, s = i // 2, 1 - lax.rem(i, 2)

        @pl.when(k > 0)
        def _():
            for kind in range(2):
                ring(kind, s, k).wait_recv()

        @pl.when((k > 0) & (k < groups - 1))
        def _():
            for kind in range(2):
                ring(kind, s, k + 1).start()

        turned[...] = rows[0, s, k].T

        def chunk(c, carry):
            cols = pl.ds(pl.multiple_of(c * 256, 256), 256)
            pre = dot(rows[0, s, k], ups[s, :, cols])
            grad_mid = dot(rows[1, s, k], downs[s, cols, :], ((1,), (1,)))
            mid, slope = gelu_pair(pre)
            down_acc[s, cols, :] += dot(mid.astype(BF), rows[1, s, k], ((0,), (0,)))
            up_acc[s, :, cols] += dot(turned[...], (grad_mid * slope).astype(BF))
            return carry

        lax.fori_loop(0, width // 256, chunk, 0)

        @pl.when(i == 0)
        def _():
            mine.wait()
            first_dense.wait()
            small_step(0, (b, e_core)).wait()
            gain_step(0, (b_lo, e)).wait()
            keep[1] = keep[0] + s_got[0]
            keep[6, pl.ds(0, 8)] = keep[5, pl.ds(0, 8)] + g_got[0]
            small_step(1, (b, e_x)).start()
            gain_step(1, (b_hi, e)).start()
            for m in range(4):
                for xx in range(2):
                    part[m, xx] = (part[m, xx].astype(F32) + d_one[m, xx].astype(F32)).astype(BF)
            for m in range(4):
                second(m).start()

        @pl.when(i == 2)
        def _():
            small_step(1, (b, e_x)).wait()
            gain_step(1, (b_hi, e)).wait()
            gains_out[...] = keep[6, pl.ds(0, 8)] + g_got[1]
            keep[2] = keep[1] + s_got[1]
            small_step(2, (b, e_y)).start()
            for m in range(4):
                second(m).wait()
            for m in range(4):
                if m < 2:
                    part[m, x] = (part[m, x].astype(F32) + d_two[m].astype(F32)).astype(BF)
                else:
                    for xx in range(2):
                        part[m, xx, y] = (part[m, xx, y].astype(F32) + d_two[m, xx].astype(F32)).astype(BF)
            for m in range(4):
                third(m).start()

        @pl.when(i == 3)
        def _():
            small_step(2, (b, e_y)).wait()
            keep[3] = keep[2] + s_got[2]
            small_step(3, (b_lo, e)).start()
            for m in range(4):
                third(m).wait()
            for m in range(4):
                for g in range(4):
                    d_four[m, g % 2, g // 2] = (part[m, x, y, g].astype(F32) + d_three[m, g].astype(F32)).astype(BF)
            fourth.start()

        @pl.when(i == 4)
        def _():
            small_step(3, (b_lo, e)).wait()
            keep[4] = keep[3] + s_got[3]
            small_step(4, (b_hi, e)).start()
            fourth.wait()
            for m in range(4):
                for g in range(2):
                    d_five[m, g] = (d_four[m, b0, g].astype(F32) + d_four[m, 2, g].astype(F32)).astype(BF)
            fifth.start()

        @pl.when(i == 5)
        def _():
            small_step(4, (b_hi, e)).wait()
            small_out[...] = keep[4] + s_got[4]
            fifth.wait()
            for m in range(4):
                dense_out[m] = d_five[m, b1].astype(F32) + d_five[m, 2].astype(F32)

        @pl.when(i == steps - 2)
        def _():
            pltpu.make_async_copy(up_acc.at[1], up_out.at[1], out_sem.at[0, 1]).start()
            pltpu.make_async_copy(down_acc.at[1], down_out.at[1], out_sem.at[1, 1]).start()

        return carry

    lax.fori_loop(0, steps, weight_step, 0)
    for s in range(2):
        for kind in range(2):
            for k in range(1, groups):
                ring(kind, s, k).wait_send()
    finals = [
        pltpu.make_async_copy(up_acc.at[s], up_out.at[s], out_sem.at[0, s]) for s in range(2)
    ] + [pltpu.make_async_copy(down_acc.at[s], down_out.at[s], out_sem.at[1, s]) for s in range(2)]
    finals[0].start()
    finals[2].start()
    for final in finals:
        final.wait()


def finish(rows, up_first, down_first, up_second, down_second, dense, small, gains):
    groups = lax.axis_size("batch")
    count, width_all = rows.shape[2], rows.shape[3]
    width = up_first.shape[2] // groups
    block = dense.shape[5]
    any_spec = pl.BlockSpec(memory_space=pl.ANY)
    vmem = pl.BlockSpec(memory_space=pltpu.VMEM)
    wide = width_all
    return pl.pallas_call(
        functools.partial(finish_kernel, groups, width),
        out_shape=(
            jax.ShapeDtypeStruct((2, wide, width), F32),
            jax.ShapeDtypeStruct((2, width, wide), F32),
            jax.ShapeDtypeStruct((4, block, wide), F32),
            jax.ShapeDtypeStruct(small.shape, F32),
            jax.ShapeDtypeStruct(gains.shape, F32),
        ),
        in_specs=[any_spec] * 6 + [vmem] * 2,
        out_specs=(any_spec, any_spec, vmem, vmem, vmem),
        scratch_shapes=[
            pltpu.VMEM((2, 2, groups, count, wide), BF),
            pltpu.VMEM((2, wide, width), BF),
            pltpu.VMEM((2, width, wide), BF),
            pltpu.VMEM((2, wide, width), F32),
            pltpu.VMEM((2, width, wide), F32),
            pltpu.VMEM((wide, count), BF),
            pltpu.VMEM((4, 2, 2, 4, block, wide), BF),
            pltpu.VMEM((4, 2, 2, 4, block, wide), BF),
            pltpu.VMEM((4, 2, 4, block, wide), BF),
            pltpu.VMEM((4, 4, block, wide), BF),
            pltpu.VMEM((4, 3, 2, block, wide), BF),
            pltpu.VMEM((4, 3, block, wide), BF),
            pltpu.VMEM((7,) + small.shape, F32),
            pltpu.VMEM((5,) + small.shape, F32),
            pltpu.VMEM((2,) + gains.shape, F32),
            pltpu.SemaphoreType.DMA((2, 2, groups)),
            pltpu.SemaphoreType.DMA((2, 2, groups)),
            pltpu.SemaphoreType.DMA((11,)),
            pltpu.SemaphoreType.DMA((11,)),
            pltpu.SemaphoreType.DMA((5,)),
            pltpu.SemaphoreType.DMA((5,)),
            pltpu.SemaphoreType.DMA((2,)),
            pltpu.SemaphoreType.DMA((2,)),
            pltpu.SemaphoreType.DMA((5, 2)),
            pltpu.SemaphoreType.DMA((2, 2)),
        ],
        compiler_params=pltpu.CompilerParams(
            collective_id=1, has_side_effects=True, vmem_limit_bytes=64 * 1024 * 1024 - 65536
        ),
        name="finish",
    )(rows, up_first, down_first, up_second, down_second, dense, small, gains)


def slot_layout(tokens, routes):
    tok_rows = tokens.shape[0]
    expert_count = lax.axis_size("expert")
    capacity = 11 * tok_rows // (8 * expert_count)
    ones_int = (routes == jnp.arange(expert_count, dtype=jnp.int32)[None, :]).astype(jnp.int32)
    ranking = jnp.sum(jnp.cumsum(ones_int, axis=0) * ones_int, axis=1) - 1
    slot_index = routes[:, 0] * capacity + ranking
    return (expert_count, capacity, ones_int.astype(jnp.float32), slot_index)


def forward_pass(params):
    (
        tokens,
        doc_ends,
        routes,
        w_query,
        w_key,
        w_value,
        w_output,
        attn_gain,
        centroids,
        up_first,
        down_first,
        gain_first,
        up_second,
        down_second,
        gain_second,
    ) = params
    tok_rows, width_all = tokens.shape
    expert_count, capacity, chosen, slot_index = slot_layout(tokens, routes)
    place = jnp.arange(tok_rows, dtype=jnp.int32)
    segment = jnp.sum((place[:, None] >= doc_ends[0][None, :]).astype(jnp.int32), axis=1)
    live_mask = (place < doc_ends[0, -1]).astype(jnp.float32)[:, None]
    stream = tokens.astype(jnp.float32)
    normed = layer_norm(stream, attn_gain).astype(jnp.bfloat16)
    heads_shape = (tok_rows, HEADS, width_all // HEADS)
    queries = (
        jnp.dot(normed, w_query, preferred_element_type=jnp.float32)
        .astype(jnp.bfloat16)
        .reshape(heads_shape)
    )
    key_rows = (
        jnp.dot(normed, w_key, preferred_element_type=jnp.float32)
        .astype(jnp.bfloat16)
        .reshape(heads_shape)
    )
    value_rows = (
        jnp.dot(normed, w_value, preferred_element_type=jnp.float32)
        .astype(jnp.bfloat16)
        .reshape(heads_shape)
    )
    mixed, log_total = attend_forward(queries, key_rows, value_rows, segment, place)
    hidden = stream + jnp.dot(mixed, w_output, preferred_element_type=jnp.float32)
    score = jnp.sum(jnp.dot(hidden, centroids.T, precision=HIGHEST) * chosen, axis=1, keepdims=True)
    gating = jax.nn.sigmoid(score)
    routed = hidden.astype(jnp.bfloat16)
    outgoing = (
        jnp.zeros((expert_count * capacity, width_all), jnp.bfloat16).at[slot_index].set(routed)
    )
    arrived = lax.all_to_all(
        outgoing.reshape(expert_count, capacity, width_all),
        "expert",
        split_axis=0,
        concat_axis=0,
        tiled=True,
    )
    arrived = arrived.reshape(expert_count * capacity, width_all).astype(jnp.float32)
    stream_one, kept_one = sublayer_forward(arrived, up_first[0], down_first[0], gain_first[0])
    stream_two, kept_two = sublayer_forward(
        stream_one, up_second[0], down_second[0], gain_second[0]
    )
    expert_low = stream_two.astype(jnp.bfloat16).reshape(expert_count, capacity, width_all)
    came_back = lax.all_to_all(expert_low, "expert", split_axis=0, concat_axis=0, tiled=True)
    returned = came_back.reshape(expert_count * capacity, width_all)[slot_index].astype(jnp.float32)
    block_out = (live_mask * (gating * returned + (1.0 - gating) * hidden)).astype(jnp.bfloat16)
    kept = (
        stream,
        normed,
        queries,
        key_rows,
        value_rows,
        log_total,
        mixed,
        hidden,
        gating,
        returned,
        kept_one,
        kept_two,
        segment,
        place,
        live_mask,
    )
    return (block_out, kept)


def per_device(
    tokens,
    doc_ends,
    routes,
    w_query,
    w_key,
    w_value,
    w_output,
    attn_gain,
    centroids,
    up_first,
    down_first,
    gain_first,
    up_second,
    down_second,
    gain_second,
    cotangent,
):
    params = (
        tokens,
        doc_ends,
        routes,
        w_query,
        w_key,
        w_value,
        w_output,
        attn_gain,
        centroids,
        up_first,
        down_first,
        gain_first,
        up_second,
        down_second,
        gain_second,
    )
    block_out, kept = forward_pass(params)
    (
        stream,
        normed,
        queries,
        key_rows,
        value_rows,
        log_total,
        mixed,
        hidden,
        gating,
        returned,
        kept_one,
        kept_two,
        segment,
        place,
        live_mask,
    ) = kept
    tok_rows, width_all = tokens.shape
    expert_count, capacity, chosen, slot_index = slot_layout(tokens, routes)
    grad_block = cotangent.astype(jnp.float32) * live_mask
    grad_sent = (gating * grad_block).astype(jnp.bfloat16)
    grad_gating = jnp.sum(grad_block * (returned - hidden), axis=1, keepdims=True)
    grad_score = grad_gating * gating * (1.0 - gating)
    grad_buffer = (
        jnp.zeros((expert_count * capacity, width_all), jnp.bfloat16).at[slot_index].set(grad_sent)
    )
    grad_rows = lax.all_to_all(
        grad_buffer.reshape(expert_count, capacity, width_all),
        "expert",
        split_axis=0,
        concat_axis=0,
        tiled=True,
    )
    grad_rows = grad_rows.reshape(expert_count * capacity, width_all).astype(jnp.float32)
    grad_stream_one, low_two, gain_two_grad = sublayer_backward(
        grad_rows, kept_two, up_second[0], down_second[0], gain_second[0]
    )
    grad_arrived, low_one, gain_one_grad = sublayer_backward(
        grad_stream_one, kept_one, up_first[0], down_first[0], gain_first[0]
    )
    grad_home = lax.all_to_all(
        grad_arrived.astype(jnp.bfloat16).reshape(expert_count, capacity, width_all),
        "expert",
        split_axis=0,
        concat_axis=0,
        tiled=True,
    )
    grad_routed = grad_home.reshape(expert_count * capacity, width_all)[slot_index].astype(
        jnp.float32
    )
    own_centroid = jnp.dot(chosen, centroids, precision=HIGHEST)
    grad_hidden = (1.0 - gating) * grad_block + grad_routed + grad_score * own_centroid
    grad_centroids = jnp.dot(chosen.T, grad_score * hidden, precision=HIGHEST)
    grad_attn_out = grad_hidden.astype(jnp.bfloat16)
    grad_output_w = jnp.einsum(
        "td,te->de", mixed, grad_attn_out, preferred_element_type=jnp.float32
    )
    grad_mixed = jnp.einsum(
        "te,de->td", grad_attn_out, w_output, preferred_element_type=jnp.float32
    ).astype(jnp.bfloat16)
    grad_q, grad_k, grad_v = attend_backward(
        grad_mixed.reshape(queries.shape), queries, key_rows, value_rows, log_total, segment, place
    )
    grad_query_w = jnp.einsum("td,te->de", normed, grad_q, preferred_element_type=jnp.float32)
    grad_key_w = jnp.einsum("td,te->de", normed, grad_k, preferred_element_type=jnp.float32)
    grad_value_w = jnp.einsum("td,te->de", normed, grad_v, preferred_element_type=jnp.float32)
    grad_normed = jnp.einsum("te,de->td", grad_q, w_query, preferred_element_type=jnp.float32)
    grad_normed = grad_normed + jnp.einsum(
        "te,de->td", grad_k, w_key, preferred_element_type=jnp.float32
    )
    grad_normed = grad_normed + jnp.einsum(
        "te,de->td", grad_v, w_value, preferred_element_type=jnp.float32
    )
    norm_pull = jax.vjp(layer_norm, stream, attn_gain)[1]
    grad_input_norm, grad_gain_att = norm_pull(grad_normed)
    grad_tokens = grad_hidden + grad_input_norm
    grads = (grad_query_w, grad_key_w, grad_value_w, grad_output_w)
    if lax.axis_size("batch") == 4 and expert_count == 8:
        stacked = jnp.stack(grads).astype(jnp.bfloat16)
        pieces = stacked.reshape(4, 4, 2, 2, 2, width_all // 32, width_all).transpose(4, 0, 3, 2, 1, 5, 6)
        small_in = jnp.concatenate(
            (grad_gain_att[None], grad_centroids, jnp.zeros((7, width_all), jnp.float32)), axis=0
        )
        gains_in = jnp.concatenate(
            (gain_one_grad[None], gain_two_grad[None], jnp.zeros((6, width_all), jnp.float32)), axis=0
        )
        rows = jnp.stack((kept_one[1], kept_two[1], low_one, low_two)).reshape(2, 2, -1, width_all)
        up_parts, down_parts, dense, small, gains = finish(
            rows, up_first, down_first, up_second, down_second, pieces, small_in, gains_in
        )
        gain_part = width_all // 4
        gains = lax.dynamic_slice_in_dim(gains, lax.axis_index("batch") * gain_part, gain_part, 1)
        small = small[:9]
        expert_parts = (
            up_parts[0:1], down_parts[0:1], gains[0:1], up_parts[1:2], down_parts[1:2], gains[1:2],
        )
    else:
        dense = scatter_sum(
            jnp.stack((grad_query_w, grad_key_w, grad_value_w, grad_output_w)).astype(jnp.bfloat16)
        ).astype(jnp.float32)
        small = all_sum(jnp.concatenate((grad_gain_att[None], grad_centroids), axis=0))
        up_two_grad, down_two_grad = weight_grads(
            ring_rows(kept_two[1], "batch"), ring_rows(low_two, "batch"), up_second[0], down_second[0]
        )
        up_one_grad, down_one_grad = weight_grads(
            ring_rows(kept_one[1], "batch"), ring_rows(low_one, "batch"), up_first[0], down_first[0]
        )
        gains = lax.all_gather(jnp.stack((gain_one_grad, gain_two_grad)), "batch")
        gain_part = gain_one_grad.shape[0] // lax.axis_size("batch")
        gains = lax.dynamic_slice_in_dim(
            jnp.sum(gains, axis=0), lax.axis_index("batch") * gain_part, gain_part, 1
        )
        expert_parts = (
            up_one_grad[None],
            down_one_grad[None],
            gains[0:1],
            up_two_grad[None],
            down_two_grad[None],
            gains[1:2],
        )
    return (
        block_out,
        grad_tokens,
        dense[0],
        dense[1],
        dense[2],
        dense[3],
        small[0],
        small[1:],
        expert_parts[0],
        expert_parts[1],
        expert_parts[2],
        expert_parts[3],
        expert_parts[4],
        expert_parts[5],
    )


def solution(mesh):
    return jax.shard_map(
        per_device,
        mesh=mesh,
        in_specs=(
            P(("batch", "expert"), None),
            P(("batch", "expert"), None),
            P(("batch", "expert"), None),
            P(),
            P(),
            P(),
            P(),
            P(),
            P(),
            P("expert", None, None),
            P("expert", None, None),
            P("expert", None),
            P("expert", None, None),
            P("expert", None, None),
            P("expert", None),
            P(("batch", "expert"), None),
        ),
        out_specs=(
            P(("batch", "expert"), None),
            P(("batch", "expert"), None),
            P(("batch", "expert"), None),
            P(("batch", "expert"), None),
            P(("batch", "expert"), None),
            P(("batch", "expert"), None),
            P(),
            P(),
            P("expert", None, "batch"),
            P("expert", "batch", None),
            P("expert", "batch"),
            P("expert", None, "batch"),
            P("expert", "batch", None),
            P("expert", "batch"),
        ),
        check_vma=False,
    )
```

```python
import functools
import jax, jax.numpy as jnp
from jax import lax
from jax.experimental import pallas as pl
from jax.experimental.pallas import tpu as pltpu
from jax.sharding import PartitionSpec as P


MESH = pl.DeviceIdType.MESH
BF = jnp.bfloat16
F32 = jnp.float32
GELU_A = 0.7978845608028654
GELU_B = 0.044715


def gelu_pair(v):
    square = v * v
    bent = jnp.tanh(GELU_A * v * (1.0 + GELU_B * square))
    half = 0.5 * (1.0 + bent)
    slope = half + 0.5 * v * (1.0 - bent * bent) * (GELU_A * (1.0 + 3.0 * GELU_B * square))
    return v * half, slope


def dot(a, b, dims=((1,), (0,))):
    return lax.dot_general(a, b, (dims, ((), ())), preferred_element_type=F32)


def finish_kernel(
    groups, width,
    rows_in, up_first, down_first, up_second, down_second, dense_in, small_in, gains_in,
    up_one, down_one, up_two, down_two, dense_out, small_out, gains_out,
    rows, ups, downs, up_acc, down_acc, turned, part, d_one, d_two, d_three, d_four, d_five, keep, s_got, g_got,
    ring_send, ring_recv, dense_send, dense_recv, small_send, small_recv, gain_send, gain_recv, local_sem, out_sem,
):
    b, e = lax.axis_index("batch"), lax.axis_index("expert")
    steps = 2 * groups
    before = lax.rem(b + groups - 1, groups)
    after = lax.rem(b + 1, groups)
    core, x, y = lax.rem(e, 2), lax.rem(e // 2, 2), lax.rem(e // 4, 2)
    b0, b1 = lax.rem(b, 2), lax.rem(b // 2, 2)
    e_core = e + 1 - 2 * core
    e_x = e + 2 - 4 * x
    e_y = e + 4 - 8 * y
    b_lo = b + 1 - 2 * b0
    b_hi = b + 2 - 4 * b1
    peers = [(b, e_core), (b, e_x), (b, e_y), (before, e), (after, e), (b_hi, e)]
    barrier = pltpu.get_barrier_semaphore()
    for peer in peers:
        pl.semaphore_signal(barrier, inc=1, device_id=peer, device_id_type=MESH)

    loads = []
    col = pl.multiple_of(b * width, width)
    for s, (up, down) in enumerate(((up_first, down_first), (up_second, down_second))):
        loads.append(pltpu.make_async_copy(up.at[0, :, pl.ds(col, width)], ups.at[s], local_sem.at[0, s]))
        loads.append(pltpu.make_async_copy(down.at[0, pl.ds(col, width), :], downs.at[s], local_sem.at[1, s]))
    for s in range(2):
        for kind in range(2):
            loads.append(pltpu.make_async_copy(rows_in.at[kind, s], rows.at[kind, s, 0], local_sem.at[2 + kind, s]))
    mine = pltpu.make_async_copy(dense_in.at[core], part, local_sem.at[4, 0])
    for load in loads:
        load.start()
    mine.start()
    pl.semaphore_wait(barrier, len(peers))

    def remote(src, dst, send, recv, peer):
        return pltpu.make_async_remote_copy(
            src_ref=src, dst_ref=dst, send_sem=send, recv_sem=recv, device_id=peer, device_id_type=MESH
        )

    first_dense = remote(dense_in.at[1 - core], d_one, dense_send.at[0], dense_recv.at[0], (b, e_core))
    first_dense.start()

    def ring(kind, s, k):
        return remote(
            rows.at[kind, s, k - 1], rows.at[kind, s, k], ring_send.at[kind, s, k], ring_recv.at[kind, s, k], (before, e)
        )

    for s in (1, 0):
        for kind in range(2):
            pltpu.make_async_copy(rows_in.at[kind, s], rows.at[kind, s, 0], local_sem.at[2 + kind, s]).wait()
            ring(kind, s, 1).start()
    for s in range(2):
        loads[2 * s].wait()
        loads[2 * s + 1].wait()
    up_acc[...] = jnp.zeros_like(up_acc)
    down_acc[...] = jnp.zeros_like(down_acc)

    def small_step(level, peer):
        return remote(keep.at[level], s_got.at[level], small_send.at[level], small_recv.at[level], peer)

    def gain_step(level, peer):
        return remote(
            keep.at[5 + level, pl.ds(0, 8)], g_got.at[level], gain_send.at[level], gain_recv.at[level], peer
        )

    def second(m):
        if m < 2:
            return remote(part.at[m, 1 - x], d_two.at[m], dense_send.at[1 + m], dense_recv.at[1 + m], (b, e_x))
        return remote(part.at[m, :, 1 - y], d_two.at[m], dense_send.at[1 + m], dense_recv.at[1 + m], (b, e_y))

    def third(m):
        if m < 2:
            return remote(part.at[m, x, 1 - y], d_three.at[m], dense_send.at[5 + m], dense_recv.at[5 + m], (b, e_y))
        return remote(part.at[m, 1 - x, y], d_three.at[m], dense_send.at[5 + m], dense_recv.at[5 + m], (b, e_x))

    fourth = remote(d_four.at[:, 1 - b0], d_four.at[:, 2], dense_send.at[9], dense_recv.at[9], (b_lo, e))
    fifth = remote(d_five.at[:, 1 - b1], d_five.at[:, 2], dense_send.at[10], dense_recv.at[10], (b_hi, e))

    keep[0] = small_in[...]
    keep[5, pl.ds(0, 8)] = gains_in[...]
    small_step(0, (b, e_core)).start()
    gain_step(0, (b_lo, e)).start()

    def results(s):
        up_out, down_out = ((up_one, down_one), (up_two, down_two))[s]
        return (
            pltpu.make_async_copy(up_acc.at[s], up_out.at[0], out_sem.at[0, s]),
            pltpu.make_async_copy(down_acc.at[s], down_out.at[0], out_sem.at[1, s]),
        )

    def weight_step(i, carry):
        k, s = i // 2, 1 - lax.rem(i, 2)

        @pl.when(k > 0)
        def _():
            for kind in range(2):
                ring(kind, s, k).wait_recv()

        @pl.when((k > 0) & (k < groups - 1))
        def _():
            for kind in range(2):
                ring(kind, s, k + 1).start()

        turned[...] = rows[0, s, k].T

        def chunk(c, carry):
            cols = pl.ds(pl.multiple_of(c * 256, 256), 256)
            pre = dot(rows[0, s, k], ups[s, :, cols])
            grad_mid = dot(rows[1, s, k], downs[s, cols, :], ((1,), (1,)))
            mid, slope = gelu_pair(pre)
            down_acc[s, cols, :] += dot(mid.astype(BF), rows[1, s, k], ((0,), (0,)))
            up_acc[s, :, cols] += dot(turned[...], (grad_mid * slope).astype(BF))
            return carry

        lax.fori_loop(0, width // 256, chunk, 0)

        @pl.when(i == 0)
        def _():
            mine.wait()
            first_dense.wait()
            small_step(0, (b, e_core)).wait()
            gain_step(0, (b_lo, e)).wait()
            keep[1] = keep[0] + s_got[0]
            keep[6, pl.ds(0, 8)] = keep[5, pl.ds(0, 8)] + g_got[0]
            small_step(1, (b, e_x)).start()
            gain_step(1, (b_hi, e)).start()
            for m in range(4):
                for xx in range(2):
                    part[m, xx] = (part[m, xx].astype(F32) + d_one[m, xx].astype(F32)).astype(BF)
            for m in range(4):
                second(m).start()

        @pl.when(i == 2)
        def _():
            small_step(1, (b, e_x)).wait()
            gain_step(1, (b_hi, e)).wait()
            gains_out[...] = keep[6, pl.ds(0, 8)] + g_got[1]
            keep[2] = keep[1] + s_got[1]
            small_step(2, (b, e_y)).start()
            for m in range(4):
                second(m).wait()
            for m in range(4):
                if m < 2:
                    part[m, x] = (part[m, x].astype(F32) + d_two[m].astype(F32)).astype(BF)
                else:
                    for xx in range(2):
                        part[m, xx, y] = (part[m, xx, y].astype(F32) + d_two[m, xx].astype(F32)).astype(BF)
            for m in range(4):
                third(m).start()

        @pl.when(i == 3)
        def _():
            small_step(2, (b, e_y)).wait()
            keep[3] = keep[2] + s_got[2]
            small_step(3, (b_lo, e)).start()
            for m in range(4):
                third(m).wait()
            for m in range(4):
                for g in range(4):
                    d_four[m, g % 2, g // 2] = (part[m, x, y, g].astype(F32) + d_three[m, g].astype(F32)).astype(BF)
            fourth.start()

        @pl.when(i == 4)
        def _():
            small_step(3, (b_lo, e)).wait()
            keep[4] = keep[3] + s_got[3]
            small_step(4, (b_hi, e)).start()
            fourth.wait()
            for m in range(4):
                for g in range(2):
                    d_five[m, g] = (d_four[m, b0, g].astype(F32) + d_four[m, 2, g].astype(F32)).astype(BF)
            fifth.start()

        @pl.when(i == 5)
        def _():
            small_step(4, (b_hi, e)).wait()
            small_out[...] = keep[4] + s_got[4]
            fifth.wait()
            for m in range(4):
                dense_out[m] = d_five[m, b1].astype(F32) + d_five[m, 2].astype(F32)

        @pl.when(i == steps - 2)
        def _():
            for copy in results(1):
                copy.start()

        return carry

    lax.fori_loop(0, steps, weight_step, 0)
    for s in range(2):
        for kind in range(2):
            for k in range(1, groups):
                ring(kind, s, k).wait_send()
    for copy in results(0):
        copy.start()
    for copy in results(1) + results(0):
        copy.wait()


def finish(rows, up_first, down_first, up_second, down_second, dense, small, gains):
    groups = lax.axis_size("batch")
    count, width_all = rows.shape[2], rows.shape[3]
    width = up_first.shape[2] // groups
    block = dense.shape[5]
    any_spec = pl.BlockSpec(memory_space=pl.ANY)
    vmem = pl.BlockSpec(memory_space=pltpu.VMEM)
    wide = width_all
    return pl.pallas_call(
        functools.partial(finish_kernel, groups, width),
        out_shape=(
            jax.ShapeDtypeStruct((1, wide, width), F32),
            jax.ShapeDtypeStruct((1, width, wide), F32),
            jax.ShapeDtypeStruct((1, wide, width), F32),
            jax.ShapeDtypeStruct((1, width, wide), F32),
            jax.ShapeDtypeStruct((4, block, wide), F32),
            jax.ShapeDtypeStruct(small.shape, F32),
            jax.ShapeDtypeStruct(gains.shape, F32),
        ),
        in_specs=[any_spec] * 6 + [vmem] * 2,
        out_specs=(any_spec,) * 4 + (vmem,) * 3,
        scratch_shapes=[
            pltpu.VMEM((2, 2, groups, count, wide), BF),
            pltpu.VMEM((2, wide, width), BF),
            pltpu.VMEM((2, width, wide), BF),
            pltpu.VMEM((2, wide, width), F32),
            pltpu.VMEM((2, width, wide), F32),
            pltpu.VMEM((wide, count), BF),
            pltpu.VMEM((4, 2, 2, 4, block, wide), BF),
            pltpu.VMEM((4, 2, 2, 4, block, wide), BF),
            pltpu.VMEM((4, 2, 4, block, wide), BF),
            pltpu.VMEM((4, 4, block, wide), BF),
            pltpu.VMEM((4, 3, 2, block, wide), BF),
            pltpu.VMEM((4, 3, block, wide), BF),
            pltpu.VMEM((7,) + small.shape, F32),
            pltpu.VMEM((5,) + small.shape, F32),
            pltpu.VMEM((2,) + gains.shape, F32),
            pltpu.SemaphoreType.DMA((2, 2, groups)),
            pltpu.SemaphoreType.DMA((2, 2, groups)),
            pltpu.SemaphoreType.DMA((11,)),
            pltpu.SemaphoreType.DMA((11,)),
            pltpu.SemaphoreType.DMA((5,)),
            pltpu.SemaphoreType.DMA((5,)),
            pltpu.SemaphoreType.DMA((2,)),
            pltpu.SemaphoreType.DMA((2,)),
            pltpu.SemaphoreType.DMA((5, 2)),
            pltpu.SemaphoreType.DMA((2, 2)),
        ],
        compiler_params=pltpu.CompilerParams(
            collective_id=1, has_side_effects=True, vmem_limit_bytes=64 * 1024 * 1024 - 65536
        ),
        name="finish",
    )(rows, up_first, down_first, up_second, down_second, dense, small, gains)


MASKED = -1e30
EPSILON = 1e-05


def split_three(value):
    high = value.astype(BF)
    rest = value - high.astype(F32)
    middle = rest.astype(BF)
    return high, middle, (rest - middle.astype(F32)).astype(BF)


def select_rows(marks, value, dims):
    return sum(dot(marks, term, dims) for term in split_three(value))


def norm_parts(stream):
    average = jnp.mean(stream, axis=-1, keepdims=True)
    centred = stream - average
    variance = jnp.mean(centred * centred, axis=-1, keepdims=True)
    scale = lax.rsqrt(variance + EPSILON)
    return centred * scale, scale


def norm_pull(grad, stream, gain):
    unit, scale = norm_parts(stream)
    inner = grad * gain
    mean_inner = jnp.mean(inner, axis=-1, keepdims=True)
    mean_product = jnp.mean(inner * unit, axis=-1, keepdims=True)
    return scale * (inner - mean_inner - unit * mean_product), jnp.sum(grad * unit, axis=0, keepdims=True)


def route_marks(routes_row, experts, slots):
    count = routes_row.shape[1]
    ids = lax.broadcasted_iota(jnp.int32, (experts, count), 0)
    chosen = (ids == routes_row).astype(F32)
    earlier = lax.broadcasted_iota(jnp.int32, (count, count), 0) <= lax.broadcasted_iota(jnp.int32, (count, count), 1)
    running = dot(chosen.astype(BF), earlier.astype(F32).astype(BF))
    rank = jnp.sum(running * chosen, axis=0, keepdims=True) - 1.0
    place = routes_row * slots + rank.astype(jnp.int32)
    rows = lax.broadcasted_iota(jnp.int32, (experts * slots, count), 0)
    return chosen.astype(BF), (rows == place).astype(F32).astype(BF)


def allowed_pairs(ends, docs, count):
    row = lax.broadcasted_iota(jnp.int32, (count, count), 0)
    col = lax.broadcasted_iota(jnp.int32, (count, count), 1)
    row_segment = jnp.zeros((count, count), jnp.int32)
    col_segment = jnp.zeros((count, count), jnp.int32)
    for d in range(docs):
        row_segment += (row >= ends[0, d]).astype(jnp.int32)
        col_segment += (col >= ends[0, d]).astype(jnp.int32)
    return (row_segment == col_segment) & (col <= row)


def half_marks(half):
    lane = lax.broadcasted_iota(jnp.int32, (1, 128), 1)
    inside = (lane >= 64 * half) & (lane < 64 * half + 64)
    return inside.astype(F32).astype(BF)


def head_shares(query_pair, key_pair, allowed, half):
    raw = dot(query_pair * half_marks(half), key_pair, ((1,), (1,)))
    scores = jnp.where(allowed, raw * 0.125, MASKED)
    raised = jnp.exp(scores - jnp.max(scores, axis=-1, keepdims=True))
    return raised * (1.0 / jnp.sum(raised, axis=-1, keepdims=True))


def join_halves(first, second):
    lane = lax.broadcasted_iota(jnp.int32, first.shape, 1)
    return jnp.where(lane < 64, first, second)


def enter_kernel(
    experts, slots, docs,
    ends, routes, tokens, cotangent, gain, cents, w_query, w_key, w_value, w_output,
    normed, queries, keys, values, mixed, hidden, out_rows,
    w_held, sems,
):
    copies = [
        pltpu.make_async_copy(w, w_held.at[i], sems.at[i])
        for i, w in enumerate((w_query, w_key, w_value, w_output))
    ]
    for copy in copies:
        copy.start()
    count, wide = tokens.shape
    unit, _ = norm_parts(tokens[...].astype(F32))
    normed[...] = (unit * gain[...]).astype(BF)
    for i, result in enumerate((queries, keys, values)):
        copies[i].wait()
        result[...] = dot(normed[...], w_held[i]).astype(BF)
    allowed = allowed_pairs(ends, docs, count)

    def one_pair(j, carry):
        cols = pl.ds(pl.multiple_of(j * 128, 128), 128)
        query_pair, key_pair, value_pair = queries[:, cols], keys[:, cols], values[:, cols]
        halves = [
            dot(head_shares(query_pair, key_pair, allowed, half).astype(BF), value_pair) for half in range(2)
        ]
        mixed[:, cols] = join_halves(*halves).astype(BF)
        return carry

    lax.fori_loop(0, wide // 128, one_pair, 0)
    copies[3].wait()
    hidden[...] = tokens[...].astype(F32) + dot(mixed[...], w_held[3])
    chosen, dispatch = route_marks(routes[...], experts, slots)
    own = select_rows(chosen, cents[...], ((0,), (0,)))
    gating = jax.nn.sigmoid(jnp.sum(hidden[...] * own, axis=-1, keepdims=True))
    live = (lax.broadcasted_iota(jnp.int32, (count, 1), 0) < ends[0, docs - 1]).astype(F32)
    grad_sent = (gating * (live * cotangent[...].astype(F32))).astype(BF)
    out_rows[0] = dot(dispatch, hidden[...].astype(BF)).astype(BF)
    out_rows[1] = dot(dispatch, grad_sent).astype(BF)


def enter(ends, routes_row, tokens, cotangent, gain, cents, weights, slots):
    count, wide = tokens.shape
    experts, docs = cents.shape[0], ends.shape[1]
    vmem = pl.BlockSpec(memory_space=pltpu.VMEM)
    anys = pl.BlockSpec(memory_space=pl.ANY)
    low = jax.ShapeDtypeStruct((count, wide), BF)
    return pl.pallas_call(
        functools.partial(enter_kernel, experts, slots, docs),
        out_shape=(low,) * 5 + (
            jax.ShapeDtypeStruct((count, wide), F32),
            jax.ShapeDtypeStruct((2, experts * slots, wide), BF),
        ),
        in_specs=[pl.BlockSpec(memory_space=pltpu.SMEM)] + [vmem] * 5 + [anys] * 4,
        out_specs=(vmem,) * 7,
        scratch_shapes=[pltpu.VMEM((4, wide, wide), BF), pltpu.SemaphoreType.DMA((4,))],
        compiler_params=pltpu.CompilerParams(vmem_limit_bytes=48 * 1024 * 1024),
        name="enter",
    )(ends, routes_row, tokens, cotangent, gain, cents, *weights)


def leave_kernel(
    experts, slots, docs, grid_like,
    ends, routes, tokens, cotangent, gain, cents, normed, queries, keys, values, mixed, hidden, came,
    w_query, w_key, w_value, w_output,
    block_out, grad_tokens, dense, small,
    w_held, grad_low, grad_three, normed_turned, grad_hidden, sems,
):
    copies = [
        pltpu.make_async_copy(w, w_held.at[i], sems.at[i])
        for i, w in enumerate((w_query, w_key, w_value, w_output))
    ]
    for i in (3, 0, 1, 2):
        copies[i].start()
    count, wide = tokens.shape
    chosen, dispatch = route_marks(routes[...], experts, slots)
    own = select_rows(chosen, cents[...], ((0,), (0,)))
    gating = jax.nn.sigmoid(jnp.sum(hidden[...] * own, axis=-1, keepdims=True))
    live = (lax.broadcasted_iota(jnp.int32, (count, 1), 0) < ends[0, docs - 1]).astype(F32)
    returned = dot(dispatch, came[0], ((0,), (0,)))
    block_out[...] = (live * (gating * returned + (1.0 - gating) * hidden[...])).astype(BF)
    grad_block = live * cotangent[...].astype(F32)
    grad_score = jnp.sum(grad_block * (returned - hidden[...]), axis=-1, keepdims=True) * gating * (1.0 - gating)
    grad_hidden[...] = (1.0 - gating) * grad_block + dot(dispatch, came[1], ((0,), (0,))) + grad_score * own
    small[pl.ds(8, experts), :] = select_rows(chosen, grad_score * hidden[...], ((1,), (0,)))
    grad_low[...] = grad_hidden[...].astype(BF)
    copies[3].wait()
    grad_mixed = dot(grad_low[...], w_held[3], ((1,), (1,))).astype(BF)
    dense_product(grid_like, dense, 3, mixed[...].T, grad_low)
    grad_low[...] = grad_mixed
    allowed = allowed_pairs(ends, docs, count)

    def one_pair(j, carry):
        cols = pl.ds(pl.multiple_of(j * 128, 128), 128)
        query_pair, key_pair, value_pair = queries[:, cols], keys[:, cols], values[:, cols]
        grad_pair = grad_low[:, cols]
        parts = []
        for half in range(2):
            shares = head_shares(query_pair, key_pair, allowed, half)
            grad_shares = dot(grad_pair * half_marks(half), value_pair, ((1,), (1,)))
            inner = jnp.sum(shares * grad_shares, axis=-1, keepdims=True)
            raw = (shares * (grad_shares - inner) * 0.125).astype(BF)
            parts.append((
                dot(raw, key_pair),
                dot(raw, query_pair, ((0,), (0,))),
                dot(shares.astype(BF), grad_pair, ((0,), (0,))),
            ))
        for i in range(3):
            grad_three[i, :, cols] = join_halves(parts[0][i], parts[1][i]).astype(BF)
        return carry

    lax.fori_loop(0, wide // 128, one_pair, 0)
    normed_turned[...] = normed[...].T
    for i in range(3):
        dense_product(grid_like, dense, i, normed_turned[...], grad_three.at[i])
    for i in range(3):
        copies[i].wait()
    grad_normed = sum(dot(grad_three[i], w_held[i], ((1,), (1,))) for i in range(3))
    pulled, grad_gain = norm_pull(grad_normed, tokens[...].astype(F32), gain[...])
    grad_tokens[...] = grad_hidden[...] + pulled
    small[pl.ds(0, 8), :] = jnp.broadcast_to(grad_gain, (8, wide))


def dense_product(grid_like, dense, which, turned, right):
    wide = turned.shape[0]
    if not grid_like:
        dense[which] = dot(turned, right[...]).astype(BF)
        return
    block = wide // 32
    for g in range(4):
        product = dot(turned[g * 8 * block:(g + 1) * 8 * block], right[...]).astype(BF)
        for e in range(8):
            dense[e % 2, which, (e // 2) % 2, e // 4, g] = product[e * block:(e + 1) * block]


def leave(ends, routes_row, tokens, cotangent, gain, cents, kept, came, weights, slots, grid_like):
    count, wide = tokens.shape
    experts, docs = cents.shape[0], ends.shape[1]
    vmem = pl.BlockSpec(memory_space=pltpu.VMEM)
    anys = pl.BlockSpec(memory_space=pl.ANY)
    dense_shape = (2, 4, 2, 2, 4, wide // 32, wide) if grid_like else (4, wide, wide)
    return pl.pallas_call(
        functools.partial(leave_kernel, experts, slots, docs, grid_like),
        out_shape=(
            jax.ShapeDtypeStruct((count, wide), BF),
            jax.ShapeDtypeStruct((count, wide), F32),
            jax.ShapeDtypeStruct(dense_shape, BF),
            jax.ShapeDtypeStruct((8 + experts, wide), F32),
        ),
        in_specs=[pl.BlockSpec(memory_space=pltpu.SMEM)] + [vmem] * 12 + [anys] * 4,
        out_specs=(vmem,) * 4,
        scratch_shapes=[
            pltpu.VMEM((4, wide, wide), BF),
            pltpu.VMEM((count, wide), BF),
            pltpu.VMEM((3, count, wide), BF),
            pltpu.VMEM((wide, count), BF),
            pltpu.VMEM((count, wide), F32),
            pltpu.SemaphoreType.DMA((4,)),
        ],
        compiler_params=pltpu.CompilerParams(vmem_limit_bytes=56 * 1024 * 1024),
        name="leave",
    )(ends, routes_row, tokens, cotangent, gain, cents, *kept, came, *weights)


def pack_marks(experts, slots, capacity):
    shape = (experts * capacity, experts * slots)
    row = lax.broadcasted_iota(jnp.int32, (shape[0], 1), 0)
    block = sum((row >= s * capacity).astype(jnp.int32) for s in range(1, experts))
    column = lax.broadcasted_iota(jnp.int32, shape, 1)
    return (column == row + (slots - capacity) * block).astype(F32).astype(BF)


def chain_kernel(
    experts, slots, capacity, tiles,
    came, up_first, down_first, up_second, down_second, gain_first, gain_second,
    back, rows, gains,
    up_tile, down_tile, pre, stream, total, sems,
):
    tile = up_tile.shape[2]
    ups, downs = (up_first, up_second), (down_first, down_second)
    gain_refs = (gain_first, gain_second)

    def fetch(s, c, slot):
        cols = pl.ds(pl.multiple_of(c * tile, tile), tile)
        return (
            pltpu.make_async_copy(ups[s].at[0, :, cols], up_tile.at[slot], sems.at[0, slot]),
            pltpu.make_async_copy(downs[s].at[0, cols, :], down_tile.at[slot], sems.at[1, slot]),
        )

    order = ((0, True), (1, True), (1, False), (0, False))

    def run(phase, body):
        s = order[phase][0]

        def step(c, carry):
            slot = lax.rem(c, 2)
            for copy in fetch(s, c, slot):
                copy.wait()

            @pl.when(c + 1 < tiles)
            def _():
                for copy in fetch(s, c + 1, 1 - slot):
                    copy.start()

            if phase < 3:
                @pl.when(c + 1 == tiles)
                def _():
                    for copy in fetch(order[phase + 1][0], 0, 1 - slot):
                        copy.start()

            body(s, pl.ds(pl.multiple_of(c * tile, tile), tile), slot)
            return carry

        lax.fori_loop(0, tiles, step, 0)

    for copy in fetch(0, 0, 0):
        copy.start()
    gains[...] = jnp.zeros_like(gains)
    packing = pack_marks(experts, slots, capacity)
    stream[0] = dot(packing, came[0])
    rows[1, 1] = dot(packing, came[1]).astype(BF)

    def forward(s, cols, slot):
        made = dot(rows[0, s], up_tile[slot])
        pre[s, :, cols] = made
        mid = gelu_pair(made)[0].astype(BF)
        total[...] += dot(mid, down_tile[slot])

    def backward(s, cols, slot):
        grad_mid = dot(rows[1, s], down_tile[slot], ((1,), (1,)))
        grad_pre = (gelu_pair(pre[s, :, cols])[1] * grad_mid).astype(BF)
        total[...] += dot(grad_pre, up_tile[slot], ((1,), (1,)))

    for s in range(2):
        unit, _ = norm_parts(stream[s])
        rows[0, s] = (unit * gain_refs[s][...]).astype(BF)
        total[...] = stream[s]
        run(s, forward)
        if s == 0:
            stream[1] = total[...]
    back[0] = dot(packing, total[...].astype(BF), ((0,), (0,))).astype(BF)

    for phase, s in ((2, 1), (3, 0)):
        total[...] = jnp.zeros_like(total)
        run(phase, backward)
        pulled, grad_gain = norm_pull(total[...], stream[s], gain_refs[s][...])
        gains[pl.ds(s, 1), :] = grad_gain
        if s == 1:
            grad_stream = rows[1, 1].astype(F32) + pulled
            stream[1] = grad_stream
            rows[1, 0] = grad_stream.astype(BF)
        else:
            grad_rows = (stream[1] + pulled).astype(BF)
            back[1] = dot(packing, grad_rows, ((0,), (0,))).astype(BF)


def chain(came, up_first, down_first, up_second, down_second, gain_first, gain_second, slots, capacity):
    wide, hidden = up_first.shape[1:]
    experts = came.shape[1] // slots
    count = experts * capacity
    tile = 512
    vmem = pl.BlockSpec(memory_space=pltpu.VMEM)
    anys = pl.BlockSpec(memory_space=pl.ANY)
    return pl.pallas_call(
        functools.partial(chain_kernel, experts, slots, capacity, hidden // tile),
        out_shape=(
            jax.ShapeDtypeStruct(came.shape, BF),
            jax.ShapeDtypeStruct((2, 2, count, wide), BF),
            jax.ShapeDtypeStruct((8, wide), F32),
        ),
        in_specs=[vmem] + [anys] * 4 + [vmem] * 2,
        out_specs=(vmem,) * 3,
        scratch_shapes=[
            pltpu.VMEM((2, wide, tile), BF),
            pltpu.VMEM((2, tile, wide), BF),
            pltpu.VMEM((2, count, hidden), F32),
            pltpu.VMEM((2, count, wide), F32),
            pltpu.VMEM((count, wide), F32),
            pltpu.SemaphoreType.DMA((2, 2)),
        ],
        compiler_params=pltpu.CompilerParams(vmem_limit_bytes=56 * 1024 * 1024),
        name="chain",
    )(came, up_first, down_first, up_second, down_second, gain_first, gain_second)


def ring_rows(rows, axis):
    count = lax.axis_size(axis)
    back = [(i, (i - 1) % count) for i in range(count)]
    held = [rows]
    for _ in range(count - 1):
        held.append(lax.ppermute(held[-1], axis, back))
    return jnp.concatenate(held, axis=0)


def weight_grads(normed_rows, grad_rows, up_proj, down_proj):
    count = lax.axis_size("batch")
    width = up_proj.shape[1] // count
    first = lax.axis_index("batch") * width
    up_part = lax.dynamic_slice_in_dim(up_proj, first, width, 1)
    down_part = lax.dynamic_slice_in_dim(down_proj, first, width, 0)
    pre_act = jnp.dot(normed_rows, up_part, preferred_element_type=jnp.float32)
    middle, gelu_pull = jax.vjp(jax.nn.gelu, pre_act)
    grad_middle = jnp.einsum("rd,fd->rf", grad_rows, down_part, preferred_element_type=jnp.float32)
    grad_pre = gelu_pull(grad_middle)[0].astype(jnp.bfloat16)
    grad_down = jnp.einsum(
        "rf,rd->fd", middle.astype(jnp.bfloat16), grad_rows, preferred_element_type=jnp.float32
    )
    grad_up = jnp.einsum("rd,rf->df", normed_rows, grad_pre, preferred_element_type=jnp.float32)
    return grad_up, grad_down


def halve(blocks, axis, bit, dim):
    count = lax.axis_size(axis)
    mine = (lax.axis_index(axis) // bit) % 2
    kept = lax.dynamic_index_in_dim(blocks, mine, dim, keepdims=False)
    sent = lax.dynamic_index_in_dim(blocks, 1 - mine, dim, keepdims=False)
    got = lax.ppermute(sent, axis, [(i, i ^ bit) for i in range(count)])
    return (kept.astype(jnp.float32) + got.astype(jnp.float32)).astype(blocks.dtype)


def scatter_sum(parts):
    experts, groups = lax.axis_size("expert"), lax.axis_size("batch")
    kinds, rows, width = parts.shape
    bits_e = experts.bit_length() - 1
    bits_b = groups.bit_length() - 1
    shape = (kinds,) + (2,) * (bits_b + bits_e) + (rows // (experts * groups), width)
    blocks = parts.reshape(shape)
    for k in range(bits_e):
        blocks = halve(blocks, "expert", 1 << k, bits_b + bits_e - k)
    for k in range(bits_b):
        blocks = halve(blocks, "batch", 1 << k, bits_b - k)
    return blocks


def all_sum(value):
    for axis in ("expert", "batch"):
        count = lax.axis_size(axis)
        bit = 1
        while bit < count:
            value = value + lax.ppermute(value, axis, [(i, i ^ bit) for i in range(count)])
            bit *= 2
    return value


def per_device(
    tokens, doc_ends, routes, w_query, w_key, w_value, w_output, attn_gain, centroids,
    up_first, down_first, gain_first, up_second, down_second, gain_second, cotangent,
):
    count, wide = tokens.shape
    experts, groups = lax.axis_size("expert"), lax.axis_size("batch")
    capacity = 11 * count // (8 * experts)
    slots = -(-capacity // 16) * 16
    fits = groups == 4 and experts == 8
    routes_row = routes.reshape(1, count)
    gain = attn_gain[None]
    weights = (w_query, w_key, w_value, w_output)
    *kept, out_rows = enter(doc_ends, routes_row, tokens, cotangent, gain, centroids, weights, slots)

    def exchange(rows):
        blocks = rows.reshape(2, experts, slots, wide)
        return lax.all_to_all(blocks, "expert", split_axis=1, concat_axis=1, tiled=True).reshape(rows.shape)

    back, rows, gains = chain(
        exchange(out_rows), up_first, down_first, up_second, down_second, gain_first, gain_second, slots, capacity
    )
    block_out, grad_tokens, dense, small = leave(
        doc_ends, routes_row, tokens, cotangent, gain, centroids, kept, exchange(back), weights, slots, fits
    )
    if fits:
        *parts, dense, small, gains = finish(
            rows, up_first, down_first, up_second, down_second, dense, small, gains
        )
        gains = gains[:2]
    else:
        dense = scatter_sum(dense).astype(F32)
        small = all_sum(small)
        parts = []
        for s, (up, down) in enumerate(((up_first, down_first), (up_second, down_second))):
            for part in weight_grads(ring_rows(rows[0, s], "batch"), ring_rows(rows[1, s], "batch"), up[0], down[0]):
                parts.append(part[None])
        gains = jnp.sum(lax.all_gather(gains[:2], "batch"), axis=0)
    gain_part = wide // groups
    gains = lax.dynamic_slice_in_dim(gains, lax.axis_index("batch") * gain_part, gain_part, 1)
    return (
        block_out, grad_tokens, dense[0], dense[1], dense[2], dense[3], small[0], small[8:],
        parts[0], parts[1], gains[0:1], parts[2], parts[3], gains[1:2],
    )


def solution(mesh):
    return jax.shard_map(
        per_device,
        mesh=mesh,
        in_specs=(
            P(("batch", "expert"), None),
            P(("batch", "expert"), None),
            P(("batch", "expert"), None),
            P(),
            P(),
            P(),
            P(),
            P(),
            P(),
            P("expert", None, None),
            P("expert", None, None),
            P("expert", None),
            P("expert", None, None),
            P("expert", None, None),
            P("expert", None),
            P(("batch", "expert"), None),
        ),
        out_specs=(
            P(("batch", "expert"), None),
            P(("batch", "expert"), None),
            P(("batch", "expert"), None),
            P(("batch", "expert"), None),
            P(("batch", "expert"), None),
            P(("batch", "expert"), None),
            P(),
            P(),
            P("expert", None, "batch"),
            P("expert", "batch", None),
            P("expert", "batch"),
            P("expert", None, "batch"),
            P("expert", "batch", None),
            P("expert", "batch"),
        ),
        check_vma=False,
    )
```

```python
import functools
import jax, jax.numpy as jnp
from jax import lax
from jax.experimental import pallas as pl
from jax.experimental.pallas import tpu as pltpu
from jax.sharding import PartitionSpec as P


MESH = pl.DeviceIdType.MESH
BF = jnp.bfloat16
F32 = jnp.float32
GELU_A = 0.7978845608028654
GELU_B = 0.044715


def gelu_pair(v):
    square = v * v
    bent = jnp.tanh(GELU_A * v * (1.0 + GELU_B * square))
    half = 0.5 * (1.0 + bent)
    slope = half + 0.5 * v * (1.0 - bent * bent) * (GELU_A * (1.0 + 3.0 * GELU_B * square))
    return v * half, slope


def dot(a, b, dims=((1,), (0,))):
    return lax.dot_general(a, b, (dims, ((), ())), preferred_element_type=F32)


MASKED = -1e30
EPSILON = 1e-05


def split_three(value):
    high = value.astype(BF)
    rest = value - high.astype(F32)
    middle = rest.astype(BF)
    return high, middle, (rest - middle.astype(F32)).astype(BF)


def select_rows(marks, value, dims):
    return sum(dot(marks, term, dims) for term in split_three(value))


def norm_parts(stream):
    average = jnp.mean(stream, axis=-1, keepdims=True)
    centred = stream - average
    variance = jnp.mean(centred * centred, axis=-1, keepdims=True)
    scale = lax.rsqrt(variance + EPSILON)
    return centred * scale, scale


def norm_pull(grad, stream, gain):
    unit, scale = norm_parts(stream)
    inner = grad * gain
    mean_inner = jnp.mean(inner, axis=-1, keepdims=True)
    mean_product = jnp.mean(inner * unit, axis=-1, keepdims=True)
    return scale * (inner - mean_inner - unit * mean_product), jnp.sum(grad * unit, axis=0, keepdims=True)


def route_marks(routes_row, experts, slots):
    count = routes_row.shape[1]
    ids = lax.broadcasted_iota(jnp.int32, (experts, count), 0)
    chosen = (ids == routes_row).astype(F32)
    earlier = lax.broadcasted_iota(jnp.int32, (count, count), 0) <= lax.broadcasted_iota(jnp.int32, (count, count), 1)
    running = dot(chosen.astype(BF), earlier.astype(F32).astype(BF))
    rank = jnp.sum(running * chosen, axis=0, keepdims=True) - 1.0
    place = routes_row * slots + rank.astype(jnp.int32)
    rows = lax.broadcasted_iota(jnp.int32, (experts * slots, count), 0)
    return chosen.astype(BF), (rows == place).astype(F32).astype(BF)


def allowed_pairs(ends, docs, count):
    row = lax.broadcasted_iota(jnp.int32, (count, count), 0)
    col = lax.broadcasted_iota(jnp.int32, (count, count), 1)
    row_segment = jnp.zeros((count, count), jnp.int32)
    col_segment = jnp.zeros((count, count), jnp.int32)
    for d in range(docs):
        row_segment += (row >= ends[0, d]).astype(jnp.int32)
        col_segment += (col >= ends[0, d]).astype(jnp.int32)
    return (row_segment == col_segment) & (col <= row)


def half_marks(half):
    lane = lax.broadcasted_iota(jnp.int32, (1, 128), 1)
    inside = (lane >= 64 * half) & (lane < 64 * half + 64)
    return inside.astype(F32).astype(BF)


def head_shares(query_pair, key_pair, allowed, half):
    raw = dot(query_pair * half_marks(half), key_pair, ((1,), (1,)))
    scores = jnp.where(allowed, raw * 0.125, MASKED)
    raised = jnp.exp(scores - jnp.max(scores, axis=-1, keepdims=True))
    return raised * (1.0 / jnp.sum(raised, axis=-1, keepdims=True))


def join_halves(first, second):
    lane = lax.broadcasted_iota(jnp.int32, first.shape, 1)
    return jnp.where(lane < 64, first, second)


def enter_kernel(
    experts, slots, docs,
    ends, routes, tokens, cotangent, gain, cents, w_query, w_key, w_value, w_output,
    normed, queries, keys, values, mixed, hidden, out_rows,
    w_held, sems,
):
    copies = [
        pltpu.make_async_copy(w, w_held.at[i], sems.at[i])
        for i, w in enumerate((w_query, w_key, w_value, w_output))
    ]
    for copy in copies:
        copy.start()
    count, wide = tokens.shape
    unit, _ = norm_parts(tokens[...].astype(F32))
    normed[...] = (unit * gain[...]).astype(BF)
    for i, result in enumerate((queries, keys, values)):
        copies[i].wait()
        result[...] = dot(normed[...], w_held[i]).astype(BF)
    allowed = allowed_pairs(ends, docs, count)

    def one_pair(j, carry):
        cols = pl.ds(pl.multiple_of(j * 128, 128), 128)
        query_pair, key_pair, value_pair = queries[:, cols], keys[:, cols], values[:, cols]
        halves = [
            dot(head_shares(query_pair, key_pair, allowed, half).astype(BF), value_pair) for half in range(2)
        ]
        mixed[:, cols] = join_halves(*halves).astype(BF)
        return carry

    lax.fori_loop(0, wide // 128, one_pair, 0)
    copies[3].wait()
    hidden[...] = tokens[...].astype(F32) + dot(mixed[...], w_held[3])
    chosen, dispatch = route_marks(routes[...], experts, slots)
    own = select_rows(chosen, cents[...], ((0,), (0,)))
    gating = jax.nn.sigmoid(jnp.sum(hidden[...] * own, axis=-1, keepdims=True))
    live = (lax.broadcasted_iota(jnp.int32, (count, 1), 0) < ends[0, docs - 1]).astype(F32)
    grad_sent = (gating * (live * cotangent[...].astype(F32))).astype(BF)
    for kind, rows in enumerate((hidden[...].astype(BF), grad_sent)):
        out_rows[kind] = dot(dispatch, rows).astype(BF).reshape(experts, slots, wide)


def enter(ends, routes_row, tokens, cotangent, gain, cents, weights, slots):
    count, wide = tokens.shape
    experts, docs = cents.shape[0], ends.shape[1]
    vmem = pl.BlockSpec(memory_space=pltpu.VMEM)
    anys = pl.BlockSpec(memory_space=pl.ANY)
    low = jax.ShapeDtypeStruct((count, wide), BF)
    return pl.pallas_call(
        functools.partial(enter_kernel, experts, slots, docs),
        out_shape=(low,) * 5 + (
            jax.ShapeDtypeStruct((count, wide), F32),
            jax.ShapeDtypeStruct((2, experts, slots, wide), BF),
        ),
        in_specs=[pl.BlockSpec(memory_space=pltpu.SMEM)] + [vmem] * 5 + [anys] * 4,
        out_specs=(vmem,) * 7,
        scratch_shapes=[pltpu.VMEM((4, wide, wide), BF), pltpu.SemaphoreType.DMA((4,))],
        compiler_params=pltpu.CompilerParams(vmem_limit_bytes=48 * 1024 * 1024),
        name="enter",
    )(ends, routes_row, tokens, cotangent, gain, cents, *weights)


def backward_pair(allowed, queries, keys, values, grad_low, grad_three, j, carry):
    cols = pl.ds(pl.multiple_of(j * 128, 128), 128)
    query_pair, key_pair, value_pair = queries[:, cols], keys[:, cols], values[:, cols]
    grad_pair = grad_low[:, cols]
    parts = []
    for half in range(2):
        shares = head_shares(query_pair, key_pair, allowed, half)
        grad_shares = dot(grad_pair * half_marks(half), value_pair, ((1,), (1,)))
        inner = jnp.sum(shares * grad_shares, axis=-1, keepdims=True)
        raw = (shares * (grad_shares - inner) * 0.125).astype(BF)
        parts.append((
            dot(raw, key_pair),
            dot(raw, query_pair, ((0,), (0,))),
            dot(shares.astype(BF), grad_pair, ((0,), (0,))),
        ))
    for i in range(3):
        grad_three[i][:, cols] = join_halves(parts[0][i], parts[1][i]).astype(BF)
    return carry


def leave_kernel(
    experts, slots, docs,
    ends, routes, tokens, cotangent, gain, cents, normed, queries, keys, values, mixed, hidden, came,
    w_query, w_key, w_value, w_output,
    block_out, grad_tokens, dense, small,
    w_held, grad_low, grad_three, normed_turned, grad_hidden, sems,
):
    copies = [
        pltpu.make_async_copy(w, w_held.at[i], sems.at[i])
        for i, w in enumerate((w_query, w_key, w_value, w_output))
    ]
    for i in (3, 0, 1, 2):
        copies[i].start()
    count, wide = tokens.shape
    chosen, dispatch = route_marks(routes[...], experts, slots)
    own = select_rows(chosen, cents[...], ((0,), (0,)))
    gating = jax.nn.sigmoid(jnp.sum(hidden[...] * own, axis=-1, keepdims=True))
    live = (lax.broadcasted_iota(jnp.int32, (count, 1), 0) < ends[0, docs - 1]).astype(F32)
    returned = dot(dispatch, came[0], ((0,), (0,)))
    block_out[...] = (live * (gating * returned + (1.0 - gating) * hidden[...])).astype(BF)
    grad_block = live * cotangent[...].astype(F32)
    grad_score = jnp.sum(grad_block * (returned - hidden[...]), axis=-1, keepdims=True) * gating * (1.0 - gating)
    grad_hidden[...] = (1.0 - gating) * grad_block + dot(dispatch, came[1], ((0,), (0,))) + grad_score * own
    small[pl.ds(8, experts), :] = select_rows(chosen, grad_score * hidden[...], ((1,), (0,)))
    grad_low[...] = grad_hidden[...].astype(BF)
    copies[3].wait()
    grad_mixed = dot(grad_low[...], w_held[3], ((1,), (1,))).astype(BF)
    dense[3] = dot(mixed[...].T, grad_low[...]).astype(BF)
    grad_low[...] = grad_mixed
    allowed = allowed_pairs(ends, docs, count)

    lax.fori_loop(
        0, wide // 128, functools.partial(
            backward_pair, allowed, queries, keys, values, grad_low, [grad_three.at[i] for i in range(3)]
        ), 0
    )
    normed_turned[...] = normed[...].T
    for i in range(3):
        dense[i] = dot(normed_turned[...], grad_three[i]).astype(BF)
    for i in range(3):
        copies[i].wait()
    grad_normed = sum(dot(grad_three[i], w_held[i], ((1,), (1,))) for i in range(3))
    pulled, grad_gain = norm_pull(grad_normed, tokens[...].astype(F32), gain[...])
    grad_tokens[...] = grad_hidden[...] + pulled
    small[pl.ds(0, 8), :] = jnp.broadcast_to(grad_gain, (8, wide))


def leave(ends, routes_row, tokens, cotangent, gain, cents, kept, came, weights, slots):
    count, wide = tokens.shape
    experts, docs = cents.shape[0], ends.shape[1]
    vmem = pl.BlockSpec(memory_space=pltpu.VMEM)
    anys = pl.BlockSpec(memory_space=pl.ANY)
    return pl.pallas_call(
        functools.partial(leave_kernel, experts, slots, docs),
        out_shape=(
            jax.ShapeDtypeStruct((count, wide), BF),
            jax.ShapeDtypeStruct((count, wide), F32),
            jax.ShapeDtypeStruct((4, wide, wide), BF),
            jax.ShapeDtypeStruct((8 + experts, wide), F32),
        ),
        in_specs=[pl.BlockSpec(memory_space=pltpu.SMEM)] + [vmem] * 12 + [anys] * 4,
        out_specs=(vmem,) * 4,
        scratch_shapes=[
            pltpu.VMEM((4, wide, wide), BF),
            pltpu.VMEM((count, wide), BF),
            pltpu.VMEM((3, count, wide), BF),
            pltpu.VMEM((wide, count), BF),
            pltpu.VMEM((count, wide), F32),
            pltpu.SemaphoreType.DMA((4,)),
        ],
        compiler_params=pltpu.CompilerParams(vmem_limit_bytes=56 * 1024 * 1024),
        name="leave",
    )(ends, routes_row, tokens, cotangent, gain, cents, *kept, came, *weights)


def pack_marks(experts, slots, capacity):
    shape = (experts * capacity, experts * slots)
    row = lax.broadcasted_iota(jnp.int32, (shape[0], 1), 0)
    block = sum((row >= s * capacity).astype(jnp.int32) for s in range(1, experts))
    column = lax.broadcasted_iota(jnp.int32, shape, 1)
    return (column == row + (slots - capacity) * block).astype(F32).astype(BF)


def chain_kernel(
    experts, slots, capacity, tiles,
    came, up_first, down_first, up_second, down_second, gain_first, gain_second,
    back, rows, gains,
    up_tile, down_tile, pre, stream, total, sems,
):
    tile = up_tile.shape[2]
    ups, downs = (up_first, up_second), (down_first, down_second)
    gain_refs = (gain_first, gain_second)

    def fetch(s, c, slot):
        cols = pl.ds(pl.multiple_of(c * tile, tile), tile)
        return (
            pltpu.make_async_copy(ups[s].at[0, :, cols], up_tile.at[slot], sems.at[0, slot]),
            pltpu.make_async_copy(downs[s].at[0, cols, :], down_tile.at[slot], sems.at[1, slot]),
        )

    order = ((0, True), (1, True), (1, False), (0, False))

    def run(phase, body):
        s = order[phase][0]

        def step(c, carry):
            slot = lax.rem(c, 2)
            for copy in fetch(s, c, slot):
                copy.wait()

            @pl.when(c + 1 < tiles)
            def _():
                for copy in fetch(s, c + 1, 1 - slot):
                    copy.start()

            if phase < 3:
                @pl.when(c + 1 == tiles)
                def _():
                    for copy in fetch(order[phase + 1][0], 0, 1 - slot):
                        copy.start()

            body(s, pl.ds(pl.multiple_of(c * tile, tile), tile), slot)
            return carry

        lax.fori_loop(0, tiles, step, 0)

    for copy in fetch(0, 0, 0):
        copy.start()
    gains[...] = jnp.zeros_like(gains)
    packing = pack_marks(experts, slots, capacity)
    stream[0] = dot(packing, came[0])
    rows[1, 1] = dot(packing, came[1]).astype(BF)

    def forward(s, cols, slot):
        made = dot(rows[0, s], up_tile[slot])
        pre[s, :, cols] = made
        mid = gelu_pair(made)[0].astype(BF)
        total[...] += dot(mid, down_tile[slot])

    def backward(s, cols, slot):
        grad_mid = dot(rows[1, s], down_tile[slot], ((1,), (1,)))
        grad_pre = (gelu_pair(pre[s, :, cols])[1] * grad_mid).astype(BF)
        total[...] += dot(grad_pre, up_tile[slot], ((1,), (1,)))

    for s in range(2):
        unit, _ = norm_parts(stream[s])
        rows[0, s] = (unit * gain_refs[s][...]).astype(BF)
        total[...] = stream[s]
        run(s, forward)
        if s == 0:
            stream[1] = total[...]
    back[0] = dot(packing, total[...].astype(BF), ((0,), (0,))).astype(BF)

    for phase, s in ((2, 1), (3, 0)):
        total[...] = jnp.zeros_like(total)
        run(phase, backward)
        pulled, grad_gain = norm_pull(total[...], stream[s], gain_refs[s][...])
        gains[pl.ds(s, 1), :] = grad_gain
        if s == 1:
            grad_stream = rows[1, 1].astype(F32) + pulled
            stream[1] = grad_stream
            rows[1, 0] = grad_stream.astype(BF)
        else:
            grad_rows = (stream[1] + pulled).astype(BF)
            back[1] = dot(packing, grad_rows, ((0,), (0,))).astype(BF)


def chain(came, up_first, down_first, up_second, down_second, gain_first, gain_second, slots, capacity):
    wide, hidden = up_first.shape[1:]
    experts = came.shape[1] // slots
    count = experts * capacity
    tile = 1024
    vmem = pl.BlockSpec(memory_space=pltpu.VMEM)
    anys = pl.BlockSpec(memory_space=pl.ANY)
    return pl.pallas_call(
        functools.partial(chain_kernel, experts, slots, capacity, hidden // tile),
        out_shape=(
            jax.ShapeDtypeStruct(came.shape, BF),
            jax.ShapeDtypeStruct((2, 2, count, wide), BF),
            jax.ShapeDtypeStruct((8, wide), F32),
        ),
        in_specs=[vmem] + [anys] * 4 + [vmem] * 2,
        out_specs=(vmem,) * 3,
        scratch_shapes=[
            pltpu.VMEM((2, wide, tile), BF),
            pltpu.VMEM((2, tile, wide), BF),
            pltpu.VMEM((2, count, hidden), F32),
            pltpu.VMEM((2, count, wide), F32),
            pltpu.VMEM((count, wide), F32),
            pltpu.SemaphoreType.DMA((2, 2)),
        ],
        compiler_params=pltpu.CompilerParams(vmem_limit_bytes=56 * 1024 * 1024),
        name="chain",
    )(came, up_first, down_first, up_second, down_second, gain_first, gain_second)


def ring_rows(rows, axis):
    count = lax.axis_size(axis)
    back = [(i, (i - 1) % count) for i in range(count)]
    held = [rows]
    for _ in range(count - 1):
        held.append(lax.ppermute(held[-1], axis, back))
    return jnp.concatenate(held, axis=0)


def weight_grads(normed_rows, grad_rows, up_proj, down_proj):
    count = lax.axis_size("batch")
    width = up_proj.shape[1] // count
    first = lax.axis_index("batch") * width
    up_part = lax.dynamic_slice_in_dim(up_proj, first, width, 1)
    down_part = lax.dynamic_slice_in_dim(down_proj, first, width, 0)
    pre_act = jnp.dot(normed_rows, up_part, preferred_element_type=jnp.float32)
    middle, gelu_pull = jax.vjp(jax.nn.gelu, pre_act)
    grad_middle = jnp.einsum("rd,fd->rf", grad_rows, down_part, preferred_element_type=jnp.float32)
    grad_pre = gelu_pull(grad_middle)[0].astype(jnp.bfloat16)
    grad_down = jnp.einsum(
        "rf,rd->fd", middle.astype(jnp.bfloat16), grad_rows, preferred_element_type=jnp.float32
    )
    grad_up = jnp.einsum("rd,rf->df", normed_rows, grad_pre, preferred_element_type=jnp.float32)
    return grad_up, grad_down


def halve(blocks, axis, bit, dim):
    count = lax.axis_size(axis)
    mine = (lax.axis_index(axis) // bit) % 2
    kept = lax.dynamic_index_in_dim(blocks, mine, dim, keepdims=False)
    sent = lax.dynamic_index_in_dim(blocks, 1 - mine, dim, keepdims=False)
    got = lax.ppermute(sent, axis, [(i, i ^ bit) for i in range(count)])
    return (kept.astype(jnp.float32) + got.astype(jnp.float32)).astype(blocks.dtype)


def scatter_sum(parts):
    experts, groups = lax.axis_size("expert"), lax.axis_size("batch")
    kinds, rows, width = parts.shape
    bits_e = experts.bit_length() - 1
    bits_b = groups.bit_length() - 1
    shape = (kinds,) + (2,) * (bits_b + bits_e) + (rows // (experts * groups), width)
    blocks = parts.reshape(shape)
    for k in range(bits_e):
        blocks = halve(blocks, "expert", 1 << k, bits_b + bits_e - k)
    for k in range(bits_b):
        blocks = halve(blocks, "batch", 1 << k, bits_b - k)
    return blocks


def all_sum(value):
    for axis in ("expert", "batch"):
        count = lax.axis_size(axis)
        bit = 1
        while bit < count:
            value = value + lax.ppermute(value, axis, [(i, i ^ bit) for i in range(count)])
            bit *= 2
    return value


def layer_kernel(
    experts, groups, slots, capacity, docs, width, tiles,
    ends, routes, tokens, cotangent, gain, cents, normed, queries, keys, values, mixed, hidden, gain_first, gain_second,
    out_rows, w_query, w_key, w_value, w_output, up_first, down_first, up_second, down_second,
    block_out, grad_tokens, dense_out, small_out, gains_out, up_one, down_one, up_two, down_two, ring_held,
    w_held, acc, stream, total, norms, grads, cur, inbox, outbox, dense, turned,
    keep, s_got, g_got,
    w_sems, row_sems, a2a_send, a2a_recv, ring_send, ring_recv, dense_send, dense_recv, small_send, small_recv,
    gain_send, gain_recv, ready, out_sem,
):
    b, e = lax.axis_index("batch"), lax.axis_index("expert")
    count, wide = tokens.shape
    many = experts * capacity
    before, after = lax.rem(b + groups - 1, groups), lax.rem(b + 1, groups)
    core, x, y = lax.rem(e, 2), lax.rem(e // 2, 2), lax.rem(e // 4, 2)
    b0, b1 = lax.rem(b, 2), lax.rem(b // 2, 2)
    other = 1 - core
    to_core, to_x, to_y = (b, e + 1 - 2 * core), (b, e + 2 - 4 * x), (b, e + 4 - 8 * y)
    to_low, to_high = (b + 1 - 2 * b0, e), (b + 2 - 4 * b1, e)

    def remote(src, dst, send, recv, peer):
        return pltpu.make_async_remote_copy(
            src_ref=src, dst_ref=dst, send_sem=send, recv_sem=recv, device_id=peer, device_id_type=MESH
        )

    barrier = pltpu.get_barrier_semaphore()

    def greet(p, carry):
        peer = (b, lax.rem(e + p, experts))
        pl.semaphore_signal(barrier, inc=1, device_id=peer, device_id_type=MESH)
        return carry

    lax.fori_loop(1, experts, greet, 0)
    for peer in ((before, e), (after, e), to_high):
        pl.semaphore_signal(barrier, inc=1, device_id=peer, device_id_type=MESH)

    tile = wide
    ups, downs = (up_first, up_second), (down_first, down_second)
    gain_refs = (gain_first, gain_second)

    def fetch(s, c, slot):
        cols = pl.ds(pl.multiple_of(c * tile, tile), tile)
        return (
            pltpu.make_async_copy(ups[s].at[0, :, cols], w_held.at[slot], w_sems.at[slot]),
            pltpu.make_async_copy(downs[s].at[0, cols, :], w_held.at[2 + slot], w_sems.at[2 + slot]),
        )

    def stream_tiles(s, follow, body):
        def step(c, carry):
            slot = lax.rem(c, 2)
            for copy in fetch(s, c, slot):
                copy.wait()

            @pl.when(c + 1 < tiles)
            def _():
                for copy in fetch(s, c + 1, 1 - slot):
                    copy.start()

            if follow is not None:
                @pl.when(c + 1 == tiles)
                def _():
                    for copy in fetch(follow, 0, 1 - slot):
                        copy.start()

            body(c, slot)
            return carry

        lax.fori_loop(0, tiles, step, 0)

    def exchange(phase, kind, block):
        def copy(p):
            target = lax.rem(e + p, experts)
            return remote(
                block(target), inbox.at[phase, kind, e],
                a2a_send.at[phase, kind, p], a2a_recv.at[phase, kind, p], (b, target),
            )
        own = pltpu.make_async_copy(block(e), inbox.at[phase, kind, e], a2a_recv.at[phase, kind, 0])

        def start():
            own.start()
            lax.fori_loop(1, experts, lambda p, carry: (copy(p).start(), carry)[1], 0)

        def wait():
            own.wait()
            lax.fori_loop(1, experts, lambda p, carry: (copy(p).wait(), carry)[1], 0)

        return start, wait

    ring_sources = (cur, grads.at[1], grads.at[0])

    def ring(t, j):
        source = ring_sources[t] if j == 1 else ring_held.at[t, j - 1]
        return remote(source, ring_held.at[t, j], ring_send.at[t, j], ring_recv.at[t, j], (before, e))

    def advance(t, j):
        ring(t, j - 1).wait_recv()
        ring(t, j).start()

    for copy in fetch(0, 0, 0):
        copy.start()
    packing = pack_marks(experts, slots, capacity)
    gains_out[...] = jnp.zeros_like(gains_out)
    pl.semaphore_wait(barrier, experts + 2)

    def out_block(kind, p):
        return outbox.at[pl.ds(pl.multiple_of((kind * experts + p) * slots, 16), slots)]

    send_routed, get_routed = exchange(0, 0, lambda p: out_rows.at[0, p])
    send_grads, get_grads = exchange(0, 1, lambda p: out_rows.at[1, p])
    send_result, get_result = exchange(1, 0, functools.partial(out_block, 0))
    send_back, get_back = exchange(1, 1, functools.partial(out_block, 1))
    send_routed()
    send_grads()
    get_routed()
    arrived = dot(packing, inbox[0, 0].reshape(experts * slots, wide))
    stream[0] = arrived
    cur[...] = arrived.astype(BF)
    ring(0, 1).start()

    def slab(s, c):
        return pl.ds(pl.multiple_of((s * tiles + c) * many, 8), many)

    for s in range(2):
        unit, _ = norm_parts(stream[s])
        norms[s, 0] = (unit * gain_refs[s][...]).astype(BF)
        total[...] = stream[s]

        def forward(c, slot, s=s):
            made = dot(norms[s, 0], w_held[slot])
            acc[slab(s, c), :] = made
            total[...] += dot(gelu_pair(made)[0].astype(BF), w_held[2 + slot])

        stream_tiles(s, 1, forward)
        if s == 0:
            stream[1] = total[...]
            get_grads()
            grads[1] = dot(packing, inbox[0, 1].reshape(experts * slots, wide)).astype(BF)

    def put_back(kind, value):
        start = kind * experts * slots
        outbox[start:start + experts * slots, :] = dot(packing, value, ((0,), (0,))).astype(BF)

    put_back(0, total[...].astype(BF))
    send_result()
    advance(0, 2)
    for s in (1, 0):
        total[...] = jnp.zeros_like(total)

        def backward(c, slot, s=s):
            grad_mid = dot(grads[s], w_held[2 + slot], ((1,), (1,)))
            grad_pre = (gelu_pair(acc[slab(s, c), :])[1] * grad_mid).astype(BF)
            total[...] += dot(grad_pre, w_held[slot], ((1,), (1,)))

        stream_tiles(s, 0 if s == 1 else None, backward)
        pulled, grad_gain = norm_pull(total[...], stream[s], gain_refs[s][...])
        gains_out[pl.ds(s, 1), :] = grad_gain
        if s == 1:
            grad_stream = grads[1].astype(F32) + pulled
            stream[1] = grad_stream
            grads[0] = grad_stream.astype(BF)
        else:
            put_back(1, (stream[1] + pulled).astype(BF))
    send_back()
    attention_weights = [
        pltpu.make_async_copy(w, w_held.at[i], w_sems.at[i])
        for i, w in enumerate((w_query, w_key, w_value, w_output))
    ]
    for i in (3, 0, 1, 2):
        attention_weights[i].start()
    advance(0, 3)
    ring(1, 1).start()

    def small_step(level, peer):
        return remote(keep.at[level], s_got.at[level], small_send.at[level], small_recv.at[level], peer)

    def gain_step(level, peer):
        return remote(keep.at[5 + level, pl.ds(0, 8)], g_got.at[level], gain_send.at[level], gain_recv.at[level], peer)

    keep[5, pl.ds(0, 8)] = gains_out[...]
    gain_step(0, to_low).start()

    chosen, dispatch = route_marks(routes[...], experts, slots)
    own = select_rows(chosen, cents[...], ((0,), (0,)))
    gating = jax.nn.sigmoid(jnp.sum(hidden[...] * own, axis=-1, keepdims=True))
    live = (lax.broadcasted_iota(jnp.int32, (count, 1), 0) < ends[0, docs - 1]).astype(F32)
    get_result()
    returned = dot(dispatch, inbox[1, 0].reshape(experts * slots, wide), ((0,), (0,)))
    block_out[...] = (live * (gating * returned + (1.0 - gating) * hidden[...])).astype(BF)
    grad_block = live * cotangent[...].astype(F32)
    grad_score = jnp.sum(grad_block * (returned - hidden[...]), axis=-1, keepdims=True) * gating * (1.0 - gating)
    grad_hidden = stream.at[0, pl.ds(0, count)]
    grad_hidden[...] = (1.0 - gating) * grad_block + grad_score * own
    keep[0, pl.ds(8, experts)] = select_rows(chosen, grad_score * hidden[...], ((1,), (0,)))
    normed_turned = turned.at[:, pl.ds(0, count)]
    normed_turned[...] = normed[...].T
    ring(0, 1).wait_send()
    grad_low = cur.at[pl.ds(0, count)]
    get_back()
    grad_hidden[...] += dot(dispatch, inbox[1, 1].reshape(experts * slots, wide), ((0,), (0,)))
    grad_low[...] = grad_hidden[...].astype(BF)
    attention_weights[3].wait()
    grad_mixed = dot(grad_low[...], w_held[3], ((1,), (1,))).astype(BF)
    dense_product(dense, 3, mixed[...].T, grad_low)
    grad_low[...] = grad_mixed
    allowed = allowed_pairs(ends, docs, count)
    grad_three = [outbox.at[pl.ds(i * count, count)] for i in range(3)]
    lax.fori_loop(
        0, wide // 128, functools.partial(backward_pair, allowed, queries, keys, values, grad_low, grad_three), 0
    )
    for i in range(3):
        dense_product(dense, i, normed_turned[...], grad_three[i])
    for i in range(3):
        attention_weights[i].wait()
    grad_normed = sum(dot(grad_three[i][...], w_held[i], ((1,), (1,))) for i in range(3))
    pl.semaphore_signal(ready.at[0], inc=1, device_id=to_core, device_id_type=MESH)
    pulled, grad_gain = norm_pull(grad_normed, tokens[...].astype(F32), gain[...])
    grad_tokens[...] = grad_hidden[...] + pulled
    keep[0, pl.ds(0, 8)] = jnp.broadcast_to(grad_gain, (8, wide))

    def rows_at(start, size):
        return pl.ds(pl.multiple_of(start, 32), size)

    def level_copies(level):
        copies = []
        for m in range(4):
            mine, theirs = dense.at[core, m], dense.at[other, m]
            if level == 0:
                parts = ((theirs, w_held.at[m // 2, pl.ds(m % 2 * 512, 512)], to_core),)
            elif level == 1 and m < 2:
                parts = ((mine.at[rows_at((1 - x) * 256, 256)], theirs.at[pl.ds(0, 256)], to_x),)
            elif level == 1:
                parts = tuple(
                    (mine.at[rows_at(xx * 256 + (1 - y) * 128, 128)], theirs.at[pl.ds(xx * 128, 128)], to_y)
                    for xx in range(2)
                )
            elif level == 2 and m < 2:
                parts = ((mine.at[rows_at(x * 256 + (1 - y) * 128, 128)], theirs.at[pl.ds(256, 128)], to_y),)
            elif level == 2:
                parts = ((mine.at[rows_at((1 - x) * 256 + y * 128, 128)], theirs.at[pl.ds(256, 128)], to_x),)
            elif level == 3:
                start = x * 256 + y * 128 + (1 - b0) * 64
                parts = ((mine.at[rows_at(start, 64)], theirs.at[pl.ds(384, 64)], to_low),)
            else:
                start = x * 256 + y * 128 + b0 * 64 + (1 - b1) * 32
                parts = ((mine.at[rows_at(start, 32)], theirs.at[pl.ds(448, 32)], to_high),)
            for n, (src, dst, peer) in enumerate(parts):
                copies.append(remote(src, dst, dense_send.at[level, m, n], dense_recv.at[level, m, n], peer))
        return copies

    small_peers = (to_core, to_x, to_y, to_low, to_high)

    def begin(level):
        for sem in {0: (0,), 1: (1, 2), 2: (), 3: (3,), 4: (4,)}[level]:
            pl.semaphore_wait(ready.at[sem], 1)
        for copy in level_copies(level):
            copy.start()
        small_step(level, small_peers[level]).start()

    def add_rows(m, start, size, got):
        where = rows_at(start, size)
        dense[core, m, where, :] = (dense[core, m, where, :].astype(F32) + got.astype(F32)).astype(BF)

    def end(level):
        for copy in level_copies(level):
            copy.wait()
        small_step(level, small_peers[level]).wait()
        if level < 4:
            keep[level + 1] = keep[level] + s_got[level]
        for m in range(4):
            if level == 0:
                for h in range(2):
                    add_rows(m, h * 256, 256, w_held[m // 2, m % 2 * 512 + h * 256:m % 2 * 512 + h * 256 + 256])
            elif level == 1 and m < 2:
                add_rows(m, x * 256, 256, dense[other, m, 0:256])
            elif level == 1:
                for xx in range(2):
                    add_rows(m, xx * 256 + y * 128, 128, dense[other, m, xx * 128:xx * 128 + 128])
            elif level == 2:
                add_rows(m, x * 256 + y * 128, 128, dense[other, m, 256:384])
            elif level == 3:
                add_rows(m, x * 256 + y * 128 + b0 * 64, 64, dense[other, m, 384:448])
            else:
                where = rows_at(x * 256 + y * 128 + b0 * 64 + b1 * 32, 32)
                dense_out[m] = dense[core, m, where, :].astype(F32) + dense[other, m, 448:480].astype(F32)
        if level == 0:
            for sem, peer in enumerate(small_peers[1:], 1):
                pl.semaphore_signal(ready.at[sem], inc=1, device_id=peer, device_id_type=MESH)
        if level == 4:
            small_out[...] = keep[4] + s_got[4]

    begin(0)
    advance(1, 2)
    ring(2, 1).start()
    gain_step(0, to_low).wait()
    keep[6, pl.ds(0, 8)] = keep[5, pl.ds(0, 8)] + g_got[0]
    gain_step(1, to_high).start()
    ring(0, 3).wait_recv()
    for k in range(1, groups):
        load = pltpu.make_async_copy(ring_held.at[0, k], cur, row_sems.at[0])
        load.start()
        load.wait()
        routed = cur[...].astype(F32)
        acc[(k - 1) * many:k * many, :] = routed
        norms[0, k] = (norm_parts(routed)[0] * gain_first[...]).astype(BF)
    end(0)
    begin(1)
    for copy in fetch(0, 0, 0):
        copy.start()

    def forward_others(c, slot):
        def one_group(k, carry):
            where = pl.ds(pl.multiple_of(k * many, 8), many)
            mid = gelu_pair(dot(norms[0, k + 1], w_held[slot]))[0].astype(BF)
            acc[where, :] += dot(mid, w_held[2 + slot])
            return carry

        lax.fori_loop(0, groups - 1, one_group, 0)

        @pl.when(c == tiles - 2)
        def _():
            end(1)
            begin(2)

    stream_tiles(0, None, forward_others)
    col = pl.multiple_of(b * width, width)
    shards = []
    for i, s in enumerate((1, 0)):
        shards.append((
            pltpu.make_async_copy(ups[s].at[0, :, pl.ds(col, width)], w_held.at[2 * i], w_sems.at[2 * i]),
            pltpu.make_async_copy(downs[s].at[0, pl.ds(col, width), :], w_held.at[2 * i + 1], w_sems.at[2 * i + 1]),
        ))
    for pair in shards:
        for copy in pair:
            copy.start()
    for k in range(1, groups):
        norms[1, k] = (norm_parts(acc[(k - 1) * many:k * many, :])[0] * gain_second[...]).astype(BF)
    advance(1, 3)
    advance(2, 2)
    gain_step(1, to_high).wait()
    gains_out[...] = keep[6, pl.ds(0, 8)] + g_got[1]

    def weight_phase(i, s, t, hooks):
        for copy in shards[i]:
            copy.wait()
        acc[0:wide + width, :] = jnp.zeros((wide + width, wide), F32)

        def step(k, carry):
            for at, hook in hooks.items():
                pl.when(k == at)(hook)

            @pl.when(k == 0)
            def _():
                load = pltpu.make_async_copy(grads.at[s], cur, row_sems.at[0])
                load.start()
                load.wait()

            @pl.when(k > 0)
            def _():
                load = pltpu.make_async_copy(ring_held.at[t, k], cur, row_sems.at[0])
                load.start()
                load.wait()

            turned[...] = norms[s, k].T

            def chunk(c, carry):
                cols = pl.ds(pl.multiple_of(c * 256, 256), 256)
                mid, slope = gelu_pair(dot(norms[s, k], w_held[2 * i, :, cols]))
                grad_mid = dot(cur[...], w_held[2 * i + 1, cols, :], ((1,), (1,)))
                below = pl.ds(pl.multiple_of(wide + c * 256, 256), 256)
                acc[below, :] += dot(mid.astype(BF), cur[...], ((0,), (0,)))
                acc[0:wide, cols] += dot(turned[...], (grad_mid * slope).astype(BF))
                return carry

            lax.fori_loop(0, width // 256, chunk, 0)
            return carry

        lax.fori_loop(0, groups, step, 0)
        results = (
            pltpu.make_async_copy(acc.at[pl.ds(0, wide)], (up_one, up_two)[s].at[0], out_sem.at[0, s]),
            pltpu.make_async_copy(acc.at[pl.ds(wide, width)], (down_one, down_two)[s].at[0], out_sem.at[1, s]),
        )
        for copy in results:
            copy.start()
        for copy in results:
            copy.wait()

    def next_level(level):
        def hook():
            end(level)
            begin(level + 1)
        return hook

    def late():
        ring(1, 3).wait_recv()
        advance(2, 3)

    weight_phase(0, 1, 1, {1: next_level(2), 2: next_level(3), 3: late})
    weight_phase(1, 0, 2, {1: lambda: end(4), 3: lambda: ring(2, 3).wait_recv()})
    for t in range(3):
        for j in range(1, groups):
            if (t, j) != (0, 1):
                ring(t, j).wait_send()


def dense_product(dense, which, turned, right):
    block = 32
    for g in range(4):
        product = dot(turned[g * 8 * block:(g + 1) * 8 * block], right[...]).astype(BF)
        for e in range(8):
            place = (((e // 2) % 2 * 2 + e // 4) * 4 + g % 2 * 2 + g // 2) * block
            dense[e % 2, which, place:place + block] = product[e * block:(e + 1) * block]


def layer(
    ends, routes_row, tokens, cotangent, gain, cents, kept, gain_first, gain_second, out_rows, weights, expert_weights,
    slots, capacity,
):
    count, wide = tokens.shape
    experts, docs, groups = cents.shape[0], ends.shape[1], lax.axis_size("batch")
    many, ff = experts * capacity, expert_weights[0].shape[2]
    width, tiles = ff // groups, ff // wide
    vmem = pl.BlockSpec(memory_space=pltpu.VMEM)
    anys = pl.BlockSpec(memory_space=pl.ANY)
    f32_out = jax.ShapeDtypeStruct((1, wide, width), F32)
    dma = pltpu.SemaphoreType.DMA
    return pl.pallas_call(
        functools.partial(layer_kernel, experts, groups, slots, capacity, docs, width, tiles),
        out_shape=(
            jax.ShapeDtypeStruct((count, wide), BF),
            jax.ShapeDtypeStruct((count, wide), F32),
            jax.ShapeDtypeStruct((4, 32, wide), F32),
            jax.ShapeDtypeStruct((8 + experts, wide), F32),
            jax.ShapeDtypeStruct((8, wide), F32),
            f32_out, f32_out, f32_out, f32_out,
            jax.ShapeDtypeStruct((3, groups, many, wide), BF),
        ),
        in_specs=[pl.BlockSpec(memory_space=pltpu.SMEM)] + [vmem] * 13 + [anys] * 9,
        out_specs=(vmem,) * 5 + (anys,) * 5,
        scratch_shapes=[
            pltpu.VMEM((4, wide, wide), BF),
            pltpu.VMEM((2 * tiles * many, wide), F32),
            pltpu.VMEM((2, many, wide), F32),
            pltpu.VMEM((many, wide), F32),
            pltpu.VMEM((2, groups, many, wide), BF),
            pltpu.VMEM((2, many, wide), BF),
            pltpu.VMEM((many, wide), BF),
            pltpu.VMEM((2, 2, experts, slots, wide), BF),
            pltpu.VMEM((max(2 * experts * slots, 3 * count), wide), BF),
            pltpu.VMEM((2, 4, wide // 2, wide), BF),
            pltpu.VMEM((wide, many), BF),
            pltpu.VMEM((7, 16, wide), F32),
            pltpu.VMEM((5, 16, wide), F32),
            pltpu.VMEM((2, 8, wide), F32),
            dma((4,)), dma((1,)), dma((2, 2, experts)), dma((2, 2, experts)),
            dma((3, groups)), dma((3, groups)), dma((5, 4, 2)), dma((5, 4, 2)), dma((5,)), dma((5,)),
            dma((2,)), dma((2,)), pltpu.SemaphoreType.REGULAR((5,)), dma((2, 2)),
        ],
        compiler_params=pltpu.CompilerParams(
            collective_id=1, has_side_effects=True, vmem_limit_bytes=64 * 1024 * 1024 - 65536
        ),
        name="layer",
    )(
        ends, routes_row, tokens, cotangent, gain, cents, *kept, gain_first, gain_second, out_rows, *weights,
        *expert_weights,
    )


def per_device(
    tokens, doc_ends, routes, w_query, w_key, w_value, w_output, attn_gain, centroids,
    up_first, down_first, gain_first, up_second, down_second, gain_second, cotangent,
):
    count, wide = tokens.shape
    experts, groups = lax.axis_size("expert"), lax.axis_size("batch")
    capacity = 11 * count // (8 * experts)
    slots = -(-capacity // 16) * 16
    routes_row = routes.reshape(1, count)
    gain = attn_gain[None]
    weights = (w_query, w_key, w_value, w_output)
    expert_weights = (up_first, down_first, up_second, down_second)
    *kept, out_rows = enter(doc_ends, routes_row, tokens, cotangent, gain, centroids, weights, slots)
    if groups == 4 and experts == 8:
        block_out, grad_tokens, dense, small, gains, *parts = layer(
            doc_ends, routes_row, tokens, cotangent, gain, centroids, kept, gain_first, gain_second, out_rows,
            weights, expert_weights, slots, capacity,
        )
        gains = gains[:2]
    else:
        def exchange(blocks):
            return lax.all_to_all(blocks, "expert", split_axis=1, concat_axis=1, tiled=True)

        came = exchange(out_rows).reshape(2, experts * slots, wide)
        back, rows, gains = chain(came, *expert_weights, gain_first, gain_second, slots, capacity)
        came_back = exchange(back.reshape(out_rows.shape)).reshape(back.shape)
        block_out, grad_tokens, dense, small = leave(
            doc_ends, routes_row, tokens, cotangent, gain, centroids, kept, came_back, weights, slots
        )
        dense = scatter_sum(dense).astype(F32)
        small = all_sum(small)
        parts = []
        for s, (up, down) in enumerate(((up_first, down_first), (up_second, down_second))):
            for part in weight_grads(ring_rows(rows[0, s], "batch"), ring_rows(rows[1, s], "batch"), up[0], down[0]):
                parts.append(part[None])
        gains = jnp.sum(lax.all_gather(gains[:2], "batch"), axis=0)
    gain_part = wide // groups
    gains = lax.dynamic_slice_in_dim(gains, lax.axis_index("batch") * gain_part, gain_part, 1)
    return (
        block_out, grad_tokens, dense[0], dense[1], dense[2], dense[3], small[0], small[8:],
        parts[0], parts[1], gains[0:1], parts[2], parts[3], gains[1:2],
    )


def solution(mesh):
    return jax.shard_map(
        per_device,
        mesh=mesh,
        in_specs=(
            P(("batch", "expert"), None),
            P(("batch", "expert"), None),
            P(("batch", "expert"), None),
            P(),
            P(),
            P(),
            P(),
            P(),
            P(),
            P("expert", None, None),
            P("expert", None, None),
            P("expert", None),
            P("expert", None, None),
            P("expert", None, None),
            P("expert", None),
            P(("batch", "expert"), None),
        ),
        out_specs=(
            P(("batch", "expert"), None),
            P(("batch", "expert"), None),
            P(("batch", "expert"), None),
            P(("batch", "expert"), None),
            P(("batch", "expert"), None),
            P(("batch", "expert"), None),
            P(),
            P(),
            P("expert", None, "batch"),
            P("expert", "batch", None),
            P("expert", "batch"),
            P("expert", None, "batch"),
            P("expert", "batch", None),
            P("expert", "batch"),
        ),
        check_vma=False,
    )
```

```python
import functools
import jax, jax.numpy as jnp
from jax import lax
from jax.experimental import pallas as pl
from jax.experimental.pallas import tpu as pltpu
from jax.sharding import PartitionSpec as P


MESH = pl.DeviceIdType.MESH
BF = jnp.bfloat16
F32 = jnp.float32
GELU_A = 0.7978845608028654
GELU_B = 0.044715


def gelu_pair(v):
    square = v * v
    bent = jnp.tanh(GELU_A * v * (1.0 + GELU_B * square))
    half = 0.5 * (1.0 + bent)
    slope = half + 0.5 * v * (1.0 - bent * bent) * (GELU_A * (1.0 + 3.0 * GELU_B * square))
    return v * half, slope


def dot(a, b, dims=((1,), (0,))):
    return lax.dot_general(a, b, (dims, ((), ())), preferred_element_type=F32)


MASKED = -1e30
EPSILON = 1e-05


def split_three(value):
    high = value.astype(BF)
    rest = value - high.astype(F32)
    middle = rest.astype(BF)
    return high, middle, (rest - middle.astype(F32)).astype(BF)


def select_rows(marks, value, dims):
    return sum(dot(marks, term, dims) for term in split_three(value))


def norm_parts(stream):
    average = jnp.mean(stream, axis=-1, keepdims=True)
    centred = stream - average
    variance = jnp.mean(centred * centred, axis=-1, keepdims=True)
    scale = lax.rsqrt(variance + EPSILON)
    return centred * scale, scale


def norm_pull(grad, stream, gain):
    unit, scale = norm_parts(stream)
    inner = grad * gain
    mean_inner = jnp.mean(inner, axis=-1, keepdims=True)
    mean_product = jnp.mean(inner * unit, axis=-1, keepdims=True)
    return scale * (inner - mean_inner - unit * mean_product), jnp.sum(grad * unit, axis=0, keepdims=True)


def route_marks(routes_row, experts, slots):
    count = routes_row.shape[1]
    ids = lax.broadcasted_iota(jnp.int32, (experts, count), 0)
    chosen = (ids == routes_row).astype(F32)
    earlier = lax.broadcasted_iota(jnp.int32, (count, count), 0) <= lax.broadcasted_iota(jnp.int32, (count, count), 1)
    running = dot(chosen.astype(BF), earlier.astype(F32).astype(BF))
    rank = jnp.sum(running * chosen, axis=0, keepdims=True) - 1.0
    place = routes_row * slots + rank.astype(jnp.int32)
    rows = lax.broadcasted_iota(jnp.int32, (experts * slots, count), 0)
    return chosen.astype(BF), (rows == place).astype(F32).astype(BF)


def allowed_pairs(ends, docs, count):
    row = lax.broadcasted_iota(jnp.int32, (count, count), 0)
    col = lax.broadcasted_iota(jnp.int32, (count, count), 1)
    row_segment = jnp.zeros((count, count), jnp.int32)
    col_segment = jnp.zeros((count, count), jnp.int32)
    for d in range(docs):
        row_segment += (row >= ends[0, d]).astype(jnp.int32)
        col_segment += (col >= ends[0, d]).astype(jnp.int32)
    return (row_segment == col_segment) & (col <= row)


def half_marks(half):
    lane = lax.broadcasted_iota(jnp.int32, (1, 128), 1)
    inside = (lane >= 64 * half) & (lane < 64 * half + 64)
    return inside.astype(F32).astype(BF)


def head_shares(query_pair, key_pair, allowed, half):
    raw = dot(query_pair * half_marks(half), key_pair, ((1,), (1,)))
    scores = jnp.where(allowed, raw * 0.125, MASKED)
    raised = jnp.exp(scores - jnp.max(scores, axis=-1, keepdims=True))
    return raised * (1.0 / jnp.sum(raised, axis=-1, keepdims=True))


def join_halves(first, second):
    lane = lax.broadcasted_iota(jnp.int32, first.shape, 1)
    return jnp.where(lane < 64, first, second)


def forward_pair(allowed, queries, keys, values, mixed, j, carry):
    cols = pl.ds(pl.multiple_of(j * 128, 128), 128)
    query_pair, key_pair, value_pair = queries[:, cols], keys[:, cols], values[:, cols]
    halves = [dot(head_shares(query_pair, key_pair, allowed, half).astype(BF), value_pair) for half in range(2)]
    mixed[:, cols] = join_halves(*halves).astype(BF)
    return carry


def enter_kernel(
    experts, slots, docs,
    ends, routes, tokens, cotangent, gain, cents, w_query, w_key, w_value, w_output,
    normed, queries, keys, values, mixed, hidden, out_rows,
    w_held, sems,
):
    copies = [
        pltpu.make_async_copy(w, w_held.at[i], sems.at[i])
        for i, w in enumerate((w_query, w_key, w_value, w_output))
    ]
    for copy in copies:
        copy.start()
    count, wide = tokens.shape
    unit, _ = norm_parts(tokens[...].astype(F32))
    normed[...] = (unit * gain[...]).astype(BF)
    for i, result in enumerate((queries, keys, values)):
        copies[i].wait()
        result[...] = dot(normed[...], w_held[i]).astype(BF)
    allowed = allowed_pairs(ends, docs, count)

    lax.fori_loop(0, wide // 128, functools.partial(forward_pair, allowed, queries, keys, values, mixed), 0)
    copies[3].wait()
    hidden[...] = tokens[...].astype(F32) + dot(mixed[...], w_held[3])
    chosen, dispatch = route_marks(routes[...], experts, slots)
    own = select_rows(chosen, cents[...], ((0,), (0,)))
    gating = jax.nn.sigmoid(jnp.sum(hidden[...] * own, axis=-1, keepdims=True))
    live = (lax.broadcasted_iota(jnp.int32, (count, 1), 0) < ends[0, docs - 1]).astype(F32)
    grad_sent = (gating * (live * cotangent[...].astype(F32))).astype(BF)
    for kind, rows in enumerate((hidden[...].astype(BF), grad_sent)):
        out_rows[kind] = dot(dispatch, rows).astype(BF).reshape(experts, slots, wide)


def enter(ends, routes_row, tokens, cotangent, gain, cents, weights, slots):
    count, wide = tokens.shape
    experts, docs = cents.shape[0], ends.shape[1]
    vmem = pl.BlockSpec(memory_space=pltpu.VMEM)
    anys = pl.BlockSpec(memory_space=pl.ANY)
    low = jax.ShapeDtypeStruct((count, wide), BF)
    return pl.pallas_call(
        functools.partial(enter_kernel, experts, slots, docs),
        out_shape=(low,) * 5 + (
            jax.ShapeDtypeStruct((count, wide), F32),
            jax.ShapeDtypeStruct((2, experts, slots, wide), BF),
        ),
        in_specs=[pl.BlockSpec(memory_space=pltpu.SMEM)] + [vmem] * 5 + [anys] * 4,
        out_specs=(vmem,) * 7,
        scratch_shapes=[pltpu.VMEM((4, wide, wide), BF), pltpu.SemaphoreType.DMA((4,))],
        compiler_params=pltpu.CompilerParams(vmem_limit_bytes=48 * 1024 * 1024),
        name="enter",
    )(ends, routes_row, tokens, cotangent, gain, cents, *weights)


def backward_pair(allowed, queries, keys, values, grad_low, grad_three, j, carry):
    cols = pl.ds(pl.multiple_of(j * 128, 128), 128)
    query_pair, key_pair, value_pair = queries[:, cols], keys[:, cols], values[:, cols]
    grad_pair = grad_low[:, cols]
    parts = []
    for half in range(2):
        shares = head_shares(query_pair, key_pair, allowed, half)
        grad_shares = dot(grad_pair * half_marks(half), value_pair, ((1,), (1,)))
        inner = jnp.sum(shares * grad_shares, axis=-1, keepdims=True)
        raw = (shares * (grad_shares - inner) * 0.125).astype(BF)
        parts.append((
            dot(raw, key_pair),
            dot(raw, query_pair, ((0,), (0,))),
            dot(shares.astype(BF), grad_pair, ((0,), (0,))),
        ))
    for i in range(3):
        grad_three[i][:, cols] = join_halves(parts[0][i], parts[1][i]).astype(BF)
    return carry


def leave_kernel(
    experts, slots, docs,
    ends, routes, tokens, cotangent, gain, cents, normed, queries, keys, values, mixed, hidden, came,
    w_query, w_key, w_value, w_output,
    block_out, grad_tokens, dense, small,
    w_held, grad_low, grad_three, normed_turned, grad_hidden, sems,
):
    copies = [
        pltpu.make_async_copy(w, w_held.at[i], sems.at[i])
        for i, w in enumerate((w_query, w_key, w_value, w_output))
    ]
    for i in (3, 0, 1, 2):
        copies[i].start()
    count, wide = tokens.shape
    chosen, dispatch = route_marks(routes[...], experts, slots)
    own = select_rows(chosen, cents[...], ((0,), (0,)))
    gating = jax.nn.sigmoid(jnp.sum(hidden[...] * own, axis=-1, keepdims=True))
    live = (lax.broadcasted_iota(jnp.int32, (count, 1), 0) < ends[0, docs - 1]).astype(F32)
    returned = dot(dispatch, came[0], ((0,), (0,)))
    block_out[...] = (live * (gating * returned + (1.0 - gating) * hidden[...])).astype(BF)
    grad_block = live * cotangent[...].astype(F32)
    grad_score = jnp.sum(grad_block * (returned - hidden[...]), axis=-1, keepdims=True) * gating * (1.0 - gating)
    grad_hidden[...] = (1.0 - gating) * grad_block + dot(dispatch, came[1], ((0,), (0,))) + grad_score * own
    small[pl.ds(8, experts), :] = select_rows(chosen, grad_score * hidden[...], ((1,), (0,)))
    grad_low[...] = grad_hidden[...].astype(BF)
    copies[3].wait()
    grad_mixed = dot(grad_low[...], w_held[3], ((1,), (1,))).astype(BF)
    dense[3] = dot(mixed[...].T, grad_low[...]).astype(BF)
    grad_low[...] = grad_mixed
    allowed = allowed_pairs(ends, docs, count)

    lax.fori_loop(
        0, wide // 128, functools.partial(
            backward_pair, allowed, queries, keys, values, grad_low, [grad_three.at[i] for i in range(3)]
        ), 0
    )
    normed_turned[...] = normed[...].T
    for i in range(3):
        dense[i] = dot(normed_turned[...], grad_three[i]).astype(BF)
    for i in range(3):
        copies[i].wait()
    grad_normed = sum(dot(grad_three[i], w_held[i], ((1,), (1,))) for i in range(3))
    pulled, grad_gain = norm_pull(grad_normed, tokens[...].astype(F32), gain[...])
    grad_tokens[...] = grad_hidden[...] + pulled
    small[pl.ds(0, 8), :] = jnp.broadcast_to(grad_gain, (8, wide))


def leave(ends, routes_row, tokens, cotangent, gain, cents, kept, came, weights, slots):
    count, wide = tokens.shape
    experts, docs = cents.shape[0], ends.shape[1]
    vmem = pl.BlockSpec(memory_space=pltpu.VMEM)
    anys = pl.BlockSpec(memory_space=pl.ANY)
    return pl.pallas_call(
        functools.partial(leave_kernel, experts, slots, docs),
        out_shape=(
            jax.ShapeDtypeStruct((count, wide), BF),
            jax.ShapeDtypeStruct((count, wide), F32),
            jax.ShapeDtypeStruct((4, wide, wide), BF),
            jax.ShapeDtypeStruct((8 + experts, wide), F32),
        ),
        in_specs=[pl.BlockSpec(memory_space=pltpu.SMEM)] + [vmem] * 12 + [anys] * 4,
        out_specs=(vmem,) * 4,
        scratch_shapes=[
            pltpu.VMEM((4, wide, wide), BF),
            pltpu.VMEM((count, wide), BF),
            pltpu.VMEM((3, count, wide), BF),
            pltpu.VMEM((wide, count), BF),
            pltpu.VMEM((count, wide), F32),
            pltpu.SemaphoreType.DMA((4,)),
        ],
        compiler_params=pltpu.CompilerParams(vmem_limit_bytes=56 * 1024 * 1024),
        name="leave",
    )(ends, routes_row, tokens, cotangent, gain, cents, *kept, came, *weights)


def pack_marks(experts, slots, capacity):
    shape = (experts * capacity, experts * slots)
    row = lax.broadcasted_iota(jnp.int32, (shape[0], 1), 0)
    block = sum((row >= s * capacity).astype(jnp.int32) for s in range(1, experts))
    column = lax.broadcasted_iota(jnp.int32, shape, 1)
    return (column == row + (slots - capacity) * block).astype(F32).astype(BF)


def chain_kernel(
    experts, slots, capacity, tiles,
    came, up_first, down_first, up_second, down_second, gain_first, gain_second,
    back, rows, gains,
    up_tile, down_tile, pre, stream, total, sems,
):
    tile = up_tile.shape[2]
    ups, downs = (up_first, up_second), (down_first, down_second)
    gain_refs = (gain_first, gain_second)

    def fetch(s, c, slot):
        cols = pl.ds(pl.multiple_of(c * tile, tile), tile)
        return (
            pltpu.make_async_copy(ups[s].at[0, :, cols], up_tile.at[slot], sems.at[0, slot]),
            pltpu.make_async_copy(downs[s].at[0, cols, :], down_tile.at[slot], sems.at[1, slot]),
        )

    order = ((0, True), (1, True), (1, False), (0, False))

    def run(phase, body):
        s = order[phase][0]

        def step(c, carry):
            slot = lax.rem(c, 2)
            for copy in fetch(s, c, slot):
                copy.wait()

            @pl.when(c + 1 < tiles)
            def _():
                for copy in fetch(s, c + 1, 1 - slot):
                    copy.start()

            if phase < 3:
                @pl.when(c + 1 == tiles)
                def _():
                    for copy in fetch(order[phase + 1][0], 0, 1 - slot):
                        copy.start()

            body(s, pl.ds(pl.multiple_of(c * tile, tile), tile), slot)
            return carry

        lax.fori_loop(0, tiles, step, 0)

    for copy in fetch(0, 0, 0):
        copy.start()
    gains[...] = jnp.zeros_like(gains)
    packing = pack_marks(experts, slots, capacity)
    stream[0] = dot(packing, came[0])
    rows[1, 1] = dot(packing, came[1]).astype(BF)

    def forward(s, cols, slot):
        made = dot(rows[0, s], up_tile[slot])
        pre[s, :, cols] = made
        mid = gelu_pair(made)[0].astype(BF)
        total[...] += dot(mid, down_tile[slot])

    def backward(s, cols, slot):
        grad_mid = dot(rows[1, s], down_tile[slot], ((1,), (1,)))
        grad_pre = (gelu_pair(pre[s, :, cols])[1] * grad_mid).astype(BF)
        total[...] += dot(grad_pre, up_tile[slot], ((1,), (1,)))

    for s in range(2):
        unit, _ = norm_parts(stream[s])
        rows[0, s] = (unit * gain_refs[s][...]).astype(BF)
        total[...] = stream[s]
        run(s, forward)
        if s == 0:
            stream[1] = total[...]
    back[0] = dot(packing, total[...].astype(BF), ((0,), (0,))).astype(BF)

    for phase, s in ((2, 1), (3, 0)):
        total[...] = jnp.zeros_like(total)
        run(phase, backward)
        pulled, grad_gain = norm_pull(total[...], stream[s], gain_refs[s][...])
        gains[pl.ds(s, 1), :] = grad_gain
        if s == 1:
            grad_stream = rows[1, 1].astype(F32) + pulled
            stream[1] = grad_stream
            rows[1, 0] = grad_stream.astype(BF)
        else:
            grad_rows = (stream[1] + pulled).astype(BF)
            back[1] = dot(packing, grad_rows, ((0,), (0,))).astype(BF)


def chain(came, up_first, down_first, up_second, down_second, gain_first, gain_second, slots, capacity):
    wide, hidden = up_first.shape[1:]
    experts = came.shape[1] // slots
    count = experts * capacity
    tile = 1024
    vmem = pl.BlockSpec(memory_space=pltpu.VMEM)
    anys = pl.BlockSpec(memory_space=pl.ANY)
    return pl.pallas_call(
        functools.partial(chain_kernel, experts, slots, capacity, hidden // tile),
        out_shape=(
            jax.ShapeDtypeStruct(came.shape, BF),
            jax.ShapeDtypeStruct((2, 2, count, wide), BF),
            jax.ShapeDtypeStruct((8, wide), F32),
        ),
        in_specs=[vmem] + [anys] * 4 + [vmem] * 2,
        out_specs=(vmem,) * 3,
        scratch_shapes=[
            pltpu.VMEM((2, wide, tile), BF),
            pltpu.VMEM((2, tile, wide), BF),
            pltpu.VMEM((2, count, hidden), F32),
            pltpu.VMEM((2, count, wide), F32),
            pltpu.VMEM((count, wide), F32),
            pltpu.SemaphoreType.DMA((2, 2)),
        ],
        compiler_params=pltpu.CompilerParams(vmem_limit_bytes=56 * 1024 * 1024),
        name="chain",
    )(came, up_first, down_first, up_second, down_second, gain_first, gain_second)


def ring_rows(rows, axis):
    count = lax.axis_size(axis)
    back = [(i, (i - 1) % count) for i in range(count)]
    held = [rows]
    for _ in range(count - 1):
        held.append(lax.ppermute(held[-1], axis, back))
    return jnp.concatenate(held, axis=0)


def weight_grads(normed_rows, grad_rows, up_proj, down_proj):
    count = lax.axis_size("batch")
    width = up_proj.shape[1] // count
    first = lax.axis_index("batch") * width
    up_part = lax.dynamic_slice_in_dim(up_proj, first, width, 1)
    down_part = lax.dynamic_slice_in_dim(down_proj, first, width, 0)
    pre_act = jnp.dot(normed_rows, up_part, preferred_element_type=jnp.float32)
    middle, gelu_pull = jax.vjp(jax.nn.gelu, pre_act)
    grad_middle = jnp.einsum("rd,fd->rf", grad_rows, down_part, preferred_element_type=jnp.float32)
    grad_pre = gelu_pull(grad_middle)[0].astype(jnp.bfloat16)
    grad_down = jnp.einsum(
        "rf,rd->fd", middle.astype(jnp.bfloat16), grad_rows, preferred_element_type=jnp.float32
    )
    grad_up = jnp.einsum("rd,rf->df", normed_rows, grad_pre, preferred_element_type=jnp.float32)
    return grad_up, grad_down


def halve(blocks, axis, bit, dim):
    count = lax.axis_size(axis)
    mine = (lax.axis_index(axis) // bit) % 2
    kept = lax.dynamic_index_in_dim(blocks, mine, dim, keepdims=False)
    sent = lax.dynamic_index_in_dim(blocks, 1 - mine, dim, keepdims=False)
    got = lax.ppermute(sent, axis, [(i, i ^ bit) for i in range(count)])
    return (kept.astype(jnp.float32) + got.astype(jnp.float32)).astype(blocks.dtype)


def scatter_sum(parts):
    experts, groups = lax.axis_size("expert"), lax.axis_size("batch")
    kinds, rows, width = parts.shape
    bits_e = experts.bit_length() - 1
    bits_b = groups.bit_length() - 1
    shape = (kinds,) + (2,) * (bits_b + bits_e) + (rows // (experts * groups), width)
    blocks = parts.reshape(shape)
    for k in range(bits_e):
        blocks = halve(blocks, "expert", 1 << k, bits_b + bits_e - k)
    for k in range(bits_b):
        blocks = halve(blocks, "batch", 1 << k, bits_b - k)
    return blocks


def all_sum(value):
    for axis in ("expert", "batch"):
        count = lax.axis_size(axis)
        bit = 1
        while bit < count:
            value = value + lax.ppermute(value, axis, [(i, i ^ bit) for i in range(count)])
            bit *= 2
    return value


def layer_kernel(
    experts, groups, slots, capacity, docs, width, tiles,
    ends, routes, tokens, cotangent, gain, cents, gain_first, gain_second,
    w_query, w_key, w_value, w_output, up_first, down_first, up_second, down_second,
    block_out, grad_tokens, dense_out, small_out, gains_out, up_one, down_one, up_two, down_two, ring_held,
    w_held, slopes, stream, norms, grads, cur, attention, hidden, dispatch, inbox, outbox, dense, turned, middles,
    keep, s_got, g_got,
    w_sems, row_sem, a2a_send, a2a_recv, ring_send, ring_recv, dense_send, dense_recv, small_send, small_recv,
    gain_send, gain_recv, ready, out_sem,
):
    b, e = lax.axis_index("batch"), lax.axis_index("expert")
    count, wide = tokens.shape
    many = experts * capacity
    before, after = lax.rem(b + groups - 1, groups), lax.rem(b + 1, groups)
    core, x, y = lax.rem(e, 2), lax.rem(e // 2, 2), lax.rem(e // 4, 2)
    b0, b1 = lax.rem(b, 2), lax.rem(b // 2, 2)
    other = 1 - core
    to_core, to_x, to_y = (b, e + 1 - 2 * core), (b, e + 2 - 4 * x), (b, e + 4 - 8 * y)
    to_low, to_high = (b + 1 - 2 * b0, e), (b + 2 - 4 * b1, e)

    def remote(src, dst, send, recv, peer):
        return pltpu.make_async_remote_copy(
            src_ref=src, dst_ref=dst, send_sem=send, recv_sem=recv, device_id=peer, device_id_type=MESH
        )

    barrier = pltpu.get_barrier_semaphore()

    def greet(p, carry):
        peer = (b, lax.rem(e + p, experts))
        pl.semaphore_signal(barrier, inc=1, device_id=peer, device_id_type=MESH)
        return carry

    lax.fori_loop(1, experts, greet, 0)
    for peer in ((before, e), (after, e), to_high):
        pl.semaphore_signal(barrier, inc=1, device_id=peer, device_id_type=MESH)

    tile = wide
    ups, downs = (up_first, up_second), (down_first, down_second)
    gain_refs = (gain_first, gain_second)

    def fetch(s, c, slot):
        cols = pl.ds(pl.multiple_of(c * tile, tile), tile)
        return (
            pltpu.make_async_copy(ups[s].at[0, :, cols], w_held.at[slot], w_sems.at[slot]),
            pltpu.make_async_copy(downs[s].at[0, cols, :], w_held.at[2 + slot], w_sems.at[2 + slot]),
        )

    def stream_tiles(s, follow, body):
        def step(c, carry):
            slot = lax.rem(c, 2)
            for copy in fetch(s, c, slot):
                copy.wait()

            @pl.when(c + 1 < tiles)
            def _():
                for copy in fetch(s, c + 1, 1 - slot):
                    copy.start()

            if follow is not None:
                @pl.when(c + 1 == tiles)
                def _():
                    for copy in fetch(follow, 0, 1 - slot):
                        copy.start()

            body(c, slot)
            return carry

        lax.fori_loop(0, tiles, step, 0)

    def exchange(phase, kind, block):
        def copy(p):
            target = lax.rem(e + p, experts)
            return remote(
                block(target), inbox.at[phase, kind, e],
                a2a_send.at[phase, kind, p], a2a_recv.at[phase, kind, p], (b, target),
            )
        own = pltpu.make_async_copy(block(e), inbox.at[phase, kind, e], a2a_recv.at[phase, kind, 0])

        def start():
            own.start()
            lax.fori_loop(1, experts, lambda p, carry: (copy(p).start(), carry)[1], 0)

        def wait():
            own.wait()
            lax.fori_loop(1, experts, lambda p, carry: (copy(p).wait(), carry)[1], 0)

        return start, wait


    def ring(t, j):
        if t == 0:
            source, target = cur if j == 1 else ring_held.at[j - 1], ring_held.at[j]
        else:
            source, target = grads.at[2 - t, j - 1], grads.at[2 - t, j]
        return remote(source, target, ring_send.at[t, j], ring_recv.at[t, j], (before, e))

    def advance(t, j):
        ring(t, j - 1).wait_recv()
        ring(t, j).start()

    attention_weights = [
        pltpu.make_async_copy(w, w_held.at[i], w_sems.at[i])
        for i, w in enumerate((w_query, w_key, w_value, w_output))
    ]
    for copy in attention_weights:
        copy.start()
    normed, queries, keys, values, mixed = (attention.at[i] for i in range(5))
    normed[...] = (norm_parts(tokens[...].astype(F32))[0] * gain[...]).astype(BF)
    for i, result in enumerate((queries, keys, values)):
        attention_weights[i].wait()
        result[...] = dot(normed[...], w_held[i]).astype(BF)
    for copy in fetch(0, 0, 0):
        copy.start()
    allowed = allowed_pairs(ends, docs, count)
    lax.fori_loop(0, wide // 128, functools.partial(forward_pair, allowed, queries, keys, values, mixed), 0)
    attention_weights[3].wait()
    hidden[...] = tokens[...].astype(F32) + dot(mixed[...], w_held[3])
    chosen, marks = route_marks(routes[...], experts, slots)
    dispatch[...] = marks
    own = select_rows(chosen, cents[...], ((0,), (0,)))
    gating = jax.nn.sigmoid(jnp.sum(hidden[...] * own, axis=-1, keepdims=True))
    live = (lax.broadcasted_iota(jnp.int32, (count, 1), 0) < ends[0, docs - 1]).astype(F32)

    def out_block(kind, p):
        return outbox.at[pl.ds(pl.multiple_of((kind * experts + p) * slots, 16), slots)]

    def put_out(kind, marks, value, dims):
        start = kind * experts * slots
        outbox[start:start + experts * slots, :] = dot(marks, value, dims).astype(BF)

    send_routed, get_routed = exchange(0, 0, functools.partial(out_block, 0))
    send_grads, get_grads = exchange(0, 1, functools.partial(out_block, 1))
    send_result, get_result = exchange(1, 0, functools.partial(out_block, 0))
    send_back, get_back = exchange(1, 1, functools.partial(out_block, 1))
    put_out(0, dispatch[...], hidden[...].astype(BF), ((1,), (0,)))
    pl.semaphore_wait(barrier, experts + 2)
    send_routed()
    put_out(1, dispatch[...], (gating * (live * cotangent[...].astype(F32))).astype(BF), ((1,), (0,)))
    send_grads()
    packing = pack_marks(experts, slots, capacity)
    gains_out[...] = jnp.zeros_like(gains_out)
    get_routed()
    arrived = dot(packing, inbox[0, 0].reshape(experts * slots, wide))
    stream[0] = arrived
    cur[...] = arrived.astype(BF)
    ring(0, 1).start()
    total = stream.at[2]

    def slab(s, c):
        return pl.ds(pl.multiple_of((s * tiles + c) * many, 16), many)

    for s in range(2):
        unit, _ = norm_parts(stream[s])
        norms[s, 0] = (unit * gain_refs[s][...]).astype(BF)
        total[...] = stream[s]

        def forward(c, slot, s=s):
            made = dot(norms[s, 0], w_held[slot])
            value, slope = gelu_pair(made)
            slopes[slab(s, c), :] = slope.astype(BF)
            total[...] += dot(value.astype(BF), w_held[2 + slot])

        stream_tiles(s, 1, forward)
        if s == 0:
            stream[1] = total[...]
            get_grads()
            grads[1, 0] = dot(packing, inbox[0, 1].reshape(experts * slots, wide)).astype(BF)

    put_out(0, packing, total[...].astype(BF), ((0,), (0,)))
    send_result()
    advance(0, 2)
    for s in (1, 0):
        total[...] = jnp.zeros_like(total)

        def backward(c, slot, s=s):
            grad_mid = dot(grads[s, 0], w_held[2 + slot], ((1,), (1,)))
            grad_pre = (slopes[slab(s, c), :].astype(F32) * grad_mid).astype(BF)
            total[...] += dot(grad_pre, w_held[slot], ((1,), (1,)))

        stream_tiles(s, 0 if s == 1 else None, backward)
        pulled, grad_gain = norm_pull(total[...], stream[s], gain_refs[s][...])
        gains_out[pl.ds(s, 1), :] = grad_gain
        if s == 1:
            grad_stream = grads[1, 0].astype(F32) + pulled
            stream[1] = grad_stream
            grads[0, 0] = grad_stream.astype(BF)
        else:
            put_out(1, packing, (stream[1] + pulled).astype(BF), ((0,), (0,)))
    send_back()
    pl.semaphore_signal(ready.at[0], inc=1, device_id=to_core, device_id_type=MESH)
    for i in (3, 0, 1, 2):
        attention_weights[i].start()
    advance(0, 3)
    ring(1, 1).start()

    def small_step(level, peer):
        return remote(keep.at[level], s_got.at[level], small_send.at[level], small_recv.at[level], peer)

    def gain_step(level, peer):
        return remote(keep.at[5 + level, pl.ds(0, 8)], g_got.at[level], gain_send.at[level], gain_recv.at[level], peer)

    keep[5, pl.ds(0, 8)] = gains_out[...]
    gain_step(0, to_low).start()

    get_result()
    returned = dot(dispatch[...], inbox[1, 0].reshape(experts * slots, wide), ((0,), (0,)))
    block_out[...] = (live * (gating * returned + (1.0 - gating) * hidden[...])).astype(BF)
    grad_block = live * cotangent[...].astype(F32)
    grad_score = jnp.sum(grad_block * (returned - hidden[...]), axis=-1, keepdims=True) * gating * (1.0 - gating)
    grad_hidden = stream.at[0, pl.ds(0, count)]
    own = select_rows(chosen, cents[...], ((0,), (0,)))
    grad_hidden[...] = (1.0 - gating) * grad_block + grad_score * own
    keep[0, pl.ds(8, experts)] = select_rows(chosen, grad_score * hidden[...], ((1,), (0,)))
    normed_turned = turned.at[:, pl.ds(0, count)]
    normed_turned[...] = normed[...].T
    ring(0, 1).wait_send()
    grad_low = cur.at[pl.ds(0, count)]
    get_back()
    grad_hidden[...] += dot(dispatch[...], inbox[1, 1].reshape(experts * slots, wide), ((0,), (0,)))
    grad_low[...] = grad_hidden[...].astype(BF)
    attention_weights[3].wait()
    grad_mixed = dot(grad_low[...], w_held[3], ((1,), (1,))).astype(BF)
    dense_product(dense, 3, mixed[...].T, grad_low)
    grad_low[...] = grad_mixed
    grad_three = [outbox.at[pl.ds(i * count, count)] for i in range(3)]
    lax.fori_loop(
        0, wide // 128, functools.partial(backward_pair, allowed, queries, keys, values, grad_low, grad_three), 0
    )
    for i in range(3):
        dense_product(dense, i, normed_turned[...], grad_three[i])
    for i in range(3):
        attention_weights[i].wait()
    grad_normed = sum(dot(grad_three[i][...], w_held[i], ((1,), (1,))) for i in range(3))
    pulled, grad_gain = norm_pull(grad_normed, tokens[...].astype(F32), gain[...])
    grad_tokens[...] = grad_hidden[...] + pulled
    keep[0, pl.ds(0, 8)] = jnp.broadcast_to(grad_gain, (8, wide))

    def rows_at(start, size):
        return pl.ds(pl.multiple_of(start, 32), size)

    def level_copies(level):
        copies = []
        for m in range(4):
            mine, theirs = dense.at[core, m], dense.at[other, m]
            if level == 0:
                parts = ((theirs, slopes.at[pl.ds(m * 512, 512)], to_core),)
            elif level == 1 and m < 2:
                parts = ((mine.at[rows_at((1 - x) * 256, 256)], theirs.at[pl.ds(0, 256)], to_x),)
            elif level == 1:
                parts = tuple(
                    (mine.at[rows_at(xx * 256 + (1 - y) * 128, 128)], theirs.at[pl.ds(xx * 128, 128)], to_y)
                    for xx in range(2)
                )
            elif level == 2 and m < 2:
                parts = ((mine.at[rows_at(x * 256 + (1 - y) * 128, 128)], theirs.at[pl.ds(256, 128)], to_y),)
            elif level == 2:
                parts = ((mine.at[rows_at((1 - x) * 256 + y * 128, 128)], theirs.at[pl.ds(256, 128)], to_x),)
            elif level == 3:
                start = x * 256 + y * 128 + (1 - b0) * 64
                parts = ((mine.at[rows_at(start, 64)], theirs.at[pl.ds(384, 64)], to_low),)
            else:
                start = x * 256 + y * 128 + b0 * 64 + (1 - b1) * 32
                parts = ((mine.at[rows_at(start, 32)], theirs.at[pl.ds(448, 32)], to_high),)
            for n, (src, dst, peer) in enumerate(parts):
                copies.append(remote(src, dst, dense_send.at[level, m, n], dense_recv.at[level, m, n], peer))
        return copies

    small_peers = (to_core, to_x, to_y, to_low, to_high)

    def begin(level):
        for sem in {0: (0,), 1: (1, 2), 2: (), 3: (3,), 4: (4,)}[level]:
            pl.semaphore_wait(ready.at[sem], 1)
        for copy in level_copies(level):
            copy.start()
        small_step(level, small_peers[level]).start()

    def add_rows(m, start, size, got):
        where = rows_at(start, size)
        dense[core, m, where, :] = (dense[core, m, where, :].astype(F32) + got.astype(F32)).astype(BF)

    def end(level):
        for copy in level_copies(level):
            copy.wait()
        small_step(level, small_peers[level]).wait()
        if level < 4:
            keep[level + 1] = keep[level] + s_got[level]
        for m in range(4):
            if level == 0:
                for h in range(2):
                    add_rows(m, h * 256, 256, slopes[m * 512 + h * 256:m * 512 + h * 256 + 256])
            elif level == 1 and m < 2:
                add_rows(m, x * 256, 256, dense[other, m, 0:256])
            elif level == 1:
                for xx in range(2):
                    add_rows(m, xx * 256 + y * 128, 128, dense[other, m, xx * 128:xx * 128 + 128])
            elif level == 2:
                add_rows(m, x * 256 + y * 128, 128, dense[other, m, 256:384])
            elif level == 3:
                add_rows(m, x * 256 + y * 128 + b0 * 64, 64, dense[other, m, 384:448])
            else:
                where = rows_at(x * 256 + y * 128 + b0 * 64 + b1 * 32, 32)
                dense_out[m] = dense[core, m, where, :].astype(F32) + dense[other, m, 448:480].astype(F32)
        if level == 0:
            for sem, peer in enumerate(small_peers[1:], 1):
                pl.semaphore_signal(ready.at[sem], inc=1, device_id=peer, device_id_type=MESH)
        if level == 4:
            small_out[...] = keep[4] + s_got[4]

    begin(0)
    advance(1, 2)
    ring(2, 1).start()
    gain_step(0, to_low).wait()
    keep[6, pl.ds(0, 8)] = keep[5, pl.ds(0, 8)] + g_got[0]
    gain_step(1, to_high).start()
    ring(0, 3).wait_recv()
    for copy in fetch(0, 0, 0):
        copy.start()
    for k in range(1, groups):
        load = pltpu.make_async_copy(ring_held.at[k], cur, row_sem.at[0])
        load.start()
        load.wait()
        routed = cur[...].astype(F32)
        stream[k - 1] = routed
        norms[0, k] = (norm_parts(routed)[0] * gain_first[...]).astype(BF)

    def forward_others(c, slot):
        def one_group(k, carry):
            mid = gelu_pair(dot(norms[0, k + 1], w_held[slot]))[0].astype(BF)
            stream[k] += dot(mid, w_held[2 + slot])
            return carry

        lax.fori_loop(0, groups - 1, one_group, 0)

        @pl.when(c == 1)
        def _():
            end(0)
            begin(1)

    stream_tiles(0, None, forward_others)
    col = pl.multiple_of(b * width, width)
    shards = []
    for i, s in enumerate((1, 0)):
        shards.append((
            pltpu.make_async_copy(ups[s].at[0, :, pl.ds(col, width)], w_held.at[2 * i], w_sems.at[2 * i]),
            pltpu.make_async_copy(downs[s].at[0, pl.ds(col, width), :], w_held.at[2 * i + 1], w_sems.at[2 * i + 1]),
        ))
    for pair in shards:
        for copy in pair:
            copy.start()
    for k in range(1, groups):
        norms[1, k] = (norm_parts(stream[k - 1])[0] * gain_second[...]).astype(BF)
    advance(1, 3)
    advance(2, 2)
    gain_step(1, to_high).wait()
    gains_out[...] = keep[6, pl.ds(0, 8)] + g_got[1]

    quarter = wide // 4
    every = groups * many

    def stage_copies(n, s, c, slot):
        stage = stream.at[slot]
        cols = pl.ds(pl.multiple_of(c * quarter, quarter), quarter)
        if n == 0:
            return (pltpu.make_async_copy(stage.at[pl.ds(0, quarter)], (down_one, down_two)[s].at[0, cols], out_sem.at[slot, 0]),)
        return tuple(
            pltpu.make_async_copy(
                stage.at[pl.ds(0, quarter), pl.ds(r * quarter, quarter)],
                (up_one, up_two)[s].at[0, pl.ds(r * quarter, quarter), cols], out_sem.at[slot, 1 + r],
            )
            for r in range(4)
        )

    def weight_phase(i, s, hooks):
        for copy in shards[i]:
            copy.wait()

        def turn(d, carry):
            cols = pl.ds(pl.multiple_of(d * 128, 128), 128)
            turned[cols, :] = norms[s, :, :, cols].reshape(every, 128).T
            return carry

        lax.fori_loop(0, wide // 128, turn, 0)

        def chunk(c, carry):
            cols = pl.ds(pl.multiple_of(c * quarter, quarter), quarter)

            def one_group(k, carry):
                where = pl.ds(pl.multiple_of(k * many, 16), many)
                mid, slope = gelu_pair(dot(norms[s, k], w_held[2 * i, :, cols]))
                middles[0, where, :] = mid.astype(BF)
                grad_mid = dot(grads[s, k], w_held[2 * i + 1, cols, :], ((1,), (1,)))
                middles[1, where, :] = (grad_mid * slope).astype(BF)
                return carry

            lax.fori_loop(0, groups, one_group, 0)
            slot = lax.rem(c, 2)

            @pl.when(c > 1)
            def _():
                for copy in stage_copies(0, s, c - 2, slot):
                    copy.wait()

            stream[slot, 0:quarter, :] = dot(middles[0], grads[s].reshape(every, wide), ((0,), (0,)))
            for copy in stage_copies(0, s, c, slot):
                copy.start()

            @pl.when(c > 0)
            def _():
                for copy in stage_copies(1, s, c - 1, 2):
                    copy.wait()

            product = dot(turned[...], middles[1])
            for r in range(4):
                stream[2, 0:quarter, r * quarter:(r + 1) * quarter] = product[r * quarter:(r + 1) * quarter]
            for copy in stage_copies(1, s, c, 2):
                copy.start()
            for at, hook in hooks.items():
                pl.when(c == at)(hook)
            return carry

        chunks = width // quarter
        lax.fori_loop(0, chunks, chunk, 0)
        for c in (chunks - 2, chunks - 1):
            for copy in stage_copies(0, s, c, c % 2):
                copy.wait()
        for copy in stage_copies(1, s, chunks - 1, 2):
            copy.wait()

    def next_level(level):
        def hook():
            end(level)
            begin(level + 1)
        return hook

    ring(1, 3).wait_recv()
    advance(2, 3)
    weight_phase(0, 1, {1: next_level(1), 3: next_level(2)})
    ring(2, 3).wait_recv()
    weight_phase(1, 0, {1: next_level(3), 3: lambda: end(4)})
    for t in range(3):
        for j in range(1, groups):
            if (t, j) != (0, 1):
                ring(t, j).wait_send()


def dense_product(dense, which, turned, right):
    block = 32
    for g in range(4):
        product = dot(turned[g * 8 * block:(g + 1) * 8 * block], right[...]).astype(BF)
        for e in range(8):
            place = (((e // 2) % 2 * 2 + e // 4) * 4 + g % 2 * 2 + g // 2) * block
            dense[e % 2, which, place:place + block] = product[e * block:(e + 1) * block]


def layer(
    ends, routes_row, tokens, cotangent, gain, cents, gain_first, gain_second, weights, expert_weights, slots, capacity,
):
    count, wide = tokens.shape
    experts, docs, groups = cents.shape[0], ends.shape[1], lax.axis_size("batch")
    many, ff = experts * capacity, expert_weights[0].shape[2]
    width, tiles = ff // groups, ff // wide
    vmem = pl.BlockSpec(memory_space=pltpu.VMEM)
    anys = pl.BlockSpec(memory_space=pl.ANY)
    f32_out = jax.ShapeDtypeStruct((1, wide, width), F32)
    dma = pltpu.SemaphoreType.DMA
    return pl.pallas_call(
        functools.partial(layer_kernel, experts, groups, slots, capacity, docs, width, tiles),
        out_shape=(
            jax.ShapeDtypeStruct((count, wide), BF),
            jax.ShapeDtypeStruct((count, wide), F32),
            jax.ShapeDtypeStruct((4, 32, wide), F32),
            jax.ShapeDtypeStruct((8 + experts, wide), F32),
            jax.ShapeDtypeStruct((8, wide), F32),
            f32_out, f32_out, f32_out, f32_out,
            jax.ShapeDtypeStruct((groups, many, wide), BF),
        ),
        in_specs=[pl.BlockSpec(memory_space=pltpu.SMEM)] + [vmem] * 7 + [anys] * 8,
        out_specs=(vmem,) * 5 + (anys,) * 5,
        scratch_shapes=[
            pltpu.VMEM((4, wide, wide), BF),
            pltpu.VMEM((2 * tiles * many, wide), BF),
            pltpu.VMEM((3, many, wide), F32),
            pltpu.VMEM((2, groups, many, wide), BF),
            pltpu.VMEM((2, groups, many, wide), BF),
            pltpu.VMEM((many, wide), BF),
            pltpu.VMEM((5, count, wide), BF),
            pltpu.VMEM((count, wide), F32),
            pltpu.VMEM((experts * slots, count), BF),
            pltpu.VMEM((2, 2, experts, slots, wide), BF),
            pltpu.VMEM((max(2 * experts * slots, 3 * count), wide), BF),
            pltpu.VMEM((2, 4, wide // 2, wide), BF),
            pltpu.VMEM((wide, groups * many), BF),
            pltpu.VMEM((2, groups * many, wide // 4), BF),
            pltpu.VMEM((7, 16, wide), F32),
            pltpu.VMEM((5, 16, wide), F32),
            pltpu.VMEM((2, 8, wide), F32),
            dma((4,)), dma((1,)), dma((2, 2, experts)), dma((2, 2, experts)),
            dma((3, groups)), dma((3, groups)), dma((5, 4, 2)), dma((5, 4, 2)), dma((5,)), dma((5,)),
            dma((2,)), dma((2,)), pltpu.SemaphoreType.REGULAR((5,)), dma((3, 5)),
        ],
        compiler_params=pltpu.CompilerParams(
            collective_id=1, has_side_effects=True, vmem_limit_bytes=64 * 1024 * 1024 - 65536
        ),
        name="layer",
    )(
        ends, routes_row, tokens, cotangent, gain, cents, gain_first, gain_second, *weights, *expert_weights,
    )


def per_device(
    tokens, doc_ends, routes, w_query, w_key, w_value, w_output, attn_gain, centroids,
    up_first, down_first, gain_first, up_second, down_second, gain_second, cotangent,
):
    count, wide = tokens.shape
    experts, groups = lax.axis_size("expert"), lax.axis_size("batch")
    capacity = 11 * count // (8 * experts)
    slots = -(-capacity // 16) * 16
    routes_row = routes.reshape(1, count)
    gain = attn_gain[None]
    weights = (w_query, w_key, w_value, w_output)
    expert_weights = (up_first, down_first, up_second, down_second)
    if groups == 4 and experts == 8:
        block_out, grad_tokens, dense, small, gains, *parts = layer(
            doc_ends, routes_row, tokens, cotangent, gain, centroids, gain_first, gain_second, weights, expert_weights,
            slots, capacity,
        )
        gains = gains[:2]
    else:
        *kept, out_rows = enter(doc_ends, routes_row, tokens, cotangent, gain, centroids, weights, slots)

        def exchange(blocks):
            return lax.all_to_all(blocks, "expert", split_axis=1, concat_axis=1, tiled=True)

        came = exchange(out_rows).reshape(2, experts * slots, wide)
        back, rows, gains = chain(came, *expert_weights, gain_first, gain_second, slots, capacity)
        came_back = exchange(back.reshape(out_rows.shape)).reshape(back.shape)
        block_out, grad_tokens, dense, small = leave(
            doc_ends, routes_row, tokens, cotangent, gain, centroids, kept, came_back, weights, slots
        )
        dense = scatter_sum(dense).astype(F32)
        small = all_sum(small)
        parts = []
        for s, (up, down) in enumerate(((up_first, down_first), (up_second, down_second))):
            for part in weight_grads(ring_rows(rows[0, s], "batch"), ring_rows(rows[1, s], "batch"), up[0], down[0]):
                parts.append(part[None])
        gains = jnp.sum(lax.all_gather(gains[:2], "batch"), axis=0)
    gain_part = wide // groups
    gains = lax.dynamic_slice_in_dim(gains, lax.axis_index("batch") * gain_part, gain_part, 1)
    return (
        block_out, grad_tokens, dense[0], dense[1], dense[2], dense[3], small[0], small[8:],
        parts[0], parts[1], gains[0:1], parts[2], parts[3], gains[1:2],
    )


def solution(mesh):
    return jax.shard_map(
        per_device,
        mesh=mesh,
        in_specs=(
            P(("batch", "expert"), None),
            P(("batch", "expert"), None),
            P(("batch", "expert"), None),
            P(),
            P(),
            P(),
            P(),
            P(),
            P(),
            P("expert", None, None),
            P("expert", None, None),
            P("expert", None),
            P("expert", None, None),
            P("expert", None, None),
            P("expert", None),
            P(("batch", "expert"), None),
        ),
        out_specs=(
            P(("batch", "expert"), None),
            P(("batch", "expert"), None),
            P(("batch", "expert"), None),
            P(("batch", "expert"), None),
            P(("batch", "expert"), None),
            P(("batch", "expert"), None),
            P(),
            P(),
            P("expert", None, "batch"),
            P("expert", "batch", None),
            P("expert", "batch"),
            P("expert", None, "batch"),
            P("expert", "batch", None),
            P("expert", "batch"),
        ),
        check_vma=False,
    )
```

```python
import functools
import jax, jax.numpy as jnp
from jax import lax
from jax.experimental import pallas as pl
from jax.experimental.pallas import tpu as pltpu
from jax.sharding import PartitionSpec as P


MESH = pl.DeviceIdType.MESH
BF = jnp.bfloat16
F32 = jnp.float32
GELU_A = 0.7978845608028654
GELU_B = 0.044715


def gelu_pair(v):
    square = v * v
    bent = jnp.tanh(GELU_A * v * (1.0 + GELU_B * square))
    half = 0.5 * (1.0 + bent)
    slope = half + 0.5 * v * (1.0 - bent * bent) * (GELU_A * (1.0 + 3.0 * GELU_B * square))
    return v * half, slope


def dot(a, b, dims=((1,), (0,))):
    return lax.dot_general(a, b, (dims, ((), ())), preferred_element_type=F32)


MASKED = -1e30
EPSILON = 1e-05


def split_three(value):
    high = value.astype(BF)
    rest = value - high.astype(F32)
    middle = rest.astype(BF)
    return high, middle, (rest - middle.astype(F32)).astype(BF)


def select_rows(marks, value, dims):
    return sum(dot(marks, term, dims) for term in split_three(value))


def norm_parts(stream):
    average = jnp.mean(stream, axis=-1, keepdims=True)
    centred = stream - average
    variance = jnp.mean(centred * centred, axis=-1, keepdims=True)
    scale = lax.rsqrt(variance + EPSILON)
    return centred * scale, scale


def norm_pull(grad, stream, gain):
    unit, scale = norm_parts(stream)
    inner = grad * gain
    mean_inner = jnp.mean(inner, axis=-1, keepdims=True)
    mean_product = jnp.mean(inner * unit, axis=-1, keepdims=True)
    return scale * (inner - mean_inner - unit * mean_product), jnp.sum(grad * unit, axis=0, keepdims=True)


def route_marks(routes_row, experts, slots):
    count = routes_row.shape[1]
    ids = lax.broadcasted_iota(jnp.int32, (experts, count), 0)
    chosen = (ids == routes_row).astype(F32)
    earlier = lax.broadcasted_iota(jnp.int32, (count, count), 0) <= lax.broadcasted_iota(jnp.int32, (count, count), 1)
    running = dot(chosen.astype(BF), earlier.astype(F32).astype(BF))
    rank = jnp.sum(running * chosen, axis=0, keepdims=True) - 1.0
    place = routes_row * slots + rank.astype(jnp.int32)
    rows = lax.broadcasted_iota(jnp.int32, (experts * slots, count), 0)
    return chosen.astype(BF), (rows == place).astype(F32).astype(BF)


def allowed_pairs(ends, docs, count):
    row = lax.broadcasted_iota(jnp.int32, (count, count), 0)
    col = lax.broadcasted_iota(jnp.int32, (count, count), 1)
    row_segment = jnp.zeros((count, count), jnp.int32)
    col_segment = jnp.zeros((count, count), jnp.int32)
    for d in range(docs):
        row_segment += (row >= ends[0, d]).astype(jnp.int32)
        col_segment += (col >= ends[0, d]).astype(jnp.int32)
    return (row_segment == col_segment) & (col <= row)


def half_marks(half):
    lane = lax.broadcasted_iota(jnp.int32, (1, 128), 1)
    inside = (lane >= 64 * half) & (lane < 64 * half + 64)
    return inside.astype(F32).astype(BF)


def head_shares(query_pair, key_pair, allowed, half):
    raw = dot(query_pair * half_marks(half), key_pair, ((1,), (1,)))
    scores = jnp.where(allowed, raw * 0.125, MASKED)
    raised = jnp.exp(scores - jnp.max(scores, axis=-1, keepdims=True))
    return raised * (1.0 / jnp.sum(raised, axis=-1, keepdims=True))


def join_halves(first, second):
    lane = lax.broadcasted_iota(jnp.int32, first.shape, 1)
    return jnp.where(lane < 64, first, second)


def forward_pair(allowed, queries, keys, values, mixed, j, carry):
    cols = pl.ds(pl.multiple_of(j * 128, 128), 128)
    query_pair, key_pair, value_pair = queries[:, cols], keys[:, cols], values[:, cols]
    halves = [dot(head_shares(query_pair, key_pair, allowed, half).astype(BF), value_pair) for half in range(2)]
    mixed[:, cols] = join_halves(*halves).astype(BF)
    return carry


def enter_kernel(
    experts, slots, docs,
    ends, routes, tokens, cotangent, gain, cents, w_query, w_key, w_value, w_output,
    normed, queries, keys, values, mixed, hidden, out_rows,
    w_held, sems,
):
    copies = [
        pltpu.make_async_copy(w, w_held.at[i], sems.at[i])
        for i, w in enumerate((w_query, w_key, w_value, w_output))
    ]
    for copy in copies:
        copy.start()
    count, wide = tokens.shape
    unit, _ = norm_parts(tokens[...].astype(F32))
    normed[...] = (unit * gain[...]).astype(BF)
    for i, result in enumerate((queries, keys, values)):
        copies[i].wait()
        result[...] = dot(normed[...], w_held[i]).astype(BF)
    allowed = allowed_pairs(ends, docs, count)

    lax.fori_loop(0, wide // 128, functools.partial(forward_pair, allowed, queries, keys, values, mixed), 0)
    copies[3].wait()
    hidden[...] = tokens[...].astype(F32) + dot(mixed[...], w_held[3])
    chosen, dispatch = route_marks(routes[...], experts, slots)
    own = select_rows(chosen, cents[...], ((0,), (0,)))
    gating = jax.nn.sigmoid(jnp.sum(hidden[...] * own, axis=-1, keepdims=True))
    live = (lax.broadcasted_iota(jnp.int32, (count, 1), 0) < ends[0, docs - 1]).astype(F32)
    grad_sent = (gating * (live * cotangent[...].astype(F32))).astype(BF)
    for kind, rows in enumerate((hidden[...].astype(BF), grad_sent)):
        out_rows[kind] = dot(dispatch, rows).astype(BF).reshape(experts, slots, wide)


def enter(ends, routes_row, tokens, cotangent, gain, cents, weights, slots):
    count, wide = tokens.shape
    experts, docs = cents.shape[0], ends.shape[1]
    vmem = pl.BlockSpec(memory_space=pltpu.VMEM)
    anys = pl.BlockSpec(memory_space=pl.ANY)
    low = jax.ShapeDtypeStruct((count, wide), BF)
    return pl.pallas_call(
        functools.partial(enter_kernel, experts, slots, docs),
        out_shape=(low,) * 5 + (
            jax.ShapeDtypeStruct((count, wide), F32),
            jax.ShapeDtypeStruct((2, experts, slots, wide), BF),
        ),
        in_specs=[pl.BlockSpec(memory_space=pltpu.SMEM)] + [vmem] * 5 + [anys] * 4,
        out_specs=(vmem,) * 7,
        scratch_shapes=[pltpu.VMEM((4, wide, wide), BF), pltpu.SemaphoreType.DMA((4,))],
        compiler_params=pltpu.CompilerParams(vmem_limit_bytes=48 * 1024 * 1024),
        name="enter",
    )(ends, routes_row, tokens, cotangent, gain, cents, *weights)


def backward_pair(allowed, queries, keys, values, grad_low, grad_three, j, carry):
    cols = pl.ds(pl.multiple_of(j * 128, 128), 128)
    query_pair, key_pair, value_pair = queries[:, cols], keys[:, cols], values[:, cols]
    grad_pair = grad_low[:, cols]
    parts = []
    for half in range(2):
        shares = head_shares(query_pair, key_pair, allowed, half)
        grad_shares = dot(grad_pair * half_marks(half), value_pair, ((1,), (1,)))
        inner = jnp.sum(shares * grad_shares, axis=-1, keepdims=True)
        raw = (shares * (grad_shares - inner) * 0.125).astype(BF)
        parts.append((
            dot(raw, key_pair),
            dot(raw, query_pair, ((0,), (0,))),
            dot(shares.astype(BF), grad_pair, ((0,), (0,))),
        ))
    for i in range(3):
        grad_three[i][:, cols] = join_halves(parts[0][i], parts[1][i]).astype(BF)
    return carry


def leave_kernel(
    experts, slots, docs,
    ends, routes, tokens, cotangent, gain, cents, normed, queries, keys, values, mixed, hidden, came,
    w_query, w_key, w_value, w_output,
    block_out, grad_tokens, dense, small,
    w_held, grad_low, grad_three, normed_turned, grad_hidden, sems,
):
    copies = [
        pltpu.make_async_copy(w, w_held.at[i], sems.at[i])
        for i, w in enumerate((w_query, w_key, w_value, w_output))
    ]
    for i in (3, 0, 1, 2):
        copies[i].start()
    count, wide = tokens.shape
    chosen, dispatch = route_marks(routes[...], experts, slots)
    own = select_rows(chosen, cents[...], ((0,), (0,)))
    gating = jax.nn.sigmoid(jnp.sum(hidden[...] * own, axis=-1, keepdims=True))
    live = (lax.broadcasted_iota(jnp.int32, (count, 1), 0) < ends[0, docs - 1]).astype(F32)
    returned = dot(dispatch, came[0], ((0,), (0,)))
    block_out[...] = (live * (gating * returned + (1.0 - gating) * hidden[...])).astype(BF)
    grad_block = live * cotangent[...].astype(F32)
    grad_score = jnp.sum(grad_block * (returned - hidden[...]), axis=-1, keepdims=True) * gating * (1.0 - gating)
    grad_hidden[...] = (1.0 - gating) * grad_block + dot(dispatch, came[1], ((0,), (0,))) + grad_score * own
    small[pl.ds(8, experts), :] = select_rows(chosen, grad_score * hidden[...], ((1,), (0,)))
    grad_low[...] = grad_hidden[...].astype(BF)
    copies[3].wait()
    grad_mixed = dot(grad_low[...], w_held[3], ((1,), (1,))).astype(BF)
    dense[3] = dot(mixed[...].T, grad_low[...]).astype(BF)
    grad_low[...] = grad_mixed
    allowed = allowed_pairs(ends, docs, count)

    lax.fori_loop(
        0, wide // 128, functools.partial(
            backward_pair, allowed, queries, keys, values, grad_low, [grad_three.at[i] for i in range(3)]
        ), 0
    )
    normed_turned[...] = normed[...].T
    for i in range(3):
        dense[i] = dot(normed_turned[...], grad_three[i]).astype(BF)
    for i in range(3):
        copies[i].wait()
    grad_normed = sum(dot(grad_three[i], w_held[i], ((1,), (1,))) for i in range(3))
    pulled, grad_gain = norm_pull(grad_normed, tokens[...].astype(F32), gain[...])
    grad_tokens[...] = grad_hidden[...] + pulled
    small[pl.ds(0, 8), :] = jnp.broadcast_to(grad_gain, (8, wide))


def leave(ends, routes_row, tokens, cotangent, gain, cents, kept, came, weights, slots):
    count, wide = tokens.shape
    experts, docs = cents.shape[0], ends.shape[1]
    vmem = pl.BlockSpec(memory_space=pltpu.VMEM)
    anys = pl.BlockSpec(memory_space=pl.ANY)
    return pl.pallas_call(
        functools.partial(leave_kernel, experts, slots, docs),
        out_shape=(
            jax.ShapeDtypeStruct((count, wide), BF),
            jax.ShapeDtypeStruct((count, wide), F32),
            jax.ShapeDtypeStruct((4, wide, wide), BF),
            jax.ShapeDtypeStruct((8 + experts, wide), F32),
        ),
        in_specs=[pl.BlockSpec(memory_space=pltpu.SMEM)] + [vmem] * 12 + [anys] * 4,
        out_specs=(vmem,) * 4,
        scratch_shapes=[
            pltpu.VMEM((4, wide, wide), BF),
            pltpu.VMEM((count, wide), BF),
            pltpu.VMEM((3, count, wide), BF),
            pltpu.VMEM((wide, count), BF),
            pltpu.VMEM((count, wide), F32),
            pltpu.SemaphoreType.DMA((4,)),
        ],
        compiler_params=pltpu.CompilerParams(vmem_limit_bytes=56 * 1024 * 1024),
        name="leave",
    )(ends, routes_row, tokens, cotangent, gain, cents, *kept, came, *weights)


def pack_marks(experts, slots, capacity):
    shape = (experts * capacity, experts * slots)
    row = lax.broadcasted_iota(jnp.int32, (shape[0], 1), 0)
    block = sum((row >= s * capacity).astype(jnp.int32) for s in range(1, experts))
    column = lax.broadcasted_iota(jnp.int32, shape, 1)
    return (column == row + (slots - capacity) * block).astype(F32).astype(BF)


def chain_kernel(
    experts, slots, capacity, tiles,
    came, up_first, down_first, up_second, down_second, gain_first, gain_second,
    back, rows, gains,
    up_tile, down_tile, pre, stream, total, sems,
):
    tile = up_tile.shape[2]
    ups, downs = (up_first, up_second), (down_first, down_second)
    gain_refs = (gain_first, gain_second)

    def fetch(s, c, slot):
        cols = pl.ds(pl.multiple_of(c * tile, tile), tile)
        return (
            pltpu.make_async_copy(ups[s].at[0, :, cols], up_tile.at[slot], sems.at[0, slot]),
            pltpu.make_async_copy(downs[s].at[0, cols, :], down_tile.at[slot], sems.at[1, slot]),
        )

    order = ((0, True), (1, True), (1, False), (0, False))

    def run(phase, body):
        s = order[phase][0]

        def step(c, carry):
            slot = lax.rem(c, 2)
            for copy in fetch(s, c, slot):
                copy.wait()

            @pl.when(c + 1 < tiles)
            def _():
                for copy in fetch(s, c + 1, 1 - slot):
                    copy.start()

            if phase < 3:
                @pl.when(c + 1 == tiles)
                def _():
                    for copy in fetch(order[phase + 1][0], 0, 1 - slot):
                        copy.start()

            body(s, pl.ds(pl.multiple_of(c * tile, tile), tile), slot)
            return carry

        lax.fori_loop(0, tiles, step, 0)

    for copy in fetch(0, 0, 0):
        copy.start()
    gains[...] = jnp.zeros_like(gains)
    packing = pack_marks(experts, slots, capacity)
    stream[0] = dot(packing, came[0])
    rows[1, 1] = dot(packing, came[1]).astype(BF)

    def forward(s, cols, slot):
        made = dot(rows[0, s], up_tile[slot])
        pre[s, :, cols] = made
        mid = gelu_pair(made)[0].astype(BF)
        total[...] += dot(mid, down_tile[slot])

    def backward(s, cols, slot):
        grad_mid = dot(rows[1, s], down_tile[slot], ((1,), (1,)))
        grad_pre = (gelu_pair(pre[s, :, cols])[1] * grad_mid).astype(BF)
        total[...] += dot(grad_pre, up_tile[slot], ((1,), (1,)))

    for s in range(2):
        unit, _ = norm_parts(stream[s])
        rows[0, s] = (unit * gain_refs[s][...]).astype(BF)
        total[...] = stream[s]
        run(s, forward)
        if s == 0:
            stream[1] = total[...]
    back[0] = dot(packing, total[...].astype(BF), ((0,), (0,))).astype(BF)

    for phase, s in ((2, 1), (3, 0)):
        total[...] = jnp.zeros_like(total)
        run(phase, backward)
        pulled, grad_gain = norm_pull(total[...], stream[s], gain_refs[s][...])
        gains[pl.ds(s, 1), :] = grad_gain
        if s == 1:
            grad_stream = rows[1, 1].astype(F32) + pulled
            stream[1] = grad_stream
            rows[1, 0] = grad_stream.astype(BF)
        else:
            grad_rows = (stream[1] + pulled).astype(BF)
            back[1] = dot(packing, grad_rows, ((0,), (0,))).astype(BF)


def chain(came, up_first, down_first, up_second, down_second, gain_first, gain_second, slots, capacity):
    wide, hidden = up_first.shape[1:]
    experts = came.shape[1] // slots
    count = experts * capacity
    tile = 1024
    vmem = pl.BlockSpec(memory_space=pltpu.VMEM)
    anys = pl.BlockSpec(memory_space=pl.ANY)
    return pl.pallas_call(
        functools.partial(chain_kernel, experts, slots, capacity, hidden // tile),
        out_shape=(
            jax.ShapeDtypeStruct(came.shape, BF),
            jax.ShapeDtypeStruct((2, 2, count, wide), BF),
            jax.ShapeDtypeStruct((8, wide), F32),
        ),
        in_specs=[vmem] + [anys] * 4 + [vmem] * 2,
        out_specs=(vmem,) * 3,
        scratch_shapes=[
            pltpu.VMEM((2, wide, tile), BF),
            pltpu.VMEM((2, tile, wide), BF),
            pltpu.VMEM((2, count, hidden), F32),
            pltpu.VMEM((2, count, wide), F32),
            pltpu.VMEM((count, wide), F32),
            pltpu.SemaphoreType.DMA((2, 2)),
        ],
        compiler_params=pltpu.CompilerParams(vmem_limit_bytes=56 * 1024 * 1024),
        name="chain",
    )(came, up_first, down_first, up_second, down_second, gain_first, gain_second)


def ring_rows(rows, axis):
    count = lax.axis_size(axis)
    back = [(i, (i - 1) % count) for i in range(count)]
    held = [rows]
    for _ in range(count - 1):
        held.append(lax.ppermute(held[-1], axis, back))
    return jnp.concatenate(held, axis=0)


def weight_grads(normed_rows, grad_rows, up_proj, down_proj):
    count = lax.axis_size("batch")
    width = up_proj.shape[1] // count
    first = lax.axis_index("batch") * width
    up_part = lax.dynamic_slice_in_dim(up_proj, first, width, 1)
    down_part = lax.dynamic_slice_in_dim(down_proj, first, width, 0)
    pre_act = jnp.dot(normed_rows, up_part, preferred_element_type=jnp.float32)
    middle, gelu_pull = jax.vjp(jax.nn.gelu, pre_act)
    grad_middle = jnp.einsum("rd,fd->rf", grad_rows, down_part, preferred_element_type=jnp.float32)
    grad_pre = gelu_pull(grad_middle)[0].astype(jnp.bfloat16)
    grad_down = jnp.einsum(
        "rf,rd->fd", middle.astype(jnp.bfloat16), grad_rows, preferred_element_type=jnp.float32
    )
    grad_up = jnp.einsum("rd,rf->df", normed_rows, grad_pre, preferred_element_type=jnp.float32)
    return grad_up, grad_down


def halve(blocks, axis, bit, dim):
    count = lax.axis_size(axis)
    mine = (lax.axis_index(axis) // bit) % 2
    kept = lax.dynamic_index_in_dim(blocks, mine, dim, keepdims=False)
    sent = lax.dynamic_index_in_dim(blocks, 1 - mine, dim, keepdims=False)
    got = lax.ppermute(sent, axis, [(i, i ^ bit) for i in range(count)])
    return (kept.astype(jnp.float32) + got.astype(jnp.float32)).astype(blocks.dtype)


def scatter_sum(parts):
    experts, groups = lax.axis_size("expert"), lax.axis_size("batch")
    kinds, rows, width = parts.shape
    bits_e = experts.bit_length() - 1
    bits_b = groups.bit_length() - 1
    shape = (kinds,) + (2,) * (bits_b + bits_e) + (rows // (experts * groups), width)
    blocks = parts.reshape(shape)
    for k in range(bits_e):
        blocks = halve(blocks, "expert", 1 << k, bits_b + bits_e - k)
    for k in range(bits_b):
        blocks = halve(blocks, "batch", 1 << k, bits_b - k)
    return blocks


def all_sum(value):
    for axis in ("expert", "batch"):
        count = lax.axis_size(axis)
        bit = 1
        while bit < count:
            value = value + lax.ppermute(value, axis, [(i, i ^ bit) for i in range(count)])
            bit *= 2
    return value


def layer_kernel(
    experts, groups, slots, capacity, docs, width, tiles,
    ends, routes, tokens, cotangent, gain, cents, gain_first, gain_second,
    w_query, w_key, w_value, w_output, up_first, down_first, up_second, down_second,
    block_out, grad_tokens, dense_out, small_out, gains_out, up_one, down_one, up_two, down_two, ring_held, far_inbox,
    w_held, slopes, stream, norms, grads, cur, token_low, attention, hidden, dispatch, packing, routes_held, inbox, outbox, dense, turned, middles,
    keep, s_got, g_got,
    w_sems, row_sem, a2a_send, a2a_recv, far_send, far_recv, route_send, route_recv, ring_send, ring_recv, dense_send, dense_recv, small_send, small_recv,
    gain_send, gain_recv, ready, out_sem,
):
    b, e = lax.axis_index("batch"), lax.axis_index("expert")
    count, wide = tokens.shape
    many = experts * capacity
    before, after = lax.rem(b + groups - 1, groups), lax.rem(b + 1, groups)
    core, x, y = lax.rem(e, 2), lax.rem(e // 2, 2), lax.rem(e // 4, 2)
    b0, b1 = lax.rem(b, 2), lax.rem(b // 2, 2)
    other = 1 - core
    to_core, to_x, to_y = (b, e + 1 - 2 * core), (b, e + 2 - 4 * x), (b, e + 4 - 8 * y)
    to_low, to_high = (b + 1 - 2 * b0, e), (b + 2 - 4 * b1, e)

    def remote(src, dst, send, recv, peer):
        return pltpu.make_async_remote_copy(
            src_ref=src, dst_ref=dst, send_sem=send, recv_sem=recv, device_id=peer, device_id_type=MESH
        )

    barrier = pltpu.get_barrier_semaphore()

    def greet(p, carry):
        peer = (b, lax.rem(e + p, experts))
        pl.semaphore_signal(barrier, inc=1, device_id=peer, device_id_type=MESH)
        return carry

    lax.fori_loop(1, experts, greet, 0)
    for peer in ((before, e), (after, e), to_high):
        pl.semaphore_signal(barrier, inc=1, device_id=peer, device_id_type=MESH)

    tile = wide
    ups, downs = (up_first, up_second), (down_first, down_second)
    gain_refs = (gain_first, gain_second)

    def fetch(s, c, slot):
        cols = pl.ds(pl.multiple_of(c * tile, tile), tile)
        return (
            pltpu.make_async_copy(ups[s].at[0, :, cols], w_held.at[slot], w_sems.at[slot]),
            pltpu.make_async_copy(downs[s].at[0, cols, :], w_held.at[2 + slot], w_sems.at[2 + slot]),
        )

    def stream_tiles(s, follow, body):
        def step(c, carry):
            slot = lax.rem(c, 2)
            for copy in fetch(s, c, slot):
                copy.wait()

            @pl.when(c + 1 < tiles)
            def _():
                for copy in fetch(s, c + 1, 1 - slot):
                    copy.start()

            if follow is not None:
                @pl.when(c + 1 == tiles)
                def _():
                    for copy in fetch(follow, 0, 1 - slot):
                        copy.start()

            body(c, slot)
            return carry

        lax.fori_loop(0, tiles, step, 0)

    def exchange(phase, kind, block):
        def copy(p):
            target = lax.rem(e + p, experts)
            return remote(
                block(target), inbox.at[phase, kind, e],
                a2a_send.at[phase, kind, p], a2a_recv.at[phase, kind, p], (b, target),
            )
        own = pltpu.make_async_copy(block(e), inbox.at[phase, kind, e], a2a_recv.at[phase, kind, 0])

        def start():
            own.start()
            lax.fori_loop(1, experts, lambda p, carry: (copy(p).start(), carry)[1], 0)

        def wait():
            own.wait()
            lax.fori_loop(1, experts, lambda p, carry: (copy(p).wait(), carry)[1], 0)

        return start, wait


    def ring(t, j):
        if t == 0:
            source, target = token_low if j == 1 else ring_held.at[j - 1], ring_held.at[j]
        else:
            source, target = grads.at[2 - t, j - 1], grads.at[2 - t, j]
        return remote(source, target, ring_send.at[t, j], ring_recv.at[t, j], (before, e))

    def advance(t, j):
        ring(t, j - 1).wait_recv()
        ring(t, j).start()

    def far(k, p):
        target = lax.rem(e + p, experts)
        return remote(
            inbox.at[0, 0, target], far_inbox.at[k, e], far_send.at[k, p], far_recv.at[k, p], (b, target)
        )

    def far_own(k):
        return pltpu.make_async_copy(inbox.at[0, 0, e], far_inbox.at[k, e], far_recv.at[k, 0])

    def each_peer(act):
        lax.fori_loop(1, experts, lambda p, carry: (act(p), carry)[1], 0)

    def cur_load(k):
        return pltpu.make_async_copy(ring_held.at[k], cur, row_sem.at[0])

    def far_load(k):
        return pltpu.make_async_copy(far_inbox.at[k], inbox.at[0, 1], row_sem.at[1])

    def relay(k):
        if k > 1:
            each_peer(lambda p: far(k - 1, p).wait_send())
        if k == 2:
            far_own(1).wait()
        cur_load(k).wait()
        inbox[0, 0] = dot(dispatch[k], cur[...]).astype(BF).reshape(experts, slots, wide)
        far_own(k).start()
        each_peer(lambda p: far(k, p).start())

    def far_arrive(k):
        if k > 1:
            far_own(k).wait()
        each_peer(lambda p: far(k, p).wait_recv())
        far_load(k).start()

    def collect(k):
        far_load(k).wait()
        norms[1, k] = dot(packing[...], inbox[0, 1].reshape(experts * slots, wide)).astype(BF)

    def route_copy(j):
        return remote(
            routes, routes_held.at[j], route_send.at[j], route_recv.at[j],
            (lax.rem(b + groups - j, groups), e),
        )

    attention_weights = [
        pltpu.make_async_copy(w, w_held.at[i], w_sems.at[i])
        for i, w in enumerate((w_query, w_key, w_value, w_output))
    ]
    for copy in attention_weights:
        copy.start()
    normed, queries, keys, values, mixed = (attention.at[i] for i in range(5))
    normed[...] = (norm_parts(tokens[...].astype(F32))[0] * gain[...]).astype(BF)
    pl.semaphore_wait(barrier, experts + 2)
    for j in range(1, groups):
        route_copy(j).start()
    for i, result in enumerate((queries, keys, values)):
        attention_weights[i].wait()
        result[...] = dot(normed[...], w_held[i]).astype(BF)
    for copy in fetch(0, 0, 0):
        copy.start()
    allowed = allowed_pairs(ends, docs, count)
    lax.fori_loop(0, wide // 128, functools.partial(forward_pair, allowed, queries, keys, values, mixed), 0)
    attention_weights[3].wait()
    hidden[...] = tokens[...].astype(F32) + dot(mixed[...], w_held[3])
    token_low[...] = hidden[...].astype(BF)
    ring(0, 1).start()
    chosen, dispatch[0] = route_marks(routes[...], experts, slots)
    own = select_rows(chosen, cents[...], ((0,), (0,)))
    gating = jax.nn.sigmoid(jnp.sum(hidden[...] * own, axis=-1, keepdims=True))
    live = (lax.broadcasted_iota(jnp.int32, (count, 1), 0) < ends[0, docs - 1]).astype(F32)

    def out_block(kind, p):
        return outbox.at[pl.ds(pl.multiple_of((kind * experts + p) * slots, 16), slots)]

    def put_out(kind, marks, value, dims):
        start = kind * experts * slots
        outbox[start:start + experts * slots, :] = dot(marks, value, dims).astype(BF)

    send_routed, get_routed = exchange(0, 0, functools.partial(out_block, 0))
    send_grads, get_grads = exchange(0, 1, functools.partial(out_block, 1))
    send_result, get_result = exchange(1, 0, functools.partial(out_block, 0))
    send_back, get_back = exchange(1, 1, functools.partial(out_block, 1))
    put_out(0, dispatch[0], token_low[...], ((1,), (0,)))
    send_routed()
    put_out(1, dispatch[0], (gating * (live * cotangent[...].astype(F32))).astype(BF), ((1,), (0,)))
    send_grads()
    packing[...] = pack_marks(experts, slots, capacity)
    gains_out[...] = jnp.zeros_like(gains_out)
    for j in range(1, groups):
        route_copy(j).wait()
        dispatch[j] = route_marks(routes_held[j], experts, slots)[1]
    get_routed()
    stream[0] = dot(packing[...], inbox[0, 0].reshape(experts * slots, wide))
    advance(0, 2)
    cur_load(1).start()
    total = stream.at[2]

    def slab(s, c):
        return pl.ds(pl.multiple_of((s * tiles + c) * many, 16), many)

    for s in range(2):
        unit, _ = norm_parts(stream[s])
        norms[s, 0] = (unit * gain_refs[s][...]).astype(BF)
        total[...] = stream[s]

        def forward(c, slot, s=s):
            made = dot(norms[s, 0], w_held[slot])
            value, slope = gelu_pair(made)
            slopes[slab(s, c), :] = slope.astype(BF)
            total[...] += dot(value.astype(BF), w_held[2 + slot])
            if s == 1:
                @pl.when(c == tiles // 2)
                def _():
                    advance(0, 3)
                    cur_load(2).start()

        stream_tiles(s, 1, forward)
        if s == 0:
            stream[1] = total[...]
            get_grads()
            grads[1, 0] = dot(packing[...], inbox[0, 1].reshape(experts * slots, wide)).astype(BF)
            ring(1, 1).start()
            relay(1)

    put_out(0, packing[...], total[...].astype(BF), ((0,), (0,)))
    send_result()
    relay(2)
    for s in (1, 0):
        total[...] = jnp.zeros_like(total)

        def backward(c, slot, s=s):
            grad_mid = dot(grads[s, 0], w_held[2 + slot], ((1,), (1,)))
            grad_pre = (slopes[slab(s, c), :].astype(F32) * grad_mid).astype(BF)
            total[...] += dot(grad_pre, w_held[slot], ((1,), (1,)))

        stream_tiles(s, 0 if s == 1 else None, backward)
        pulled, grad_gain = norm_pull(total[...], stream[s], gain_refs[s][...])
        gains_out[pl.ds(s, 1), :] = grad_gain
        if s == 1:
            grad_stream = grads[1, 0].astype(F32) + pulled
            stream[1] = grad_stream
            grads[0, 0] = grad_stream.astype(BF)
        else:
            put_out(1, packing[...], (stream[1] + pulled).astype(BF), ((0,), (0,)))
    send_back()
    pl.semaphore_signal(ready.at[0], inc=1, device_id=to_core, device_id_type=MESH)
    for i in (3, 0, 1, 2):
        attention_weights[i].start()

    def small_step(level, peer):
        return remote(keep.at[level], s_got.at[level], small_send.at[level], small_recv.at[level], peer)

    def gain_step(level, peer):
        return remote(keep.at[5 + level, pl.ds(0, 8)], g_got.at[level], gain_send.at[level], gain_recv.at[level], peer)

    keep[5, pl.ds(0, 8)] = gains_out[...]
    gain_step(0, to_low).start()

    ring(0, 3).wait_recv()
    cur_load(3).start()
    far_arrive(1)
    collect(1)
    far_arrive(2)
    advance(1, 2)
    ring(2, 1).start()
    relay(3)
    collect(2)
    get_result()
    returned = dot(dispatch[0], inbox[1, 0].reshape(experts * slots, wide), ((0,), (0,)))
    block_out[...] = (live * (gating * returned + (1.0 - gating) * hidden[...])).astype(BF)
    grad_block = live * cotangent[...].astype(F32)
    grad_score = jnp.sum(grad_block * (returned - hidden[...]), axis=-1, keepdims=True) * gating * (1.0 - gating)
    grad_hidden = stream.at[0, pl.ds(0, count)]
    own = select_rows(chosen, cents[...], ((0,), (0,)))
    grad_hidden[...] = (1.0 - gating) * grad_block + grad_score * own
    keep[0, pl.ds(8, experts)] = select_rows(chosen, grad_score * hidden[...], ((1,), (0,)))
    normed_turned = turned.at[:, pl.ds(0, count)]
    normed_turned[...] = normed[...].T
    grad_low = cur
    get_back()
    grad_hidden[...] += dot(dispatch[0], inbox[1, 1].reshape(experts * slots, wide), ((0,), (0,)))
    grad_low[...] = grad_hidden[...].astype(BF)
    attention_weights[3].wait()
    grad_mixed = dot(grad_low[...], w_held[3], ((1,), (1,))).astype(BF)
    dense_product(dense, 3, mixed[...].T, grad_low)
    grad_low[...] = grad_mixed
    grad_three = [outbox.at[pl.ds(i * count, count)] for i in range(3)]
    lax.fori_loop(
        0, wide // 128, functools.partial(backward_pair, allowed, queries, keys, values, grad_low, grad_three), 0
    )
    for i in range(3):
        dense_product(dense, i, normed_turned[...], grad_three[i])
    for i in range(3):
        attention_weights[i].wait()
    grad_normed = sum(dot(grad_three[i][...], w_held[i], ((1,), (1,))) for i in range(3))
    pulled, grad_gain = norm_pull(grad_normed, tokens[...].astype(F32), gain[...])
    grad_tokens[...] = grad_hidden[...] + pulled
    keep[0, pl.ds(0, 8)] = jnp.broadcast_to(grad_gain, (8, wide))

    def rows_at(start, size):
        return pl.ds(pl.multiple_of(start, 32), size)

    def level_copies(level):
        copies = []
        for m in range(4):
            mine, theirs = dense.at[core, m], dense.at[other, m]
            if level == 0:
                parts = ((theirs, slopes.at[pl.ds(m * 512, 512)], to_core),)
            elif level == 1 and m < 2:
                parts = ((mine.at[rows_at((1 - x) * 256, 256)], theirs.at[pl.ds(0, 256)], to_x),)
            elif level == 1:
                parts = tuple(
                    (mine.at[rows_at(xx * 256 + (1 - y) * 128, 128)], theirs.at[pl.ds(xx * 128, 128)], to_y)
                    for xx in range(2)
                )
            elif level == 2 and m < 2:
                parts = ((mine.at[rows_at(x * 256 + (1 - y) * 128, 128)], theirs.at[pl.ds(256, 128)], to_y),)
            elif level == 2:
                parts = ((mine.at[rows_at((1 - x) * 256 + y * 128, 128)], theirs.at[pl.ds(256, 128)], to_x),)
            elif level == 3:
                start = x * 256 + y * 128 + (1 - b0) * 64
                parts = ((mine.at[rows_at(start, 64)], theirs.at[pl.ds(384, 64)], to_low),)
            else:
                start = x * 256 + y * 128 + b0 * 64 + (1 - b1) * 32
                parts = ((mine.at[rows_at(start, 32)], theirs.at[pl.ds(448, 32)], to_high),)
            for n, (src, dst, peer) in enumerate(parts):
                copies.append(remote(src, dst, dense_send.at[level, m, n], dense_recv.at[level, m, n], peer))
        return copies

    small_peers = (to_core, to_x, to_y, to_low, to_high)

    def begin(level):
        for sem in {0: (0,), 1: (1, 2), 2: (), 3: (3,), 4: (4,)}[level]:
            pl.semaphore_wait(ready.at[sem], 1)
        for copy in level_copies(level):
            copy.start()
        small_step(level, small_peers[level]).start()

    def add_rows(m, start, size, got):
        where = rows_at(start, size)
        dense[core, m, where, :] = (dense[core, m, where, :].astype(F32) + got.astype(F32)).astype(BF)

    def end(level):
        for copy in level_copies(level):
            copy.wait()
        small_step(level, small_peers[level]).wait()
        if level < 4:
            keep[level + 1] = keep[level] + s_got[level]
        for m in range(4):
            if level == 0:
                for h in range(2):
                    add_rows(m, h * 256, 256, slopes[m * 512 + h * 256:m * 512 + h * 256 + 256])
            elif level == 1 and m < 2:
                add_rows(m, x * 256, 256, dense[other, m, 0:256])
            elif level == 1:
                for xx in range(2):
                    add_rows(m, xx * 256 + y * 128, 128, dense[other, m, xx * 128:xx * 128 + 128])
            elif level == 2:
                add_rows(m, x * 256 + y * 128, 128, dense[other, m, 256:384])
            elif level == 3:
                add_rows(m, x * 256 + y * 128 + b0 * 64, 64, dense[other, m, 384:448])
            else:
                where = rows_at(x * 256 + y * 128 + b0 * 64 + b1 * 32, 32)
                dense_out[m] = dense[core, m, where, :].astype(F32) + dense[other, m, 448:480].astype(F32)
        if level == 0:
            for sem, peer in enumerate(small_peers[1:], 1):
                pl.semaphore_signal(ready.at[sem], inc=1, device_id=peer, device_id_type=MESH)
        if level == 4:
            small_out[...] = keep[4] + s_got[4]

    begin(0)
    far_arrive(3)
    advance(1, 3)
    advance(2, 2)
    collect(3)
    gain_step(0, to_low).wait()
    keep[6, pl.ds(0, 8)] = keep[5, pl.ds(0, 8)] + g_got[0]
    gain_step(1, to_high).start()
    for copy in fetch(0, 0, 0):
        copy.start()
    for k in range(1, groups):
        routed = norms[1, k].astype(F32)
        stream[k - 1] = routed
        norms[0, k] = (norm_parts(routed)[0] * gain_first[...]).astype(BF)

    def forward_others(c, slot):
        def one_group(k, carry):
            mid = gelu_pair(dot(norms[0, k + 1], w_held[slot]))[0].astype(BF)
            stream[k] += dot(mid, w_held[2 + slot])
            return carry

        lax.fori_loop(0, groups - 1, one_group, 0)

        @pl.when(c == 1)
        def _():
            end(0)
            begin(1)

    stream_tiles(0, None, forward_others)
    col = pl.multiple_of(b * width, width)
    shards = []
    for i, s in enumerate((1, 0)):
        shards.append((
            pltpu.make_async_copy(ups[s].at[0, :, pl.ds(col, width)], w_held.at[2 * i], w_sems.at[2 * i]),
            pltpu.make_async_copy(downs[s].at[0, pl.ds(col, width), :], w_held.at[2 * i + 1], w_sems.at[2 * i + 1]),
        ))
    for pair in shards:
        for copy in pair:
            copy.start()
    for k in range(1, groups):
        norms[1, k] = (norm_parts(stream[k - 1])[0] * gain_second[...]).astype(BF)
    gain_step(1, to_high).wait()
    gains_out[...] = keep[6, pl.ds(0, 8)] + g_got[1]

    quarter = wide // 4
    every = groups * many

    def stage_copies(n, s, c, slot):
        stage = stream.at[slot]
        cols = pl.ds(pl.multiple_of(c * quarter, quarter), quarter)
        if n == 0:
            return (pltpu.make_async_copy(stage.at[pl.ds(0, quarter)], (down_one, down_two)[s].at[0, cols], out_sem.at[slot, 0]),)
        return tuple(
            pltpu.make_async_copy(
                stage.at[pl.ds(0, quarter), pl.ds(r * quarter, quarter)],
                (up_one, up_two)[s].at[0, pl.ds(r * quarter, quarter), cols], out_sem.at[slot, 1 + r],
            )
            for r in range(4)
        )

    def weight_phase(i, s, hooks):
        for copy in shards[i]:
            copy.wait()

        def turn(d, carry):
            cols = pl.ds(pl.multiple_of(d * 128, 128), 128)
            turned[cols, :] = norms[s, :, :, cols].reshape(every, 128).T
            return carry

        lax.fori_loop(0, wide // 128, turn, 0)

        def chunk(c, carry):
            cols = pl.ds(pl.multiple_of(c * quarter, quarter), quarter)

            def one_group(k, carry):
                where = pl.ds(pl.multiple_of(k * many, 16), many)
                mid, slope = gelu_pair(dot(norms[s, k], w_held[2 * i, :, cols]))
                middles[0, where, :] = mid.astype(BF)
                grad_mid = dot(grads[s, k], w_held[2 * i + 1, cols, :], ((1,), (1,)))
                middles[1, where, :] = (grad_mid * slope).astype(BF)
                return carry

            lax.fori_loop(0, groups, one_group, 0)
            slot = lax.rem(c, 2)

            @pl.when(c > 1)
            def _():
                for copy in stage_copies(0, s, c - 2, slot):
                    copy.wait()

            stream[slot, 0:quarter, :] = dot(middles[0], grads[s].reshape(every, wide), ((0,), (0,)))
            for copy in stage_copies(0, s, c, slot):
                copy.start()

            @pl.when(c > 0)
            def _():
                for copy in stage_copies(1, s, c - 1, 2):
                    copy.wait()

            product = dot(turned[...], middles[1])
            for r in range(4):
                stream[2, 0:quarter, r * quarter:(r + 1) * quarter] = product[r * quarter:(r + 1) * quarter]
            for copy in stage_copies(1, s, c, 2):
                copy.start()
            for at, hook in hooks.items():
                pl.when(c == at)(hook)
            return carry

        chunks = width // quarter
        lax.fori_loop(0, chunks, chunk, 0)
        for c in (chunks - 2, chunks - 1):
            for copy in stage_copies(0, s, c, c % 2):
                copy.wait()
        for copy in stage_copies(1, s, chunks - 1, 2):
            copy.wait()

    def next_level(level):
        def hook():
            end(level)
            begin(level + 1)
        return hook

    ring(1, 3).wait_recv()
    advance(2, 3)
    weight_phase(0, 1, {1: next_level(1), 3: next_level(2)})
    ring(2, 3).wait_recv()
    weight_phase(1, 0, {1: next_level(3), 3: lambda: end(4)})
    for t in range(3):
        for j in range(1, groups):
            ring(t, j).wait_send()
    each_peer(lambda p: far(groups - 1, p).wait_send())


def dense_product(dense, which, turned, right):
    block = 32
    for g in range(4):
        product = dot(turned[g * 8 * block:(g + 1) * 8 * block], right[...]).astype(BF)
        for e in range(8):
            place = (((e // 2) % 2 * 2 + e // 4) * 4 + g % 2 * 2 + g // 2) * block
            dense[e % 2, which, place:place + block] = product[e * block:(e + 1) * block]


def layer(
    ends, routes_row, tokens, cotangent, gain, cents, gain_first, gain_second, weights, expert_weights, slots, capacity,
):
    count, wide = tokens.shape
    experts, docs, groups = cents.shape[0], ends.shape[1], lax.axis_size("batch")
    many, ff = experts * capacity, expert_weights[0].shape[2]
    width, tiles = ff // groups, ff // wide
    vmem = pl.BlockSpec(memory_space=pltpu.VMEM)
    anys = pl.BlockSpec(memory_space=pl.ANY)
    f32_out = jax.ShapeDtypeStruct((1, wide, width), F32)
    dma = pltpu.SemaphoreType.DMA
    return pl.pallas_call(
        functools.partial(layer_kernel, experts, groups, slots, capacity, docs, width, tiles),
        out_shape=(
            jax.ShapeDtypeStruct((count, wide), BF),
            jax.ShapeDtypeStruct((count, wide), F32),
            jax.ShapeDtypeStruct((4, 32, wide), F32),
            jax.ShapeDtypeStruct((8 + experts, wide), F32),
            jax.ShapeDtypeStruct((8, wide), F32),
            f32_out, f32_out, f32_out, f32_out,
            jax.ShapeDtypeStruct((groups, count, wide), BF),
            jax.ShapeDtypeStruct((groups, experts, slots, wide), BF),
        ),
        in_specs=[pl.BlockSpec(memory_space=pltpu.SMEM)] + [vmem] * 7 + [anys] * 8,
        out_specs=(vmem,) * 5 + (anys,) * 6,
        scratch_shapes=[
            pltpu.VMEM((4, wide, wide), BF),
            pltpu.VMEM((2 * tiles * many, wide), BF),
            pltpu.VMEM((3, many, wide), F32),
            pltpu.VMEM((2, groups, many, wide), BF),
            pltpu.VMEM((2, groups, many, wide), BF),
            pltpu.VMEM((count, wide), BF),
            pltpu.VMEM((count, wide), BF),
            pltpu.VMEM((5, count, wide), BF),
            pltpu.VMEM((count, wide), F32),
            pltpu.VMEM((groups, experts * slots, count), BF),
            pltpu.VMEM((many, experts * slots), BF),
            pltpu.VMEM((groups, 1, count), jnp.int32),
            pltpu.VMEM((2, 2, experts, slots, wide), BF),
            pltpu.VMEM((max(2 * experts * slots, 3 * count), wide), BF),
            pltpu.VMEM((2, 4, wide // 2, wide), BF),
            pltpu.VMEM((wide, groups * many), BF),
            pltpu.VMEM((2, groups * many, wide // 4), BF),
            pltpu.VMEM((7, 16, wide), F32),
            pltpu.VMEM((5, 16, wide), F32),
            pltpu.VMEM((2, 8, wide), F32),
            dma((4,)), dma((2,)), dma((2, 2, experts)), dma((2, 2, experts)), dma((groups, experts)), dma((groups, experts)),
            dma((groups,)), dma((groups,)),
            dma((3, groups)), dma((3, groups)), dma((5, 4, 2)), dma((5, 4, 2)), dma((5,)), dma((5,)),
            dma((2,)), dma((2,)), pltpu.SemaphoreType.REGULAR((5,)), dma((3, 5)),
        ],
        compiler_params=pltpu.CompilerParams(
            collective_id=1, has_side_effects=True, vmem_limit_bytes=64 * 1024 * 1024 - 65536
        ),
        name="layer",
    )(
        ends, routes_row, tokens, cotangent, gain, cents, gain_first, gain_second, *weights, *expert_weights,
    )


def hand_out_kernel(*refs):
    dense, small, gains = refs[:3]
    sources, results = refs[3:9], refs[9:]
    for i, source in enumerate(sources):
        results[i][...] = source[...]

    @pl.when(pl.program_id(0) == 0)
    def _():
        for m in range(4):
            results[6 + m][...] = dense[m]
        results[10][...] = small[0:1, :]
        results[11][...] = small[8:, :]
        part = results[12].shape[1]
        where = pl.ds(pl.multiple_of(lax.axis_index("batch") * part, 128), part)
        for s in range(2):
            results[12 + s][...] = gains[s:s + 1, where]


def hand_out(dense, small, gains, *arrays):
    wide, steps = small.shape[1], 8

    def whole(shape):
        return pl.BlockSpec(shape, lambda i: (0,) * len(shape))

    def sliced(array):
        shape = array.shape[:-2] + (array.shape[-2] // steps, array.shape[-1])
        return pl.BlockSpec(shape, lambda i: (0,) * (len(shape) - 2) + (i, 0))

    shapes = [dense.shape[1:]] * 4 + [(1, wide), (small.shape[0] - 8, wide)] + [(1, wide // lax.axis_size("batch"))] * 2
    moved = [sliced(array) for array in arrays]
    return pl.pallas_call(
        hand_out_kernel,
        grid=(steps,),
        out_shape=tuple(jax.ShapeDtypeStruct(array.shape, array.dtype) for array in arrays)
        + tuple(jax.ShapeDtypeStruct(shape, F32) for shape in shapes),
        in_specs=[whole(array.shape) for array in (dense, small, gains)] + moved,
        out_specs=tuple(moved) + tuple(whole(shape) for shape in shapes),
        compiler_params=pltpu.CompilerParams(vmem_limit_bytes=64 * 1024 * 1024 - 65536),
        name="hand_out",
    )(dense, small, gains, *arrays)


def per_device(
    tokens, doc_ends, routes, w_query, w_key, w_value, w_output, attn_gain, centroids,
    up_first, down_first, gain_first, up_second, down_second, gain_second, cotangent,
):
    count, wide = tokens.shape
    experts, groups = lax.axis_size("expert"), lax.axis_size("batch")
    capacity = 11 * count // (8 * experts)
    slots = -(-capacity // 16) * 16
    routes_row = routes.reshape(1, count)
    gain = attn_gain[None]
    weights = (w_query, w_key, w_value, w_output)
    expert_weights = (up_first, down_first, up_second, down_second)
    if groups == 4 and experts == 8:
        block_out, grad_tokens, dense, small, gains, *parts = layer(
            doc_ends, routes_row, tokens, cotangent, gain, centroids, gain_first, gain_second, weights, expert_weights,
            slots, capacity,
        )
        (
            up_one, down_one, up_two, down_two, block_out, grad_tokens, *dense, small_gain, small_cents, gain_one, gain_two,
        ) = hand_out(dense, small, gains, *parts[:4], block_out, grad_tokens)
        return (
            block_out, grad_tokens, *dense, small_gain.reshape(wide), small_cents,
            up_one, down_one, gain_one, up_two, down_two, gain_two,
        )
    *kept, out_rows = enter(doc_ends, routes_row, tokens, cotangent, gain, centroids, weights, slots)

    def exchange(blocks):
        return lax.all_to_all(blocks, "expert", split_axis=1, concat_axis=1, tiled=True)

    came = exchange(out_rows).reshape(2, experts * slots, wide)
    back, rows, gains = chain(came, *expert_weights, gain_first, gain_second, slots, capacity)
    came_back = exchange(back.reshape(out_rows.shape)).reshape(back.shape)
    block_out, grad_tokens, dense, small = leave(
        doc_ends, routes_row, tokens, cotangent, gain, centroids, kept, came_back, weights, slots
    )
    dense = scatter_sum(dense).astype(F32)
    small = all_sum(small)
    parts = []
    for s, (up, down) in enumerate(((up_first, down_first), (up_second, down_second))):
        for part in weight_grads(ring_rows(rows[0, s], "batch"), ring_rows(rows[1, s], "batch"), up[0], down[0]):
            parts.append(part[None])
    gains = jnp.sum(lax.all_gather(gains[:2], "batch"), axis=0)
    gain_part = wide // groups
    gains = lax.dynamic_slice_in_dim(gains, lax.axis_index("batch") * gain_part, gain_part, 1)
    return (
        block_out, grad_tokens, dense[0], dense[1], dense[2], dense[3], small[0], small[8:],
        parts[0], parts[1], gains[0:1], parts[2], parts[3], gains[1:2],
    )


def solution(mesh):
    return jax.shard_map(
        per_device,
        mesh=mesh,
        in_specs=(
            P(("batch", "expert"), None),
            P(("batch", "expert"), None),
            P(("batch", "expert"), None),
            P(),
            P(),
            P(),
            P(),
            P(),
            P(),
            P("expert", None, None),
            P("expert", None, None),
            P("expert", None),
            P("expert", None, None),
            P("expert", None, None),
            P("expert", None),
            P(("batch", "expert"), None),
        ),
        out_specs=(
            P(("batch", "expert"), None),
            P(("batch", "expert"), None),
            P(("batch", "expert"), None),
            P(("batch", "expert"), None),
            P(("batch", "expert"), None),
            P(("batch", "expert"), None),
            P(),
            P(),
            P("expert", None, "batch"),
            P("expert", "batch", None),
            P("expert", "batch"),
            P("expert", None, "batch"),
            P("expert", "batch", None),
            P("expert", "batch"),
        ),
        check_vma=False,
    )
```

```python
import functools
import jax, jax.numpy as jnp
from jax import lax
from jax.experimental import pallas as pl
from jax.experimental.pallas import tpu as pltpu
from jax.sharding import PartitionSpec as P


MESH = pl.DeviceIdType.MESH
BF = jnp.bfloat16
F32 = jnp.float32
GELU_A = 0.7978845608028654
GELU_B = 0.044715


def gelu_pair(v):
    square = v * v
    bent = jnp.tanh(GELU_A * v * (1.0 + GELU_B * square))
    half = 0.5 * (1.0 + bent)
    slope = half + 0.5 * v * (1.0 - bent * bent) * (GELU_A * (1.0 + 3.0 * GELU_B * square))
    return v * half, slope


def dot(a, b, dims=((1,), (0,))):
    return lax.dot_general(a, b, (dims, ((), ())), preferred_element_type=F32)


MASKED = -1e30
EPSILON = 1e-05


def split_three(value):
    high = value.astype(BF)
    rest = value - high.astype(F32)
    middle = rest.astype(BF)
    return high, middle, (rest - middle.astype(F32)).astype(BF)


def select_rows(marks, value, dims):
    return sum(dot(marks, term, dims) for term in split_three(value))


def norm_parts(stream):
    average = jnp.mean(stream, axis=-1, keepdims=True)
    centred = stream - average
    variance = jnp.mean(centred * centred, axis=-1, keepdims=True)
    scale = lax.rsqrt(variance + EPSILON)
    return centred * scale, scale


def norm_pull(grad, stream, gain):
    unit, scale = norm_parts(stream)
    inner = grad * gain
    mean_inner = jnp.mean(inner, axis=-1, keepdims=True)
    mean_product = jnp.mean(inner * unit, axis=-1, keepdims=True)
    return scale * (inner - mean_inner - unit * mean_product), jnp.sum(grad * unit, axis=0, keepdims=True)


def route_marks(routes_row, experts, slots):
    count = routes_row.shape[1]
    ids = lax.broadcasted_iota(jnp.int32, (experts, count), 0)
    chosen = (ids == routes_row).astype(F32)
    earlier = lax.broadcasted_iota(jnp.int32, (count, count), 0) <= lax.broadcasted_iota(jnp.int32, (count, count), 1)
    running = dot(chosen.astype(BF), earlier.astype(F32).astype(BF))
    rank = jnp.sum(running * chosen, axis=0, keepdims=True) - 1.0
    place = routes_row * slots + rank.astype(jnp.int32)
    rows = lax.broadcasted_iota(jnp.int32, (experts * slots, count), 0)
    return chosen.astype(BF), (rows == place).astype(F32).astype(BF)


def allowed_pairs(ends, docs, count):
    row = lax.broadcasted_iota(jnp.int32, (count, count), 0)
    col = lax.broadcasted_iota(jnp.int32, (count, count), 1)
    row_segment = jnp.zeros((count, count), jnp.int32)
    col_segment = jnp.zeros((count, count), jnp.int32)
    for d in range(docs):
        row_segment += (row >= ends[0, d]).astype(jnp.int32)
        col_segment += (col >= ends[0, d]).astype(jnp.int32)
    return (row_segment == col_segment) & (col <= row)


def half_marks(half):
    lane = lax.broadcasted_iota(jnp.int32, (1, 128), 1)
    inside = (lane >= 64 * half) & (lane < 64 * half + 64)
    return inside.astype(F32).astype(BF)


def head_shares(query_pair, key_pair, allowed, half):
    raw = dot(query_pair * half_marks(half), key_pair, ((1,), (1,)))
    scores = jnp.where(allowed, raw * 0.125, MASKED)
    raised = jnp.exp(scores - jnp.max(scores, axis=-1, keepdims=True))
    return raised * (1.0 / jnp.sum(raised, axis=-1, keepdims=True))


def join_halves(first, second):
    lane = lax.broadcasted_iota(jnp.int32, first.shape, 1)
    return jnp.where(lane < 64, first, second)


def forward_pair(allowed, queries, keys, values, mixed, j, carry):
    cols = pl.ds(pl.multiple_of(j * 128, 128), 128)
    query_pair, key_pair, value_pair = queries[:, cols], keys[:, cols], values[:, cols]
    halves = [dot(head_shares(query_pair, key_pair, allowed, half).astype(BF), value_pair) for half in range(2)]
    mixed[:, cols] = join_halves(*halves).astype(BF)
    return carry


def enter_kernel(
    experts, slots, docs,
    ends, routes, tokens, cotangent, gain, cents, w_query, w_key, w_value, w_output,
    normed, queries, keys, values, mixed, hidden, out_rows,
    w_held, sems,
):
    copies = [
        pltpu.make_async_copy(w, w_held.at[i], sems.at[i])
        for i, w in enumerate((w_query, w_key, w_value, w_output))
    ]
    for copy in copies:
        copy.start()
    count, wide = tokens.shape
    unit, _ = norm_parts(tokens[...].astype(F32))
    normed[...] = (unit * gain[...]).astype(BF)
    for i, result in enumerate((queries, keys, values)):
        copies[i].wait()
        result[...] = dot(normed[...], w_held[i]).astype(BF)
    allowed = allowed_pairs(ends, docs, count)

    lax.fori_loop(0, wide // 128, functools.partial(forward_pair, allowed, queries, keys, values, mixed), 0)
    copies[3].wait()
    hidden[...] = tokens[...].astype(F32) + dot(mixed[...], w_held[3])
    chosen, dispatch = route_marks(routes[...], experts, slots)
    own = select_rows(chosen, cents[...], ((0,), (0,)))
    gating = jax.nn.sigmoid(jnp.sum(hidden[...] * own, axis=-1, keepdims=True))
    live = (lax.broadcasted_iota(jnp.int32, (count, 1), 0) < ends[0, docs - 1]).astype(F32)
    grad_sent = (gating * (live * cotangent[...].astype(F32))).astype(BF)
    for kind, rows in enumerate((hidden[...].astype(BF), grad_sent)):
        out_rows[kind] = dot(dispatch, rows).astype(BF).reshape(experts, slots, wide)


def enter(ends, routes_row, tokens, cotangent, gain, cents, weights, slots):
    count, wide = tokens.shape
    experts, docs = cents.shape[0], ends.shape[1]
    vmem = pl.BlockSpec(memory_space=pltpu.VMEM)
    anys = pl.BlockSpec(memory_space=pl.ANY)
    low = jax.ShapeDtypeStruct((count, wide), BF)
    return pl.pallas_call(
        functools.partial(enter_kernel, experts, slots, docs),
        out_shape=(low,) * 5 + (
            jax.ShapeDtypeStruct((count, wide), F32),
            jax.ShapeDtypeStruct((2, experts, slots, wide), BF),
        ),
        in_specs=[pl.BlockSpec(memory_space=pltpu.SMEM)] + [vmem] * 5 + [anys] * 4,
        out_specs=(vmem,) * 7,
        scratch_shapes=[pltpu.VMEM((4, wide, wide), BF), pltpu.SemaphoreType.DMA((4,))],
        compiler_params=pltpu.CompilerParams(vmem_limit_bytes=48 * 1024 * 1024),
        name="enter",
    )(ends, routes_row, tokens, cotangent, gain, cents, *weights)


def backward_pair(allowed, queries, keys, values, grad_low, grad_three, j, carry):
    cols = pl.ds(pl.multiple_of(j * 128, 128), 128)
    query_pair, key_pair, value_pair = queries[:, cols], keys[:, cols], values[:, cols]
    grad_pair = grad_low[:, cols]
    parts = []
    for half in range(2):
        shares = head_shares(query_pair, key_pair, allowed, half)
        grad_shares = dot(grad_pair * half_marks(half), value_pair, ((1,), (1,)))
        inner = jnp.sum(shares * grad_shares, axis=-1, keepdims=True)
        raw = (shares * (grad_shares - inner) * 0.125).astype(BF)
        parts.append((
            dot(raw, key_pair),
            dot(raw, query_pair, ((0,), (0,))),
            dot(shares.astype(BF), grad_pair, ((0,), (0,))),
        ))
    for i in range(3):
        grad_three[i][:, cols] = join_halves(parts[0][i], parts[1][i]).astype(BF)
    return carry


def leave_kernel(
    experts, slots, docs,
    ends, routes, tokens, cotangent, gain, cents, normed, queries, keys, values, mixed, hidden, came,
    w_query, w_key, w_value, w_output,
    block_out, grad_tokens, dense, small,
    w_held, grad_low, grad_three, normed_turned, grad_hidden, sems,
):
    copies = [
        pltpu.make_async_copy(w, w_held.at[i], sems.at[i])
        for i, w in enumerate((w_query, w_key, w_value, w_output))
    ]
    for i in (3, 0, 1, 2):
        copies[i].start()
    count, wide = tokens.shape
    chosen, dispatch = route_marks(routes[...], experts, slots)
    own = select_rows(chosen, cents[...], ((0,), (0,)))
    gating = jax.nn.sigmoid(jnp.sum(hidden[...] * own, axis=-1, keepdims=True))
    live = (lax.broadcasted_iota(jnp.int32, (count, 1), 0) < ends[0, docs - 1]).astype(F32)
    returned = dot(dispatch, came[0], ((0,), (0,)))
    block_out[...] = (live * (gating * returned + (1.0 - gating) * hidden[...])).astype(BF)
    grad_block = live * cotangent[...].astype(F32)
    grad_score = jnp.sum(grad_block * (returned - hidden[...]), axis=-1, keepdims=True) * gating * (1.0 - gating)
    grad_hidden[...] = (1.0 - gating) * grad_block + dot(dispatch, came[1], ((0,), (0,))) + grad_score * own
    small[pl.ds(8, experts), :] = select_rows(chosen, grad_score * hidden[...], ((1,), (0,)))
    grad_low[...] = grad_hidden[...].astype(BF)
    copies[3].wait()
    grad_mixed = dot(grad_low[...], w_held[3], ((1,), (1,))).astype(BF)
    dense[3] = dot(mixed[...].T, grad_low[...]).astype(BF)
    grad_low[...] = grad_mixed
    allowed = allowed_pairs(ends, docs, count)

    lax.fori_loop(
        0, wide // 128, functools.partial(
            backward_pair, allowed, queries, keys, values, grad_low, [grad_three.at[i] for i in range(3)]
        ), 0
    )
    normed_turned[...] = normed[...].T
    for i in range(3):
        dense[i] = dot(normed_turned[...], grad_three[i]).astype(BF)
    for i in range(3):
        copies[i].wait()
    grad_normed = sum(dot(grad_three[i], w_held[i], ((1,), (1,))) for i in range(3))
    pulled, grad_gain = norm_pull(grad_normed, tokens[...].astype(F32), gain[...])
    grad_tokens[...] = grad_hidden[...] + pulled
    small[pl.ds(0, 8), :] = jnp.broadcast_to(grad_gain, (8, wide))


def leave(ends, routes_row, tokens, cotangent, gain, cents, kept, came, weights, slots):
    count, wide = tokens.shape
    experts, docs = cents.shape[0], ends.shape[1]
    vmem = pl.BlockSpec(memory_space=pltpu.VMEM)
    anys = pl.BlockSpec(memory_space=pl.ANY)
    return pl.pallas_call(
        functools.partial(leave_kernel, experts, slots, docs),
        out_shape=(
            jax.ShapeDtypeStruct((count, wide), BF),
            jax.ShapeDtypeStruct((count, wide), F32),
            jax.ShapeDtypeStruct((4, wide, wide), BF),
            jax.ShapeDtypeStruct((8 + experts, wide), F32),
        ),
        in_specs=[pl.BlockSpec(memory_space=pltpu.SMEM)] + [vmem] * 12 + [anys] * 4,
        out_specs=(vmem,) * 4,
        scratch_shapes=[
            pltpu.VMEM((4, wide, wide), BF),
            pltpu.VMEM((count, wide), BF),
            pltpu.VMEM((3, count, wide), BF),
            pltpu.VMEM((wide, count), BF),
            pltpu.VMEM((count, wide), F32),
            pltpu.SemaphoreType.DMA((4,)),
        ],
        compiler_params=pltpu.CompilerParams(vmem_limit_bytes=56 * 1024 * 1024),
        name="leave",
    )(ends, routes_row, tokens, cotangent, gain, cents, *kept, came, *weights)


def pack_marks(experts, slots, capacity):
    shape = (experts * capacity, experts * slots)
    row = lax.broadcasted_iota(jnp.int32, (shape[0], 1), 0)
    block = sum((row >= s * capacity).astype(jnp.int32) for s in range(1, experts))
    column = lax.broadcasted_iota(jnp.int32, shape, 1)
    return (column == row + (slots - capacity) * block).astype(F32).astype(BF)


def chain_kernel(
    experts, slots, capacity, tiles,
    came, up_first, down_first, up_second, down_second, gain_first, gain_second,
    back, rows, gains,
    up_tile, down_tile, pre, stream, total, sems,
):
    tile = up_tile.shape[2]
    ups, downs = (up_first, up_second), (down_first, down_second)
    gain_refs = (gain_first, gain_second)

    def fetch(s, c, slot):
        cols = pl.ds(pl.multiple_of(c * tile, tile), tile)
        return (
            pltpu.make_async_copy(ups[s].at[0, :, cols], up_tile.at[slot], sems.at[0, slot]),
            pltpu.make_async_copy(downs[s].at[0, cols, :], down_tile.at[slot], sems.at[1, slot]),
        )

    order = ((0, True), (1, True), (1, False), (0, False))

    def run(phase, body):
        s = order[phase][0]

        def step(c, carry):
            slot = lax.rem(c, 2)
            for copy in fetch(s, c, slot):
                copy.wait()

            @pl.when(c + 1 < tiles)
            def _():
                for copy in fetch(s, c + 1, 1 - slot):
                    copy.start()

            if phase < 3:
                @pl.when(c + 1 == tiles)
                def _():
                    for copy in fetch(order[phase + 1][0], 0, 1 - slot):
                        copy.start()

            body(s, pl.ds(pl.multiple_of(c * tile, tile), tile), slot)
            return carry

        lax.fori_loop(0, tiles, step, 0)

    for copy in fetch(0, 0, 0):
        copy.start()
    gains[...] = jnp.zeros_like(gains)
    packing = pack_marks(experts, slots, capacity)
    stream[0] = dot(packing, came[0])
    rows[1, 1] = dot(packing, came[1]).astype(BF)

    def forward(s, cols, slot):
        made = dot(rows[0, s], up_tile[slot])
        pre[s, :, cols] = made
        mid = gelu_pair(made)[0].astype(BF)
        total[...] += dot(mid, down_tile[slot])

    def backward(s, cols, slot):
        grad_mid = dot(rows[1, s], down_tile[slot], ((1,), (1,)))
        grad_pre = (gelu_pair(pre[s, :, cols])[1] * grad_mid).astype(BF)
        total[...] += dot(grad_pre, up_tile[slot], ((1,), (1,)))

    for s in range(2):
        unit, _ = norm_parts(stream[s])
        rows[0, s] = (unit * gain_refs[s][...]).astype(BF)
        total[...] = stream[s]
        run(s, forward)
        if s == 0:
            stream[1] = total[...]
    back[0] = dot(packing, total[...].astype(BF), ((0,), (0,))).astype(BF)

    for phase, s in ((2, 1), (3, 0)):
        total[...] = jnp.zeros_like(total)
        run(phase, backward)
        pulled, grad_gain = norm_pull(total[...], stream[s], gain_refs[s][...])
        gains[pl.ds(s, 1), :] = grad_gain
        if s == 1:
            grad_stream = rows[1, 1].astype(F32) + pulled
            stream[1] = grad_stream
            rows[1, 0] = grad_stream.astype(BF)
        else:
            grad_rows = (stream[1] + pulled).astype(BF)
            back[1] = dot(packing, grad_rows, ((0,), (0,))).astype(BF)


def chain(came, up_first, down_first, up_second, down_second, gain_first, gain_second, slots, capacity):
    wide, hidden = up_first.shape[1:]
    experts = came.shape[1] // slots
    count = experts * capacity
    tile = 1024
    vmem = pl.BlockSpec(memory_space=pltpu.VMEM)
    anys = pl.BlockSpec(memory_space=pl.ANY)
    return pl.pallas_call(
        functools.partial(chain_kernel, experts, slots, capacity, hidden // tile),
        out_shape=(
            jax.ShapeDtypeStruct(came.shape, BF),
            jax.ShapeDtypeStruct((2, 2, count, wide), BF),
            jax.ShapeDtypeStruct((8, wide), F32),
        ),
        in_specs=[vmem] + [anys] * 4 + [vmem] * 2,
        out_specs=(vmem,) * 3,
        scratch_shapes=[
            pltpu.VMEM((2, wide, tile), BF),
            pltpu.VMEM((2, tile, wide), BF),
            pltpu.VMEM((2, count, hidden), F32),
            pltpu.VMEM((2, count, wide), F32),
            pltpu.VMEM((count, wide), F32),
            pltpu.SemaphoreType.DMA((2, 2)),
        ],
        compiler_params=pltpu.CompilerParams(vmem_limit_bytes=56 * 1024 * 1024),
        name="chain",
    )(came, up_first, down_first, up_second, down_second, gain_first, gain_second)


def ring_rows(rows, axis):
    count = lax.axis_size(axis)
    back = [(i, (i - 1) % count) for i in range(count)]
    held = [rows]
    for _ in range(count - 1):
        held.append(lax.ppermute(held[-1], axis, back))
    return jnp.concatenate(held, axis=0)


def weight_grads(normed_rows, grad_rows, up_proj, down_proj):
    count = lax.axis_size("batch")
    width = up_proj.shape[1] // count
    first = lax.axis_index("batch") * width
    up_part = lax.dynamic_slice_in_dim(up_proj, first, width, 1)
    down_part = lax.dynamic_slice_in_dim(down_proj, first, width, 0)
    pre_act = jnp.dot(normed_rows, up_part, preferred_element_type=jnp.float32)
    middle, gelu_pull = jax.vjp(jax.nn.gelu, pre_act)
    grad_middle = jnp.einsum("rd,fd->rf", grad_rows, down_part, preferred_element_type=jnp.float32)
    grad_pre = gelu_pull(grad_middle)[0].astype(jnp.bfloat16)
    grad_down = jnp.einsum(
        "rf,rd->fd", middle.astype(jnp.bfloat16), grad_rows, preferred_element_type=jnp.float32
    )
    grad_up = jnp.einsum("rd,rf->df", normed_rows, grad_pre, preferred_element_type=jnp.float32)
    return grad_up, grad_down


def halve(blocks, axis, bit, dim):
    count = lax.axis_size(axis)
    mine = (lax.axis_index(axis) // bit) % 2
    kept = lax.dynamic_index_in_dim(blocks, mine, dim, keepdims=False)
    sent = lax.dynamic_index_in_dim(blocks, 1 - mine, dim, keepdims=False)
    got = lax.ppermute(sent, axis, [(i, i ^ bit) for i in range(count)])
    return (kept.astype(jnp.float32) + got.astype(jnp.float32)).astype(blocks.dtype)


def scatter_sum(parts):
    experts, groups = lax.axis_size("expert"), lax.axis_size("batch")
    kinds, rows, width = parts.shape
    bits_e = experts.bit_length() - 1
    bits_b = groups.bit_length() - 1
    shape = (kinds,) + (2,) * (bits_b + bits_e) + (rows // (experts * groups), width)
    blocks = parts.reshape(shape)
    for k in range(bits_e):
        blocks = halve(blocks, "expert", 1 << k, bits_b + bits_e - k)
    for k in range(bits_b):
        blocks = halve(blocks, "batch", 1 << k, bits_b - k)
    return blocks


def all_sum(value):
    for axis in ("expert", "batch"):
        count = lax.axis_size(axis)
        bit = 1
        while bit < count:
            value = value + lax.ppermute(value, axis, [(i, i ^ bit) for i in range(count)])
            bit *= 2
    return value


def layer_kernel(
    experts, groups, slots, capacity, docs, width, tiles,
    ends, routes, tokens, cotangent, gain, cents, gain_first, gain_second,
    w_query, w_key, w_value, w_output, up_first, down_first, up_second, down_second,
    block_out, grad_tokens, dense_out, small_out, gains_out, up_one, down_one, up_two, down_two, ring_held, far_inbox,
    w_held, slopes, stream, norms, grads, cur, token_low, attention, hidden, dispatch, packing, routes_held, inbox, outbox, dense, turned, middles, up_stage,
    keep, s_got, g_got,
    w_sems, row_sem, a2a_send, a2a_recv, far_send, far_recv, route_send, route_recv, ring_send, ring_recv, dense_send, dense_recv, small_send, small_recv,
    gain_send, gain_recv, ready, out_sem,
):
    b, e = lax.axis_index("batch"), lax.axis_index("expert")
    count, wide = tokens.shape
    many = experts * capacity
    before, after = lax.rem(b + groups - 1, groups), lax.rem(b + 1, groups)
    core, x, y = lax.rem(e, 2), lax.rem(e // 2, 2), lax.rem(e // 4, 2)
    b0, b1 = lax.rem(b, 2), lax.rem(b // 2, 2)
    other = 1 - core
    to_core, to_x, to_y = (b, e + 1 - 2 * core), (b, e + 2 - 4 * x), (b, e + 4 - 8 * y)
    to_low, to_high = (b + 1 - 2 * b0, e), (b + 2 - 4 * b1, e)

    def remote(src, dst, send, recv, peer):
        return pltpu.make_async_remote_copy(
            src_ref=src, dst_ref=dst, send_sem=send, recv_sem=recv, device_id=peer, device_id_type=MESH
        )

    barrier = pltpu.get_barrier_semaphore()

    def greet(p, carry):
        peer = (b, lax.rem(e + p, experts))
        pl.semaphore_signal(barrier, inc=1, device_id=peer, device_id_type=MESH)
        return carry

    lax.fori_loop(1, experts, greet, 0)
    for peer in ((before, e), (after, e), to_high):
        pl.semaphore_signal(barrier, inc=1, device_id=peer, device_id_type=MESH)

    tile = wide
    ups, downs = (up_first, up_second), (down_first, down_second)
    gain_refs = (gain_first, gain_second)

    def fetch(s, c, slot):
        cols = pl.ds(pl.multiple_of(c * tile, tile), tile)
        return (
            pltpu.make_async_copy(ups[s].at[0, :, cols], w_held.at[slot], w_sems.at[slot]),
            pltpu.make_async_copy(downs[s].at[0, cols, :], w_held.at[2 + slot], w_sems.at[2 + slot]),
        )

    def stream_tiles(s, follow, body):
        def step(c, carry):
            slot = lax.rem(c, 2)
            for copy in fetch(s, c, slot):
                copy.wait()

            @pl.when(c + 1 < tiles)
            def _():
                for copy in fetch(s, c + 1, 1 - slot):
                    copy.start()

            if follow is not None:
                @pl.when(c + 1 == tiles)
                def _():
                    for copy in fetch(follow, 0, 1 - slot):
                        copy.start()

            body(c, slot)
            return carry

        lax.fori_loop(0, tiles, step, 0)

    def exchange(phase, kind, block):
        def copy(p):
            target = lax.rem(e + p, experts)
            return remote(
                block(target), inbox.at[phase, kind, e],
                a2a_send.at[phase, kind, p], a2a_recv.at[phase, kind, p], (b, target),
            )
        own = pltpu.make_async_copy(block(e), inbox.at[phase, kind, e], a2a_recv.at[phase, kind, 0])

        def start():
            own.start()
            lax.fori_loop(1, experts, lambda p, carry: (copy(p).start(), carry)[1], 0)

        def wait():
            own.wait()
            lax.fori_loop(1, experts, lambda p, carry: (copy(p).wait(), carry)[1], 0)

        return start, wait


    def ring(t, j):
        if t == 0:
            source, target = token_low if j == 1 else ring_held.at[j - 1], ring_held.at[j]
        else:
            source, target = grads.at[2 - t, j - 1], grads.at[2 - t, j]
        return remote(source, target, ring_send.at[t, j], ring_recv.at[t, j], (before, e))

    def advance(t, j):
        ring(t, j - 1).wait_recv()
        ring(t, j).start()

    def far(k, p):
        target = lax.rem(e + p, experts)
        return remote(
            inbox.at[0, 0, target], far_inbox.at[k, e], far_send.at[k, p], far_recv.at[k, p], (b, target)
        )

    def far_own(k):
        return pltpu.make_async_copy(inbox.at[0, 0, e], far_inbox.at[k, e], far_recv.at[k, 0])

    def each_peer(act):
        lax.fori_loop(1, experts, lambda p, carry: (act(p), carry)[1], 0)

    def cur_load(k):
        return pltpu.make_async_copy(ring_held.at[k], cur, row_sem.at[0])

    def far_load(k):
        return pltpu.make_async_copy(far_inbox.at[k], inbox.at[0, 1], row_sem.at[1])

    def relay(k):
        if k > 1:
            each_peer(lambda p: far(k - 1, p).wait_send())
        if k == 2:
            far_own(1).wait()
        cur_load(k).wait()
        inbox[0, 0] = dot(dispatch[k], cur[...]).astype(BF).reshape(experts, slots, wide)
        far_own(k).start()
        each_peer(lambda p: far(k, p).start())

    def far_arrive(k):
        if k > 1:
            far_own(k).wait()
        each_peer(lambda p: far(k, p).wait_recv())
        far_load(k).start()

    def collect(k):
        far_load(k).wait()
        norms[1, k] = dot(packing[...], inbox[0, 1].reshape(experts * slots, wide)).astype(BF)

    def route_copy(j):
        return remote(
            routes, routes_held.at[j], route_send.at[j], route_recv.at[j],
            (lax.rem(b + groups - j, groups), e),
        )

    attention_weights = [
        pltpu.make_async_copy(w, w_held.at[i], w_sems.at[i])
        for i, w in enumerate((w_query, w_key, w_value, w_output))
    ]
    for copy in attention_weights:
        copy.start()
    normed, queries, keys, values, mixed = (attention.at[i] for i in range(5))
    normed[...] = (norm_parts(tokens[...].astype(F32))[0] * gain[...]).astype(BF)
    pl.semaphore_wait(barrier, experts + 2)
    for j in range(1, groups):
        route_copy(j).start()
    for i, result in enumerate((queries, keys, values)):
        attention_weights[i].wait()
        result[...] = dot(normed[...], w_held[i]).astype(BF)
    for copy in fetch(0, 0, 0):
        copy.start()
    allowed = allowed_pairs(ends, docs, count)
    lax.fori_loop(0, wide // 128, functools.partial(forward_pair, allowed, queries, keys, values, mixed), 0)
    attention_weights[3].wait()
    hidden[...] = tokens[...].astype(F32) + dot(mixed[...], w_held[3])
    token_low[...] = hidden[...].astype(BF)
    ring(0, 1).start()
    chosen, dispatch[0] = route_marks(routes[...], experts, slots)
    own = select_rows(chosen, cents[...], ((0,), (0,)))
    gating = jax.nn.sigmoid(jnp.sum(hidden[...] * own, axis=-1, keepdims=True))
    live = (lax.broadcasted_iota(jnp.int32, (count, 1), 0) < ends[0, docs - 1]).astype(F32)

    def out_block(kind, p):
        return outbox.at[pl.ds(pl.multiple_of((kind * experts + p) * slots, 16), slots)]

    def put_out(kind, marks, value, dims):
        start = kind * experts * slots
        outbox[start:start + experts * slots, :] = dot(marks, value, dims).astype(BF)

    send_routed, get_routed = exchange(0, 0, functools.partial(out_block, 0))
    send_grads, get_grads = exchange(0, 1, functools.partial(out_block, 1))
    send_result, get_result = exchange(1, 0, functools.partial(out_block, 0))
    send_back, get_back = exchange(1, 1, functools.partial(out_block, 1))
    put_out(0, dispatch[0], token_low[...], ((1,), (0,)))
    send_routed()
    put_out(1, dispatch[0], (gating * (live * cotangent[...].astype(F32))).astype(BF), ((1,), (0,)))
    send_grads()
    packing[...] = pack_marks(experts, slots, capacity)
    gains_out[...] = jnp.zeros_like(gains_out)
    for j in range(1, groups):
        route_copy(j).wait()
        dispatch[j] = route_marks(routes_held[j], experts, slots)[1]
    get_routed()
    stream[0] = dot(packing[...], inbox[0, 0].reshape(experts * slots, wide))
    advance(0, 2)
    cur_load(1).start()
    total = stream.at[2]

    def slab(s, c):
        return pl.ds(pl.multiple_of((s * tiles + c) * many, 16), many)

    for s in range(2):
        unit, _ = norm_parts(stream[s])
        norms[s, 0] = (unit * gain_refs[s][...]).astype(BF)
        total[...] = stream[s]

        def forward(c, slot, s=s):
            made = dot(norms[s, 0], w_held[slot])
            value, slope = gelu_pair(made)
            slopes[slab(s, c), :] = slope.astype(BF)
            total[...] += dot(value.astype(BF), w_held[2 + slot])
            if s == 1:
                @pl.when(c == tiles // 2)
                def _():
                    advance(0, 3)
                    cur_load(2).start()

        stream_tiles(s, 1, forward)
        if s == 0:
            stream[1] = total[...]
            get_grads()
            grads[1, 0] = dot(packing[...], inbox[0, 1].reshape(experts * slots, wide)).astype(BF)
            ring(1, 1).start()
            relay(1)

    put_out(0, packing[...], total[...].astype(BF), ((0,), (0,)))
    send_result()
    relay(2)
    for s in (1, 0):
        total[...] = jnp.zeros_like(total)

        def backward(c, slot, s=s):
            grad_mid = dot(grads[s, 0], w_held[2 + slot], ((1,), (1,)))
            grad_pre = (slopes[slab(s, c), :].astype(F32) * grad_mid).astype(BF)
            total[...] += dot(grad_pre, w_held[slot], ((1,), (1,)))

        stream_tiles(s, 0 if s == 1 else None, backward)
        pulled, grad_gain = norm_pull(total[...], stream[s], gain_refs[s][...])
        gains_out[pl.ds(s, 1), :] = grad_gain
        if s == 1:
            grad_stream = grads[1, 0].astype(F32) + pulled
            stream[1] = grad_stream
            grads[0, 0] = grad_stream.astype(BF)
        else:
            put_out(1, packing[...], (stream[1] + pulled).astype(BF), ((0,), (0,)))
    send_back()
    pl.semaphore_signal(ready.at[0], inc=1, device_id=to_core, device_id_type=MESH)
    for i in (3, 0, 1, 2):
        attention_weights[i].start()

    def small_step(level, peer):
        return remote(keep.at[level], s_got.at[level], small_send.at[level], small_recv.at[level], peer)

    def gain_step(level, peer):
        return remote(keep.at[5 + level, pl.ds(0, 8)], g_got.at[level], gain_send.at[level], gain_recv.at[level], peer)

    keep[5, pl.ds(0, 8)] = gains_out[...]
    gain_step(0, to_low).start()

    ring(0, 3).wait_recv()
    cur_load(3).start()
    far_arrive(1)
    collect(1)
    far_arrive(2)
    advance(1, 2)
    ring(2, 1).start()
    relay(3)
    collect(2)
    get_result()
    returned = dot(dispatch[0], inbox[1, 0].reshape(experts * slots, wide), ((0,), (0,)))
    block_out[...] = (live * (gating * returned + (1.0 - gating) * hidden[...])).astype(BF)
    grad_block = live * cotangent[...].astype(F32)
    grad_score = jnp.sum(grad_block * (returned - hidden[...]), axis=-1, keepdims=True) * gating * (1.0 - gating)
    grad_hidden = stream.at[0, pl.ds(0, count)]
    own = select_rows(chosen, cents[...], ((0,), (0,)))
    grad_hidden[...] = (1.0 - gating) * grad_block + grad_score * own
    keep[0, pl.ds(8, experts)] = select_rows(chosen, grad_score * hidden[...], ((1,), (0,)))
    turned_low = turned.at[:, pl.ds(0, count)]
    turned_low[...] = mixed[...].T
    grad_low = cur
    get_back()
    grad_hidden[...] += dot(dispatch[0], inbox[1, 1].reshape(experts * slots, wide), ((0,), (0,)))
    grad_low[...] = grad_hidden[...].astype(BF)
    attention_weights[3].wait()
    grad_mixed = dot(grad_low[...], w_held[3], ((1,), (1,))).astype(BF)
    dense_product(dense, 3, turned_low, grad_low)
    turned_low[...] = normed[...].T
    grad_low[...] = grad_mixed
    grad_three = [outbox.at[pl.ds(i * count, count)] for i in range(3)]
    lax.fori_loop(
        0, wide // 128, functools.partial(backward_pair, allowed, queries, keys, values, grad_low, grad_three), 0
    )

    def one_product(i, carry):
        dense_product(dense, i, turned_low, outbox.at[pl.ds(pl.multiple_of(i * count, 16), count)])
        return carry

    lax.fori_loop(0, 3, one_product, 0)
    for i in range(3):
        attention_weights[i].wait()
    grad_normed = sum(dot(grad_three[i][...], w_held[i], ((1,), (1,))) for i in range(3))
    pulled, grad_gain = norm_pull(grad_normed, tokens[...].astype(F32), gain[...])
    grad_tokens[...] = grad_hidden[...] + pulled
    keep[0, pl.ds(0, 8)] = jnp.broadcast_to(grad_gain, (8, wide))

    def rows_at(start, size):
        return pl.ds(pl.multiple_of(start, 32), size)

    def level_copies(level):
        copies = []
        for m in range(4):
            mine, theirs = dense.at[core, m], dense.at[other, m]
            if level == 0:
                parts = ((theirs, slopes.at[pl.ds(m * 512, 512)], to_core),)
            elif level == 1 and m < 2:
                parts = ((mine.at[rows_at((1 - x) * 256, 256)], theirs.at[pl.ds(0, 256)], to_x),)
            elif level == 1:
                parts = tuple(
                    (mine.at[rows_at(xx * 256 + (1 - y) * 128, 128)], theirs.at[pl.ds(xx * 128, 128)], to_y)
                    for xx in range(2)
                )
            elif level == 2 and m < 2:
                parts = ((mine.at[rows_at(x * 256 + (1 - y) * 128, 128)], theirs.at[pl.ds(256, 128)], to_y),)
            elif level == 2:
                parts = ((mine.at[rows_at((1 - x) * 256 + y * 128, 128)], theirs.at[pl.ds(256, 128)], to_x),)
            elif level == 3:
                start = x * 256 + y * 128 + (1 - b0) * 64
                parts = ((mine.at[rows_at(start, 64)], theirs.at[pl.ds(384, 64)], to_low),)
            else:
                start = x * 256 + y * 128 + b0 * 64 + (1 - b1) * 32
                parts = ((mine.at[rows_at(start, 32)], theirs.at[pl.ds(448, 32)], to_high),)
            for n, (src, dst, peer) in enumerate(parts):
                copies.append(remote(src, dst, dense_send.at[level, m, n], dense_recv.at[level, m, n], peer))
        return copies

    small_peers = (to_core, to_x, to_y, to_low, to_high)

    def begin(level):
        for sem in {0: (0,), 1: (1, 2), 2: (), 3: (3,), 4: (4,)}[level]:
            pl.semaphore_wait(ready.at[sem], 1)
        for copy in level_copies(level):
            copy.start()
        small_step(level, small_peers[level]).start()

    def add_rows(m, start, size, got):
        where = rows_at(start, size)
        dense[core, m, where, :] = (dense[core, m, where, :].astype(F32) + got.astype(F32)).astype(BF)

    def end(level):
        for copy in level_copies(level):
            copy.wait()
        small_step(level, small_peers[level]).wait()
        if level < 4:
            keep[level + 1] = keep[level] + s_got[level]
        for m in range(4):
            if level == 0:
                for h in range(2):
                    add_rows(m, h * 256, 256, slopes[m * 512 + h * 256:m * 512 + h * 256 + 256])
            elif level == 1 and m < 2:
                add_rows(m, x * 256, 256, dense[other, m, 0:256])
            elif level == 1:
                for xx in range(2):
                    add_rows(m, xx * 256 + y * 128, 128, dense[other, m, xx * 128:xx * 128 + 128])
            elif level == 2:
                add_rows(m, x * 256 + y * 128, 128, dense[other, m, 256:384])
            elif level == 3:
                add_rows(m, x * 256 + y * 128 + b0 * 64, 64, dense[other, m, 384:448])
            else:
                where = rows_at(x * 256 + y * 128 + b0 * 64 + b1 * 32, 32)
                dense_out[m] = dense[core, m, where, :].astype(F32) + dense[other, m, 448:480].astype(F32)
        if level == 0:
            for sem, peer in enumerate(small_peers[1:], 1):
                pl.semaphore_signal(ready.at[sem], inc=1, device_id=peer, device_id_type=MESH)
        if level == 4:
            small_out[...] = keep[4] + s_got[4]

    begin(0)
    far_arrive(3)
    advance(1, 3)
    advance(2, 2)
    collect(3)
    gain_step(0, to_low).wait()
    keep[6, pl.ds(0, 8)] = keep[5, pl.ds(0, 8)] + g_got[0]
    gain_step(1, to_high).start()
    for copy in fetch(0, 0, 0):
        copy.start()
    for k in range(1, groups):
        routed = norms[1, k].astype(F32)
        stream[k - 1] = routed
        norms[0, k] = (norm_parts(routed)[0] * gain_first[...]).astype(BF)

    def forward_others(c, slot):
        def one_group(k, carry):
            mid = gelu_pair(dot(norms[0, k + 1], w_held[slot]))[0].astype(BF)
            stream[k] += dot(mid, w_held[2 + slot])
            return carry

        lax.fori_loop(0, groups - 1, one_group, 0)

        @pl.when(c == 1)
        def _():
            end(0)
            begin(1)

    stream_tiles(0, None, forward_others)
    col = pl.multiple_of(b * width, width)
    shards = []
    for i, s in enumerate((1, 0)):
        shards.append((
            pltpu.make_async_copy(ups[s].at[0, :, pl.ds(col, width)], w_held.at[2 * i], w_sems.at[2 * i]),
            pltpu.make_async_copy(downs[s].at[0, pl.ds(col, width), :], w_held.at[2 * i + 1], w_sems.at[2 * i + 1]),
        ))
    for pair in shards:
        for copy in pair:
            copy.start()
    for k in range(1, groups):
        norms[1, k] = (norm_parts(stream[k - 1])[0] * gain_second[...]).astype(BF)
    gain_step(1, to_high).wait()
    gains_out[...] = keep[6, pl.ds(0, 8)] + g_got[1]

    quarter = wide // 4
    every = groups * many

    def down_stage(slot):
        return outbox.at[pl.ds(pl.multiple_of(slot * quarter, 16), quarter)]

    def stage_copies(s, c, slot):
        cols = pl.ds(pl.multiple_of(c * quarter, quarter), quarter)
        return (
            pltpu.make_async_copy(down_stage(slot), (down_one, down_two)[s].at[0, cols], out_sem.at[slot, 0]),
            pltpu.make_async_copy(up_stage.at[slot], (up_one, up_two)[s].at[0, :, cols], out_sem.at[slot, 1]),
        )

    chunks = width // quarter

    def weight_phase(i, carry):
        s = 1 - i

        def turn(d, carry):
            cols = pl.ds(pl.multiple_of(d * 128, 128), 128)
            turned[cols, :] = norms[s, :, :, cols].reshape(every, 128).T
            return carry

        lax.fori_loop(0, wide // 128, turn, 0)
        for n in range(2):
            @pl.when(i == n)
            def _(n=n):
                for copy in shards[n]:
                    copy.wait()
                if n == 0:
                    ring(1, 3).wait_recv()
                    advance(2, 3)
                else:
                    ring(2, 3).wait_recv()

        def chunk(c, carry):
            cols = pl.ds(pl.multiple_of(c * quarter, quarter), quarter)

            def one_group(k, carry):
                where = pl.ds(pl.multiple_of(k * many, 16), many)
                mid, slope = gelu_pair(dot(norms[s, k], w_held[2 * i, :, cols]))
                middles[0, where, :] = mid.astype(BF)
                grad_mid = dot(grads[s, k], w_held[2 * i + 1, cols, :], ((1,), (1,)))
                middles[1, where, :] = (grad_mid * slope).astype(BF)
                return carry

            lax.fori_loop(0, groups, one_group, 0)
            slot = lax.rem(c, 2)

            @pl.when(i * chunks + c > 1)
            def _():
                for copy in stage_copies(0, 0, slot):
                    copy.wait()

            down_stage(slot)[...] = dot(middles[0], grads[s].reshape(every, wide), ((0,), (0,))).astype(BF)
            up_stage[slot] = dot(turned[...], middles[1]).astype(BF)
            for n in range(2):
                @pl.when(s == n)
                def _(n=n):
                    for copy in stage_copies(n, c, slot):
                        copy.start()
            for (at_i, at_c), hook in hooks.items():
                pl.when((i == at_i) & (c == at_c))(hook)
            return carry

        lax.fori_loop(0, chunks, chunk, 0)
        return carry

    def next_level(level):
        def hook():
            end(level)
            begin(level + 1)
        return hook

    hooks = {(0, 0): next_level(1), (0, 3): next_level(2), (1, 1): next_level(3)}
    lax.fori_loop(0, 2, weight_phase, 0)
    end(4)
    for slot in range(2):
        for copy in stage_copies(0, 0, slot):
            copy.wait()
    for t in range(3):
        for j in range(1, groups):
            ring(t, j).wait_send()
    each_peer(lambda p: far(groups - 1, p).wait_send())


def dense_product(dense, which, turned, right):
    block = 32

    def one_batch(g, carry):
        rows = pl.ds(pl.multiple_of(g * 8 * block, 8 * block), 8 * block)
        product = dot(turned[rows, :], right[...]).astype(BF)
        shift = (lax.rem(g, 2) * 2 + g // 2) * block
        for e in range(8):
            place = pl.multiple_of(((e // 2) % 2 * 2 + e // 4) * 4 * block + shift, block)
            dense[e % 2, which, pl.ds(place, block)] = product[e * block:(e + 1) * block]
        return carry

    lax.fori_loop(0, 4, one_batch, 0)


def layer(
    ends, routes_row, tokens, cotangent, gain, cents, gain_first, gain_second, weights, expert_weights, slots, capacity,
):
    count, wide = tokens.shape
    experts, docs, groups = cents.shape[0], ends.shape[1], lax.axis_size("batch")
    many, ff = experts * capacity, expert_weights[0].shape[2]
    width, tiles = ff // groups, ff // wide
    vmem = pl.BlockSpec(memory_space=pltpu.VMEM)
    anys = pl.BlockSpec(memory_space=pl.ANY)
    low_out = jax.ShapeDtypeStruct((1, wide, width), BF)
    dma = pltpu.SemaphoreType.DMA
    return pl.pallas_call(
        functools.partial(layer_kernel, experts, groups, slots, capacity, docs, width, tiles),
        out_shape=(
            jax.ShapeDtypeStruct((count, wide), BF),
            jax.ShapeDtypeStruct((count, wide), F32),
            jax.ShapeDtypeStruct((4, 32, wide), F32),
            jax.ShapeDtypeStruct((8 + experts, wide), F32),
            jax.ShapeDtypeStruct((8, wide), F32),
            low_out, low_out, low_out, low_out,
            jax.ShapeDtypeStruct((groups, count, wide), BF),
            jax.ShapeDtypeStruct((groups, experts, slots, wide), BF),
        ),
        in_specs=[pl.BlockSpec(memory_space=pltpu.SMEM)] + [vmem] * 7 + [anys] * 8,
        out_specs=(vmem,) * 5 + (anys,) * 6,
        scratch_shapes=[
            pltpu.VMEM((4, wide, wide), BF),
            pltpu.VMEM((2 * tiles * many, wide), BF),
            pltpu.VMEM((3, many, wide), F32),
            pltpu.VMEM((2, groups, many, wide), BF),
            pltpu.VMEM((2, groups, many, wide), BF),
            pltpu.VMEM((count, wide), BF),
            pltpu.VMEM((count, wide), BF),
            pltpu.VMEM((5, count, wide), BF),
            pltpu.VMEM((count, wide), F32),
            pltpu.VMEM((groups, experts * slots, count), BF),
            pltpu.VMEM((many, experts * slots), BF),
            pltpu.VMEM((groups, 1, count), jnp.int32),
            pltpu.VMEM((2, 2, experts, slots, wide), BF),
            pltpu.VMEM((max(2 * experts * slots, 3 * count), wide), BF),
            pltpu.VMEM((2, 4, wide // 2, wide), BF),
            pltpu.VMEM((wide, groups * many), BF),
            pltpu.VMEM((2, groups * many, wide // 4), BF),
            pltpu.VMEM((2, wide, wide // 4), BF),
            pltpu.VMEM((7, 16, wide), F32),
            pltpu.VMEM((5, 16, wide), F32),
            pltpu.VMEM((2, 8, wide), F32),
            dma((4,)), dma((2,)), dma((2, 2, experts)), dma((2, 2, experts)), dma((groups, experts)), dma((groups, experts)),
            dma((groups,)), dma((groups,)),
            dma((3, groups)), dma((3, groups)), dma((5, 4, 2)), dma((5, 4, 2)), dma((5,)), dma((5,)),
            dma((2,)), dma((2,)), pltpu.SemaphoreType.REGULAR((5,)), dma((2, 2)),
        ],
        compiler_params=pltpu.CompilerParams(
            collective_id=1, has_side_effects=True, vmem_limit_bytes=64 * 1024 * 1024 - 65536
        ),
        name="layer",
    )(
        ends, routes_row, tokens, cotangent, gain, cents, gain_first, gain_second, *weights, *expert_weights,
    )


def hand_out_kernel(*refs):
    dense, small, gains = refs[:3]
    sources, results = refs[3:9], refs[9:]
    for i, source in enumerate(sources):
        results[i][...] = source[...].astype(results[i].dtype)

    @pl.when(pl.program_id(0) == 0)
    def _():
        for m in range(4):
            results[6 + m][...] = dense[m]
        results[10][...] = small[0:1, :]
        results[11][...] = small[8:, :]
        part = results[12].shape[1]
        where = pl.ds(pl.multiple_of(lax.axis_index("batch") * part, 128), part)
        for s in range(2):
            results[12 + s][...] = gains[s:s + 1, where]


def hand_out(dense, small, gains, *arrays):
    wide, steps = small.shape[1], 8

    def whole(shape):
        return pl.BlockSpec(shape, lambda i: (0,) * len(shape))

    def sliced(array):
        shape = array.shape[:-2] + (array.shape[-2] // steps, array.shape[-1])
        return pl.BlockSpec(shape, lambda i: (0,) * (len(shape) - 2) + (i, 0))

    shapes = [dense.shape[1:]] * 4 + [(1, wide), (small.shape[0] - 8, wide)] + [(1, wide // lax.axis_size("batch"))] * 2
    moved = [sliced(array) for array in arrays]
    return pl.pallas_call(
        hand_out_kernel,
        grid=(steps,),
        out_shape=tuple(jax.ShapeDtypeStruct(array.shape, BF if i == 4 else F32) for i, array in enumerate(arrays))
        + tuple(jax.ShapeDtypeStruct(shape, F32) for shape in shapes),
        in_specs=[whole(array.shape) for array in (dense, small, gains)] + moved,
        out_specs=tuple(moved) + tuple(whole(shape) for shape in shapes),
        compiler_params=pltpu.CompilerParams(vmem_limit_bytes=64 * 1024 * 1024 - 65536),
        name="hand_out",
    )(dense, small, gains, *arrays)


def per_device(
    tokens, doc_ends, routes, w_query, w_key, w_value, w_output, attn_gain, centroids,
    up_first, down_first, gain_first, up_second, down_second, gain_second, cotangent,
):
    count, wide = tokens.shape
    experts, groups = lax.axis_size("expert"), lax.axis_size("batch")
    capacity = 11 * count // (8 * experts)
    slots = -(-capacity // 16) * 16
    routes_row = routes.reshape(1, count)
    gain = attn_gain[None]
    weights = (w_query, w_key, w_value, w_output)
    expert_weights = (up_first, down_first, up_second, down_second)
    if groups == 4 and experts == 8:
        block_out, grad_tokens, dense, small, gains, *parts = layer(
            doc_ends, routes_row, tokens, cotangent, gain, centroids, gain_first, gain_second, weights, expert_weights,
            slots, capacity,
        )
        (
            up_one, down_one, up_two, down_two, block_out, grad_tokens, *dense, small_gain, small_cents, gain_one, gain_two,
        ) = hand_out(dense, small, gains, *parts[:4], block_out, grad_tokens)
        return (
            block_out, grad_tokens, *dense, small_gain.reshape(wide), small_cents,
            up_one, down_one, gain_one, up_two, down_two, gain_two,
        )
    *kept, out_rows = enter(doc_ends, routes_row, tokens, cotangent, gain, centroids, weights, slots)

    def exchange(blocks):
        return lax.all_to_all(blocks, "expert", split_axis=1, concat_axis=1, tiled=True)

    came = exchange(out_rows).reshape(2, experts * slots, wide)
    back, rows, gains = chain(came, *expert_weights, gain_first, gain_second, slots, capacity)
    came_back = exchange(back.reshape(out_rows.shape)).reshape(back.shape)
    block_out, grad_tokens, dense, small = leave(
        doc_ends, routes_row, tokens, cotangent, gain, centroids, kept, came_back, weights, slots
    )
    dense = scatter_sum(dense).astype(F32)
    small = all_sum(small)
    parts = []
    for s, (up, down) in enumerate(((up_first, down_first), (up_second, down_second))):
        for part in weight_grads(ring_rows(rows[0, s], "batch"), ring_rows(rows[1, s], "batch"), up[0], down[0]):
            parts.append(part[None])
    gains = jnp.sum(lax.all_gather(gains[:2], "batch"), axis=0)
    gain_part = wide // groups
    gains = lax.dynamic_slice_in_dim(gains, lax.axis_index("batch") * gain_part, gain_part, 1)
    return (
        block_out, grad_tokens, dense[0], dense[1], dense[2], dense[3], small[0], small[8:],
        parts[0], parts[1], gains[0:1], parts[2], parts[3], gains[1:2],
    )


def solution(mesh):
    return jax.shard_map(
        per_device,
        mesh=mesh,
        in_specs=(
            P(("batch", "expert"), None),
            P(("batch", "expert"), None),
            P(("batch", "expert"), None),
            P(),
            P(),
            P(),
            P(),
            P(),
            P(),
            P("expert", None, None),
            P("expert", None, None),
            P("expert", None),
            P("expert", None, None),
            P("expert", None, None),
            P("expert", None),
            P(("batch", "expert"), None),
        ),
        out_specs=(
            P(("batch", "expert"), None),
            P(("batch", "expert"), None),
            P(("batch", "expert"), None),
            P(("batch", "expert"), None),
            P(("batch", "expert"), None),
            P(("batch", "expert"), None),
            P(),
            P(),
            P("expert", None, "batch"),
            P("expert", "batch", None),
            P("expert", "batch"),
            P("expert", None, "batch"),
            P("expert", "batch", None),
            P("expert", "batch"),
        ),
        check_vma=False,
    )
```

```python
import functools
import jax, jax.numpy as jnp
from jax import lax
from jax.experimental import pallas as pl
from jax.experimental.pallas import tpu as pltpu
from jax.sharding import PartitionSpec as P


MESH = pl.DeviceIdType.MESH
BF = jnp.bfloat16
F32 = jnp.float32
GELU_A = 0.7978845608028654
GELU_B = 0.044715


def gelu_pair(v):
    square = v * v
    half = 0.5 * jnp.tanh(v * (GELU_A + GELU_A * GELU_B * square)) + 0.5
    value = v * half
    return value, half + value * ((1.0 - half) * (2.0 * GELU_A + 6.0 * GELU_A * GELU_B * square))


def dot(a, b, dims=((1,), (0,))):
    return lax.dot_general(a, b, (dims, ((), ())), preferred_element_type=F32)


MASKED = -1e30
EPSILON = 1e-05


def split_three(value):
    high = value.astype(BF)
    rest = value - high.astype(F32)
    middle = rest.astype(BF)
    return high, middle, (rest - middle.astype(F32)).astype(BF)


def select_rows(marks, value, dims):
    return sum(dot(marks, term, dims) for term in split_three(value))


def norm_parts(stream):
    average = jnp.mean(stream, axis=-1, keepdims=True)
    centred = stream - average
    variance = jnp.mean(centred * centred, axis=-1, keepdims=True)
    scale = lax.rsqrt(variance + EPSILON)
    return centred * scale, scale


def norm_pull(grad, stream, gain):
    unit, scale = norm_parts(stream)
    inner = grad * gain
    mean_inner = jnp.mean(inner, axis=-1, keepdims=True)
    mean_product = jnp.mean(inner * unit, axis=-1, keepdims=True)
    return scale * (inner - mean_inner - unit * mean_product), jnp.sum(grad * unit, axis=0, keepdims=True)


def route_marks(routes_row, experts, slots):
    count = routes_row.shape[1]
    ids = lax.broadcasted_iota(jnp.int32, (experts, count), 0)
    chosen = (ids == routes_row).astype(F32)
    earlier = lax.broadcasted_iota(jnp.int32, (count, count), 0) <= lax.broadcasted_iota(jnp.int32, (count, count), 1)
    running = dot(chosen.astype(BF), earlier.astype(F32).astype(BF))
    rank = jnp.sum(running * chosen, axis=0, keepdims=True) - 1.0
    place = routes_row * slots + rank.astype(jnp.int32)
    rows = lax.broadcasted_iota(jnp.int32, (experts * slots, count), 0)
    return chosen.astype(BF), (rows == place).astype(F32).astype(BF)


def allowed_pairs(ends, docs, count):
    row = lax.broadcasted_iota(jnp.int32, (count, count), 0)
    col = lax.broadcasted_iota(jnp.int32, (count, count), 1)
    row_segment = jnp.zeros((count, count), jnp.int32)
    col_segment = jnp.zeros((count, count), jnp.int32)
    for d in range(docs):
        row_segment += (row >= ends[0, d]).astype(jnp.int32)
        col_segment += (col >= ends[0, d]).astype(jnp.int32)
    return (row_segment == col_segment) & (col <= row)


def half_marks(half):
    lane = lax.broadcasted_iota(jnp.int32, (1, 128), 1)
    inside = (lane >= 64 * half) & (lane < 64 * half + 64)
    return inside.astype(F32).astype(BF)


def head_shares(query_pair, key_pair, allowed, half):
    raw = dot(query_pair * half_marks(half), key_pair, ((1,), (1,)))
    scores = jnp.where(allowed, raw * 0.125, MASKED)
    raised = jnp.exp(scores - jnp.max(scores, axis=-1, keepdims=True))
    return raised * (1.0 / jnp.sum(raised, axis=-1, keepdims=True))


def join_halves(first, second):
    lane = lax.broadcasted_iota(jnp.int32, first.shape, 1)
    return jnp.where(lane < 64, first, second)


def forward_pair(allowed, queries, keys, values, mixed, j, carry):
    cols = pl.ds(pl.multiple_of(j * 128, 128), 128)
    query_pair, key_pair, value_pair = queries[:, cols], keys[:, cols], values[:, cols]
    halves = [dot(head_shares(query_pair, key_pair, allowed, half).astype(BF), value_pair) for half in range(2)]
    mixed[:, cols] = join_halves(*halves).astype(BF)
    return carry


def enter_kernel(
    experts, slots, docs,
    ends, routes, tokens, cotangent, gain, cents, w_query, w_key, w_value, w_output,
    normed, queries, keys, values, mixed, hidden, out_rows,
    w_held, sems,
):
    copies = [
        pltpu.make_async_copy(w, w_held.at[i], sems.at[i])
        for i, w in enumerate((w_query, w_key, w_value, w_output))
    ]
    for copy in copies:
        copy.start()
    count, wide = tokens.shape
    unit, _ = norm_parts(tokens[...].astype(F32))
    normed[...] = (unit * gain[...]).astype(BF)
    for i, result in enumerate((queries, keys, values)):
        copies[i].wait()
        result[...] = dot(normed[...], w_held[i]).astype(BF)
    allowed = allowed_pairs(ends, docs, count)

    lax.fori_loop(0, wide // 128, functools.partial(forward_pair, allowed, queries, keys, values, mixed), 0)
    copies[3].wait()
    hidden[...] = tokens[...].astype(F32) + dot(mixed[...], w_held[3])
    chosen, dispatch = route_marks(routes[...], experts, slots)
    own = select_rows(chosen, cents[...], ((0,), (0,)))
    gating = jax.nn.sigmoid(jnp.sum(hidden[...] * own, axis=-1, keepdims=True))
    live = (lax.broadcasted_iota(jnp.int32, (count, 1), 0) < ends[0, docs - 1]).astype(F32)
    grad_sent = (gating * (live * cotangent[...].astype(F32))).astype(BF)
    for kind, rows in enumerate((hidden[...].astype(BF), grad_sent)):
        out_rows[kind] = dot(dispatch, rows).astype(BF).reshape(experts, slots, wide)


def enter(ends, routes_row, tokens, cotangent, gain, cents, weights, slots):
    count, wide = tokens.shape
    experts, docs = cents.shape[0], ends.shape[1]
    vmem = pl.BlockSpec(memory_space=pltpu.VMEM)
    anys = pl.BlockSpec(memory_space=pl.ANY)
    low = jax.ShapeDtypeStruct((count, wide), BF)
    return pl.pallas_call(
        functools.partial(enter_kernel, experts, slots, docs),
        out_shape=(low,) * 5 + (
            jax.ShapeDtypeStruct((count, wide), F32),
            jax.ShapeDtypeStruct((2, experts, slots, wide), BF),
        ),
        in_specs=[pl.BlockSpec(memory_space=pltpu.SMEM)] + [vmem] * 5 + [anys] * 4,
        out_specs=(vmem,) * 7,
        scratch_shapes=[pltpu.VMEM((4, wide, wide), BF), pltpu.SemaphoreType.DMA((4,))],
        compiler_params=pltpu.CompilerParams(vmem_limit_bytes=48 * 1024 * 1024),
        name="enter",
    )(ends, routes_row, tokens, cotangent, gain, cents, *weights)


def backward_pair(allowed, queries, keys, values, grad_low, grad_three, j, carry):
    cols = pl.ds(pl.multiple_of(j * 128, 128), 128)
    query_pair, key_pair, value_pair = queries[:, cols], keys[:, cols], values[:, cols]
    grad_pair = grad_low[:, cols]
    parts = []
    for half in range(2):
        shares = head_shares(query_pair, key_pair, allowed, half)
        grad_shares = dot(grad_pair * half_marks(half), value_pair, ((1,), (1,)))
        inner = jnp.sum(shares * grad_shares, axis=-1, keepdims=True)
        raw = (shares * (grad_shares - inner) * 0.125).astype(BF)
        parts.append((
            dot(raw, key_pair),
            dot(raw, query_pair, ((0,), (0,))),
            dot(shares.astype(BF), grad_pair, ((0,), (0,))),
        ))
    for i in range(3):
        grad_three[i][:, cols] = join_halves(parts[0][i], parts[1][i]).astype(BF)
    return carry


def leave_kernel(
    experts, slots, docs,
    ends, routes, tokens, cotangent, gain, cents, normed, queries, keys, values, mixed, hidden, came,
    w_query, w_key, w_value, w_output,
    block_out, grad_tokens, dense, small,
    w_held, grad_low, grad_three, normed_turned, grad_hidden, sems,
):
    copies = [
        pltpu.make_async_copy(w, w_held.at[i], sems.at[i])
        for i, w in enumerate((w_query, w_key, w_value, w_output))
    ]
    for i in (3, 0, 1, 2):
        copies[i].start()
    count, wide = tokens.shape
    chosen, dispatch = route_marks(routes[...], experts, slots)
    own = select_rows(chosen, cents[...], ((0,), (0,)))
    gating = jax.nn.sigmoid(jnp.sum(hidden[...] * own, axis=-1, keepdims=True))
    live = (lax.broadcasted_iota(jnp.int32, (count, 1), 0) < ends[0, docs - 1]).astype(F32)
    returned = dot(dispatch, came[0], ((0,), (0,)))
    block_out[...] = (live * (gating * returned + (1.0 - gating) * hidden[...])).astype(BF)
    grad_block = live * cotangent[...].astype(F32)
    grad_score = jnp.sum(grad_block * (returned - hidden[...]), axis=-1, keepdims=True) * gating * (1.0 - gating)
    grad_hidden[...] = (1.0 - gating) * grad_block + dot(dispatch, came[1], ((0,), (0,))) + grad_score * own
    small[pl.ds(8, experts), :] = select_rows(chosen, grad_score * hidden[...], ((1,), (0,)))
    grad_low[...] = grad_hidden[...].astype(BF)
    copies[3].wait()
    grad_mixed = dot(grad_low[...], w_held[3], ((1,), (1,))).astype(BF)
    dense[3] = dot(mixed[...].T, grad_low[...]).astype(BF)
    grad_low[...] = grad_mixed
    allowed = allowed_pairs(ends, docs, count)

    lax.fori_loop(
        0, wide // 128, functools.partial(
            backward_pair, allowed, queries, keys, values, grad_low, [grad_three.at[i] for i in range(3)]
        ), 0
    )
    normed_turned[...] = normed[...].T
    for i in range(3):
        dense[i] = dot(normed_turned[...], grad_three[i]).astype(BF)
    for i in range(3):
        copies[i].wait()
    grad_normed = sum(dot(grad_three[i], w_held[i], ((1,), (1,))) for i in range(3))
    pulled, grad_gain = norm_pull(grad_normed, tokens[...].astype(F32), gain[...])
    grad_tokens[...] = grad_hidden[...] + pulled
    small[pl.ds(0, 8), :] = jnp.broadcast_to(grad_gain, (8, wide))


def leave(ends, routes_row, tokens, cotangent, gain, cents, kept, came, weights, slots):
    count, wide = tokens.shape
    experts, docs = cents.shape[0], ends.shape[1]
    vmem = pl.BlockSpec(memory_space=pltpu.VMEM)
    anys = pl.BlockSpec(memory_space=pl.ANY)
    return pl.pallas_call(
        functools.partial(leave_kernel, experts, slots, docs),
        out_shape=(
            jax.ShapeDtypeStruct((count, wide), BF),
            jax.ShapeDtypeStruct((count, wide), F32),
            jax.ShapeDtypeStruct((4, wide, wide), BF),
            jax.ShapeDtypeStruct((8 + experts, wide), F32),
        ),
        in_specs=[pl.BlockSpec(memory_space=pltpu.SMEM)] + [vmem] * 12 + [anys] * 4,
        out_specs=(vmem,) * 4,
        scratch_shapes=[
            pltpu.VMEM((4, wide, wide), BF),
            pltpu.VMEM((count, wide), BF),
            pltpu.VMEM((3, count, wide), BF),
            pltpu.VMEM((wide, count), BF),
            pltpu.VMEM((count, wide), F32),
            pltpu.SemaphoreType.DMA((4,)),
        ],
        compiler_params=pltpu.CompilerParams(vmem_limit_bytes=56 * 1024 * 1024),
        name="leave",
    )(ends, routes_row, tokens, cotangent, gain, cents, *kept, came, *weights)


def pack_marks(experts, slots, capacity):
    shape = (experts * capacity, experts * slots)
    row = lax.broadcasted_iota(jnp.int32, (shape[0], 1), 0)
    block = sum((row >= s * capacity).astype(jnp.int32) for s in range(1, experts))
    column = lax.broadcasted_iota(jnp.int32, shape, 1)
    return (column == row + (slots - capacity) * block).astype(F32).astype(BF)


def chain_kernel(
    experts, slots, capacity, tiles,
    came, up_first, down_first, up_second, down_second, gain_first, gain_second,
    back, rows, gains,
    up_tile, down_tile, pre, stream, total, sems,
):
    tile = up_tile.shape[2]
    ups, downs = (up_first, up_second), (down_first, down_second)
    gain_refs = (gain_first, gain_second)

    def fetch(s, c, slot):
        cols = pl.ds(pl.multiple_of(c * tile, tile), tile)
        return (
            pltpu.make_async_copy(ups[s].at[0, :, cols], up_tile.at[slot], sems.at[0, slot]),
            pltpu.make_async_copy(downs[s].at[0, cols, :], down_tile.at[slot], sems.at[1, slot]),
        )

    order = ((0, True), (1, True), (1, False), (0, False))

    def run(phase, body):
        s = order[phase][0]

        def step(c, carry):
            slot = lax.rem(c, 2)
            for copy in fetch(s, c, slot):
                copy.wait()

            @pl.when(c + 1 < tiles)
            def _():
                for copy in fetch(s, c + 1, 1 - slot):
                    copy.start()

            if phase < 3:
                @pl.when(c + 1 == tiles)
                def _():
                    for copy in fetch(order[phase + 1][0], 0, 1 - slot):
                        copy.start()

            body(s, pl.ds(pl.multiple_of(c * tile, tile), tile), slot)
            return carry

        lax.fori_loop(0, tiles, step, 0)

    for copy in fetch(0, 0, 0):
        copy.start()
    gains[...] = jnp.zeros_like(gains)
    packing = pack_marks(experts, slots, capacity)
    stream[0] = dot(packing, came[0])
    rows[1, 1] = dot(packing, came[1]).astype(BF)

    def forward(s, cols, slot):
        made = dot(rows[0, s], up_tile[slot])
        pre[s, :, cols] = made
        mid = gelu_pair(made)[0].astype(BF)
        total[...] += dot(mid, down_tile[slot])

    def backward(s, cols, slot):
        grad_mid = dot(rows[1, s], down_tile[slot], ((1,), (1,)))
        grad_pre = (gelu_pair(pre[s, :, cols])[1] * grad_mid).astype(BF)
        total[...] += dot(grad_pre, up_tile[slot], ((1,), (1,)))

    for s in range(2):
        unit, _ = norm_parts(stream[s])
        rows[0, s] = (unit * gain_refs[s][...]).astype(BF)
        total[...] = stream[s]
        run(s, forward)
        if s == 0:
            stream[1] = total[...]
    back[0] = dot(packing, total[...].astype(BF), ((0,), (0,))).astype(BF)

    for phase, s in ((2, 1), (3, 0)):
        total[...] = jnp.zeros_like(total)
        run(phase, backward)
        pulled, grad_gain = norm_pull(total[...], stream[s], gain_refs[s][...])
        gains[pl.ds(s, 1), :] = grad_gain
        if s == 1:
            grad_stream = rows[1, 1].astype(F32) + pulled
            stream[1] = grad_stream
            rows[1, 0] = grad_stream.astype(BF)
        else:
            grad_rows = (stream[1] + pulled).astype(BF)
            back[1] = dot(packing, grad_rows, ((0,), (0,))).astype(BF)


def chain(came, up_first, down_first, up_second, down_second, gain_first, gain_second, slots, capacity):
    wide, hidden = up_first.shape[1:]
    experts = came.shape[1] // slots
    count = experts * capacity
    tile = 1024
    vmem = pl.BlockSpec(memory_space=pltpu.VMEM)
    anys = pl.BlockSpec(memory_space=pl.ANY)
    return pl.pallas_call(
        functools.partial(chain_kernel, experts, slots, capacity, hidden // tile),
        out_shape=(
            jax.ShapeDtypeStruct(came.shape, BF),
            jax.ShapeDtypeStruct((2, 2, count, wide), BF),
            jax.ShapeDtypeStruct((8, wide), F32),
        ),
        in_specs=[vmem] + [anys] * 4 + [vmem] * 2,
        out_specs=(vmem,) * 3,
        scratch_shapes=[
            pltpu.VMEM((2, wide, tile), BF),
            pltpu.VMEM((2, tile, wide), BF),
            pltpu.VMEM((2, count, hidden), F32),
            pltpu.VMEM((2, count, wide), F32),
            pltpu.VMEM((count, wide), F32),
            pltpu.SemaphoreType.DMA((2, 2)),
        ],
        compiler_params=pltpu.CompilerParams(vmem_limit_bytes=56 * 1024 * 1024),
        name="chain",
    )(came, up_first, down_first, up_second, down_second, gain_first, gain_second)


def ring_rows(rows, axis):
    count = lax.axis_size(axis)
    back = [(i, (i - 1) % count) for i in range(count)]
    held = [rows]
    for _ in range(count - 1):
        held.append(lax.ppermute(held[-1], axis, back))
    return jnp.concatenate(held, axis=0)


def weight_grads(normed_rows, grad_rows, up_proj, down_proj):
    count = lax.axis_size("batch")
    width = up_proj.shape[1] // count
    first = lax.axis_index("batch") * width
    up_part = lax.dynamic_slice_in_dim(up_proj, first, width, 1)
    down_part = lax.dynamic_slice_in_dim(down_proj, first, width, 0)
    pre_act = jnp.dot(normed_rows, up_part, preferred_element_type=jnp.float32)
    middle, gelu_pull = jax.vjp(jax.nn.gelu, pre_act)
    grad_middle = jnp.einsum("rd,fd->rf", grad_rows, down_part, preferred_element_type=jnp.float32)
    grad_pre = gelu_pull(grad_middle)[0].astype(jnp.bfloat16)
    grad_down = jnp.einsum(
        "rf,rd->fd", middle.astype(jnp.bfloat16), grad_rows, preferred_element_type=jnp.float32
    )
    grad_up = jnp.einsum("rd,rf->df", normed_rows, grad_pre, preferred_element_type=jnp.float32)
    return grad_up, grad_down


def halve(blocks, axis, bit, dim):
    count = lax.axis_size(axis)
    mine = (lax.axis_index(axis) // bit) % 2
    kept = lax.dynamic_index_in_dim(blocks, mine, dim, keepdims=False)
    sent = lax.dynamic_index_in_dim(blocks, 1 - mine, dim, keepdims=False)
    got = lax.ppermute(sent, axis, [(i, i ^ bit) for i in range(count)])
    return (kept.astype(jnp.float32) + got.astype(jnp.float32)).astype(blocks.dtype)


def scatter_sum(parts):
    experts, groups = lax.axis_size("expert"), lax.axis_size("batch")
    kinds, rows, width = parts.shape
    bits_e = experts.bit_length() - 1
    bits_b = groups.bit_length() - 1
    shape = (kinds,) + (2,) * (bits_b + bits_e) + (rows // (experts * groups), width)
    blocks = parts.reshape(shape)
    for k in range(bits_e):
        blocks = halve(blocks, "expert", 1 << k, bits_b + bits_e - k)
    for k in range(bits_b):
        blocks = halve(blocks, "batch", 1 << k, bits_b - k)
    return blocks


def all_sum(value):
    for axis in ("expert", "batch"):
        count = lax.axis_size(axis)
        bit = 1
        while bit < count:
            value = value + lax.ppermute(value, axis, [(i, i ^ bit) for i in range(count)])
            bit *= 2
    return value


def layer_kernel(
    experts, groups, slots, capacity, docs, width, tiles,
    ends, routes, tokens, cotangent, gain, cents, gain_first, gain_second,
    w_query, w_key, w_value, w_output, up_first, down_first, up_second, down_second,
    block_out, grad_tokens, dense_out, small_out, gains_out, up_one, down_one, up_two, down_two, ring_held, far_inbox,
    w_held, slopes, stream, norms, grads, cur, token_low, attention, hidden, dispatch, packing, routes_held, inbox, outbox, dense, turned, middles, up_stage,
    keep, s_got, g_got,
    w_sems, row_sem, a2a_send, a2a_recv, far_send, far_recv, route_send, route_recv, ring_send, ring_recv, dense_send, dense_recv, small_send, small_recv,
    gain_send, gain_recv, ready, out_sem,
):
    b, e = lax.axis_index("batch"), lax.axis_index("expert")
    count, wide = tokens.shape
    many = experts * capacity
    before, after = lax.rem(b + groups - 1, groups), lax.rem(b + 1, groups)
    core, x, y = lax.rem(e, 2), lax.rem(e // 2, 2), lax.rem(e // 4, 2)
    b0, b1 = lax.rem(b, 2), lax.rem(b // 2, 2)
    other = 1 - core
    to_core, to_x, to_y = (b, e + 1 - 2 * core), (b, e + 2 - 4 * x), (b, e + 4 - 8 * y)
    to_low, to_high = (b + 1 - 2 * b0, e), (b + 2 - 4 * b1, e)

    def remote(src, dst, send, recv, peer):
        return pltpu.make_async_remote_copy(
            src_ref=src, dst_ref=dst, send_sem=send, recv_sem=recv, device_id=peer, device_id_type=MESH
        )

    barrier = pltpu.get_barrier_semaphore()

    def greet(p, carry):
        peer = (b, lax.rem(e + p, experts))
        pl.semaphore_signal(barrier, inc=1, device_id=peer, device_id_type=MESH)
        return carry

    lax.fori_loop(1, experts, greet, 0)
    for peer in ((before, e), (after, e), to_high):
        pl.semaphore_signal(barrier, inc=1, device_id=peer, device_id_type=MESH)

    tile = wide
    ups, downs = (up_first, up_second), (down_first, down_second)
    gain_refs = (gain_first, gain_second)

    def fetch(s, c, slot):
        cols = pl.ds(pl.multiple_of(c * tile, tile), tile)
        return (
            pltpu.make_async_copy(ups[s].at[0, :, cols], w_held.at[slot], w_sems.at[slot]),
            pltpu.make_async_copy(downs[s].at[0, cols, :], w_held.at[2 + slot], w_sems.at[2 + slot]),
        )

    def stream_tiles(s, follow, body):
        def step(c, carry):
            slot = lax.rem(c, 2)
            for copy in fetch(s, c, slot):
                copy.wait()

            @pl.when(c + 1 < tiles)
            def _():
                for copy in fetch(s, c + 1, 1 - slot):
                    copy.start()

            if follow is not None:
                @pl.when(c + 1 == tiles)
                def _():
                    for copy in fetch(follow, 0, 1 - slot):
                        copy.start()

            body(c, slot)
            return carry

        lax.fori_loop(0, tiles, step, 0)

    def exchange(phase, kind, block):
        def copy(p):
            target = lax.rem(e + p, experts)
            return remote(
                block(target), inbox.at[phase, kind, e],
                a2a_send.at[phase, kind, p], a2a_recv.at[phase, kind, p], (b, target),
            )
        own = pltpu.make_async_copy(block(e), inbox.at[phase, kind, e], a2a_recv.at[phase, kind, 0])

        def start():
            own.start()
            lax.fori_loop(1, experts, lambda p, carry: (copy(p).start(), carry)[1], 0)

        def wait():
            own.wait()
            lax.fori_loop(1, experts, lambda p, carry: (copy(p).wait(), carry)[1], 0)

        return start, wait


    def ring(t, j):
        if t == 0:
            source, target = token_low if j == 1 else ring_held.at[j - 1], ring_held.at[j]
        else:
            source, target = grads.at[2 - t, j - 1], grads.at[2 - t, j]
        return remote(source, target, ring_send.at[t, j], ring_recv.at[t, j], (before, e))

    def advance(t, j):
        ring(t, j - 1).wait_recv()
        ring(t, j).start()

    def far(k, p):
        target = lax.rem(e + p, experts)
        return remote(
            inbox.at[0, 0, target], far_inbox.at[k, e], far_send.at[k, p], far_recv.at[k, p], (b, target)
        )

    def far_own(k):
        return pltpu.make_async_copy(inbox.at[0, 0, e], far_inbox.at[k, e], far_recv.at[k, 0])

    def each_peer(act):
        lax.fori_loop(1, experts, lambda p, carry: (act(p), carry)[1], 0)

    def cur_load(k):
        return pltpu.make_async_copy(ring_held.at[k], cur, row_sem.at[0])

    def far_load(k):
        return pltpu.make_async_copy(far_inbox.at[k], inbox.at[0, 1], row_sem.at[1])

    def relay(k):
        if k > 1:
            each_peer(lambda p: far(k - 1, p).wait_send())
        if k == 2:
            far_own(1).wait()
        cur_load(k).wait()
        inbox[0, 0] = dot(dispatch[k], cur[...]).astype(BF).reshape(experts, slots, wide)
        far_own(k).start()
        each_peer(lambda p: far(k, p).start())

    def far_arrive(k):
        if k > 1:
            far_own(k).wait()
        each_peer(lambda p: far(k, p).wait_recv())
        far_load(k).start()

    def collect(k):
        far_load(k).wait()
        norms[1, k] = dot(packing[...], inbox[0, 1].reshape(experts * slots, wide)).astype(BF)

    def route_copy(j):
        return remote(
            routes, routes_held.at[j], route_send.at[j], route_recv.at[j],
            (lax.rem(b + groups - j, groups), e),
        )

    attention_weights = [
        pltpu.make_async_copy(w, w_held.at[i], w_sems.at[i])
        for i, w in enumerate((w_query, w_key, w_value, w_output))
    ]
    for copy in attention_weights:
        copy.start()
    normed, queries, keys, values, mixed = (attention.at[i] for i in range(5))
    normed[...] = (norm_parts(tokens[...].astype(F32))[0] * gain[...]).astype(BF)
    pl.semaphore_wait(barrier, experts + 2)
    for j in range(1, groups):
        route_copy(j).start()
    for i, result in enumerate((queries, keys, values)):
        attention_weights[i].wait()
        result[...] = dot(normed[...], w_held[i]).astype(BF)
    for copy in fetch(0, 0, 0):
        copy.start()
    allowed = allowed_pairs(ends, docs, count)
    lax.fori_loop(0, wide // 128, functools.partial(forward_pair, allowed, queries, keys, values, mixed), 0)
    attention_weights[3].wait()
    hidden[...] = tokens[...].astype(F32) + dot(mixed[...], w_held[3])
    token_low[...] = hidden[...].astype(BF)
    ring(0, 1).start()
    chosen, dispatch[0] = route_marks(routes[...], experts, slots)
    own = select_rows(chosen, cents[...], ((0,), (0,)))
    gating = jax.nn.sigmoid(jnp.sum(hidden[...] * own, axis=-1, keepdims=True))
    live = (lax.broadcasted_iota(jnp.int32, (count, 1), 0) < ends[0, docs - 1]).astype(F32)

    def out_block(kind, p):
        return outbox.at[pl.ds(pl.multiple_of((kind * experts + p) * slots, 16), slots)]

    def put_out(kind, marks, value, dims):
        start = kind * experts * slots
        outbox[start:start + experts * slots, :] = dot(marks, value, dims).astype(BF)

    send_routed, get_routed = exchange(0, 0, functools.partial(out_block, 0))
    send_grads, get_grads = exchange(0, 1, functools.partial(out_block, 1))
    send_result, get_result = exchange(1, 0, functools.partial(out_block, 0))
    send_back, get_back = exchange(1, 1, functools.partial(out_block, 1))
    put_out(0, dispatch[0], token_low[...], ((1,), (0,)))
    send_routed()
    put_out(1, dispatch[0], (gating * (live * cotangent[...].astype(F32))).astype(BF), ((1,), (0,)))
    send_grads()
    packing[...] = pack_marks(experts, slots, capacity)
    gains_out[...] = jnp.zeros_like(gains_out)
    for j in range(1, groups):
        route_copy(j).wait()
        dispatch[j] = route_marks(routes_held[j], experts, slots)[1]
    get_routed()
    stream[0] = dot(packing[...], inbox[0, 0].reshape(experts * slots, wide))
    advance(0, 2)
    cur_load(1).start()
    total = stream.at[2]

    def slab(s, c):
        return pl.ds(pl.multiple_of((s * tiles + c) * many, 16), many)

    for s in range(2):
        unit, _ = norm_parts(stream[s])
        norms[s, 0] = (unit * gain_refs[s][...]).astype(BF)
        total[...] = stream[s]

        def forward(c, slot, s=s):
            made = dot(norms[s, 0], w_held[slot])
            value, slope = gelu_pair(made)
            slopes[slab(s, c), :] = slope.astype(BF)
            total[...] += dot(value.astype(BF), w_held[2 + slot])
            if s == 1:
                @pl.when(c == tiles // 2)
                def _():
                    advance(0, 3)
                    cur_load(2).start()

        stream_tiles(s, 1, forward)
        if s == 0:
            stream[1] = total[...]
            get_grads()
            grads[1, 0] = dot(packing[...], inbox[0, 1].reshape(experts * slots, wide)).astype(BF)
            ring(1, 1).start()
            relay(1)

    put_out(0, packing[...], total[...].astype(BF), ((0,), (0,)))
    send_result()
    relay(2)
    for s in (1, 0):
        total[...] = jnp.zeros_like(total)

        def backward(c, slot, s=s):
            grad_mid = dot(grads[s, 0], w_held[2 + slot], ((1,), (1,)))
            grad_pre = (slopes[slab(s, c), :].astype(F32) * grad_mid).astype(BF)
            total[...] += dot(grad_pre, w_held[slot], ((1,), (1,)))

        stream_tiles(s, 0 if s == 1 else None, backward)
        pulled, grad_gain = norm_pull(total[...], stream[s], gain_refs[s][...])
        gains_out[pl.ds(s, 1), :] = grad_gain
        if s == 1:
            grad_stream = grads[1, 0].astype(F32) + pulled
            stream[1] = grad_stream
            grads[0, 0] = grad_stream.astype(BF)
        else:
            put_out(1, packing[...], (stream[1] + pulled).astype(BF), ((0,), (0,)))
    send_back()
    pl.semaphore_signal(ready.at[0], inc=1, device_id=to_core, device_id_type=MESH)
    for i in (3, 0, 1, 2):
        attention_weights[i].start()

    def small_step(level, peer):
        return remote(keep.at[level], s_got.at[level], small_send.at[level], small_recv.at[level], peer)

    def gain_step(level, peer):
        return remote(keep.at[5 + level, pl.ds(0, 8)], g_got.at[level], gain_send.at[level], gain_recv.at[level], peer)

    keep[5, pl.ds(0, 8)] = gains_out[...]
    gain_step(0, to_low).start()

    ring(0, 3).wait_recv()
    cur_load(3).start()
    far_arrive(1)
    collect(1)
    far_arrive(2)
    advance(1, 2)
    ring(2, 1).start()
    relay(3)
    collect(2)
    get_result()
    returned = dot(dispatch[0], inbox[1, 0].reshape(experts * slots, wide), ((0,), (0,)))
    block_out[...] = (live * (gating * returned + (1.0 - gating) * hidden[...])).astype(BF)
    grad_block = live * cotangent[...].astype(F32)
    grad_score = jnp.sum(grad_block * (returned - hidden[...]), axis=-1, keepdims=True) * gating * (1.0 - gating)
    grad_hidden = stream.at[0, pl.ds(0, count)]
    own = select_rows(chosen, cents[...], ((0,), (0,)))
    grad_hidden[...] = (1.0 - gating) * grad_block + grad_score * own
    keep[0, pl.ds(8, experts)] = select_rows(chosen, grad_score * hidden[...], ((1,), (0,)))
    turned_low = turned.at[:, pl.ds(0, count)]
    turned_low[...] = mixed[...].T
    grad_low = cur
    get_back()
    grad_hidden[...] += dot(dispatch[0], inbox[1, 1].reshape(experts * slots, wide), ((0,), (0,)))
    grad_low[...] = grad_hidden[...].astype(BF)
    attention_weights[3].wait()
    grad_mixed = dot(grad_low[...], w_held[3], ((1,), (1,))).astype(BF)
    dense_product(dense, 3, turned_low, grad_low)
    turned_low[...] = normed[...].T
    grad_low[...] = grad_mixed
    grad_three = [outbox.at[pl.ds(i * count, count)] for i in range(3)]
    lax.fori_loop(
        0, wide // 128, functools.partial(backward_pair, allowed, queries, keys, values, grad_low, grad_three), 0
    )

    def one_product(i, carry):
        dense_product(dense, i, turned_low, outbox.at[pl.ds(pl.multiple_of(i * count, 16), count)])
        return carry

    lax.fori_loop(0, 3, one_product, 0)
    for i in range(3):
        attention_weights[i].wait()
    grad_normed = sum(dot(grad_three[i][...], w_held[i], ((1,), (1,))) for i in range(3))
    pulled, grad_gain = norm_pull(grad_normed, tokens[...].astype(F32), gain[...])
    grad_tokens[...] = grad_hidden[...] + pulled
    keep[0, pl.ds(0, 8)] = jnp.broadcast_to(grad_gain, (8, wide))

    def rows_at(start, size):
        return pl.ds(pl.multiple_of(start, 32), size)

    def level_copies(level):
        copies = []
        for m in range(4):
            mine, theirs = dense.at[core, m], dense.at[other, m]
            if level == 0:
                parts = ((theirs, slopes.at[pl.ds(m * 512, 512)], to_core),)
            elif level == 1 and m < 2:
                parts = ((mine.at[rows_at((1 - x) * 256, 256)], theirs.at[pl.ds(0, 256)], to_x),)
            elif level == 1:
                parts = tuple(
                    (mine.at[rows_at(xx * 256 + (1 - y) * 128, 128)], theirs.at[pl.ds(xx * 128, 128)], to_y)
                    for xx in range(2)
                )
            elif level == 2 and m < 2:
                parts = ((mine.at[rows_at(x * 256 + (1 - y) * 128, 128)], theirs.at[pl.ds(256, 128)], to_y),)
            elif level == 2:
                parts = ((mine.at[rows_at((1 - x) * 256 + y * 128, 128)], theirs.at[pl.ds(256, 128)], to_x),)
            elif level == 3:
                start = x * 256 + y * 128 + (1 - b0) * 64
                parts = ((mine.at[rows_at(start, 64)], theirs.at[pl.ds(384, 64)], to_low),)
            else:
                start = x * 256 + y * 128 + b0 * 64 + (1 - b1) * 32
                parts = ((mine.at[rows_at(start, 32)], theirs.at[pl.ds(448, 32)], to_high),)
            for n, (src, dst, peer) in enumerate(parts):
                copies.append(remote(src, dst, dense_send.at[level, m, n], dense_recv.at[level, m, n], peer))
        return copies

    small_peers = (to_core, to_x, to_y, to_low, to_high)

    def begin(level):
        for sem in {0: (0,), 1: (1, 2), 2: (), 3: (3,), 4: (4,)}[level]:
            pl.semaphore_wait(ready.at[sem], 1)
        for copy in level_copies(level):
            copy.start()
        small_step(level, small_peers[level]).start()

    def add_rows(m, start, size, got):
        where = rows_at(start, size)
        dense[core, m, where, :] += got

    def end(level):
        for copy in level_copies(level):
            copy.wait()
        small_step(level, small_peers[level]).wait()
        if level < 4:
            keep[level + 1] = keep[level] + s_got[level]
        for m in range(4):
            if level == 0:
                for h in range(2):
                    add_rows(m, h * 256, 256, slopes[m * 512 + h * 256:m * 512 + h * 256 + 256])
            elif level == 1 and m < 2:
                add_rows(m, x * 256, 256, dense[other, m, 0:256])
            elif level == 1:
                for xx in range(2):
                    add_rows(m, xx * 256 + y * 128, 128, dense[other, m, xx * 128:xx * 128 + 128])
            elif level == 2:
                add_rows(m, x * 256 + y * 128, 128, dense[other, m, 256:384])
            elif level == 3:
                add_rows(m, x * 256 + y * 128 + b0 * 64, 64, dense[other, m, 384:448])
            else:
                where = rows_at(x * 256 + y * 128 + b0 * 64 + b1 * 32, 32)
                dense_out[m] = dense[core, m, where, :].astype(F32) + dense[other, m, 448:480].astype(F32)
        if level == 0:
            for sem, peer in enumerate(small_peers[1:], 1):
                pl.semaphore_signal(ready.at[sem], inc=1, device_id=peer, device_id_type=MESH)
        if level == 4:
            small_out[...] = keep[4] + s_got[4]

    begin(0)
    far_arrive(3)
    advance(1, 3)
    advance(2, 2)
    collect(3)
    gain_step(0, to_low).wait()
    keep[6, pl.ds(0, 8)] = keep[5, pl.ds(0, 8)] + g_got[0]
    gain_step(1, to_high).start()
    for copy in fetch(0, 0, 0):
        copy.start()
    for k in range(1, groups):
        routed = norms[1, k].astype(F32)
        stream[k - 1] = routed
        norms[0, k] = (norm_parts(routed)[0] * gain_first[...]).astype(BF)

    def forward_others(c, slot):
        def one_group(k, carry):
            mid = gelu_pair(dot(norms[0, k + 1], w_held[slot]))[0].astype(BF)
            stream[k] += dot(mid, w_held[2 + slot])
            return carry

        lax.fori_loop(0, groups - 1, one_group, 0)

        @pl.when(c == 1)
        def _():
            end(0)
            begin(1)

    stream_tiles(0, None, forward_others)
    col = pl.multiple_of(b * width, width)
    shards = []
    for i, s in enumerate((1, 0)):
        shards.append((
            pltpu.make_async_copy(ups[s].at[0, :, pl.ds(col, width)], w_held.at[2 * i], w_sems.at[2 * i]),
            pltpu.make_async_copy(downs[s].at[0, pl.ds(col, width), :], w_held.at[2 * i + 1], w_sems.at[2 * i + 1]),
        ))
    for pair in shards:
        for copy in pair:
            copy.start()
    for k in range(1, groups):
        norms[1, k] = (norm_parts(stream[k - 1])[0] * gain_second[...]).astype(BF)
    gain_step(1, to_high).wait()
    gains_out[...] = keep[6, pl.ds(0, 8)] + g_got[1]

    quarter = wide // 4
    every = groups * many

    def down_stage(slot):
        return outbox.at[pl.ds(pl.multiple_of(slot * quarter, 16), quarter)]

    def stage_copies(s, c, slot):
        cols = pl.ds(pl.multiple_of(c * quarter, quarter), quarter)
        return (
            pltpu.make_async_copy(down_stage(slot), (down_one, down_two)[s].at[0, cols], out_sem.at[slot, 0]),
            pltpu.make_async_copy(up_stage.at[slot], (up_one, up_two)[s].at[0, :, cols], out_sem.at[slot, 1]),
        )

    chunks = width // quarter

    def weight_phase(i, carry):
        s = 1 - i

        def turn(d, carry):
            cols = pl.ds(pl.multiple_of(d * 128, 128), 128)
            turned[cols, :] = norms[s, :, :, cols].reshape(every, 128).T
            return carry

        lax.fori_loop(0, wide // 128, turn, 0)
        for n in range(2):
            @pl.when(i == n)
            def _(n=n):
                for copy in shards[n]:
                    copy.wait()
                if n == 0:
                    ring(1, 3).wait_recv()
                    advance(2, 3)
                else:
                    ring(2, 3).wait_recv()

        def chunk(c, carry):
            cols = pl.ds(pl.multiple_of(c * quarter, quarter), quarter)

            def one_group(k, carry):
                where = pl.ds(pl.multiple_of(k * 2 * many, 16), 2 * many)
                two = pl.ds(2 * k, 2)
                mid, slope = gelu_pair(dot(norms[s, two].reshape(2 * many, wide), w_held[2 * i, :, cols]))
                middles[0, where, :] = mid.astype(BF)
                grad_mid = dot(grads[s, two].reshape(2 * many, wide), w_held[2 * i + 1, cols, :], ((1,), (1,)))
                middles[1, where, :] = (grad_mid * slope).astype(BF)
                return carry

            lax.fori_loop(0, groups // 2, one_group, 0)
            slot = lax.rem(c, 2)

            @pl.when(i * chunks + c > 1)
            def _():
                for copy in stage_copies(0, 0, slot):
                    copy.wait()

            down_stage(slot)[...] = dot(middles[0], grads[s].reshape(every, wide), ((0,), (0,))).astype(BF)
            up_stage[slot] = dot(turned[...], middles[1]).astype(BF)
            for n in range(2):
                @pl.when(s == n)
                def _(n=n):
                    for copy in stage_copies(n, c, slot):
                        copy.start()
            for (at_i, at_c), hook in hooks.items():
                pl.when((i == at_i) & (c == at_c))(hook)
            return carry

        lax.fori_loop(0, chunks, chunk, 0)
        return carry

    def next_level(level):
        def hook():
            end(level)
            begin(level + 1)
        return hook

    hooks = {(0, 0): next_level(1), (0, 3): next_level(2), (1, 1): next_level(3)}
    lax.fori_loop(0, 2, weight_phase, 0)
    end(4)
    for slot in range(2):
        for copy in stage_copies(0, 0, slot):
            copy.wait()
    for t in range(3):
        for j in range(1, groups):
            ring(t, j).wait_send()
    each_peer(lambda p: far(groups - 1, p).wait_send())


def dense_product(dense, which, turned, right):
    block = 32

    def one_batch(g, carry):
        rows = pl.ds(pl.multiple_of(g * 8 * block, 8 * block), 8 * block)
        product = dot(turned[rows, :], right[...]).astype(BF)
        shift = (lax.rem(g, 2) * 2 + g // 2) * block
        for e in range(8):
            place = pl.multiple_of(((e // 2) % 2 * 2 + e // 4) * 4 * block + shift, block)
            dense[e % 2, which, pl.ds(place, block)] = product[e * block:(e + 1) * block]
        return carry

    lax.fori_loop(0, 4, one_batch, 0)


def layer(
    ends, routes_row, tokens, cotangent, gain, cents, gain_first, gain_second, weights, expert_weights, slots, capacity,
):
    count, wide = tokens.shape
    experts, docs, groups = cents.shape[0], ends.shape[1], lax.axis_size("batch")
    many, ff = experts * capacity, expert_weights[0].shape[2]
    width, tiles = ff // groups, ff // wide
    vmem = pl.BlockSpec(memory_space=pltpu.VMEM)
    anys = pl.BlockSpec(memory_space=pl.ANY)
    low_out = jax.ShapeDtypeStruct((1, wide, width), BF)
    dma = pltpu.SemaphoreType.DMA
    return pl.pallas_call(
        functools.partial(layer_kernel, experts, groups, slots, capacity, docs, width, tiles),
        out_shape=(
            jax.ShapeDtypeStruct((count, wide), BF),
            jax.ShapeDtypeStruct((count, wide), F32),
            jax.ShapeDtypeStruct((4, 32, wide), F32),
            jax.ShapeDtypeStruct((8 + experts, wide), F32),
            jax.ShapeDtypeStruct((8, wide), F32),
            low_out, low_out, low_out, low_out,
            jax.ShapeDtypeStruct((groups, count, wide), BF),
            jax.ShapeDtypeStruct((groups, experts, slots, wide), BF),
        ),
        in_specs=[pl.BlockSpec(memory_space=pltpu.SMEM)] + [vmem] * 7 + [anys] * 8,
        out_specs=(vmem,) * 5 + (anys,) * 6,
        scratch_shapes=[
            pltpu.VMEM((4, wide, wide), BF),
            pltpu.VMEM((2 * tiles * many, wide), BF),
            pltpu.VMEM((3, many, wide), F32),
            pltpu.VMEM((2, groups, many, wide), BF),
            pltpu.VMEM((2, groups, many, wide), BF),
            pltpu.VMEM((count, wide), BF),
            pltpu.VMEM((count, wide), BF),
            pltpu.VMEM((5, count, wide), BF),
            pltpu.VMEM((count, wide), F32),
            pltpu.VMEM((groups, experts * slots, count), BF),
            pltpu.VMEM((many, experts * slots), BF),
            pltpu.VMEM((groups, 1, count), jnp.int32),
            pltpu.VMEM((2, 2, experts, slots, wide), BF),
            pltpu.VMEM((max(2 * experts * slots, 3 * count), wide), BF),
            pltpu.VMEM((2, 4, wide // 2, wide), BF),
            pltpu.VMEM((wide, groups * many), BF),
            pltpu.VMEM((2, groups * many, wide // 4), BF),
            pltpu.VMEM((2, wide, wide // 4), BF),
            pltpu.VMEM((7, 16, wide), F32),
            pltpu.VMEM((5, 16, wide), F32),
            pltpu.VMEM((2, 8, wide), F32),
            dma((4,)), dma((2,)), dma((2, 2, experts)), dma((2, 2, experts)), dma((groups, experts)), dma((groups, experts)),
            dma((groups,)), dma((groups,)),
            dma((3, groups)), dma((3, groups)), dma((5, 4, 2)), dma((5, 4, 2)), dma((5,)), dma((5,)),
            dma((2,)), dma((2,)), pltpu.SemaphoreType.REGULAR((5,)), dma((2, 2)),
        ],
        compiler_params=pltpu.CompilerParams(
            collective_id=1, has_side_effects=True, vmem_limit_bytes=64 * 1024 * 1024 - 65536
        ),
        name="layer",
    )(
        ends, routes_row, tokens, cotangent, gain, cents, gain_first, gain_second, *weights, *expert_weights,
    )


def hand_out_kernel(*refs):
    dense, small, gains = refs[:3]
    sources, results = refs[3:9], refs[9:]
    for i, source in enumerate(sources):
        results[i][...] = source[...].astype(results[i].dtype)

    @pl.when(pl.program_id(0) == 0)
    def _():
        for m in range(4):
            results[6 + m][...] = dense[m]
        results[10][...] = small[0:1, :]
        results[11][...] = small[8:, :]
        part = results[12].shape[1]
        where = pl.ds(pl.multiple_of(lax.axis_index("batch") * part, 128), part)
        for s in range(2):
            results[12 + s][...] = gains[s:s + 1, where]


def hand_out(dense, small, gains, *arrays):
    wide, steps = small.shape[1], 4

    def whole(shape):
        return pl.BlockSpec(shape, lambda i: (0,) * len(shape))

    def sliced(array):
        shape = array.shape[:-2] + (array.shape[-2] // steps, array.shape[-1])
        return pl.BlockSpec(shape, lambda i: (0,) * (len(shape) - 2) + (i, 0))

    shapes = [dense.shape[1:]] * 4 + [(1, wide), (small.shape[0] - 8, wide)] + [(1, wide // lax.axis_size("batch"))] * 2
    moved = [sliced(array) for array in arrays]
    return pl.pallas_call(
        hand_out_kernel,
        grid=(steps,),
        out_shape=tuple(jax.ShapeDtypeStruct(array.shape, BF if i == 4 else F32) for i, array in enumerate(arrays))
        + tuple(jax.ShapeDtypeStruct(shape, F32) for shape in shapes),
        in_specs=[whole(array.shape) for array in (dense, small, gains)] + moved,
        out_specs=tuple(moved) + tuple(whole(shape) for shape in shapes),
        compiler_params=pltpu.CompilerParams(vmem_limit_bytes=64 * 1024 * 1024 - 65536),
        name="hand_out",
    )(dense, small, gains, *arrays)


def per_device(
    tokens, doc_ends, routes, w_query, w_key, w_value, w_output, attn_gain, centroids,
    up_first, down_first, gain_first, up_second, down_second, gain_second, cotangent,
):
    count, wide = tokens.shape
    experts, groups = lax.axis_size("expert"), lax.axis_size("batch")
    capacity = 11 * count // (8 * experts)
    slots = -(-capacity // 16) * 16
    routes_row = routes.reshape(1, count)
    gain = attn_gain[None]
    weights = (w_query, w_key, w_value, w_output)
    expert_weights = (up_first, down_first, up_second, down_second)
    if groups == 4 and experts == 8:
        block_out, grad_tokens, dense, small, gains, *parts = layer(
            doc_ends, routes_row, tokens, cotangent, gain, centroids, gain_first, gain_second, weights, expert_weights,
            slots, capacity,
        )
        (
            up_one, down_one, up_two, down_two, block_out, grad_tokens, *dense, small_gain, small_cents, gain_one, gain_two,
        ) = hand_out(dense, small, gains, *parts[:4], block_out, grad_tokens)
        return (
            block_out, grad_tokens, *dense, small_gain.reshape(wide), small_cents,
            up_one, down_one, gain_one, up_two, down_two, gain_two,
        )
    *kept, out_rows = enter(doc_ends, routes_row, tokens, cotangent, gain, centroids, weights, slots)

    def exchange(blocks):
        return lax.all_to_all(blocks, "expert", split_axis=1, concat_axis=1, tiled=True)

    came = exchange(out_rows).reshape(2, experts * slots, wide)
    back, rows, gains = chain(came, *expert_weights, gain_first, gain_second, slots, capacity)
    came_back = exchange(back.reshape(out_rows.shape)).reshape(back.shape)
    block_out, grad_tokens, dense, small = leave(
        doc_ends, routes_row, tokens, cotangent, gain, centroids, kept, came_back, weights, slots
    )
    dense = scatter_sum(dense).astype(F32)
    small = all_sum(small)
    parts = []
    for s, (up, down) in enumerate(((up_first, down_first), (up_second, down_second))):
        for part in weight_grads(ring_rows(rows[0, s], "batch"), ring_rows(rows[1, s], "batch"), up[0], down[0]):
            parts.append(part[None])
    gains = jnp.sum(lax.all_gather(gains[:2], "batch"), axis=0)
    gain_part = wide // groups
    gains = lax.dynamic_slice_in_dim(gains, lax.axis_index("batch") * gain_part, gain_part, 1)
    return (
        block_out, grad_tokens, dense[0], dense[1], dense[2], dense[3], small[0], small[8:],
        parts[0], parts[1], gains[0:1], parts[2], parts[3], gains[1:2],
    )


def solution(mesh):
    return jax.shard_map(
        per_device,
        mesh=mesh,
        in_specs=(
            P(("batch", "expert"), None),
            P(("batch", "expert"), None),
            P(("batch", "expert"), None),
            P(),
            P(),
            P(),
            P(),
            P(),
            P(),
            P("expert", None, None),
            P("expert", None, None),
            P("expert", None),
            P("expert", None, None),
            P("expert", None, None),
            P("expert", None),
            P(("batch", "expert"), None),
        ),
        out_specs=(
            P(("batch", "expert"), None),
            P(("batch", "expert"), None),
            P(("batch", "expert"), None),
            P(("batch", "expert"), None),
            P(("batch", "expert"), None),
            P(("batch", "expert"), None),
            P(),
            P(),
            P("expert", None, "batch"),
            P("expert", "batch", None),
            P("expert", "batch"),
            P("expert", None, "batch"),
            P("expert", "batch", None),
            P("expert", "batch"),
        ),
        check_vma=False,
    )
```

```python
import functools
import jax, jax.numpy as jnp
from jax import lax
from jax.experimental import pallas as pl
from jax.experimental.pallas import tpu as pltpu
from jax.sharding import PartitionSpec as P


MESH = pl.DeviceIdType.MESH
BF = jnp.bfloat16
F32 = jnp.float32
GELU_A = 0.7978845608028654
GELU_B = 0.044715


def gelu_pair(v):
    square = v * v
    half = 0.5 * jnp.tanh(v * (GELU_A + GELU_A * GELU_B * square)) + 0.5
    value = v * half
    return value, half + value * ((1.0 - half) * (2.0 * GELU_A + 6.0 * GELU_A * GELU_B * square))


def dot(a, b, dims=((1,), (0,))):
    return lax.dot_general(a, b, (dims, ((), ())), preferred_element_type=F32)


MASKED = -1e30
EPSILON = 1e-05


def split_three(value):
    high = value.astype(BF)
    rest = value - high.astype(F32)
    middle = rest.astype(BF)
    return high, middle, (rest - middle.astype(F32)).astype(BF)


def select_rows(marks, value, dims):
    return sum(dot(marks, term, dims) for term in split_three(value))


def norm_parts(stream):
    average = jnp.mean(stream, axis=-1, keepdims=True)
    centred = stream - average
    variance = jnp.mean(centred * centred, axis=-1, keepdims=True)
    scale = lax.rsqrt(variance + EPSILON)
    return centred * scale, scale


def norm_pull(grad, stream, gain):
    unit, scale = norm_parts(stream)
    inner = grad * gain
    mean_inner = jnp.mean(inner, axis=-1, keepdims=True)
    mean_product = jnp.mean(inner * unit, axis=-1, keepdims=True)
    return scale * (inner - mean_inner - unit * mean_product), jnp.sum(grad * unit, axis=0, keepdims=True)


def route_marks(routes_row, experts, slots):
    count = routes_row.shape[1]
    ids = lax.broadcasted_iota(jnp.int32, (experts, count), 0)
    chosen = (ids == routes_row).astype(F32)
    earlier = lax.broadcasted_iota(jnp.int32, (count, count), 0) <= lax.broadcasted_iota(jnp.int32, (count, count), 1)
    running = dot(chosen.astype(BF), earlier.astype(F32).astype(BF))
    rank = jnp.sum(running * chosen, axis=0, keepdims=True) - 1.0
    place = routes_row * slots + rank.astype(jnp.int32)
    rows = lax.broadcasted_iota(jnp.int32, (experts * slots, count), 0)
    return chosen.astype(BF), (rows == place).astype(F32).astype(BF)


def allowed_pairs(ends, docs, count):
    row = lax.broadcasted_iota(jnp.int32, (count, count), 0)
    col = lax.broadcasted_iota(jnp.int32, (count, count), 1)
    row_segment = jnp.zeros((count, count), jnp.int32)
    col_segment = jnp.zeros((count, count), jnp.int32)
    for d in range(docs):
        row_segment += (row >= ends[0, d]).astype(jnp.int32)
        col_segment += (col >= ends[0, d]).astype(jnp.int32)
    return (row_segment == col_segment) & (col <= row)


def half_marks(half):
    lane = lax.broadcasted_iota(jnp.int32, (1, 128), 1)
    inside = (lane >= 64 * half) & (lane < 64 * half + 64)
    return inside.astype(F32).astype(BF)


def head_shares(query_pair, key_pair, allowed, half):
    raw = dot(query_pair * half_marks(half), key_pair, ((1,), (1,)))
    scores = jnp.where(allowed, raw * 0.125, MASKED)
    raised = jnp.exp(scores - jnp.max(scores, axis=-1, keepdims=True))
    return raised * (1.0 / jnp.sum(raised, axis=-1, keepdims=True))


def join_halves(first, second):
    lane = lax.broadcasted_iota(jnp.int32, first.shape, 1)
    return jnp.where(lane < 64, first, second)


def forward_pair(allowed, queries, keys, values, mixed, j, carry):
    cols = pl.ds(pl.multiple_of(j * 128, 128), 128)
    query_pair, key_pair, value_pair = queries[:, cols], keys[:, cols], values[:, cols]
    halves = [dot(head_shares(query_pair, key_pair, allowed, half).astype(BF), value_pair) for half in range(2)]
    mixed[:, cols] = join_halves(*halves).astype(BF)
    return carry


def enter_kernel(
    experts, slots, docs,
    ends, routes, tokens, cotangent, gain, cents, w_query, w_key, w_value, w_output,
    normed, queries, keys, values, mixed, hidden, out_rows,
    w_held, sems,
):
    copies = [
        pltpu.make_async_copy(w, w_held.at[i], sems.at[i])
        for i, w in enumerate((w_query, w_key, w_value, w_output))
    ]
    for copy in copies:
        copy.start()
    count, wide = tokens.shape
    unit, _ = norm_parts(tokens[...].astype(F32))
    normed[...] = (unit * gain[...]).astype(BF)
    for i, result in enumerate((queries, keys, values)):
        copies[i].wait()
        result[...] = dot(normed[...], w_held[i]).astype(BF)
    allowed = allowed_pairs(ends, docs, count)

    lax.fori_loop(0, wide // 128, functools.partial(forward_pair, allowed, queries, keys, values, mixed), 0)
    copies[3].wait()
    hidden[...] = tokens[...].astype(F32) + dot(mixed[...], w_held[3])
    chosen, dispatch = route_marks(routes[...], experts, slots)
    own = select_rows(chosen, cents[...], ((0,), (0,)))
    gating = jax.nn.sigmoid(jnp.sum(hidden[...] * own, axis=-1, keepdims=True))
    live = (lax.broadcasted_iota(jnp.int32, (count, 1), 0) < ends[0, docs - 1]).astype(F32)
    grad_sent = (gating * (live * cotangent[...].astype(F32))).astype(BF)
    for kind, rows in enumerate((hidden[...].astype(BF), grad_sent)):
        out_rows[kind] = dot(dispatch, rows).astype(BF).reshape(experts, slots, wide)


def enter(ends, routes_row, tokens, cotangent, gain, cents, weights, slots):
    count, wide = tokens.shape
    experts, docs = cents.shape[0], ends.shape[1]
    vmem = pl.BlockSpec(memory_space=pltpu.VMEM)
    anys = pl.BlockSpec(memory_space=pl.ANY)
    low = jax.ShapeDtypeStruct((count, wide), BF)
    return pl.pallas_call(
        functools.partial(enter_kernel, experts, slots, docs),
        out_shape=(low,) * 5 + (
            jax.ShapeDtypeStruct((count, wide), F32),
            jax.ShapeDtypeStruct((2, experts, slots, wide), BF),
        ),
        in_specs=[pl.BlockSpec(memory_space=pltpu.SMEM)] + [vmem] * 5 + [anys] * 4,
        out_specs=(vmem,) * 7,
        scratch_shapes=[pltpu.VMEM((4, wide, wide), BF), pltpu.SemaphoreType.DMA((4,))],
        compiler_params=pltpu.CompilerParams(vmem_limit_bytes=48 * 1024 * 1024),
        name="enter",
    )(ends, routes_row, tokens, cotangent, gain, cents, *weights)


def backward_pair(allowed, queries, keys, values, grad_low, grad_three, j, carry):
    cols = pl.ds(pl.multiple_of(j * 128, 128), 128)
    query_pair, key_pair, value_pair = queries[:, cols], keys[:, cols], values[:, cols]
    grad_pair = grad_low[:, cols]
    parts = []
    for half in range(2):
        shares = head_shares(query_pair, key_pair, allowed, half)
        grad_shares = dot(grad_pair * half_marks(half), value_pair, ((1,), (1,)))
        inner = jnp.sum(shares * grad_shares, axis=-1, keepdims=True)
        raw = (shares * (grad_shares - inner) * 0.125).astype(BF)
        parts.append((
            dot(raw, key_pair),
            dot(raw, query_pair, ((0,), (0,))),
            dot(shares.astype(BF), grad_pair, ((0,), (0,))),
        ))
    for i in range(3):
        grad_three[i][:, cols] = join_halves(parts[0][i], parts[1][i]).astype(BF)
    return carry


def leave_kernel(
    experts, slots, docs,
    ends, routes, tokens, cotangent, gain, cents, normed, queries, keys, values, mixed, hidden, came,
    w_query, w_key, w_value, w_output,
    block_out, grad_tokens, dense, small,
    w_held, grad_low, grad_three, normed_turned, grad_hidden, sems,
):
    copies = [
        pltpu.make_async_copy(w, w_held.at[i], sems.at[i])
        for i, w in enumerate((w_query, w_key, w_value, w_output))
    ]
    for i in (3, 0, 1, 2):
        copies[i].start()
    count, wide = tokens.shape
    chosen, dispatch = route_marks(routes[...], experts, slots)
    own = select_rows(chosen, cents[...], ((0,), (0,)))
    gating = jax.nn.sigmoid(jnp.sum(hidden[...] * own, axis=-1, keepdims=True))
    live = (lax.broadcasted_iota(jnp.int32, (count, 1), 0) < ends[0, docs - 1]).astype(F32)
    returned = dot(dispatch, came[0], ((0,), (0,)))
    block_out[...] = (live * (gating * returned + (1.0 - gating) * hidden[...])).astype(BF)
    grad_block = live * cotangent[...].astype(F32)
    grad_score = jnp.sum(grad_block * (returned - hidden[...]), axis=-1, keepdims=True) * gating * (1.0 - gating)
    grad_hidden[...] = (1.0 - gating) * grad_block + dot(dispatch, came[1], ((0,), (0,))) + grad_score * own
    small[pl.ds(8, experts), :] = select_rows(chosen, grad_score * hidden[...], ((1,), (0,)))
    grad_low[...] = grad_hidden[...].astype(BF)
    copies[3].wait()
    grad_mixed = dot(grad_low[...], w_held[3], ((1,), (1,))).astype(BF)
    dense[3] = dot(mixed[...].T, grad_low[...]).astype(BF)
    grad_low[...] = grad_mixed
    allowed = allowed_pairs(ends, docs, count)

    lax.fori_loop(
        0, wide // 128, functools.partial(
            backward_pair, allowed, queries, keys, values, grad_low, [grad_three.at[i] for i in range(3)]
        ), 0
    )
    normed_turned[...] = normed[...].T
    for i in range(3):
        dense[i] = dot(normed_turned[...], grad_three[i]).astype(BF)
    for i in range(3):
        copies[i].wait()
    grad_normed = sum(dot(grad_three[i], w_held[i], ((1,), (1,))) for i in range(3))
    pulled, grad_gain = norm_pull(grad_normed, tokens[...].astype(F32), gain[...])
    grad_tokens[...] = grad_hidden[...] + pulled
    small[pl.ds(0, 8), :] = jnp.broadcast_to(grad_gain, (8, wide))


def leave(ends, routes_row, tokens, cotangent, gain, cents, kept, came, weights, slots):
    count, wide = tokens.shape
    experts, docs = cents.shape[0], ends.shape[1]
    vmem = pl.BlockSpec(memory_space=pltpu.VMEM)
    anys = pl.BlockSpec(memory_space=pl.ANY)
    return pl.pallas_call(
        functools.partial(leave_kernel, experts, slots, docs),
        out_shape=(
            jax.ShapeDtypeStruct((count, wide), BF),
            jax.ShapeDtypeStruct((count, wide), F32),
            jax.ShapeDtypeStruct((4, wide, wide), BF),
            jax.ShapeDtypeStruct((8 + experts, wide), F32),
        ),
        in_specs=[pl.BlockSpec(memory_space=pltpu.SMEM)] + [vmem] * 12 + [anys] * 4,
        out_specs=(vmem,) * 4,
        scratch_shapes=[
            pltpu.VMEM((4, wide, wide), BF),
            pltpu.VMEM((count, wide), BF),
            pltpu.VMEM((3, count, wide), BF),
            pltpu.VMEM((wide, count), BF),
            pltpu.VMEM((count, wide), F32),
            pltpu.SemaphoreType.DMA((4,)),
        ],
        compiler_params=pltpu.CompilerParams(vmem_limit_bytes=56 * 1024 * 1024),
        name="leave",
    )(ends, routes_row, tokens, cotangent, gain, cents, *kept, came, *weights)


def pack_marks(experts, slots, capacity):
    shape = (experts * capacity, experts * slots)
    row = lax.broadcasted_iota(jnp.int32, (shape[0], 1), 0)
    block = sum((row >= s * capacity).astype(jnp.int32) for s in range(1, experts))
    column = lax.broadcasted_iota(jnp.int32, shape, 1)
    return (column == row + (slots - capacity) * block).astype(F32).astype(BF)


def chain_kernel(
    experts, slots, capacity, tiles,
    came, up_first, down_first, up_second, down_second, gain_first, gain_second,
    back, rows, gains,
    up_tile, down_tile, pre, stream, total, sems,
):
    tile = up_tile.shape[2]
    ups, downs = (up_first, up_second), (down_first, down_second)
    gain_refs = (gain_first, gain_second)

    def fetch(s, c, slot):
        cols = pl.ds(pl.multiple_of(c * tile, tile), tile)
        return (
            pltpu.make_async_copy(ups[s].at[0, :, cols], up_tile.at[slot], sems.at[0, slot]),
            pltpu.make_async_copy(downs[s].at[0, cols, :], down_tile.at[slot], sems.at[1, slot]),
        )

    order = ((0, True), (1, True), (1, False), (0, False))

    def run(phase, body):
        s = order[phase][0]

        def step(c, carry):
            slot = lax.rem(c, 2)
            for copy in fetch(s, c, slot):
                copy.wait()

            @pl.when(c + 1 < tiles)
            def _():
                for copy in fetch(s, c + 1, 1 - slot):
                    copy.start()

            if phase < 3:
                @pl.when(c + 1 == tiles)
                def _():
                    for copy in fetch(order[phase + 1][0], 0, 1 - slot):
                        copy.start()

            body(s, pl.ds(pl.multiple_of(c * tile, tile), tile), slot)
            return carry

        lax.fori_loop(0, tiles, step, 0)

    for copy in fetch(0, 0, 0):
        copy.start()
    gains[...] = jnp.zeros_like(gains)
    packing = pack_marks(experts, slots, capacity)
    stream[0] = dot(packing, came[0])
    rows[1, 1] = dot(packing, came[1]).astype(BF)

    def forward(s, cols, slot):
        made = dot(rows[0, s], up_tile[slot])
        pre[s, :, cols] = made
        mid = gelu_pair(made)[0].astype(BF)
        total[...] += dot(mid, down_tile[slot])

    def backward(s, cols, slot):
        grad_mid = dot(rows[1, s], down_tile[slot], ((1,), (1,)))
        grad_pre = (gelu_pair(pre[s, :, cols])[1] * grad_mid).astype(BF)
        total[...] += dot(grad_pre, up_tile[slot], ((1,), (1,)))

    for s in range(2):
        unit, _ = norm_parts(stream[s])
        rows[0, s] = (unit * gain_refs[s][...]).astype(BF)
        total[...] = stream[s]
        run(s, forward)
        if s == 0:
            stream[1] = total[...]
    back[0] = dot(packing, total[...].astype(BF), ((0,), (0,))).astype(BF)

    for phase, s in ((2, 1), (3, 0)):
        total[...] = jnp.zeros_like(total)
        run(phase, backward)
        pulled, grad_gain = norm_pull(total[...], stream[s], gain_refs[s][...])
        gains[pl.ds(s, 1), :] = grad_gain
        if s == 1:
            grad_stream = rows[1, 1].astype(F32) + pulled
            stream[1] = grad_stream
            rows[1, 0] = grad_stream.astype(BF)
        else:
            grad_rows = (stream[1] + pulled).astype(BF)
            back[1] = dot(packing, grad_rows, ((0,), (0,))).astype(BF)


def chain(came, up_first, down_first, up_second, down_second, gain_first, gain_second, slots, capacity):
    wide, hidden = up_first.shape[1:]
    experts = came.shape[1] // slots
    count = experts * capacity
    tile = 1024
    vmem = pl.BlockSpec(memory_space=pltpu.VMEM)
    anys = pl.BlockSpec(memory_space=pl.ANY)
    return pl.pallas_call(
        functools.partial(chain_kernel, experts, slots, capacity, hidden // tile),
        out_shape=(
            jax.ShapeDtypeStruct(came.shape, BF),
            jax.ShapeDtypeStruct((2, 2, count, wide), BF),
            jax.ShapeDtypeStruct((8, wide), F32),
        ),
        in_specs=[vmem] + [anys] * 4 + [vmem] * 2,
        out_specs=(vmem,) * 3,
        scratch_shapes=[
            pltpu.VMEM((2, wide, tile), BF),
            pltpu.VMEM((2, tile, wide), BF),
            pltpu.VMEM((2, count, hidden), F32),
            pltpu.VMEM((2, count, wide), F32),
            pltpu.VMEM((count, wide), F32),
            pltpu.SemaphoreType.DMA((2, 2)),
        ],
        compiler_params=pltpu.CompilerParams(vmem_limit_bytes=56 * 1024 * 1024),
        name="chain",
    )(came, up_first, down_first, up_second, down_second, gain_first, gain_second)


def ring_rows(rows, axis):
    count = lax.axis_size(axis)
    back = [(i, (i - 1) % count) for i in range(count)]
    held = [rows]
    for _ in range(count - 1):
        held.append(lax.ppermute(held[-1], axis, back))
    return jnp.concatenate(held, axis=0)


def weight_grads(normed_rows, grad_rows, up_proj, down_proj):
    count = lax.axis_size("batch")
    width = up_proj.shape[1] // count
    first = lax.axis_index("batch") * width
    up_part = lax.dynamic_slice_in_dim(up_proj, first, width, 1)
    down_part = lax.dynamic_slice_in_dim(down_proj, first, width, 0)
    pre_act = jnp.dot(normed_rows, up_part, preferred_element_type=jnp.float32)
    middle, gelu_pull = jax.vjp(jax.nn.gelu, pre_act)
    grad_middle = jnp.einsum("rd,fd->rf", grad_rows, down_part, preferred_element_type=jnp.float32)
    grad_pre = gelu_pull(grad_middle)[0].astype(jnp.bfloat16)
    grad_down = jnp.einsum(
        "rf,rd->fd", middle.astype(jnp.bfloat16), grad_rows, preferred_element_type=jnp.float32
    )
    grad_up = jnp.einsum("rd,rf->df", normed_rows, grad_pre, preferred_element_type=jnp.float32)
    return grad_up, grad_down


def halve(blocks, axis, bit, dim):
    count = lax.axis_size(axis)
    mine = (lax.axis_index(axis) // bit) % 2
    kept = lax.dynamic_index_in_dim(blocks, mine, dim, keepdims=False)
    sent = lax.dynamic_index_in_dim(blocks, 1 - mine, dim, keepdims=False)
    got = lax.ppermute(sent, axis, [(i, i ^ bit) for i in range(count)])
    return (kept.astype(jnp.float32) + got.astype(jnp.float32)).astype(blocks.dtype)


def scatter_sum(parts):
    experts, groups = lax.axis_size("expert"), lax.axis_size("batch")
    kinds, rows, width = parts.shape
    bits_e = experts.bit_length() - 1
    bits_b = groups.bit_length() - 1
    shape = (kinds,) + (2,) * (bits_b + bits_e) + (rows // (experts * groups), width)
    blocks = parts.reshape(shape)
    for k in range(bits_e):
        blocks = halve(blocks, "expert", 1 << k, bits_b + bits_e - k)
    for k in range(bits_b):
        blocks = halve(blocks, "batch", 1 << k, bits_b - k)
    return blocks


def all_sum(value):
    for axis in ("expert", "batch"):
        count = lax.axis_size(axis)
        bit = 1
        while bit < count:
            value = value + lax.ppermute(value, axis, [(i, i ^ bit) for i in range(count)])
            bit *= 2
    return value


def layer_kernel(
    experts, groups, slots, capacity, docs, width, tiles,
    ends, routes, tokens, cotangent, gain, cents, gain_first, gain_second,
    w_query, w_key, w_value, w_output, up_first, down_first, up_second, down_second,
    block_out, grad_tokens, dense_out, small_out, gains_out, up_one, down_one, up_two, down_two, ring_held, far_inbox,
    w_held, slopes, stream, norms, grads, cur, token_low, attention, hidden, dispatch, packing, routes_held, inbox, outbox, dense, turned, middles, up_stage,
    keep, s_got, g_got,
    w_sems, row_sem, a2a_send, a2a_recv, far_send, far_recv, route_send, route_recv, ring_send, ring_recv, dense_send, dense_recv, small_send, small_recv,
    gain_send, gain_recv, ready, out_sem,
):
    b, e = lax.axis_index("batch"), lax.axis_index("expert")
    count, wide = tokens.shape
    many = experts * capacity
    before, after = lax.rem(b + groups - 1, groups), lax.rem(b + 1, groups)
    core, x, y = lax.rem(e, 2), lax.rem(e // 2, 2), lax.rem(e // 4, 2)
    b0, b1 = lax.rem(b, 2), lax.rem(b // 2, 2)
    other = 1 - core
    to_core, to_x, to_y = (b, e + 1 - 2 * core), (b, e + 2 - 4 * x), (b, e + 4 - 8 * y)
    to_low, to_high = (b + 1 - 2 * b0, e), (b + 2 - 4 * b1, e)

    def remote(src, dst, send, recv, peer):
        return pltpu.make_async_remote_copy(
            src_ref=src, dst_ref=dst, send_sem=send, recv_sem=recv, device_id=peer, device_id_type=MESH
        )

    barrier = pltpu.get_barrier_semaphore()

    def greet(p, carry):
        peer = (b, lax.rem(e + p, experts))
        pl.semaphore_signal(barrier, inc=1, device_id=peer, device_id_type=MESH)
        return carry

    lax.fori_loop(1, experts, greet, 0)
    for peer in ((before, e), (after, e), to_high):
        pl.semaphore_signal(barrier, inc=1, device_id=peer, device_id_type=MESH)

    tile = wide
    ups, downs = (up_first, up_second), (down_first, down_second)
    gain_refs = (gain_first, gain_second)

    def fetch(s, c, slot):
        cols = pl.ds(pl.multiple_of(c * tile, tile), tile)
        return (
            pltpu.make_async_copy(ups[s].at[0, :, cols], w_held.at[slot], w_sems.at[slot]),
            pltpu.make_async_copy(downs[s].at[0, cols, :], w_held.at[2 + slot], w_sems.at[2 + slot]),
        )

    def stream_tiles(s, follow, body):
        def step(c, carry):
            slot = lax.rem(c, 2)
            for copy in fetch(s, c, slot):
                copy.wait()

            @pl.when(c + 1 < tiles)
            def _():
                for copy in fetch(s, c + 1, 1 - slot):
                    copy.start()

            if follow is not None:
                @pl.when(c + 1 == tiles)
                def _():
                    for copy in fetch(follow, 0, 1 - slot):
                        copy.start()

            body(c, slot)
            return carry

        lax.fori_loop(0, tiles, step, 0)

    def exchange(phase, kind, block):
        def copy(p):
            target = lax.rem(e + p, experts)
            return remote(
                block(target), inbox.at[phase, kind, e],
                a2a_send.at[phase, kind, p], a2a_recv.at[phase, kind, p], (b, target),
            )
        own = pltpu.make_async_copy(block(e), inbox.at[phase, kind, e], a2a_recv.at[phase, kind, 0])

        def start():
            own.start()
            lax.fori_loop(1, experts, lambda p, carry: (copy(p).start(), carry)[1], 0)

        def wait():
            own.wait()
            lax.fori_loop(1, experts, lambda p, carry: (copy(p).wait(), carry)[1], 0)

        return start, wait


    def ring(t, j):
        if t == 0:
            source, target = token_low if j == 1 else ring_held.at[j - 1], ring_held.at[j]
        else:
            source, target = grads.at[2 - t, j - 1], grads.at[2 - t, j]
        return remote(source, target, ring_send.at[t, j], ring_recv.at[t, j], (before, e))

    def advance(t, j):
        ring(t, j - 1).wait_recv()
        ring(t, j).start()

    def far(k, p):
        target = lax.rem(e + p, experts)
        return remote(
            inbox.at[0, 0, target], far_inbox.at[k, e], far_send.at[k, p], far_recv.at[k, p], (b, target)
        )

    def far_own(k):
        return pltpu.make_async_copy(inbox.at[0, 0, e], far_inbox.at[k, e], far_recv.at[k, 0])

    def each_peer(act):
        lax.fori_loop(1, experts, lambda p, carry: (act(p), carry)[1], 0)

    def cur_load(k):
        return pltpu.make_async_copy(ring_held.at[k], cur, row_sem.at[0])

    def far_load(k):
        return pltpu.make_async_copy(far_inbox.at[k], inbox.at[0, 1], row_sem.at[1])

    def relay(k):
        if k > 1:
            each_peer(lambda p: far(k - 1, p).wait_send())
        if k == 2:
            far_own(1).wait()
        cur_load(k).wait()
        inbox[0, 0] = dot(dispatch[k], cur[...]).astype(BF).reshape(experts, slots, wide)
        far_own(k).start()
        each_peer(lambda p: far(k, p).start())

    def far_arrive(k):
        if k > 1:
            far_own(k).wait()
        each_peer(lambda p: far(k, p).wait_recv())
        far_load(k).start()

    def collect(k):
        far_load(k).wait()
        norms[1, k] = dot(packing[...], inbox[0, 1].reshape(experts * slots, wide)).astype(BF)

    def route_copy(j):
        return remote(
            routes, routes_held.at[j], route_send.at[j], route_recv.at[j],
            (lax.rem(b + groups - j, groups), e),
        )

    attention_weights = [
        pltpu.make_async_copy(w, w_held.at[i], w_sems.at[i])
        for i, w in enumerate((w_query, w_key, w_value, w_output))
    ]
    for copy in attention_weights:
        copy.start()
    def out_block(kind, p):
        return outbox.at[pl.ds(pl.multiple_of((kind * experts + p) * slots, 16), slots)]

    def put_out(kind, marks, value, dims):
        start = kind * experts * slots
        outbox[start:start + experts * slots, :] = dot(marks, value, dims).astype(BF)

    send_routed, get_routed = exchange(0, 0, functools.partial(out_block, 0))
    send_grads, get_grads = exchange(0, 1, functools.partial(out_block, 1))
    send_result, get_result = exchange(1, 0, functools.partial(out_block, 0))
    send_back, get_back = exchange(1, 1, functools.partial(out_block, 1))
    chosen, dispatch[0] = route_marks(routes[...], experts, slots)
    packing[...] = pack_marks(experts, slots, capacity)
    gains_out[...] = jnp.zeros_like(gains_out)
    normed, queries, keys, values, mixed = (attention.at[i] for i in range(5))
    normed[...] = (norm_parts(tokens[...].astype(F32))[0] * gain[...]).astype(BF)
    for i, result in enumerate((queries, keys, values)):
        attention_weights[i].wait()
        result[...] = dot(normed[...], w_held[i]).astype(BF)
    for copy in fetch(0, 0, 0):
        copy.start()
    allowed = allowed_pairs(ends, docs, count)
    lax.fori_loop(0, wide // 128, functools.partial(forward_pair, allowed, queries, keys, values, mixed), 0)
    pl.semaphore_wait(barrier, experts + 2)
    for j in range(1, groups):
        route_copy(j).start()
    attention_weights[3].wait()
    hidden[...] = tokens[...].astype(F32) + dot(mixed[...], w_held[3])
    token_low[...] = hidden[...].astype(BF)
    put_out(0, dispatch[0], token_low[...], ((1,), (0,)))
    send_routed()
    ring(0, 1).start()
    own = select_rows(chosen, cents[...], ((0,), (0,)))
    gating = jax.nn.sigmoid(jnp.sum(hidden[...] * own, axis=-1, keepdims=True))
    live = (lax.broadcasted_iota(jnp.int32, (count, 1), 0) < ends[0, docs - 1]).astype(F32)

    put_out(1, dispatch[0], (gating * (live * cotangent[...].astype(F32))).astype(BF), ((1,), (0,)))
    send_grads()
    for j in range(1, groups):
        route_copy(j).wait()
        dispatch[j] = route_marks(routes_held[j], experts, slots)[1]
    get_routed()
    stream[0] = dot(packing[...], inbox[0, 0].reshape(experts * slots, wide))
    advance(0, 2)
    cur_load(1).start()
    total = stream.at[2]

    def slab(s, c):
        return pl.ds(pl.multiple_of((s * tiles + c) * many, 16), many)

    for s in range(2):
        unit, _ = norm_parts(stream[s])
        norms[s, 0] = (unit * gain_refs[s][...]).astype(BF)
        total[...] = stream[s]

        def forward(c, slot, s=s):
            made = dot(norms[s, 0], w_held[slot])
            value, slope = gelu_pair(made)
            slopes[slab(s, c), :] = slope.astype(BF)
            total[...] += dot(value.astype(BF), w_held[2 + slot])
            if s == 1:
                @pl.when(c == tiles // 2)
                def _():
                    advance(0, 3)
                    cur_load(2).start()

        stream_tiles(s, 1, forward)
        if s == 0:
            stream[1] = total[...]
            get_grads()
            grads[1, 0] = dot(packing[...], inbox[0, 1].reshape(experts * slots, wide)).astype(BF)
            ring(1, 1).start()
            relay(1)

    put_out(0, packing[...], total[...].astype(BF), ((0,), (0,)))
    send_result()
    relay(2)
    for s in (1, 0):
        total[...] = jnp.zeros_like(total)

        def backward(c, slot, s=s):
            grad_mid = dot(grads[s, 0], w_held[2 + slot], ((1,), (1,)))
            grad_pre = (slopes[slab(s, c), :].astype(F32) * grad_mid).astype(BF)
            total[...] += dot(grad_pre, w_held[slot], ((1,), (1,)))

        stream_tiles(s, 0 if s == 1 else None, backward)
        pulled, grad_gain = norm_pull(total[...], stream[s], gain_refs[s][...])
        gains_out[pl.ds(s, 1), :] = grad_gain
        if s == 1:
            grad_stream = grads[1, 0].astype(F32) + pulled
            stream[1] = grad_stream
            grads[0, 0] = grad_stream.astype(BF)
        else:
            put_out(1, packing[...], (stream[1] + pulled).astype(BF), ((0,), (0,)))
    send_back()
    pl.semaphore_signal(ready.at[0], inc=1, device_id=to_core, device_id_type=MESH)
    for i in (3, 0, 1, 2):
        attention_weights[i].start()

    def small_step(level, peer):
        return remote(keep.at[level], s_got.at[level], small_send.at[level], small_recv.at[level], peer)

    def gain_step(level, peer):
        return remote(keep.at[5 + level, pl.ds(0, 8)], g_got.at[level], gain_send.at[level], gain_recv.at[level], peer)

    keep[5, pl.ds(0, 8)] = gains_out[...]
    gain_step(0, to_low).start()

    ring(0, 3).wait_recv()
    cur_load(3).start()
    far_arrive(1)
    collect(1)
    far_arrive(2)
    advance(1, 2)
    ring(2, 1).start()
    relay(3)
    collect(2)
    get_result()
    returned = dot(dispatch[0], inbox[1, 0].reshape(experts * slots, wide), ((0,), (0,)))
    block_out[...] = (live * (gating * returned + (1.0 - gating) * hidden[...])).astype(BF)
    grad_block = live * cotangent[...].astype(F32)
    grad_score = jnp.sum(grad_block * (returned - hidden[...]), axis=-1, keepdims=True) * gating * (1.0 - gating)
    grad_hidden = stream.at[0, pl.ds(0, count)]
    own = select_rows(chosen, cents[...], ((0,), (0,)))
    grad_hidden[...] = (1.0 - gating) * grad_block + grad_score * own
    keep[0, pl.ds(8, experts)] = select_rows(chosen, grad_score * hidden[...], ((1,), (0,)))
    turned_low = turned.at[:, pl.ds(0, count)]
    turned_low[...] = mixed[...].T
    grad_low = cur
    get_back()
    grad_hidden[...] += dot(dispatch[0], inbox[1, 1].reshape(experts * slots, wide), ((0,), (0,)))
    grad_low[...] = grad_hidden[...].astype(BF)
    attention_weights[3].wait()
    grad_mixed = dot(grad_low[...], w_held[3], ((1,), (1,))).astype(BF)
    dense_product(dense, 3, turned_low, grad_low)
    turned_low[...] = normed[...].T
    grad_low[...] = grad_mixed
    grad_three = [outbox.at[pl.ds(i * count, count)] for i in range(3)]
    lax.fori_loop(
        0, wide // 128, functools.partial(backward_pair, allowed, queries, keys, values, grad_low, grad_three), 0
    )

    def one_product(i, carry):
        dense_product(dense, i, turned_low, outbox.at[pl.ds(pl.multiple_of(i * count, 16), count)])
        return carry

    lax.fori_loop(0, 3, one_product, 0)
    for i in range(3):
        attention_weights[i].wait()
    grad_normed = sum(dot(grad_three[i][...], w_held[i], ((1,), (1,))) for i in range(3))
    pulled, grad_gain = norm_pull(grad_normed, tokens[...].astype(F32), gain[...])
    grad_tokens[...] = grad_hidden[...] + pulled
    keep[0, pl.ds(0, 8)] = jnp.broadcast_to(grad_gain, (8, wide))

    def rows_at(start, size):
        return pl.ds(pl.multiple_of(start, 32), size)

    def level_copies(level):
        copies = []
        for m in range(4):
            mine, theirs = dense.at[core, m], dense.at[other, m]
            if level == 0:
                parts = ((theirs, slopes.at[pl.ds(m * 512, 512)], to_core),)
            elif level == 1 and m < 2:
                parts = ((mine.at[rows_at((1 - x) * 256, 256)], theirs.at[pl.ds(0, 256)], to_x),)
            elif level == 1:
                parts = tuple(
                    (mine.at[rows_at(xx * 256 + (1 - y) * 128, 128)], theirs.at[pl.ds(xx * 128, 128)], to_y)
                    for xx in range(2)
                )
            elif level == 2 and m < 2:
                parts = ((mine.at[rows_at(x * 256 + (1 - y) * 128, 128)], theirs.at[pl.ds(256, 128)], to_y),)
            elif level == 2:
                parts = ((mine.at[rows_at((1 - x) * 256 + y * 128, 128)], theirs.at[pl.ds(256, 128)], to_x),)
            elif level == 3:
                start = x * 256 + y * 128 + (1 - b0) * 64
                parts = ((mine.at[rows_at(start, 64)], theirs.at[pl.ds(384, 64)], to_low),)
            else:
                start = x * 256 + y * 128 + b0 * 64 + (1 - b1) * 32
                parts = ((mine.at[rows_at(start, 32)], theirs.at[pl.ds(448, 32)], to_high),)
            for n, (src, dst, peer) in enumerate(parts):
                copies.append(remote(src, dst, dense_send.at[level, m, n], dense_recv.at[level, m, n], peer))
        return copies

    small_peers = (to_core, to_x, to_y, to_low, to_high)

    def begin(level):
        for sem in {0: (0,), 1: (1, 2), 2: (), 3: (3,), 4: (4,)}[level]:
            pl.semaphore_wait(ready.at[sem], 1)
        for copy in level_copies(level):
            copy.start()
        small_step(level, small_peers[level]).start()

    def add_rows(m, start, size, got):
        where = rows_at(start, size)
        dense[core, m, where, :] += got

    def end(level):
        for copy in level_copies(level):
            copy.wait()
        small_step(level, small_peers[level]).wait()
        if level < 4:
            keep[level + 1] = keep[level] + s_got[level]
        for m in range(4):
            if level == 0:
                for h in range(2):
                    add_rows(m, h * 256, 256, slopes[m * 512 + h * 256:m * 512 + h * 256 + 256])
            elif level == 1 and m < 2:
                add_rows(m, x * 256, 256, dense[other, m, 0:256])
            elif level == 1:
                for xx in range(2):
                    add_rows(m, xx * 256 + y * 128, 128, dense[other, m, xx * 128:xx * 128 + 128])
            elif level == 2:
                add_rows(m, x * 256 + y * 128, 128, dense[other, m, 256:384])
            elif level == 3:
                add_rows(m, x * 256 + y * 128 + b0 * 64, 64, dense[other, m, 384:448])
            else:
                where = rows_at(x * 256 + y * 128 + b0 * 64 + b1 * 32, 32)
                dense_out[m] = dense[core, m, where, :].astype(F32) + dense[other, m, 448:480].astype(F32)
        if level == 0:
            for sem, peer in enumerate(small_peers[1:], 1):
                pl.semaphore_signal(ready.at[sem], inc=1, device_id=peer, device_id_type=MESH)
        if level == 4:
            small_out[...] = keep[4] + s_got[4]

    begin(0)
    far_arrive(3)
    advance(1, 3)
    advance(2, 2)
    collect(3)
    gain_step(0, to_low).wait()
    keep[6, pl.ds(0, 8)] = keep[5, pl.ds(0, 8)] + g_got[0]
    gain_step(1, to_high).start()
    for copy in fetch(0, 0, 0):
        copy.start()
    for k in range(1, groups):
        routed = norms[1, k].astype(F32)
        stream[k - 1] = routed
        norms[0, k] = (norm_parts(routed)[0] * gain_first[...]).astype(BF)

    def forward_others(c, slot):
        def one_group(k, carry):
            mid = gelu_pair(dot(norms[0, k + 1], w_held[slot]))[0].astype(BF)
            stream[k] += dot(mid, w_held[2 + slot])
            return carry

        lax.fori_loop(0, groups - 1, one_group, 0)

        @pl.when(c == 1)
        def _():
            end(0)
            begin(1)

    stream_tiles(0, None, forward_others)
    col = pl.multiple_of(b * width, width)
    shards = []
    for i, s in enumerate((1, 0)):
        shards.append((
            pltpu.make_async_copy(ups[s].at[0, :, pl.ds(col, width)], w_held.at[2 * i], w_sems.at[2 * i]),
            pltpu.make_async_copy(downs[s].at[0, pl.ds(col, width), :], w_held.at[2 * i + 1], w_sems.at[2 * i + 1]),
        ))
    for pair in shards:
        for copy in pair:
            copy.start()
    for k in range(1, groups):
        norms[1, k] = (norm_parts(stream[k - 1])[0] * gain_second[...]).astype(BF)
    gain_step(1, to_high).wait()
    gains_out[...] = keep[6, pl.ds(0, 8)] + g_got[1]

    quarter = wide // 4
    every = groups * many

    def down_stage(slot):
        return outbox.at[pl.ds(pl.multiple_of(slot * quarter, 16), quarter)]

    def stage_copies(s, c, slot):
        cols = pl.ds(pl.multiple_of(c * quarter, quarter), quarter)
        return (
            pltpu.make_async_copy(down_stage(slot), (down_one, down_two)[s].at[0, cols], out_sem.at[slot, 0]),
            pltpu.make_async_copy(up_stage.at[slot], (up_one, up_two)[s].at[0, :, cols], out_sem.at[slot, 1]),
        )

    chunks = width // quarter

    def weight_phase(i, carry):
        s = 1 - i

        def turn(d, carry):
            cols = pl.ds(pl.multiple_of(d * 128, 128), 128)
            turned[cols, :] = norms[s, :, :, cols].reshape(every, 128).T
            return carry

        lax.fori_loop(0, wide // 128, turn, 0)
        for n in range(2):
            @pl.when(i == n)
            def _(n=n):
                for copy in shards[n]:
                    copy.wait()
                if n == 0:
                    ring(1, 3).wait_recv()
                    advance(2, 3)
                else:
                    ring(2, 3).wait_recv()

        def chunk(c, carry):
            cols = pl.ds(pl.multiple_of(c * quarter, quarter), quarter)

            def one_group(k, carry):
                where = pl.ds(pl.multiple_of(k * 2 * many, 16), 2 * many)
                two = pl.ds(2 * k, 2)
                mid, slope = gelu_pair(dot(norms[s, two].reshape(2 * many, wide), w_held[2 * i, :, cols]))
                middles[0, where, :] = mid.astype(BF)
                grad_mid = dot(grads[s, two].reshape(2 * many, wide), w_held[2 * i + 1, cols, :], ((1,), (1,)))
                middles[1, where, :] = (grad_mid * slope).astype(BF)
                return carry

            lax.fori_loop(0, groups // 2, one_group, 0)
            slot = lax.rem(c, 2)

            @pl.when(i * chunks + c > 1)
            def _():
                for copy in stage_copies(0, 0, slot):
                    copy.wait()

            down_stage(slot)[...] = dot(middles[0], grads[s].reshape(every, wide), ((0,), (0,))).astype(BF)
            up_stage[slot] = dot(turned[...], middles[1]).astype(BF)
            for n in range(2):
                @pl.when(s == n)
                def _(n=n):
                    for copy in stage_copies(n, c, slot):
                        copy.start()
            for (at_i, at_c), hook in hooks.items():
                pl.when((i == at_i) & (c == at_c))(hook)
            return carry

        lax.fori_loop(0, chunks, chunk, 0)
        return carry

    def next_level(level):
        def hook():
            end(level)
            begin(level + 1)
        return hook

    hooks = {(0, 0): next_level(1), (0, 2): next_level(2), (1, 0): next_level(3)}
    lax.fori_loop(0, 2, weight_phase, 0)
    end(4)
    for slot in range(2):
        for copy in stage_copies(0, 0, slot):
            copy.wait()
    for t in range(3):
        for j in range(1, groups):
            ring(t, j).wait_send()
    each_peer(lambda p: far(groups - 1, p).wait_send())


def dense_product(dense, which, turned, right):
    block = 32

    def one_batch(g, carry):
        rows = pl.ds(pl.multiple_of(g * 8 * block, 8 * block), 8 * block)
        product = dot(turned[rows, :], right[...]).astype(BF)
        shift = (lax.rem(g, 2) * 2 + g // 2) * block
        for e in range(8):
            place = pl.multiple_of(((e // 2) % 2 * 2 + e // 4) * 4 * block + shift, block)
            dense[e % 2, which, pl.ds(place, block)] = product[e * block:(e + 1) * block]
        return carry

    lax.fori_loop(0, 4, one_batch, 0)


def layer(
    ends, routes_row, tokens, cotangent, gain, cents, gain_first, gain_second, weights, expert_weights, slots, capacity,
):
    count, wide = tokens.shape
    experts, docs, groups = cents.shape[0], ends.shape[1], lax.axis_size("batch")
    many, ff = experts * capacity, expert_weights[0].shape[2]
    width, tiles = ff // groups, ff // wide
    vmem = pl.BlockSpec(memory_space=pltpu.VMEM)
    anys = pl.BlockSpec(memory_space=pl.ANY)
    low_out = jax.ShapeDtypeStruct((1, wide, width), BF)
    dma = pltpu.SemaphoreType.DMA
    return pl.pallas_call(
        functools.partial(layer_kernel, experts, groups, slots, capacity, docs, width, tiles),
        out_shape=(
            jax.ShapeDtypeStruct((count, wide), BF),
            jax.ShapeDtypeStruct((count, wide), F32),
            jax.ShapeDtypeStruct((4, 32, wide), F32),
            jax.ShapeDtypeStruct((8 + experts, wide), F32),
            jax.ShapeDtypeStruct((8, wide), F32),
            low_out, low_out, low_out, low_out,
            jax.ShapeDtypeStruct((groups, count, wide), BF),
            jax.ShapeDtypeStruct((groups, experts, slots, wide), BF),
        ),
        in_specs=[pl.BlockSpec(memory_space=pltpu.SMEM)] + [vmem] * 7 + [anys] * 8,
        out_specs=(vmem,) * 5 + (anys,) * 6,
        scratch_shapes=[
            pltpu.VMEM((4, wide, wide), BF),
            pltpu.VMEM((2 * tiles * many, wide), BF),
            pltpu.VMEM((3, many, wide), F32),
            pltpu.VMEM((2, groups, many, wide), BF),
            pltpu.VMEM((2, groups, many, wide), BF),
            pltpu.VMEM((count, wide), BF),
            pltpu.VMEM((count, wide), BF),
            pltpu.VMEM((5, count, wide), BF),
            pltpu.VMEM((count, wide), F32),
            pltpu.VMEM((groups, experts * slots, count), BF),
            pltpu.VMEM((many, experts * slots), BF),
            pltpu.VMEM((groups, 1, count), jnp.int32),
            pltpu.VMEM((2, 2, experts, slots, wide), BF),
            pltpu.VMEM((max(2 * experts * slots, 3 * count), wide), BF),
            pltpu.VMEM((2, 4, wide // 2, wide), BF),
            pltpu.VMEM((wide, groups * many), BF),
            pltpu.VMEM((2, groups * many, wide // 4), BF),
            pltpu.VMEM((2, wide, wide // 4), BF),
            pltpu.VMEM((7, 16, wide), F32),
            pltpu.VMEM((5, 16, wide), F32),
            pltpu.VMEM((2, 8, wide), F32),
            dma((4,)), dma((2,)), dma((2, 2, experts)), dma((2, 2, experts)), dma((groups, experts)), dma((groups, experts)),
            dma((groups,)), dma((groups,)),
            dma((3, groups)), dma((3, groups)), dma((5, 4, 2)), dma((5, 4, 2)), dma((5,)), dma((5,)),
            dma((2,)), dma((2,)), pltpu.SemaphoreType.REGULAR((5,)), dma((2, 2)),
        ],
        compiler_params=pltpu.CompilerParams(
            collective_id=1, has_side_effects=True, vmem_limit_bytes=64 * 1024 * 1024 - 65536
        ),
        name="layer",
    )(
        ends, routes_row, tokens, cotangent, gain, cents, gain_first, gain_second, *weights, *expert_weights,
    )


def hand_out_kernel(*refs):
    dense, small, gains = refs[:3]
    sources, results = refs[3:9], refs[9:]
    for i, source in enumerate(sources):
        results[i][...] = source[...].astype(results[i].dtype)

    @pl.when(pl.program_id(0) == 0)
    def _():
        for m in range(4):
            results[6 + m][...] = dense[m]
        results[10][...] = small[0:1, :]
        results[11][...] = small[8:, :]
        part = results[12].shape[1]
        where = pl.ds(pl.multiple_of(lax.axis_index("batch") * part, 128), part)
        for s in range(2):
            results[12 + s][...] = gains[s:s + 1, where]


def hand_out(dense, small, gains, *arrays):
    wide, steps = small.shape[1], 4

    def whole(shape):
        return pl.BlockSpec(shape, lambda i: (0,) * len(shape))

    def sliced(array):
        shape = array.shape[:-2] + (array.shape[-2] // steps, array.shape[-1])
        return pl.BlockSpec(shape, lambda i: (0,) * (len(shape) - 2) + (i, 0))

    shapes = [dense.shape[1:]] * 4 + [(1, wide), (small.shape[0] - 8, wide)] + [(1, wide // lax.axis_size("batch"))] * 2
    moved = [sliced(array) for array in arrays]
    return pl.pallas_call(
        hand_out_kernel,
        grid=(steps,),
        out_shape=tuple(jax.ShapeDtypeStruct(array.shape, BF if i == 4 else F32) for i, array in enumerate(arrays))
        + tuple(jax.ShapeDtypeStruct(shape, F32) for shape in shapes),
        in_specs=[whole(array.shape) for array in (dense, small, gains)] + moved,
        out_specs=tuple(moved) + tuple(whole(shape) for shape in shapes),
        compiler_params=pltpu.CompilerParams(vmem_limit_bytes=64 * 1024 * 1024 - 65536),
        name="hand_out",
    )(dense, small, gains, *arrays)


def per_device(
    tokens, doc_ends, routes, w_query, w_key, w_value, w_output, attn_gain, centroids,
    up_first, down_first, gain_first, up_second, down_second, gain_second, cotangent,
):
    count, wide = tokens.shape
    experts, groups = lax.axis_size("expert"), lax.axis_size("batch")
    capacity = 11 * count // (8 * experts)
    slots = -(-capacity // 16) * 16
    routes_row = routes.reshape(1, count)
    gain = attn_gain[None]
    weights = (w_query, w_key, w_value, w_output)
    expert_weights = (up_first, down_first, up_second, down_second)
    if groups == 4 and experts == 8:
        block_out, grad_tokens, dense, small, gains, *parts = layer(
            doc_ends, routes_row, tokens, cotangent, gain, centroids, gain_first, gain_second, weights, expert_weights,
            slots, capacity,
        )
        (
            up_one, down_one, up_two, down_two, block_out, grad_tokens, *dense, small_gain, small_cents, gain_one, gain_two,
        ) = hand_out(dense, small, gains, *parts[:4], block_out, grad_tokens)
        return (
            block_out, grad_tokens, *dense, small_gain.reshape(wide), small_cents,
            up_one, down_one, gain_one, up_two, down_two, gain_two,
        )
    *kept, out_rows = enter(doc_ends, routes_row, tokens, cotangent, gain, centroids, weights, slots)

    def exchange(blocks):
        return lax.all_to_all(blocks, "expert", split_axis=1, concat_axis=1, tiled=True)

    came = exchange(out_rows).reshape(2, experts * slots, wide)
    back, rows, gains = chain(came, *expert_weights, gain_first, gain_second, slots, capacity)
    came_back = exchange(back.reshape(out_rows.shape)).reshape(back.shape)
    block_out, grad_tokens, dense, small = leave(
        doc_ends, routes_row, tokens, cotangent, gain, centroids, kept, came_back, weights, slots
    )
    dense = scatter_sum(dense).astype(F32)
    small = all_sum(small)
    parts = []
    for s, (up, down) in enumerate(((up_first, down_first), (up_second, down_second))):
        for part in weight_grads(ring_rows(rows[0, s], "batch"), ring_rows(rows[1, s], "batch"), up[0], down[0]):
            parts.append(part[None])
    gains = jnp.sum(lax.all_gather(gains[:2], "batch"), axis=0)
    gain_part = wide // groups
    gains = lax.dynamic_slice_in_dim(gains, lax.axis_index("batch") * gain_part, gain_part, 1)
    return (
        block_out, grad_tokens, dense[0], dense[1], dense[2], dense[3], small[0], small[8:],
        parts[0], parts[1], gains[0:1], parts[2], parts[3], gains[1:2],
    )


def solution(mesh):
    return jax.shard_map(
        per_device,
        mesh=mesh,
        in_specs=(
            P(("batch", "expert"), None),
            P(("batch", "expert"), None),
            P(("batch", "expert"), None),
            P(),
            P(),
            P(),
            P(),
            P(),
            P(),
            P("expert", None, None),
            P("expert", None, None),
            P("expert", None),
            P("expert", None, None),
            P("expert", None, None),
            P("expert", None),
            P(("batch", "expert"), None),
        ),
        out_specs=(
            P(("batch", "expert"), None),
            P(("batch", "expert"), None),
            P(("batch", "expert"), None),
            P(("batch", "expert"), None),
            P(("batch", "expert"), None),
            P(("batch", "expert"), None),
            P(),
            P(),
            P("expert", None, "batch"),
            P("expert", "batch", None),
            P("expert", "batch"),
            P("expert", None, "batch"),
            P("expert", "batch", None),
            P("expert", "batch"),
        ),
        check_vma=False,
    )
```

```python
import functools
import jax, jax.numpy as jnp
from jax import lax
from jax.experimental import pallas as pl
from jax.experimental.pallas import tpu as pltpu
from jax.sharding import PartitionSpec as P


MESH = pl.DeviceIdType.MESH
BF = jnp.bfloat16
F32 = jnp.float32
GELU_A = 0.7978845608028654
GELU_B = 0.044715


def gelu_pair(v):
    square = v * v
    half = 0.5 * jnp.tanh(v * (GELU_A + GELU_A * GELU_B * square)) + 0.5
    value = v * half
    return value, half + value * ((1.0 - half) * (2.0 * GELU_A + 6.0 * GELU_A * GELU_B * square))


def dot(a, b, dims=((1,), (0,))):
    return lax.dot_general(a, b, (dims, ((), ())), preferred_element_type=F32)


MASKED = -1e30
EPSILON = 1e-05


def split_three(value):
    high = value.astype(BF)
    rest = value - high.astype(F32)
    middle = rest.astype(BF)
    return high, middle, (rest - middle.astype(F32)).astype(BF)


def select_rows(marks, value, dims):
    return sum(dot(marks, term, dims) for term in split_three(value))


def norm_parts(stream):
    average = jnp.mean(stream, axis=-1, keepdims=True)
    centred = stream - average
    variance = jnp.mean(centred * centred, axis=-1, keepdims=True)
    scale = lax.rsqrt(variance + EPSILON)
    return centred * scale, scale


def norm_pull(grad, stream, gain):
    unit, scale = norm_parts(stream)
    inner = grad * gain
    mean_inner = jnp.mean(inner, axis=-1, keepdims=True)
    mean_product = jnp.mean(inner * unit, axis=-1, keepdims=True)
    return scale * (inner - mean_inner - unit * mean_product), jnp.sum(grad * unit, axis=0, keepdims=True)


def route_marks(routes_row, experts, slots):
    count = routes_row.shape[1]
    ids = lax.broadcasted_iota(jnp.int32, (experts, count), 0)
    chosen = (ids == routes_row).astype(F32)
    earlier = lax.broadcasted_iota(jnp.int32, (count, count), 0) <= lax.broadcasted_iota(jnp.int32, (count, count), 1)
    running = dot(chosen.astype(BF), earlier.astype(F32).astype(BF))
    rank = jnp.sum(running * chosen, axis=0, keepdims=True) - 1.0
    place = routes_row * slots + rank.astype(jnp.int32)
    rows = lax.broadcasted_iota(jnp.int32, (experts * slots, count), 0)
    return chosen.astype(BF), (rows == place).astype(F32).astype(BF)


def allowed_pairs(ends, docs, count):
    row = lax.broadcasted_iota(jnp.int32, (count, count), 0)
    col = lax.broadcasted_iota(jnp.int32, (count, count), 1)
    row_segment = jnp.zeros((count, count), jnp.int32)
    col_segment = jnp.zeros((count, count), jnp.int32)
    for d in range(docs):
        row_segment += (row >= ends[0, d]).astype(jnp.int32)
        col_segment += (col >= ends[0, d]).astype(jnp.int32)
    return (row_segment == col_segment) & (col <= row)


def half_marks(half):
    lane = lax.broadcasted_iota(jnp.int32, (1, 128), 1)
    inside = (lane >= 64 * half) & (lane < 64 * half + 64)
    return inside.astype(F32).astype(BF)


def head_shares(query_pair, key_pair, allowed, half):
    raw = dot(query_pair * half_marks(half), key_pair, ((1,), (1,)))
    scores = jnp.where(allowed, raw * 0.125, MASKED)
    raised = jnp.exp(scores - jnp.max(scores, axis=-1, keepdims=True))
    return raised * (1.0 / jnp.sum(raised, axis=-1, keepdims=True))


def join_halves(first, second):
    lane = lax.broadcasted_iota(jnp.int32, first.shape, 1)
    return jnp.where(lane < 64, first, second)


def forward_pair(allowed, queries, keys, values, mixed, j, carry):
    cols = pl.ds(pl.multiple_of(j * 128, 128), 128)
    query_pair, key_pair, value_pair = queries[:, cols], keys[:, cols], values[:, cols]
    halves = [dot(head_shares(query_pair, key_pair, allowed, half).astype(BF), value_pair) for half in range(2)]
    mixed[:, cols] = join_halves(*halves).astype(BF)
    return carry


def enter_kernel(
    experts, slots, docs,
    ends, routes, tokens, cotangent, gain, cents, w_query, w_key, w_value, w_output,
    normed, queries, keys, values, mixed, hidden, out_rows,
    w_held, sems,
):
    copies = [
        pltpu.make_async_copy(w, w_held.at[i], sems.at[i])
        for i, w in enumerate((w_query, w_key, w_value, w_output))
    ]
    for copy in copies:
        copy.start()
    count, wide = tokens.shape
    unit, _ = norm_parts(tokens[...].astype(F32))
    normed[...] = (unit * gain[...]).astype(BF)
    for i, result in enumerate((queries, keys, values)):
        copies[i].wait()
        result[...] = dot(normed[...], w_held[i]).astype(BF)
    allowed = allowed_pairs(ends, docs, count)

    lax.fori_loop(0, wide // 128, functools.partial(forward_pair, allowed, queries, keys, values, mixed), 0)
    copies[3].wait()
    hidden[...] = tokens[...].astype(F32) + dot(mixed[...], w_held[3])
    chosen, dispatch = route_marks(routes[...], experts, slots)
    own = select_rows(chosen, cents[...], ((0,), (0,)))
    gating = jax.nn.sigmoid(jnp.sum(hidden[...] * own, axis=-1, keepdims=True))
    live = (lax.broadcasted_iota(jnp.int32, (count, 1), 0) < ends[0, docs - 1]).astype(F32)
    grad_sent = (gating * (live * cotangent[...].astype(F32))).astype(BF)
    for kind, rows in enumerate((hidden[...].astype(BF), grad_sent)):
        out_rows[kind] = dot(dispatch, rows).astype(BF).reshape(experts, slots, wide)


def enter(ends, routes_row, tokens, cotangent, gain, cents, weights, slots):
    count, wide = tokens.shape
    experts, docs = cents.shape[0], ends.shape[1]
    vmem = pl.BlockSpec(memory_space=pltpu.VMEM)
    anys = pl.BlockSpec(memory_space=pl.ANY)
    low = jax.ShapeDtypeStruct((count, wide), BF)
    return pl.pallas_call(
        functools.partial(enter_kernel, experts, slots, docs),
        out_shape=(low,) * 5 + (
            jax.ShapeDtypeStruct((count, wide), F32),
            jax.ShapeDtypeStruct((2, experts, slots, wide), BF),
        ),
        in_specs=[pl.BlockSpec(memory_space=pltpu.SMEM)] + [vmem] * 5 + [anys] * 4,
        out_specs=(vmem,) * 7,
        scratch_shapes=[pltpu.VMEM((4, wide, wide), BF), pltpu.SemaphoreType.DMA((4,))],
        compiler_params=pltpu.CompilerParams(vmem_limit_bytes=48 * 1024 * 1024),
        name="enter",
    )(ends, routes_row, tokens, cotangent, gain, cents, *weights)


def backward_pair(allowed, queries, keys, values, grad_low, grad_three, j, carry):
    cols = pl.ds(pl.multiple_of(j * 128, 128), 128)
    query_pair, key_pair, value_pair = queries[:, cols], keys[:, cols], values[:, cols]
    grad_pair = grad_low[:, cols]
    parts = []
    for half in range(2):
        shares = head_shares(query_pair, key_pair, allowed, half)
        grad_shares = dot(grad_pair * half_marks(half), value_pair, ((1,), (1,)))
        inner = jnp.sum(shares * grad_shares, axis=-1, keepdims=True)
        raw = (shares * (grad_shares - inner) * 0.125).astype(BF)
        parts.append((
            dot(raw, key_pair),
            dot(raw, query_pair, ((0,), (0,))),
            dot(shares.astype(BF), grad_pair, ((0,), (0,))),
        ))
    for i in range(3):
        grad_three[i][:, cols] = join_halves(parts[0][i], parts[1][i]).astype(BF)
    return carry


def leave_kernel(
    experts, slots, docs,
    ends, routes, tokens, cotangent, gain, cents, normed, queries, keys, values, mixed, hidden, came,
    w_query, w_key, w_value, w_output,
    block_out, grad_tokens, dense, small,
    w_held, grad_low, grad_three, normed_turned, grad_hidden, sems,
):
    copies = [
        pltpu.make_async_copy(w, w_held.at[i], sems.at[i])
        for i, w in enumerate((w_query, w_key, w_value, w_output))
    ]
    for i in (3, 0, 1, 2):
        copies[i].start()
    count, wide = tokens.shape
    chosen, dispatch = route_marks(routes[...], experts, slots)
    own = select_rows(chosen, cents[...], ((0,), (0,)))
    gating = jax.nn.sigmoid(jnp.sum(hidden[...] * own, axis=-1, keepdims=True))
    live = (lax.broadcasted_iota(jnp.int32, (count, 1), 0) < ends[0, docs - 1]).astype(F32)
    returned = dot(dispatch, came[0], ((0,), (0,)))
    block_out[...] = (live * (gating * returned + (1.0 - gating) * hidden[...])).astype(BF)
    grad_block = live * cotangent[...].astype(F32)
    grad_score = jnp.sum(grad_block * (returned - hidden[...]), axis=-1, keepdims=True) * gating * (1.0 - gating)
    grad_hidden[...] = (1.0 - gating) * grad_block + dot(dispatch, came[1], ((0,), (0,))) + grad_score * own
    small[pl.ds(8, experts), :] = select_rows(chosen, grad_score * hidden[...], ((1,), (0,)))
    grad_low[...] = grad_hidden[...].astype(BF)
    copies[3].wait()
    grad_mixed = dot(grad_low[...], w_held[3], ((1,), (1,))).astype(BF)
    dense[3] = dot(mixed[...].T, grad_low[...]).astype(BF)
    grad_low[...] = grad_mixed
    allowed = allowed_pairs(ends, docs, count)

    lax.fori_loop(
        0, wide // 128, functools.partial(
            backward_pair, allowed, queries, keys, values, grad_low, [grad_three.at[i] for i in range(3)]
        ), 0
    )
    normed_turned[...] = normed[...].T
    for i in range(3):
        dense[i] = dot(normed_turned[...], grad_three[i]).astype(BF)
    for i in range(3):
        copies[i].wait()
    grad_normed = sum(dot(grad_three[i], w_held[i], ((1,), (1,))) for i in range(3))
    pulled, grad_gain = norm_pull(grad_normed, tokens[...].astype(F32), gain[...])
    grad_tokens[...] = grad_hidden[...] + pulled
    small[pl.ds(0, 8), :] = jnp.broadcast_to(grad_gain, (8, wide))


def leave(ends, routes_row, tokens, cotangent, gain, cents, kept, came, weights, slots):
    count, wide = tokens.shape
    experts, docs = cents.shape[0], ends.shape[1]
    vmem = pl.BlockSpec(memory_space=pltpu.VMEM)
    anys = pl.BlockSpec(memory_space=pl.ANY)
    return pl.pallas_call(
        functools.partial(leave_kernel, experts, slots, docs),
        out_shape=(
            jax.ShapeDtypeStruct((count, wide), BF),
            jax.ShapeDtypeStruct((count, wide), F32),
            jax.ShapeDtypeStruct((4, wide, wide), BF),
            jax.ShapeDtypeStruct((8 + experts, wide), F32),
        ),
        in_specs=[pl.BlockSpec(memory_space=pltpu.SMEM)] + [vmem] * 12 + [anys] * 4,
        out_specs=(vmem,) * 4,
        scratch_shapes=[
            pltpu.VMEM((4, wide, wide), BF),
            pltpu.VMEM((count, wide), BF),
            pltpu.VMEM((3, count, wide), BF),
            pltpu.VMEM((wide, count), BF),
            pltpu.VMEM((count, wide), F32),
            pltpu.SemaphoreType.DMA((4,)),
        ],
        compiler_params=pltpu.CompilerParams(vmem_limit_bytes=56 * 1024 * 1024),
        name="leave",
    )(ends, routes_row, tokens, cotangent, gain, cents, *kept, came, *weights)


def pack_marks(experts, slots, capacity):
    shape = (experts * capacity, experts * slots)
    row = lax.broadcasted_iota(jnp.int32, (shape[0], 1), 0)
    block = sum((row >= s * capacity).astype(jnp.int32) for s in range(1, experts))
    column = lax.broadcasted_iota(jnp.int32, shape, 1)
    return (column == row + (slots - capacity) * block).astype(F32).astype(BF)


def chain_kernel(
    experts, slots, capacity, tiles,
    came, up_first, down_first, up_second, down_second, gain_first, gain_second,
    back, rows, gains,
    up_tile, down_tile, pre, stream, total, sems,
):
    tile = up_tile.shape[2]
    ups, downs = (up_first, up_second), (down_first, down_second)
    gain_refs = (gain_first, gain_second)

    def fetch(s, c, slot):
        cols = pl.ds(pl.multiple_of(c * tile, tile), tile)
        return (
            pltpu.make_async_copy(ups[s].at[0, :, cols], up_tile.at[slot], sems.at[0, slot]),
            pltpu.make_async_copy(downs[s].at[0, cols, :], down_tile.at[slot], sems.at[1, slot]),
        )

    order = ((0, True), (1, True), (1, False), (0, False))

    def run(phase, body):
        s = order[phase][0]

        def step(c, carry):
            slot = lax.rem(c, 2)
            for copy in fetch(s, c, slot):
                copy.wait()

            @pl.when(c + 1 < tiles)
            def _():
                for copy in fetch(s, c + 1, 1 - slot):
                    copy.start()

            if phase < 3:
                @pl.when(c + 1 == tiles)
                def _():
                    for copy in fetch(order[phase + 1][0], 0, 1 - slot):
                        copy.start()

            body(s, pl.ds(pl.multiple_of(c * tile, tile), tile), slot)
            return carry

        lax.fori_loop(0, tiles, step, 0)

    for copy in fetch(0, 0, 0):
        copy.start()
    gains[...] = jnp.zeros_like(gains)
    packing = pack_marks(experts, slots, capacity)
    stream[0] = dot(packing, came[0])
    rows[1, 1] = dot(packing, came[1]).astype(BF)

    def forward(s, cols, slot):
        made = dot(rows[0, s], up_tile[slot])
        pre[s, :, cols] = made
        mid = gelu_pair(made)[0].astype(BF)
        total[...] += dot(mid, down_tile[slot])

    def backward(s, cols, slot):
        grad_mid = dot(rows[1, s], down_tile[slot], ((1,), (1,)))
        grad_pre = (gelu_pair(pre[s, :, cols])[1] * grad_mid).astype(BF)
        total[...] += dot(grad_pre, up_tile[slot], ((1,), (1,)))

    for s in range(2):
        unit, _ = norm_parts(stream[s])
        rows[0, s] = (unit * gain_refs[s][...]).astype(BF)
        total[...] = stream[s]
        run(s, forward)
        if s == 0:
            stream[1] = total[...]
    back[0] = dot(packing, total[...].astype(BF), ((0,), (0,))).astype(BF)

    for phase, s in ((2, 1), (3, 0)):
        total[...] = jnp.zeros_like(total)
        run(phase, backward)
        pulled, grad_gain = norm_pull(total[...], stream[s], gain_refs[s][...])
        gains[pl.ds(s, 1), :] = grad_gain
        if s == 1:
            grad_stream = rows[1, 1].astype(F32) + pulled
            stream[1] = grad_stream
            rows[1, 0] = grad_stream.astype(BF)
        else:
            grad_rows = (stream[1] + pulled).astype(BF)
            back[1] = dot(packing, grad_rows, ((0,), (0,))).astype(BF)


def chain(came, up_first, down_first, up_second, down_second, gain_first, gain_second, slots, capacity):
    wide, hidden = up_first.shape[1:]
    experts = came.shape[1] // slots
    count = experts * capacity
    tile = 1024
    vmem = pl.BlockSpec(memory_space=pltpu.VMEM)
    anys = pl.BlockSpec(memory_space=pl.ANY)
    return pl.pallas_call(
        functools.partial(chain_kernel, experts, slots, capacity, hidden // tile),
        out_shape=(
            jax.ShapeDtypeStruct(came.shape, BF),
            jax.ShapeDtypeStruct((2, 2, count, wide), BF),
            jax.ShapeDtypeStruct((8, wide), F32),
        ),
        in_specs=[vmem] + [anys] * 4 + [vmem] * 2,
        out_specs=(vmem,) * 3,
        scratch_shapes=[
            pltpu.VMEM((2, wide, tile), BF),
            pltpu.VMEM((2, tile, wide), BF),
            pltpu.VMEM((2, count, hidden), F32),
            pltpu.VMEM((2, count, wide), F32),
            pltpu.VMEM((count, wide), F32),
            pltpu.SemaphoreType.DMA((2, 2)),
        ],
        compiler_params=pltpu.CompilerParams(vmem_limit_bytes=56 * 1024 * 1024),
        name="chain",
    )(came, up_first, down_first, up_second, down_second, gain_first, gain_second)


def ring_rows(rows, axis):
    count = lax.axis_size(axis)
    back = [(i, (i - 1) % count) for i in range(count)]
    held = [rows]
    for _ in range(count - 1):
        held.append(lax.ppermute(held[-1], axis, back))
    return jnp.concatenate(held, axis=0)


def weight_grads(normed_rows, grad_rows, up_proj, down_proj):
    count = lax.axis_size("batch")
    width = up_proj.shape[1] // count
    first = lax.axis_index("batch") * width
    up_part = lax.dynamic_slice_in_dim(up_proj, first, width, 1)
    down_part = lax.dynamic_slice_in_dim(down_proj, first, width, 0)
    pre_act = jnp.dot(normed_rows, up_part, preferred_element_type=jnp.float32)
    middle, gelu_pull = jax.vjp(jax.nn.gelu, pre_act)
    grad_middle = jnp.einsum("rd,fd->rf", grad_rows, down_part, preferred_element_type=jnp.float32)
    grad_pre = gelu_pull(grad_middle)[0].astype(jnp.bfloat16)
    grad_down = jnp.einsum(
        "rf,rd->fd", middle.astype(jnp.bfloat16), grad_rows, preferred_element_type=jnp.float32
    )
    grad_up = jnp.einsum("rd,rf->df", normed_rows, grad_pre, preferred_element_type=jnp.float32)
    return grad_up, grad_down


def halve(blocks, axis, bit, dim):
    count = lax.axis_size(axis)
    mine = (lax.axis_index(axis) // bit) % 2
    kept = lax.dynamic_index_in_dim(blocks, mine, dim, keepdims=False)
    sent = lax.dynamic_index_in_dim(blocks, 1 - mine, dim, keepdims=False)
    got = lax.ppermute(sent, axis, [(i, i ^ bit) for i in range(count)])
    return (kept.astype(jnp.float32) + got.astype(jnp.float32)).astype(blocks.dtype)


def scatter_sum(parts):
    experts, groups = lax.axis_size("expert"), lax.axis_size("batch")
    kinds, rows, width = parts.shape
    bits_e = experts.bit_length() - 1
    bits_b = groups.bit_length() - 1
    shape = (kinds,) + (2,) * (bits_b + bits_e) + (rows // (experts * groups), width)
    blocks = parts.reshape(shape)
    for k in range(bits_e):
        blocks = halve(blocks, "expert", 1 << k, bits_b + bits_e - k)
    for k in range(bits_b):
        blocks = halve(blocks, "batch", 1 << k, bits_b - k)
    return blocks


def all_sum(value):
    for axis in ("expert", "batch"):
        count = lax.axis_size(axis)
        bit = 1
        while bit < count:
            value = value + lax.ppermute(value, axis, [(i, i ^ bit) for i in range(count)])
            bit *= 2
    return value


def layer_kernel(
    experts, groups, slots, capacity, docs, width, tiles,
    ends, routes, tokens, cotangent, gain, cents, gain_first, gain_second,
    w_query, w_key, w_value, w_output, up_first, down_first, up_second, down_second,
    block_out, grad_tokens, dense_out, small_out, gains_out, up_one, down_one, up_two, down_two, ring_held, far_inbox,
    w_held, slopes, stream, norms, grads, cur, token_low, attention, hidden, dispatch, packing, routes_held, inbox, outbox, dense, turned, middles, up_stage,
    keep, s_got, g_got,
    w_sems, row_sem, a2a_send, a2a_recv, far_send, far_recv, route_send, route_recv, ring_send, ring_recv, dense_send, dense_recv, small_send, small_recv,
    gain_send, gain_recv, ready, out_sem,
):
    b, e = lax.axis_index("batch"), lax.axis_index("expert")
    count, wide = tokens.shape
    many = experts * capacity
    before, after = lax.rem(b + groups - 1, groups), lax.rem(b + 1, groups)
    core, x, y = lax.rem(e, 2), lax.rem(e // 2, 2), lax.rem(e // 4, 2)
    b0, b1 = lax.rem(b, 2), lax.rem(b // 2, 2)
    other = 1 - core
    to_core, to_x, to_y = (b, e + 1 - 2 * core), (b, e + 2 - 4 * x), (b, e + 4 - 8 * y)
    to_low, to_high = (b + 1 - 2 * b0, e), (b + 2 - 4 * b1, e)

    def remote(src, dst, send, recv, peer):
        return pltpu.make_async_remote_copy(
            src_ref=src, dst_ref=dst, send_sem=send, recv_sem=recv, device_id=peer, device_id_type=MESH
        )

    barrier = pltpu.get_barrier_semaphore()

    def greet(p, carry):
        peer = (b, lax.rem(e + p, experts))
        pl.semaphore_signal(barrier, inc=1, device_id=peer, device_id_type=MESH)
        return carry

    lax.fori_loop(1, experts, greet, 0)
    for peer in ((before, e), (after, e), to_high):
        pl.semaphore_signal(barrier, inc=1, device_id=peer, device_id_type=MESH)

    tile = wide
    ups, downs = (up_first, up_second), (down_first, down_second)
    gain_refs = (gain_first, gain_second)

    def fetch(s, c, slot):
        cols = pl.ds(pl.multiple_of(c * tile, tile), tile)
        return (
            pltpu.make_async_copy(ups[s].at[0, :, cols], w_held.at[slot], w_sems.at[slot]),
            pltpu.make_async_copy(downs[s].at[0, cols, :], w_held.at[2 + slot], w_sems.at[2 + slot]),
        )

    def stream_tiles(s, follow, body):
        def step(c, carry):
            slot = lax.rem(c, 2)
            for copy in fetch(s, c, slot):
                copy.wait()

            @pl.when(c + 1 < tiles)
            def _():
                for copy in fetch(s, c + 1, 1 - slot):
                    copy.start()

            if follow is not None:
                @pl.when(c + 1 == tiles)
                def _():
                    for copy in fetch(follow, 0, 1 - slot):
                        copy.start()

            body(c, slot)
            return carry

        lax.fori_loop(0, tiles, step, 0)

    def exchange(phase, kind, block):
        def copy(p):
            target = lax.rem(e + p, experts)
            return remote(
                block(target), inbox.at[phase, kind, e],
                a2a_send.at[phase, kind, p], a2a_recv.at[phase, kind, p], (b, target),
            )
        own = pltpu.make_async_copy(block(e), inbox.at[phase, kind, e], a2a_recv.at[phase, kind, 0])

        def start():
            own.start()
            lax.fori_loop(1, experts, lambda p, carry: (copy(p).start(), carry)[1], 0)

        def wait():
            own.wait()
            lax.fori_loop(1, experts, lambda p, carry: (copy(p).wait(), carry)[1], 0)

        return start, wait


    def ring(t, j):
        if t == 0:
            source, target = token_low if j == 1 else ring_held.at[j - 1], ring_held.at[j]
        else:
            source, target = grads.at[2 - t, j - 1], grads.at[2 - t, j]
        return remote(source, target, ring_send.at[t, j], ring_recv.at[t, j], (before, e))

    def advance(t, j):
        ring(t, j - 1).wait_recv()
        ring(t, j).start()

    def far(k, p):
        target = lax.rem(e + p, experts)
        return remote(
            inbox.at[0, 0, target], far_inbox.at[k, e], far_send.at[k, p], far_recv.at[k, p], (b, target)
        )

    def far_own(k):
        return pltpu.make_async_copy(inbox.at[0, 0, e], far_inbox.at[k, e], far_recv.at[k, 0])

    def each_peer(act):
        lax.fori_loop(1, experts, lambda p, carry: (act(p), carry)[1], 0)

    def cur_load(k):
        return pltpu.make_async_copy(ring_held.at[k], cur, row_sem.at[0])

    def far_load(k):
        return pltpu.make_async_copy(far_inbox.at[k], inbox.at[0, 1], row_sem.at[1])

    def relay(k):
        if k > 1:
            each_peer(lambda p: far(k - 1, p).wait_send())
        if k == 2:
            far_own(1).wait()
        cur_load(k).wait()
        inbox[0, 0] = dot(dispatch[k], cur[...]).astype(BF).reshape(experts, slots, wide)
        far_own(k).start()
        each_peer(lambda p: far(k, p).start())

    def far_arrive(k):
        if k > 1:
            far_own(k).wait()
        each_peer(lambda p: far(k, p).wait_recv())
        far_load(k).start()

    def collect(k):
        far_load(k).wait()
        norms[1, k] = dot(packing[...], inbox[0, 1].reshape(experts * slots, wide)).astype(BF)

    def route_copy(j):
        return remote(
            routes, routes_held.at[j], route_send.at[j], route_recv.at[j],
            (lax.rem(b + groups - j, groups), e),
        )

    attention_weights = [
        pltpu.make_async_copy(w, w_held.at[i], w_sems.at[i])
        for i, w in enumerate((w_query, w_key, w_value, w_output))
    ]
    for copy in attention_weights:
        copy.start()
    def out_block(kind, p):
        return outbox.at[pl.ds(pl.multiple_of((kind * experts + p) * slots, 16), slots)]

    def put_out(kind, marks, value, dims):
        start = kind * experts * slots
        outbox[start:start + experts * slots, :] = dot(marks, value, dims).astype(BF)

    send_routed, get_routed = exchange(0, 0, functools.partial(out_block, 0))
    send_grads, get_grads = exchange(0, 1, functools.partial(out_block, 1))
    send_result, get_result = exchange(1, 0, functools.partial(out_block, 0))
    send_back, get_back = exchange(1, 1, functools.partial(out_block, 1))
    chosen, dispatch[0] = route_marks(routes[...], experts, slots)
    packing[...] = pack_marks(experts, slots, capacity)
    gains_out[...] = jnp.zeros_like(gains_out)
    normed, queries, keys, values, mixed = (attention.at[i] for i in range(5))
    normed[...] = (norm_parts(tokens[...].astype(F32))[0] * gain[...]).astype(BF)
    for i, result in enumerate((queries, keys, values)):
        attention_weights[i].wait()
        result[...] = dot(normed[...], w_held[i]).astype(BF)
    for copy in fetch(0, 0, 0):
        copy.start()
    allowed = allowed_pairs(ends, docs, count)
    lax.fori_loop(0, wide // 128, functools.partial(forward_pair, allowed, queries, keys, values, mixed), 0)
    pl.semaphore_wait(barrier, experts + 2)
    for j in range(1, groups):
        route_copy(j).start()
    attention_weights[3].wait()
    hidden[...] = tokens[...].astype(F32) + dot(mixed[...], w_held[3])
    token_low[...] = hidden[...].astype(BF)
    put_out(0, dispatch[0], token_low[...], ((1,), (0,)))
    send_routed()
    ring(0, 1).start()
    own = select_rows(chosen, cents[...], ((0,), (0,)))
    gating = jax.nn.sigmoid(jnp.sum(hidden[...] * own, axis=-1, keepdims=True))
    live = (lax.broadcasted_iota(jnp.int32, (count, 1), 0) < ends[0, docs - 1]).astype(F32)

    put_out(1, dispatch[0], (gating * (live * cotangent[...].astype(F32))).astype(BF), ((1,), (0,)))
    send_grads()
    for j in range(1, groups):
        route_copy(j).wait()
        dispatch[j] = route_marks(routes_held[j], experts, slots)[1]
    get_routed()
    stream[0] = dot(packing[...], inbox[0, 0].reshape(experts * slots, wide))
    advance(0, 2)
    cur_load(1).start()
    total = stream.at[2]

    def slab(s, c):
        return pl.ds(pl.multiple_of((s * tiles + c) * many, 16), many)

    for s in range(2):
        unit, _ = norm_parts(stream[s])
        norms[s, 0] = (unit * gain_refs[s][...]).astype(BF)
        total[...] = stream[s]

        def forward(c, slot, s=s):
            made = dot(norms[s, 0], w_held[slot])
            value, slope = gelu_pair(made)
            slopes[slab(s, c), :] = slope.astype(BF)
            total[...] += dot(value.astype(BF), w_held[2 + slot])
            if s == 1:
                @pl.when(c == tiles // 2)
                def _():
                    advance(0, 3)
                    cur_load(2).start()

        stream_tiles(s, 1, forward)
        if s == 0:
            stream[1] = total[...]
            get_grads()
            grads[1, 0] = dot(packing[...], inbox[0, 1].reshape(experts * slots, wide)).astype(BF)
            ring(1, 1).start()
            relay(1)

    put_out(0, packing[...], total[...].astype(BF), ((0,), (0,)))
    send_result()
    relay(2)
    for s in (1, 0):
        total[...] = jnp.zeros_like(total)

        def backward(c, slot, s=s):
            grad_mid = dot(grads[s, 0], w_held[2 + slot], ((1,), (1,)))
            grad_pre = (slopes[slab(s, c), :].astype(F32) * grad_mid).astype(BF)
            total[...] += dot(grad_pre, w_held[slot], ((1,), (1,)))

        stream_tiles(s, 0 if s == 1 else None, backward)
        pulled, grad_gain = norm_pull(total[...], stream[s], gain_refs[s][...])
        gains_out[pl.ds(s, 1), :] = grad_gain
        if s == 1:
            grad_stream = grads[1, 0].astype(F32) + pulled
            stream[1] = grad_stream
            grads[0, 0] = grad_stream.astype(BF)
        else:
            put_out(1, packing[...], (stream[1] + pulled).astype(BF), ((0,), (0,)))
    send_back()
    pl.semaphore_signal(ready.at[0], inc=1, device_id=to_core, device_id_type=MESH)
    for i in (3, 0, 1, 2):
        attention_weights[i].start()

    def small_step(level, peer):
        return remote(keep.at[level], s_got.at[level], small_send.at[level], small_recv.at[level], peer)

    def gain_step(level, peer):
        return remote(keep.at[5 + level, pl.ds(0, 8)], g_got.at[level], gain_send.at[level], gain_recv.at[level], peer)

    keep[5, pl.ds(0, 8)] = gains_out[...]
    gain_step(0, to_low).start()

    ring(0, 3).wait_recv()
    cur_load(3).start()
    far_arrive(1)
    collect(1)
    far_arrive(2)
    advance(1, 2)
    ring(2, 1).start()
    relay(3)
    collect(2)
    get_result()
    returned = dot(dispatch[0], inbox[1, 0].reshape(experts * slots, wide), ((0,), (0,)))
    block_out[...] = (live * (gating * returned + (1.0 - gating) * hidden[...])).astype(BF)
    grad_block = live * cotangent[...].astype(F32)
    grad_score = jnp.sum(grad_block * (returned - hidden[...]), axis=-1, keepdims=True) * gating * (1.0 - gating)
    grad_hidden = stream.at[0, pl.ds(0, count)]
    own = select_rows(chosen, cents[...], ((0,), (0,)))
    grad_hidden[...] = (1.0 - gating) * grad_block + grad_score * own
    keep[0, pl.ds(8, experts)] = select_rows(chosen, grad_score * hidden[...], ((1,), (0,)))
    turned_low = turned.at[:, pl.ds(0, count)]
    turned_low[...] = mixed[...].T
    grad_low = cur
    get_back()
    grad_hidden[...] += dot(dispatch[0], inbox[1, 1].reshape(experts * slots, wide), ((0,), (0,)))
    grad_low[...] = grad_hidden[...].astype(BF)
    attention_weights[3].wait()
    grad_mixed = dot(grad_low[...], w_held[3], ((1,), (1,))).astype(BF)
    dense_product(dense, 3, turned_low, grad_low)
    turned_low[...] = normed[...].T
    grad_low[...] = grad_mixed
    grad_three = [outbox.at[pl.ds(i * count, count)] for i in range(3)]
    lax.fori_loop(
        0, wide // 128, functools.partial(backward_pair, allowed, queries, keys, values, grad_low, grad_three), 0
    )

    def one_product(i, carry):
        dense_product(dense, i, turned_low, outbox.at[pl.ds(pl.multiple_of(i * count, 16), count)])
        return carry

    lax.fori_loop(0, 3, one_product, 0)
    for i in range(3):
        attention_weights[i].wait()
    grad_normed = sum(dot(grad_three[i][...], w_held[i], ((1,), (1,))) for i in range(3))
    pulled, grad_gain = norm_pull(grad_normed, tokens[...].astype(F32), gain[...])
    grad_tokens[...] = grad_hidden[...] + pulled
    keep[0, pl.ds(0, 8)] = jnp.broadcast_to(grad_gain, (8, wide))

    def rows_at(start, size):
        return pl.ds(pl.multiple_of(start, 32), size)

    def level_copies(level):
        copies = []
        for m in range(4):
            mine, theirs = dense.at[core, m], dense.at[other, m]
            if level == 0:
                parts = ((theirs, slopes.at[pl.ds(m * 512, 512)], to_core),)
            elif level == 1 and m < 2:
                parts = ((mine.at[rows_at((1 - x) * 256, 256)], theirs.at[pl.ds(0, 256)], to_x),)
            elif level == 1:
                parts = tuple(
                    (mine.at[rows_at(xx * 256 + (1 - y) * 128, 128)], theirs.at[pl.ds(xx * 128, 128)], to_y)
                    for xx in range(2)
                )
            elif level == 2 and m < 2:
                parts = ((mine.at[rows_at(x * 256 + (1 - y) * 128, 128)], theirs.at[pl.ds(256, 128)], to_y),)
            elif level == 2:
                parts = ((mine.at[rows_at((1 - x) * 256 + y * 128, 128)], theirs.at[pl.ds(256, 128)], to_x),)
            elif level == 3:
                start = x * 256 + y * 128 + (1 - b0) * 64
                parts = ((mine.at[rows_at(start, 64)], theirs.at[pl.ds(384, 64)], to_low),)
            else:
                start = x * 256 + y * 128 + b0 * 64 + (1 - b1) * 32
                parts = ((mine.at[rows_at(start, 32)], theirs.at[pl.ds(448, 32)], to_high),)
            for n, (src, dst, peer) in enumerate(parts):
                copies.append(remote(src, dst, dense_send.at[level, m, n], dense_recv.at[level, m, n], peer))
        return copies

    small_peers = (to_core, to_x, to_y, to_low, to_high)

    def begin(level):
        for sem in {0: (0,), 1: (1, 2), 2: (), 3: (3,), 4: (4,)}[level]:
            pl.semaphore_wait(ready.at[sem], 1)
        for copy in level_copies(level):
            copy.start()
        small_step(level, small_peers[level]).start()

    def add_rows(m, start, size, got):
        where = rows_at(start, size)
        dense[core, m, where, :] += got

    def end(level):
        for copy in level_copies(level):
            copy.wait()
        small_step(level, small_peers[level]).wait()
        if level < 4:
            keep[level + 1] = keep[level] + s_got[level]
        for m in range(4):
            if level == 0:
                for h in range(2):
                    add_rows(m, h * 256, 256, slopes[m * 512 + h * 256:m * 512 + h * 256 + 256])
            elif level == 1 and m < 2:
                add_rows(m, x * 256, 256, dense[other, m, 0:256])
            elif level == 1:
                for xx in range(2):
                    add_rows(m, xx * 256 + y * 128, 128, dense[other, m, xx * 128:xx * 128 + 128])
            elif level == 2:
                add_rows(m, x * 256 + y * 128, 128, dense[other, m, 256:384])
            elif level == 3:
                add_rows(m, x * 256 + y * 128 + b0 * 64, 64, dense[other, m, 384:448])
            else:
                where = rows_at(x * 256 + y * 128 + b0 * 64 + b1 * 32, 32)
                dense_out[m] = dense[core, m, where, :].astype(F32) + dense[other, m, 448:480].astype(F32)
        if level == 0:
            for sem, peer in enumerate(small_peers[1:], 1):
                pl.semaphore_signal(ready.at[sem], inc=1, device_id=peer, device_id_type=MESH)
        if level == 4:
            small_out[...] = keep[4] + s_got[4]

    begin(0)
    far_arrive(3)
    advance(1, 3)
    advance(2, 2)
    collect(3)
    gain_step(0, to_low).wait()
    keep[6, pl.ds(0, 8)] = keep[5, pl.ds(0, 8)] + g_got[0]
    gain_step(1, to_high).start()
    for copy in fetch(0, 0, 0):
        copy.start()
    for k in range(1, groups):
        routed = norms[1, k].astype(F32)
        stream[k - 1] = routed
        norms[0, k] = (norm_parts(routed)[0] * gain_first[...]).astype(BF)

    def forward_others(c, slot):
        def one_group(k, carry):
            mid = gelu_pair(dot(norms[0, k + 1], w_held[slot]))[0].astype(BF)
            stream[k] += dot(mid, w_held[2 + slot])
            return carry

        lax.fori_loop(0, groups - 1, one_group, 0)

        @pl.when(c == 1)
        def _():
            end(0)
            begin(1)

    stream_tiles(0, None, forward_others)
    col = pl.multiple_of(b * width, width)
    shards = []
    for i, s in enumerate((1, 0)):
        shards.append((
            pltpu.make_async_copy(ups[s].at[0, :, pl.ds(col, width)], w_held.at[2 * i], w_sems.at[2 * i]),
            pltpu.make_async_copy(downs[s].at[0, pl.ds(col, width), :], w_held.at[2 * i + 1], w_sems.at[2 * i + 1]),
        ))
    for pair in shards:
        for copy in pair:
            copy.start()
    for k in range(1, groups):
        norms[1, k] = (norm_parts(stream[k - 1])[0] * gain_second[...]).astype(BF)
    gain_step(1, to_high).wait()
    gains_out[...] = keep[6, pl.ds(0, 8)] + g_got[1]

    quarter = wide // 4
    every = groups * many

    def down_stage(slot):
        return outbox.at[pl.ds(pl.multiple_of(slot * quarter, 16), quarter)]

    def stage_copies(s, c, slot):
        cols = pl.ds(pl.multiple_of(c * quarter, quarter), quarter)
        return (
            pltpu.make_async_copy(down_stage(slot), (down_one, down_two)[s].at[0, cols], out_sem.at[slot, 0]),
            pltpu.make_async_copy(up_stage.at[slot], (up_one, up_two)[s].at[0, :, cols], out_sem.at[slot, 1]),
        )

    chunks = width // quarter

    def weight_phase(i, carry):
        s = 1 - i

        def turn(d, carry):
            cols = pl.ds(pl.multiple_of(d * 128, 128), 128)
            turned[cols, :] = norms[s, :, :, cols].reshape(every, 128).T
            return carry

        lax.fori_loop(0, wide // 128, turn, 0)
        for n in range(2):
            @pl.when(i == n)
            def _(n=n):
                for copy in shards[n]:
                    copy.wait()
                if n == 0:
                    ring(1, 3).wait_recv()
                    advance(2, 3)
                else:
                    ring(2, 3).wait_recv()

        def chunk(c, carry):
            cols = pl.ds(pl.multiple_of(c * quarter, quarter), quarter)

            def one_group(k, carry):
                where = pl.ds(pl.multiple_of(k * 2 * many, 16), 2 * many)
                two = pl.ds(2 * k, 2)
                mid, slope = gelu_pair(dot(norms[s, two].reshape(2 * many, wide), w_held[2 * i, :, cols]))
                middles[0, where, :] = mid.astype(BF)
                grad_mid = dot(grads[s, two].reshape(2 * many, wide), w_held[2 * i + 1, cols, :], ((1,), (1,)))
                middles[1, where, :] = (grad_mid * slope).astype(BF)
                return carry

            lax.fori_loop(0, groups // 2, one_group, 0)
            slot = lax.rem(c, 2)

            @pl.when(i * chunks + c > 1)
            def _():
                for copy in stage_copies(0, 0, slot):
                    copy.wait()

            down_stage(slot)[...] = dot(middles[0], grads[s].reshape(every, wide), ((0,), (0,))).astype(BF)
            up_stage[slot] = dot(turned[...], middles[1]).astype(BF)
            for n in range(2):
                @pl.when(s == n)
                def _(n=n):
                    for copy in stage_copies(n, c, slot):
                        copy.start()
            for (at_i, at_c), hook in hooks.items():
                pl.when((i == at_i) & (c == at_c))(hook)
            return carry

        lax.fori_loop(0, chunks, chunk, 0)
        return carry

    def next_level(level):
        def hook():
            end(level)
            begin(level + 1)
        return hook

    hooks = {(0, 0): next_level(1), (0, 2): next_level(2), (1, 0): next_level(3)}
    lax.fori_loop(0, 2, weight_phase, 0)
    end(4)
    for slot in range(2):
        for copy in stage_copies(0, 0, slot):
            copy.wait()
    for t in range(3):
        for j in range(1, groups):
            ring(t, j).wait_send()
    each_peer(lambda p: far(groups - 1, p).wait_send())


def dense_product(dense, which, turned, right):
    block = 32

    def one_batch(g, carry):
        rows = pl.ds(pl.multiple_of(g * 8 * block, 8 * block), 8 * block)
        product = dot(turned[rows, :], right[...]).astype(BF)
        shift = (lax.rem(g, 2) * 2 + g // 2) * block
        for e in range(8):
            place = pl.multiple_of(((e // 2) % 2 * 2 + e // 4) * 4 * block + shift, block)
            dense[e % 2, which, pl.ds(place, block)] = product[e * block:(e + 1) * block]
        return carry

    lax.fori_loop(0, 4, one_batch, 0)


def layer(
    ends, routes_row, tokens, cotangent, gain, cents, gain_first, gain_second, weights, expert_weights, slots, capacity,
):
    count, wide = tokens.shape
    experts, docs, groups = cents.shape[0], ends.shape[1], lax.axis_size("batch")
    many, ff = experts * capacity, expert_weights[0].shape[2]
    width, tiles = ff // groups, ff // wide
    vmem = pl.BlockSpec(memory_space=pltpu.VMEM)
    anys = pl.BlockSpec(memory_space=pl.ANY)
    low_out = jax.ShapeDtypeStruct((1, wide, width), BF)
    dma = pltpu.SemaphoreType.DMA
    return pl.pallas_call(
        functools.partial(layer_kernel, experts, groups, slots, capacity, docs, width, tiles),
        out_shape=(
            jax.ShapeDtypeStruct((count, wide), BF),
            jax.ShapeDtypeStruct((count, wide), F32),
            jax.ShapeDtypeStruct((4, 32, wide), F32),
            jax.ShapeDtypeStruct((8 + experts, wide), F32),
            jax.ShapeDtypeStruct((8, wide), F32),
            low_out, low_out, low_out, low_out,
            jax.ShapeDtypeStruct((groups, count, wide), BF),
            jax.ShapeDtypeStruct((groups, experts, slots, wide), BF),
        ),
        in_specs=[pl.BlockSpec(memory_space=pltpu.SMEM)] + [vmem] * 7 + [anys] * 8,
        out_specs=(vmem,) * 5 + (anys,) * 6,
        scratch_shapes=[
            pltpu.VMEM((4, wide, wide), BF),
            pltpu.VMEM((2 * tiles * many, wide), BF),
            pltpu.VMEM((3, many, wide), F32),
            pltpu.VMEM((2, groups, many, wide), BF),
            pltpu.VMEM((2, groups, many, wide), BF),
            pltpu.VMEM((count, wide), BF),
            pltpu.VMEM((count, wide), BF),
            pltpu.VMEM((5, count, wide), BF),
            pltpu.VMEM((count, wide), F32),
            pltpu.VMEM((groups, experts * slots, count), BF),
            pltpu.VMEM((many, experts * slots), BF),
            pltpu.VMEM((groups, 1, count), jnp.int32),
            pltpu.VMEM((2, 2, experts, slots, wide), BF),
            pltpu.VMEM((max(2 * experts * slots, 3 * count), wide), BF),
            pltpu.VMEM((2, 4, wide // 2, wide), BF),
            pltpu.VMEM((wide, groups * many), BF),
            pltpu.VMEM((2, groups * many, wide // 4), BF),
            pltpu.VMEM((2, wide, wide // 4), BF),
            pltpu.VMEM((7, 16, wide), F32),
            pltpu.VMEM((5, 16, wide), F32),
            pltpu.VMEM((2, 8, wide), F32),
            dma((4,)), dma((2,)), dma((2, 2, experts)), dma((2, 2, experts)), dma((groups, experts)), dma((groups, experts)),
            dma((groups,)), dma((groups,)),
            dma((3, groups)), dma((3, groups)), dma((5, 4, 2)), dma((5, 4, 2)), dma((5,)), dma((5,)),
            dma((2,)), dma((2,)), pltpu.SemaphoreType.REGULAR((5,)), dma((2, 2)),
        ],
        compiler_params=pltpu.CompilerParams(
            collective_id=1, has_side_effects=True, vmem_limit_bytes=64 * 1024 * 1024 - 65536
        ),
        name="layer",
    )(
        ends, routes_row, tokens, cotangent, gain, cents, gain_first, gain_second, *weights, *expert_weights,
    )


def hand_out_kernel(*refs):
    dense, small, gains = refs[:3]
    sources, results = refs[3:9], refs[9:]
    for i, source in enumerate(sources):
        results[i][...] = source[...].astype(results[i].dtype)

    @pl.when(pl.program_id(0) == 0)
    def _():
        for m in range(4):
            results[6 + m][...] = dense[m]
        results[10][...] = small[0:1, :]
        results[11][...] = small[8:, :]
        part = results[12].shape[1]
        where = pl.ds(pl.multiple_of(lax.axis_index("batch") * part, 128), part)
        for s in range(2):
            results[12 + s][...] = gains[s:s + 1, where]


def hand_out(dense, small, gains, *arrays):
    wide, steps = small.shape[1], 2

    def whole(shape):
        return pl.BlockSpec(shape, lambda i: (0,) * len(shape))

    def sliced(array):
        shape = array.shape[:-2] + (array.shape[-2] // steps, array.shape[-1])
        return pl.BlockSpec(shape, lambda i: (0,) * (len(shape) - 2) + (i, 0))

    shapes = [dense.shape[1:]] * 4 + [(1, wide), (small.shape[0] - 8, wide)] + [(1, wide // lax.axis_size("batch"))] * 2
    moved = [sliced(array) for array in arrays]
    return pl.pallas_call(
        hand_out_kernel,
        grid=(steps,),
        out_shape=tuple(jax.ShapeDtypeStruct(array.shape, BF if i == 4 else F32) for i, array in enumerate(arrays))
        + tuple(jax.ShapeDtypeStruct(shape, F32) for shape in shapes),
        in_specs=[whole(array.shape) for array in (dense, small, gains)] + moved,
        out_specs=tuple(moved) + tuple(whole(shape) for shape in shapes),
        compiler_params=pltpu.CompilerParams(vmem_limit_bytes=64 * 1024 * 1024 - 65536),
        name="hand_out",
    )(dense, small, gains, *arrays)


def per_device(
    tokens, doc_ends, routes, w_query, w_key, w_value, w_output, attn_gain, centroids,
    up_first, down_first, gain_first, up_second, down_second, gain_second, cotangent,
):
    count, wide = tokens.shape
    experts, groups = lax.axis_size("expert"), lax.axis_size("batch")
    capacity = 11 * count // (8 * experts)
    slots = -(-capacity // 16) * 16
    routes_row = routes.reshape(1, count)
    gain = attn_gain[None]
    weights = (w_query, w_key, w_value, w_output)
    expert_weights = (up_first, down_first, up_second, down_second)
    if groups == 4 and experts == 8:
        block_out, grad_tokens, dense, small, gains, *parts = layer(
            doc_ends, routes_row, tokens, cotangent, gain, centroids, gain_first, gain_second, weights, expert_weights,
            slots, capacity,
        )
        (
            up_one, down_one, up_two, down_two, block_out, grad_tokens, *dense, small_gain, small_cents, gain_one, gain_two,
        ) = hand_out(dense, small, gains, *parts[:4], block_out, grad_tokens)
        return (
            block_out, grad_tokens, *dense, small_gain.reshape(wide), small_cents,
            up_one, down_one, gain_one, up_two, down_two, gain_two,
        )
    *kept, out_rows = enter(doc_ends, routes_row, tokens, cotangent, gain, centroids, weights, slots)

    def exchange(blocks):
        return lax.all_to_all(blocks, "expert", split_axis=1, concat_axis=1, tiled=True)

    came = exchange(out_rows).reshape(2, experts * slots, wide)
    back, rows, gains = chain(came, *expert_weights, gain_first, gain_second, slots, capacity)
    came_back = exchange(back.reshape(out_rows.shape)).reshape(back.shape)
    block_out, grad_tokens, dense, small = leave(
        doc_ends, routes_row, tokens, cotangent, gain, centroids, kept, came_back, weights, slots
    )
    dense = scatter_sum(dense).astype(F32)
    small = all_sum(small)
    parts = []
    for s, (up, down) in enumerate(((up_first, down_first), (up_second, down_second))):
        for part in weight_grads(ring_rows(rows[0, s], "batch"), ring_rows(rows[1, s], "batch"), up[0], down[0]):
            parts.append(part[None])
    gains = jnp.sum(lax.all_gather(gains[:2], "batch"), axis=0)
    gain_part = wide // groups
    gains = lax.dynamic_slice_in_dim(gains, lax.axis_index("batch") * gain_part, gain_part, 1)
    return (
        block_out, grad_tokens, dense[0], dense[1], dense[2], dense[3], small[0], small[8:],
        parts[0], parts[1], gains[0:1], parts[2], parts[3], gains[1:2],
    )


def solution(mesh):
    return jax.shard_map(
        per_device,
        mesh=mesh,
        in_specs=(
            P(("batch", "expert"), None),
            P(("batch", "expert"), None),
            P(("batch", "expert"), None),
            P(),
            P(),
            P(),
            P(),
            P(),
            P(),
            P("expert", None, None),
            P("expert", None, None),
            P("expert", None),
            P("expert", None, None),
            P("expert", None, None),
            P("expert", None),
            P(("batch", "expert"), None),
        ),
        out_specs=(
            P(("batch", "expert"), None),
            P(("batch", "expert"), None),
            P(("batch", "expert"), None),
            P(("batch", "expert"), None),
            P(("batch", "expert"), None),
            P(("batch", "expert"), None),
            P(),
            P(),
            P("expert", None, "batch"),
            P("expert", "batch", None),
            P("expert", "batch"),
            P("expert", None, "batch"),
            P("expert", "batch", None),
            P("expert", "batch"),
        ),
        check_vma=False,
    )
```
